32 devices in a mesh: fsdp: 4 (over y, core), ctx: 2 (over x), tp: 4 (over z).
Axes of the slice: x: 2, y: 2, z: 4, core: 2. Of those that a mesh axis runs over, the one named last changes fastest.
Arguments:
- tokens: bfloat16 [8, 1024, 1024], P('fsdp', 'ctx'), may hold values from -16 to 16
- gain1: bfloat16 [1024], P('fsdp'), may hold values from 0.5 to 1.5
- w_latent: bfloat16 [1024, 512], P('fsdp'), may hold values from -0.1875 to 0.1875
- w_query: bfloat16 [1024, 1024], P('fsdp', 'tp'), may hold values from -0.1875 to 0.1875
- w_key: bfloat16 [256, 1024], P('fsdp', 'tp'), may hold values from -0.375 to 0.375
- w_value: bfloat16 [256, 1024], P('fsdp', 'tp'), may hold values from -0.375 to 0.375
- w_out: bfloat16 [1024, 1024], P('tp', 'fsdp'), may hold values from -1.5 to 1.5
- gain2: bfloat16 [1024], P('fsdp'), may hold values from 0.5 to 1.5
- w_gate: bfloat16 [1024, 2816], P('fsdp', 'tp'), may hold values from -0.1875 to 0.1875
- w_up: bfloat16 [1024, 2816], P('fsdp', 'tp'), may hold values from -0.1875 to 0.1875
- w_down: bfloat16 [2816, 1024], P('tp', 'fsdp'), may hold values from -0.109375 to 0.109375
- segments: int32 [8, 1024], P('fsdp', 'ctx'), may hold values from 0 to 7, never falling along the last dimension, each value on 1 to 512 neighbouring positions
- cotangent: bfloat16 [8, 1024, 1024], P('fsdp', 'ctx'), may hold values from -6 to 6
Outputs:
- mixed: bfloat16 [8, 1024, 1024], P('fsdp', 'ctx')
- grad_tokens: bfloat16 [8, 1024, 1024], P('fsdp', 'ctx')
- grad_gain1: float32 [1024], P('fsdp')
- grad_latent: float32 [1024, 512], P('fsdp')
- grad_query: float32 [1024, 1024], P('fsdp', 'tp')
- grad_key: float32 [256, 1024], P('fsdp', 'tp')
- grad_value: float32 [256, 1024], P('fsdp', 'tp')
- grad_out: float32 [1024, 1024], P('tp', 'fsdp')
- grad_gain2: float32 [1024], P('fsdp')
- grad_gate: float32 [1024, 2816], P('fsdp', 'tp')
- grad_up: float32 [1024, 2816], P('fsdp', 'tp')
- grad_down: float32 [2816, 1024], P('tp', 'fsdp')
- stats: float32 [8, 3], P('fsdp')
- grad_radial: float32 [8, 1024], P('fsdp', 'ctx')
The draws below stay inside these ranges and needn't reach their ends.
Inputs may be any that keep to these rules, and one draw needn't show every extreme that they name: `segments`: ids never fall along a sequence; every id of 0 to 7 names 1 to 512 consecutive tokens of each sequence, and some id names exactly 512; the largest id of a sequence marks its padding.
All inputs are finite; a program needn't handle non-finite values.
Results may differ from the reference program's by a relative error of at most 0.013.
The reference program's roundings to bfloat16 on the way count: a program that leaves them out, or rounds other values in their place, can miss the bound.
Values may be sent and summed in bfloat16 or wider, within the bound.
A program may use at most 128 MiB of HBM per device.

```python
import math
import jax
import jax.numpy as jnp
import numpy as np
from jax import lax

D = 1024
HEADS = 16
HEAD_DIM = 64
GROUPS = 2
LATENT = 256
FF = 2816
SEQS = 8
LENGTH = 1024
SEG_COUNT = 8
MOST_LEN = 512


def draw_tokens(key, part):
    first_key, second_key = jax.random.split(key)
    place = (jnp.arange(LENGTH, dtype=jnp.float32) / LENGTH).reshape(1, LENGTH, 1)
    falling = jnp.exp(-place * math.log(3.0)) * 3.0
    base = jnp.clip(jax.random.normal(first_key, (SEQS, LENGTH, D), jnp.float32), -5.0, 5.0)
    spread = jnp.exp(jax.random.uniform(second_key, (SEQS, LENGTH, 1), jnp.float32, 0.0, math.log(4.0)))
    return (base * falling * spread * 0.25).astype(jnp.bfloat16)


def shard_levels(rng, dims, shards, least, top_value):
    loudness = 1.0
    for dim, parts in shards:
        steps = jax.random.uniform(jax.random.fold_in(jax.random.fold_in(rng, 6), dim), (parts,), jnp.float32, least / len(shards), top_value / len(shards))
        loudness = loudness * jnp.repeat(jnp.exp(steps), dims[dim] // parts).reshape((-1,) + (1,) * (len(dims) - 1 - dim))
    return loudness


def split_up(count, total, bound, skew):
    portions = [(1 << 20) // math.isqrt(standing ** skew) + 1 for standing in range(2, count + 1)]
    surplus, given = total - bound - (count - 1), [1] * (count - 1)
    while surplus > 0:
        free = [i for i in range(count - 1) if given[i] < bound]
        pool, left = sum([portions[i] for i in free]), surplus
        for i in free:
            extra = min(bound - given[i], max(1, left * portions[i] // pool), surplus)
            given[i] = given[i] + extra
            surplus = surplus - extra
    return np.array([bound] + given)


def uneven(own_key, amount, total, most, slope):
    if amount == 2:
        one = jax.random.randint(own_key, (), max(1, total - most), min(most, total - 1) + 1)
        return jnp.stack([one, total - one])
    sizes = jnp.asarray(split_up(amount, total, most, slope), jnp.int32)
    pairs = (amount - 1) // 2
    source_of, sink = sizes[1:1 + 2 * pairs:2], sizes[2:2 + 2 * pairs:2]
    slack = jnp.minimum(source_of - 1, most - sink)
    passed = jax.random.randint(jax.random.fold_in(own_key, 1), (pairs,), 0, 1 << 20) % (slack + 1)
    sizes = sizes.at[1:1 + 2 * pairs:2].set(source_of - passed).at[2:2 + 2 * pairs:2].set(sink + passed)
    return sizes[jax.random.permutation(jax.random.fold_in(own_key, 2), amount)]


def centred(stream_key, dims, deviation, limit, cuts=(), kind=jnp.bfloat16):
    values = jax.random.normal(stream_key, dims, jnp.float32) * deviation
    if len(cuts) > 0:
        values = shard_levels(stream_key, dims, cuts, -0.22, 0.18) * values
    return jnp.clip(values, min=-limit, max=limit).astype(kind)


def setup_inputs(seed: int = 0) -> dict:
    seeds = jax.random.split(jax.random.key(seed), 14)
    tokens = draw_tokens(jax.random.fold_in(seeds[13], 71), 0)
    gain1 = jnp.clip(1.0 + 0.1 * jax.random.normal(seeds[1], (D,), jnp.float32), 0.5, 1.5).astype(jnp.bfloat16)
    w_latent = centred(seeds[2], (D, GROUPS * LATENT), D ** -0.5, 0.1875, ((0, 4),))
    w_query = centred(seeds[3], (D, HEADS * HEAD_DIM), D ** -0.5, 0.1875, ((0, 4), (1, 4)))
    w_key = centred(seeds[4], (LATENT, HEADS * HEAD_DIM), LATENT ** -0.5, 0.375, ((0, 4), (1, 4)))
    w_value = centred(seeds[5], (LATENT, HEADS * HEAD_DIM), LATENT ** -0.5, 0.375, ((0, 4), (1, 4)))
    w_out = centred(seeds[6], (HEADS * HEAD_DIM, D), (HEADS * HEAD_DIM // 64) ** -0.5, 1.5, ((0, 4), (1, 4)))
    gain2 = jnp.clip(1.0 + 0.1 * jax.random.normal(seeds[7], (D,), jnp.float32), 0.5, 1.5).astype(jnp.bfloat16)
    w_gate = centred(seeds[8], (D, FF), D ** -0.5, 0.1875, ((0, 4), (1, 4)))
    w_up = centred(seeds[9], (D, FF), D ** -0.5, 0.1875, ((0, 4), (1, 4)))
    w_down = centred(seeds[10], (FF, D), FF ** -0.5, 0.109375, ((0, 4), (1, 4)))
    segments = jax.vmap(lambda own: jnp.searchsorted(jnp.cumsum(uneven(own, SEG_COUNT, LENGTH, MOST_LEN, 2)), jnp.arange(LENGTH), side="right"))(jax.random.split(seeds[11], SEQS)).reshape((SEQS, LENGTH)).astype(jnp.int32)
    cotangent = centred(seeds[12], (SEQS, LENGTH, D), 1.0, 6.0, ((0, 4), (1, 2)))
    return dict(tokens=tokens, gain1=gain1, w_latent=w_latent, w_query=w_query, w_key=w_key, w_value=w_value, w_out=w_out, gain2=gain2, w_gate=w_gate, w_up=w_up, w_down=w_down, segments=segments, cotangent=cotangent)


@jax.custom_vjp
def low(v):
    return lax.optimization_barrier(v.astype(jnp.bfloat16)).astype(jnp.float32)

@jax.custom_vjp
def low_back(v):
    return v

def low_keep(v):
    return (low(v), None)

def low_pass(kept, grad):
    return (grad,)

def back_keep(v):
    return (v, None)

def back_low(kept, grad):
    return (low(grad),)
low.defvjp(low_keep, low_pass)
low_back.defvjp(back_keep, back_low)
eps = 1e-05

def rounded_both(value):
    return low_back(low(value))

def matmul(left, right):
    return jnp.dot(left, right, precision=lax.Precision.HIGHEST)

def attend(query, keys, values, seg_row):
    q_block = min(512, LENGTH)
    n_block = LENGTH // q_block
    places = jnp.arange(LENGTH, dtype=jnp.int32)

    def one_block(packed):
        q_part, q_place, q_seg = packed
        scores = jnp.einsum('qhd,khd->hqk', q_part, keys, precision=lax.Precision.HIGHEST) * 0.125
        scores = low_back(scores)
        counted = (places[None, :] <= q_place[:, None]) & (seg_row[None, :] == q_seg[:, None])
        masked = jnp.where(counted[None], scores, -1e+30)
        top = lax.optimization_barrier(jnp.max(masked, axis=-1, keepdims=True))
        lse = top + jnp.log(lax.optimization_barrier(jnp.sum(jnp.exp(masked - top), axis=-1, keepdims=True)))
        probs = jnp.where(counted[None], jnp.exp(masked - lse), 0.0)
        result = jnp.einsum('hqk,khd->qhd', low(probs), values, precision=lax.Precision.HIGHEST)
        return rounded_both(result)
    outputs = lax.map(jax.checkpoint(one_block), (query.reshape(n_block, q_block, HEADS, HEAD_DIM), places.reshape(n_block, q_block), seg_row.reshape(n_block, q_block)))
    return outputs.reshape(LENGTH, HEADS, HEAD_DIM)

def layer(stream, gain_one, w_lat, w_qry, w_kproj, w_vproj, w_outp, gain_two, w_gatep, w_upp, w_downp, seg_ids):
    r_one = lax.rsqrt(lax.optimization_barrier(jnp.mean(stream * stream, axis=-1, keepdims=True)) + eps)
    xn_one = low(stream * r_one * gain_one)
    latent = low(matmul(xn_one, w_lat))
    query = rounded_both(matmul(xn_one, w_qry)).reshape(SEQS, LENGTH, HEADS, HEAD_DIM)
    lat_groups = latent.reshape(SEQS, LENGTH, GROUPS, LATENT)
    key_four = w_kproj.reshape(LATENT, GROUPS, HEADS // GROUPS, HEAD_DIM)
    val_four = w_vproj.reshape(LATENT, GROUPS, HEADS // GROUPS, HEAD_DIM)
    keys = rounded_both(jnp.einsum('slgc,cgjd->slgjd', lat_groups, key_four, precision=lax.Precision.HIGHEST)).reshape(SEQS, LENGTH, HEADS, HEAD_DIM)
    values = rounded_both(jnp.einsum('slgc,cgjd->slgjd', lat_groups, val_four, precision=lax.Precision.HIGHEST)).reshape(SEQS, LENGTH, HEADS, HEAD_DIM)

    def per_sequence(packed):
        return attend(packed[0], packed[1], packed[2], packed[3])
    attended = lax.map(per_sequence, (query, keys, values, seg_ids))
    branch = low_back(matmul(attended.reshape(SEQS, LENGTH, HEADS * HEAD_DIM), w_outp))
    middle = stream + branch
    r_two = lax.rsqrt(lax.optimization_barrier(jnp.mean(middle * middle, axis=-1, keepdims=True)) + eps)
    xn_two = low(middle * r_two * gain_two)
    gate = low_back(matmul(xn_two, w_gatep))
    upper = low_back(matmul(xn_two, w_upp))
    hidden = low(jax.nn.silu(gate) * upper)
    feed = low_back(matmul(hidden, w_downp))
    return (middle + feed, (branch, feed))

def reference(tokens, gain1, w_latent, w_query, w_key, w_value, w_out, gain2, w_gate, w_up, w_down, segments, cotangent):
    params = (tokens, gain1, w_latent, w_query, w_key, w_value, w_out, gain2, w_gate, w_up, w_down)
    params = tuple((item.astype(jnp.float32) for item in params))

    def forward(*values):
        return layer(*values, segments)
    mixed, pullback, extras = jax.vjp(forward, *params, has_aux=True)
    branch, feed = extras
    grads = pullback(cotangent.astype(jnp.float32))
    valid = (segments != segments[:, -1:]).astype(jnp.float32)[:, :, None]
    total = lax.optimization_barrier(jnp.sum(valid, axis=(1, 2)))[:, None] * D
    squares = jnp.stack([lax.optimization_barrier(jnp.sum(valid * mixed * mixed, axis=(1, 2))), lax.optimization_barrier(jnp.sum(valid * branch * branch, axis=(1, 2))), lax.optimization_barrier(jnp.sum(valid * feed * feed, axis=(1, 2)))], axis=1)
    stats = jnp.sqrt(squares / total)
    stream = params[0]
    unit_one = stream * lax.rsqrt(lax.optimization_barrier(jnp.mean(stream * stream, axis=-1, keepdims=True)) + eps)
    radial = lax.optimization_barrier(jnp.sum(unit_one * grads[0], axis=-1)) / jnp.sqrt(jnp.float32(D))
    return (mixed.astype(jnp.bfloat16), grads[0].astype(jnp.bfloat16), grads[1], grads[2], grads[3], grads[4], grads[5], grads[6], grads[7], grads[8], grads[9], grads[10], stats, radial)
```

```python
import jax
import jax.numpy as jnp
from jax import lax
from jax.experimental import pallas as pl
from jax.experimental.pallas import tpu as pltpu
from jax.sharding import PartitionSpec as P

HEADS = 16
HEAD_DIM = 64
GROUPS = 2
LATENT = 256
MESH = pl.DeviceIdType.MESH
VMEM = pl.BlockSpec(memory_space=pltpu.VMEM)
F32 = jnp.float32
BF16 = jnp.bfloat16

eps = 1e-05


def remote(src, dst, send_sem, recv_sem, device):
    return pltpu.make_async_remote_copy(
        src_ref=src,
        dst_ref=dst,
        send_sem=send_sem,
        recv_sem=recv_sem,
        device_id=device,
        device_id_type=MESH,
    )


def wait_sent(ref, sem, recv_sem):
    remote(ref, ref, sem, recv_sem, {"tp": lax.axis_index("tp")}).wait_send()


def wait_came(ref, send_sem, sem):
    remote(ref, ref, send_sem, sem, {"tp": lax.axis_index("tp")}).wait_recv()


def meet(line=0, fsdp=0, ctx=0):
    barrier = pltpu.get_barrier_semaphore()

    def greet(device):
        pl.semaphore_signal(barrier, inc=1, device_id=device, device_id_type=MESH)

    known = 0
    if fsdp:
        f = lax.axis_index("fsdp")
        greet({"fsdp": sibling(f)})
        for k in range(1, fsdp // 2):
            greet({"fsdp": lax.rem(f + 2 * k, fsdp)})
        known += fsdp // 2
    if ctx:
        x = lax.axis_index("ctx")
        for k in range(1, ctx):
            greet({"ctx": lax.rem(x + k, ctx)})
        known += ctx - 1
    if line > 1:
        me = lax.axis_index("tp")

        @pl.when(me > 0)
        def _():
            greet({"tp": me - 1})

        @pl.when(me < line - 1)
        def _():
            greet({"tp": me + 1})

        @pl.when((me > 0) & (me < line - 1))
        def _():
            pl.semaphore_wait(barrier, known + 2)

        @pl.when((me == 0) | (me == line - 1))
        def _():
            pl.semaphore_wait(barrier, known + 1)

    else:
        pl.semaphore_wait(barrier, known)


def sibling(f):
    return f + 1 - 2 * lax.rem(f, 2)


def block(ref, axis, index, size):
    at = pl.ds(pl.multiple_of(index * size, size), size)
    return ref.at[at] if axis == 0 else ref.at[:, at]


class Spread:
    def __init__(self, fsdp, pairs, axes, recv, sent, own):
        self.fsdp, self.pairs, self.axes = fsdp, pairs, axes
        self.recv, self.sent, self.own = recv, sent, own
        self.f = lax.axis_index("fsdp")

    def size(self, a):
        return self.pairs[a][0].shape[self.axes[a]]

    def target(self, a, f):
        return block(self.pairs[a][1], self.axes[a], f, self.size(a))

    def start(self):
        f = self.f
        for a, (src, dst) in enumerate(self.pairs):
            for k in range(1, self.fsdp // 2):
                remote(src, self.target(a, f), self.sent.at[a], self.recv.at[a, f],
                       {"fsdp": lax.rem(f + 2 * k, self.fsdp)}).start()
        for a, (src, dst) in enumerate(self.pairs):
            remote(src, self.target(a, f), self.sent.at[a], self.recv.at[a, f],
                   {"fsdp": sibling(f)}).start()
            pltpu.make_async_copy(src, self.target(a, f), self.own.at[a]).start()

    def relay(self):
        for a in range(len(self.pairs)):
            for k in range(1, self.fsdp // 2):
                other = lax.rem(self.f + 2 * k, self.fsdp)
                here = self.target(a, other)
                wait_came(here, self.sent.at[a], self.recv.at[a, other])
                remote(here, here, self.sent.at[a], self.recv.at[a, other],
                       {"fsdp": sibling(self.f)}).start()

    def finish(self):
        for a, (src, dst) in enumerate(self.pairs):
            for k in range(0, self.fsdp // 2):
                other = lax.rem(sibling(self.f) + 2 * k, self.fsdp)
                wait_came(self.target(a, other), self.sent.at[a], self.recv.at[a, other])
            pltpu.make_async_copy(src, self.target(a, self.f), self.own.at[a]).wait()
            many = (self.fsdp - 1) * self.size(a)
            ref = dst.at[pl.ds(0, many)] if self.axes[a] == 0 else dst.at[:, pl.ds(0, many)]
            wait_sent(ref, self.sent.at[a], self.recv.at[a, 0])

    @staticmethod
    def scratch(fsdp, arrays):
        return [
            pltpu.SemaphoreType.DMA((arrays, fsdp)),
            pltpu.SemaphoreType.DMA((arrays,)),
            pltpu.SemaphoreType.DMA((arrays,)),
        ]


class CtxShare:
    def __init__(self, ctx, src, dst, recv, sent, own):
        self.ctx, self.src, self.dst = ctx, src, dst
        self.recv, self.sent, self.own = recv, sent, own
        self.x = lax.axis_index("ctx")

    def start(self):
        for k in range(1, self.ctx):
            remote(self.src, self.dst.at[self.x], self.sent.at[k - 1], self.recv.at[self.x],
                   {"ctx": lax.rem(self.x + k, self.ctx)}).start()
        pltpu.make_async_copy(self.src, self.dst.at[self.x], self.own).start()

    def finish(self):
        for k in range(1, self.ctx):
            other = lax.rem(self.x + k, self.ctx)
            wait_came(self.dst.at[other], self.sent.at[k - 1], self.recv.at[other])
            wait_sent(self.src, self.sent.at[k - 1], self.recv.at[other])
        pltpu.make_async_copy(self.src, self.dst.at[self.x], self.own).wait()

    @staticmethod
    def scratch(ctx):
        return [
            pltpu.SemaphoreType.DMA((ctx,)),
            pltpu.SemaphoreType.DMA((ctx,)),
            pltpu.SemaphoreType.DMA,
        ]


class LineGather:
    def __init__(self, n, chunk, src, dst, recv, sent, own):
        self.n, self.chunk, self.src, self.dst = n, chunk, src, dst
        self.width = src.shape[1]
        self.count = src.shape[0] // chunk
        self.recv, self.sent, self.own = recv, sent, own
        self.me = lax.axis_index("tp")

    def steps(self):
        return self.n * self.count

    def place(self, tp, at):
        rows = pl.ds(pl.multiple_of(at * self.chunk, self.chunk), self.chunk)
        return self.dst.at[rows, pl.ds(pl.multiple_of(tp * self.width, self.width), self.width)]

    def begin(self):
        pltpu.make_async_copy(
            self.src, self.dst.at[:, pl.ds(pl.multiple_of(self.me * self.width, self.width), self.width)],
            self.own,
        ).start()

    def step(self, s):
        n, me, count = self.n, self.me, self.count
        left, right = {"tp": me - 1}, {"tp": me + 1}

        @pl.when(s < count)
        def _():
            rows = pl.ds(pl.multiple_of(s * self.chunk, self.chunk), self.chunk)

            @pl.when(me > 0)
            def _():
                remote(self.src.at[rows], self.place(me, s), self.sent.at[0], self.recv.at[me, s], left).start()

            @pl.when(me < n - 1)
            def _():
                remote(self.src.at[rows], self.place(me, s), self.sent.at[1], self.recv.at[me, s], right).start()

        @pl.when(s >= count)
        def _():
            away = s // count
            at = s - away * count
            for sign, onward in ((-1, right), (1, left)):
                tp = me + sign * away

                @pl.when((tp >= 0) & (tp < n))
                def _(tp=tp, onward=onward, sign=sign):
                    here = self.place(tp, at)
                    wait_came(here, self.sent.at[2], self.recv.at[tp, at])

                    @pl.when((me < n - 1) if sign < 0 else (me > 0))
                    def _():
                        remote(here, here, self.sent.at[2], self.recv.at[tp, at], onward).start()

    def drain(self):
        n, me = self.n, self.me
        pltpu.make_async_copy(
            self.src, self.dst.at[:, pl.ds(pl.multiple_of(me * self.width, self.width), self.width)],
            self.own,
        ).wait()

        @pl.when(me > 0)
        def _():
            wait_sent(self.src, self.sent.at[0], self.recv.at[0, 0])

        @pl.when(me < n - 1)
        def _():
            wait_sent(self.src, self.sent.at[1], self.recv.at[0, 0])

        @pl.when((me > 0) & (me < n - 1))
        def _():
            wait_sent(self.dst.at[:, pl.ds(0, (n - 1) * self.width)], self.sent.at[2], self.recv.at[0, 0])

    @staticmethod
    def scratch(n, count):
        return [
            pltpu.SemaphoreType.DMA((n, count)),
            pltpu.SemaphoreType.DMA((3,)),
            pltpu.SemaphoreType.DMA,
        ]


class LineSum:
    def __init__(self, n, chunk, hop, part, from_left, from_right, out, recv, sent, finish):
        self.n, self.chunk, self.hop = n, chunk, hop
        self.total_rows = part.shape[0]
        self.owners = (n // 2 - 1, n // 2)
        self.count = self.total_rows // 2 // chunk
        self.part, self.from_left, self.from_right, self.out = part, from_left, from_right, out
        self.recv, self.sent = recv, sent
        self.finish = finish
        self.me = lax.axis_index("tp")

    def steps(self):
        return self.count + self.hop * 2 * (self.n // 2)

    def rows(self, slot, at):
        return pl.ds(pl.multiple_of((slot * self.count + at) * self.chunk, self.chunk), self.chunk)

    def step(self, s):
        n, me, hop = self.n, self.me, self.hop
        left, right = {"tp": me - 1}, {"tp": me + 1}
        reach = n // 2
        for slot, owner in enumerate(self.owners):
            for side in (0, 1):
                lag = me if side == 0 else n - 1 - me
                at = s - hop * lag
                here = (me < owner) if side == 0 else (me > owner)
                held = self.from_left if side == 0 else self.from_right
                to = right if side == 0 else left
                here = here & (at >= 0) & (at < self.count)

                @pl.when(here & (lag == 0))
                def _(at=at, held=held, to=to, side=side, slot=slot):
                    rows = self.rows(slot, at)
                    remote(self.part.at[rows], held.at[rows], self.sent.at[0],
                           self.recv.at[side, slot, at], to).start()

                if n > 2:

                    @pl.when(here & (lag > 0))
                    def _(at=at, held=held, to=to, side=side, slot=slot):
                        rows = self.rows(slot, at)
                        wait_came(held.at[rows], self.sent.at[0], self.recv.at[side, slot, at])
                        held[rows, :] = (held[rows, :].astype(F32) + self.part[rows, :].astype(F32)).astype(BF16)
                        remote(held.at[rows], held.at[rows], self.sent.at[0],
                               self.recv.at[side, slot, at], to).start()

            at = s - hop * reach

            @pl.when((me == owner) & (at >= 0) & (at < self.count))
            def _(at=at, slot=slot, owner=owner):
                rows = self.rows(slot, at)
                total = self.part[rows, :].astype(F32)
                if owner > 0:
                    wait_came(self.from_left.at[rows], self.sent.at[0], self.recv.at[0, slot, at])
                    total = total + self.from_left[rows, :].astype(F32)
                wait_came(self.from_right.at[rows], self.sent.at[0], self.recv.at[1, slot, at])
                total = total + self.from_right[rows, :].astype(F32)
                own = pl.ds(pl.multiple_of(at * self.chunk, self.chunk), self.chunk)
                self.out[rows, :] = self.finish(rows, own, total)
                if owner > 0:
                    remote(self.out.at[rows], self.out.at[rows], self.sent.at[1],
                           self.recv.at[2, slot, at], left).start()
                remote(self.out.at[rows], self.out.at[rows], self.sent.at[2],
                       self.recv.at[2, slot, at], right).start()

        for slot, owner in enumerate(self.owners):
            away = jnp.abs(me - owner)
            at = s - hop * (reach + away)

            @pl.when((me != owner) & (at >= 0) & (at < self.count))
            def _(at=at, slot=slot, owner=owner):
                rows = self.rows(slot, at)
                here = self.out.at[rows]
                wait_came(here, self.sent.at[3], self.recv.at[2, slot, at])

                @pl.when((me < owner) & (me > 0))
                def _():
                    remote(here, here, self.sent.at[3], self.recv.at[2, slot, at], left).start()

                @pl.when((me > owner) & (me < n - 1))
                def _():
                    remote(here, here, self.sent.at[3], self.recv.at[2, slot, at], right).start()

    def drain(self):
        n, me, half = self.n, self.me, self.total_rows // 2
        lo, hi = self.owners

        def wait(sem, size):
            wait_sent(self.part.at[pl.ds(0, size)], self.sent.at[sem], self.recv.at[0, 0, 0])

        middle = (me == lo) | (me == hi)

        @pl.when(middle)
        def _():
            wait(0, half)
            wait(2, half)

        @pl.when((me != lo) & (me != hi))
        def _():
            wait(0, 2 * half)

        if lo > 0:

            @pl.when(middle)
            def _():
                wait(1, half)
                wait(3, half)

            if n > 4:

                @pl.when((me != lo) & (me != hi) & (me > 0) & (me < n - 1))
                def _():
                    wait(3, 2 * half)
        else:

            @pl.when(me == hi)
            def _():
                wait(1, half)

    @staticmethod
    def scratch(n, rows, width, chunk):
        return [
            pltpu.VMEM((rows, width), BF16),
            pltpu.VMEM((rows, width), BF16),
            pltpu.SemaphoreType.DMA((3, 2, rows // 2 // chunk)),
            pltpu.SemaphoreType.DMA((4,)),
        ]


class GradSum:
    def __init__(self, fsdp, ctx, parts, axes, outs, held, recv, sent):
        self.fsdp, self.ctx, self.parts, self.axes, self.outs = fsdp, ctx, parts, axes, outs
        self.ys = fsdp // 2
        self.held, self.recv, self.sent = held, recv, sent
        self.f = lax.axis_index("fsdp")
        self.x = lax.axis_index("ctx")
        self.y, self.c = self.f // 2, lax.rem(self.f, 2)

    @staticmethod
    def block_shape(part, axis, fsdp):
        r, c = part.shape
        return (r // fsdp, c) if axis == 0 else (r, c // fsdp)

    @staticmethod
    def scratch(fsdp, ctx, shapes):
        held = []
        for shape in shapes:
            held += [
                pltpu.VMEM((fsdp // 2,) + shape, BF16),
                pltpu.VMEM((max(fsdp // 2 - 1, 1),) + shape, BF16),
                pltpu.VMEM((ctx,) + shape, BF16),
            ]
        many = max(fsdp // 2, ctx)
        return held, [
            pltpu.SemaphoreType.DMA((len(shapes), 3, many)),
            pltpu.SemaphoreType.DMA((len(shapes), 3, many)),
        ]

    def part(self, a, f):
        shape = self.held[a][0].shape[1:]
        return block(self.parts[a], self.axes[a], f, shape[self.axes[a]])

    def each(self, a, body):
        rows = self.held[a][0].shape[1]
        size = 32 if rows % 32 == 0 else 16

        def step(i, carry):
            body(pl.ds(pl.multiple_of(i * size, size), size))
            return carry

        lax.fori_loop(0, rows // size, step, 0)

    def start(self):
        for a in range(len(self.parts)):
            for k in range(self.ys):
                remote(self.part(a, 2 * k + 1 - self.c), self.held[a][0].at[k], self.sent.at[a, 0, k],
                       self.recv.at[a, 0, k], {"fsdp": sibling(self.f)}).start()

    def second(self):
        for a in range(len(self.parts)):
            first, later = self.held[a][0], self.held[a][1]
            for k in range(self.ys):
                wait_came(first.at[k], self.sent.at[a, 0, k], self.recv.at[a, 0, k])
                mine = self.part(a, 2 * k + self.c)

                def add(rows, first=first, k=k, mine=mine):
                    first[k, rows, :] = (first[k, rows, :].astype(F32) + mine[rows, :].astype(F32)).astype(BF16)

                self.each(a, add)
            for k in range(1, self.ys):
                to = lax.rem(self.y + k, self.ys)
                remote(first.at[to], later.at[k - 1], self.sent.at[a, 1, k], self.recv.at[a, 1, k],
                       {"fsdp": 2 * to + self.c}).start()

    def third(self):
        for a in range(len(self.parts)):
            first, later, last = self.held[a]
            for k in range(1, self.ys):
                wait_came(later.at[k - 1], self.sent.at[a, 1, k], self.recv.at[a, 1, k])

            def add(rows, first=first, later=later, last=last):
                total = first[self.y, rows, :].astype(F32)
                for k in range(1, self.ys):
                    total = total + later[k - 1, rows, :].astype(F32)
                last[self.x, rows, :] = total.astype(BF16)

            self.each(a, add)
            for k in range(1, self.ctx):
                remote(last.at[self.x], last.at[self.x], self.sent.at[a, 2, k], self.recv.at[a, 2, self.x],
                       {"ctx": lax.rem(self.x + k, self.ctx)}).start()

    def fourth(self, store):
        for a in range(len(self.parts)):
            last = self.held[a][2]
            for k in range(1, self.ctx):
                other = lax.rem(self.x + k, self.ctx)
                wait_came(last.at[other], self.sent.at[a, 2, k], self.recv.at[a, 2, other])

            def add(rows, last=last, a=a):
                total = last[0, rows, :].astype(F32)
                for k in range(1, self.ctx):
                    total = total + last[k, rows, :].astype(F32)
                store(a, rows, total)

            self.each(a, add)

    def drain(self):
        for a in range(len(self.parts)):
            first, later, last = self.held[a]
            for k in range(self.ys):
                wait_sent(first.at[k], self.sent.at[a, 0, k], self.recv.at[a, 0, k])
            for k in range(1, self.ys):
                wait_sent(later.at[k - 1], self.sent.at[a, 1, k], self.recv.at[a, 1, k])
            for k in range(1, self.ctx):
                wait_sent(last.at[self.x], self.sent.at[a, 2, k], self.recv.at[a, 2, 0])


def loop(first, last, body):
    def step(s, carry):
        body(s)
        return carry

    lax.fori_loop(first, last, step, 0)


def params(ident, mib):
    return pltpu.CompilerParams(collective_id=ident, has_side_effects=True, vmem_limit_bytes=mib << 20)


def shape_of(shape, dtype):
    return jax.ShapeDtypeStruct(shape, dtype)


def gather_first(shards, w_out, segments, fsdp, ctx, n):
    count = len(shards)
    full = [shape_of((s.shape[0] * fsdp,) + s.shape[1:], s.dtype) for s in shards]

    def kernel(*refs):
        srcs, (wo, seg), refs = refs[:count], refs[count : count + 2], refs[count + 2 :]
        dsts, (wo_all, seg_all), refs = refs[:count], refs[count : count + 2], refs[count + 2 :]
        meet(n, fsdp, ctx)
        spread = Spread(fsdp, list(zip(srcs, dsts)), [0] * count, *refs[:3])
        share = CtxShare(ctx, seg, seg_all, *refs[3:6])
        line = RowGather(n, wo, wo_all, *refs[6:9])
        spread.start()
        share.start()
        line.start()
        spread.relay()
        line.relay()
        spread.finish()
        share.finish()
        line.finish()

    out = pl.pallas_call(
        kernel,
        out_shape=tuple(full)
        + (
            shape_of((n,) + w_out.shape, w_out.dtype),
            shape_of((ctx,) + segments.shape, segments.dtype),
        ),
        in_specs=[VMEM] * (count + 2),
        out_specs=(VMEM,) * (count + 2),
        scratch_shapes=Spread.scratch(fsdp, count) + CtxShare.scratch(ctx) + RowGather.scratch(n),
        compiler_params=params(1, 24),
    )(*shards, w_out, segments)
    return out[:count], out[count], out[count + 1]


class RowGather:
    def __init__(self, n, src, dst, recv, sent, own):
        self.n, self.src, self.dst = n, src, dst
        self.recv, self.sent, self.own = recv, sent, own
        self.me = lax.axis_index("tp")

    def start(self):
        me = self.me
        pltpu.make_async_copy(self.src, self.dst.at[me], self.own).start()

        @pl.when(me > 0)
        def _():
            remote(self.src, self.dst.at[me], self.sent.at[0, 0], self.recv.at[me], {"tp": me - 1}).start()

        @pl.when(me < self.n - 1)
        def _():
            remote(self.src, self.dst.at[me], self.sent.at[1, 0], self.recv.at[me], {"tp": me + 1}).start()

    def each(self, body):
        me, n = self.me, self.n
        for away in range(1, n):
            for way, tp in ((1, me - away), (0, me + away)):

                @pl.when((tp >= 0) & (tp < n))
                def _(tp=tp, way=way, away=away):
                    onward = (me < n - 1) if way == 1 else (me > 0)
                    body(away, way, tp, onward, {"tp": me + 1} if way == 1 else {"tp": me - 1})

    def relay(self):
        def body(away, way, tp, onward, to):
            here = self.dst.at[tp]
            wait_came(here, self.sent.at[way, away], self.recv.at[tp])

            @pl.when(onward)
            def _():
                remote(here, here, self.sent.at[way, away], self.recv.at[tp], to).start()

        self.each(body)

    def finish(self):
        me = self.me
        pltpu.make_async_copy(self.src, self.dst.at[me], self.own).wait()

        @pl.when(me > 0)
        def _():
            wait_sent(self.src, self.sent.at[0, 0], self.recv.at[0])

        @pl.when(me < self.n - 1)
        def _():
            wait_sent(self.src, self.sent.at[1, 0], self.recv.at[0])

        def body(away, way, tp, onward, to):
            @pl.when(onward)
            def _():
                wait_sent(self.src, self.sent.at[way, away], self.recv.at[0])

        self.each(body)

    @staticmethod
    def scratch(n):
        return [
            pltpu.SemaphoreType.DMA((n,)),
            pltpu.SemaphoreType.DMA((2, n)),
            pltpu.SemaphoreType.DMA,
        ]


def share_latent(latent, ctx):
    def kernel(src, dst, *sems):
        meet(ctx=ctx)
        share = CtxShare(ctx, src, dst, *sems)
        share.start()
        share.finish()

    return pl.pallas_call(
        kernel,
        out_shape=shape_of((ctx,) + latent.shape, latent.dtype),
        in_specs=[VMEM],
        out_specs=VMEM,
        scratch_shapes=CtxShare.scratch(ctx),
        compiler_params=params(2, 24),
    )(latent)


def gather_attended(attended, shards, axes, fsdp, n):
    count = len(shards)
    rows, width = attended.shape
    chunk = 128

    def full(s, axis):
        shape = (s.shape[0] * fsdp, s.shape[1]) if axis == 0 else (s.shape[0], s.shape[1] * fsdp)
        return shape_of(shape, s.dtype)

    def kernel(*refs):
        src, srcs, refs = refs[0], refs[1 : 1 + count], refs[1 + count :]
        dst, dsts, refs = refs[0], refs[1 : 1 + count], refs[1 + count :]
        meet(n, fsdp)
        line = LineGather(n, chunk, src, dst, *refs[:3])
        spread = Spread(fsdp, list(zip(srcs, dsts)), axes, *refs[3:6])
        line.begin()
        spread.start()
        loop(0, line.steps(), line.step)
        spread.relay()
        spread.finish()
        line.drain()

    out = pl.pallas_call(
        kernel,
        out_shape=(shape_of((rows, n * width), BF16),) + tuple(full(s, a) for s, a in zip(shards, axes)),
        in_specs=[VMEM] * (1 + count),
        out_specs=(VMEM,) * (1 + count),
        scratch_shapes=LineGather.scratch(n, rows // chunk) + Spread.scratch(fsdp, count),
        compiler_params=params(3, 40),
    )(attended, *shards)
    return out[0], out[1:]


def second_norm_back(part_two, part_feed, middle, r_two, out_grad, gain_two, grads, axes, fsdp, ctx, n):
    rows, width = part_two.shape
    chunk, hop = 32, 2
    half = rows // 2
    count = len(grads)
    blocks = [GradSum.block_shape(g, a, fsdp) for g, a in zip(grads, axes)]
    held, sems = GradSum.scratch(fsdp, ctx, blocks)

    def kernel(*refs):
        (p_two, p_feed, mid, r2, cot, g2), refs = refs[:6], refs[6:]
        parts, refs = refs[:count], refs[count:]
        (o_branch, o_mixed, o_dmid, o_gain, o_sq), refs = refs[:5], refs[5:]
        outs, refs = refs[:count], refs[count:]
        one, two, refs = refs[:4], refs[4:8], refs[8:]
        keep, refs = refs[: 3 * count], refs[3 * count :]
        meet(n, fsdp, ctx)
        o_gain[...] = jnp.zeros_like(o_gain)
        o_sq[...] = jnp.zeros_like(o_sq)

        def back(at, own, total):
            unit = mid[at, :] * r2[at, :]
            o_gain[...] += jnp.sum((total * unit).reshape(chunk // 8, 8, width), axis=0)
            scaled = total * g2[...]
            inner = jnp.mean(scaled * unit, axis=-1, keepdims=True)
            d_mid = cot[at, :].astype(F32) + r2[at, :] * (scaled - unit * inner)
            o_dmid[own, :] = d_mid
            return d_mid.astype(BF16)

        def forward(at, own, total):
            mixed = mid[at, :] + total
            o_sq[own, 0:1] = jnp.sum(mixed * mixed, axis=-1, keepdims=True)
            o_sq[own, 1:2] = jnp.sum(total * total, axis=-1, keepdims=True)
            return mixed.astype(BF16)

        first = LineSum(n, chunk, hop, p_two, one[0], one[1], o_branch, one[2], one[3], back)
        second = LineSum(n, chunk, hop, p_feed, two[0], two[1], o_mixed, two[2], two[3], forward)
        grad = GradSum(fsdp, ctx, parts, axes, outs, [keep[3 * a : 3 * a + 3] for a in range(count)], *refs)
        grad.start()
        third = half // chunk

        def both(s):
            first.step(s)
            second.step(s - third)

        last = third + second.steps()
        loop(0, last // 4, both)
        grad.second()
        loop(last // 4, last * 5 // 8, both)
        grad.third()
        loop(last * 5 // 8, last, both)

        def store(a, at, total):
            outs[a][at, :] = total

        grad.fourth(store)
        first.drain()
        second.drain()
        grad.drain()

    out = pl.pallas_call(
        kernel,
        out_shape=(
            shape_of((rows, width), BF16),
            shape_of((rows, width), BF16),
            shape_of((half, width), F32),
            shape_of((8, width), F32),
            shape_of((half, 2), F32),
        )
        + tuple(shape_of(b, F32) for b in blocks),
        in_specs=[VMEM] * (6 + count),
        out_specs=(VMEM,) * (5 + count),
        scratch_shapes=LineSum.scratch(n, rows, width, chunk) * 2 + held + sems,
        compiler_params=params(4, 62),
    )(part_two, part_feed, middle, r_two, out_grad, gain_two, *grads)
    return out[:5], out[5:]


def reduce_latent(blocks, ctx):
    size = blocks.shape[1:]

    def kernel(src, dst, came, recv, sent):
        meet(ctx=ctx)
        x = lax.axis_index("ctx")
        for k in range(1, ctx):
            to = lax.rem(x + k, ctx)
            remote(src.at[to], came.at[k - 1], sent.at[k - 1], recv.at[k - 1], {"ctx": to}).start()
        for k in range(1, ctx):
            wait_came(came.at[k - 1], sent.at[k - 1], recv.at[k - 1])

        def body(i):
            rows = pl.ds(pl.multiple_of(i * 64, 64), 64)
            total = src[x, rows, :].astype(F32)
            for k in range(1, ctx):
                total = total + came[k - 1, rows, :].astype(F32)
            dst[rows, :] = total.astype(BF16)

        loop(0, size[0] // 64, body)
        for k in range(1, ctx):
            wait_sent(came.at[k - 1], sent.at[k - 1], recv.at[k - 1])

    return pl.pallas_call(
        kernel,
        out_shape=shape_of(size, BF16),
        in_specs=[VMEM],
        out_specs=VMEM,
        scratch_shapes=[
            pltpu.VMEM((ctx - 1,) + size, BF16),
            pltpu.SemaphoreType.DMA((ctx,)),
            pltpu.SemaphoreType.DMA((ctx,)),
        ],
        compiler_params=params(5, 24),
    )(blocks)


def first_norm_back(part_one, tokens, r_one, gain_one, d_middle, grads, axes, fsdp, ctx, n):
    rows, width = part_one.shape
    chunk, hop = 32, 2
    half = rows // 2
    count = len(grads)
    blocks = [GradSum.block_shape(g, a, fsdp) for g, a in zip(grads, axes)]
    held, sems = GradSum.scratch(fsdp, ctx, blocks)
    lat = blocks[-1]

    def kernel(*refs):
        (p_one, tok, r1, g1, dmid), refs = refs[:5], refs[5:]
        parts, refs = refs[:count], refs[count:]
        (o_tok, o_gain, o_radial), refs = refs[:3], refs[3:]
        outs, refs = refs[:count], refs[count:]
        one, refs = refs[:4], refs[4:]
        keep, refs = refs[: 3 * count], refs[3 * count :]
        gsems, (lat_own, lat_all), lsems = refs[:2], refs[2:4], refs[4:7]
        meet(n, fsdp, ctx)
        o_gain[...] = jnp.zeros_like(o_gain)
        o_radial[...] = jnp.zeros_like(o_radial)

        def back(at, own, total):
            unit = tok[at, :].astype(F32) * r1[at, :]
            o_gain[...] += jnp.sum((total * unit).reshape(chunk // 8, 8, width), axis=0)
            scaled = total * g1[...]
            inner = jnp.mean(scaled * unit, axis=-1, keepdims=True)
            d_tok = dmid[own, :] + r1[at, :] * (scaled - unit * inner)
            o_radial[own, :] = jnp.sum(unit * d_tok, axis=-1, keepdims=True)
            return d_tok.astype(BF16)

        first = LineSum(n, chunk, hop, p_one, one[0], one[1], o_tok, one[2], one[3], back)
        grad = GradSum(fsdp, ctx, parts, axes, outs, [keep[3 * a : 3 * a + 3] for a in range(count)], *gsems)
        line = RowGather(n, lat_own, lat_all, *lsems)
        grad.start()
        last = first.steps()
        loop(0, last // 8, first.step)
        grad.second()
        loop(last // 8, last * 3 // 8, first.step)
        grad.third()
        loop(last * 3 // 8, last * 5 // 8, first.step)

        def store(a, at, total):
            if a < count - 1:
                outs[a][at, :] = total
            else:
                lat_own[at, :] = total.astype(BF16)

        grad.fourth(store)
        line.start()
        loop(last * 5 // 8, last, first.step)
        line.relay()
        line.finish()

        def gather(i):
            at = pl.ds(pl.multiple_of(i * 16, 16), 16)
            for g in range(GROUPS):
                total = jnp.zeros((16, lat[1]), F32)
                for t in range(n):
                    if t * GROUPS // n == g:
                        total = total + lat_all[t, at, :].astype(F32)
                outs[count - 1][at, g * lat[1] : (g + 1) * lat[1]] = total

        loop(0, lat[0] // 16, gather)
        first.drain()
        grad.drain()

    out = pl.pallas_call(
        kernel,
        out_shape=(
            shape_of((rows, width), BF16),
            shape_of((8, width), F32),
            shape_of((half, 1), F32),
        )
        + tuple(shape_of(b, F32) for b in blocks[:-1])
        + (shape_of((lat[0], GROUPS * lat[1]), F32),),
        in_specs=[VMEM] * (5 + count),
        out_specs=(VMEM,) * (3 + count),
        scratch_shapes=LineSum.scratch(n, rows, width, chunk)
        + held
        + sems
        + [pltpu.VMEM(lat, BF16), pltpu.VMEM((n,) + lat, BF16)]
        + RowGather.scratch(n),
        compiler_params=params(6, 56),
    )(part_one, tokens, r_one, gain_one, d_middle, *grads)
    return out[:3], out[3:]


def dot(left, right):
    return jnp.dot(left, right, preferred_element_type=F32)


def block_scores(query_seq, key_seq, seg_keys, seg_query, q_place, block, tok_dev):
    key_blk = lax.dynamic_slice_in_dim(key_seq, block * tok_dev, tok_dev, 0)
    seg_blk = lax.dynamic_slice_in_dim(seg_keys, block * tok_dev, tok_dev, 0)
    k_place = block * tok_dev + jnp.arange(tok_dev, dtype=jnp.int32)
    counted = (k_place[None, :] <= q_place[:, None]) & (seg_blk[None, :] == seg_query[:, None])
    scores = jnp.einsum("qhd,khd->hqk", query_seq, key_blk, preferred_element_type=F32) * 0.125
    return (jnp.where(counted[None], scores, -1e30), counted, key_blk)


def attend(query, keys, values, seg_keys, seg_query, q_place, last_blk, n_ctx):
    seq_dev, tok_dev, heads_here, _ = query.shape
    bounds, lse_list, attn_list = [], [], []
    for seq_at in range(seq_dev):
        query_seq, key_seq, value_seq = query[seq_at], keys[seq_at], values[seq_at]
        seg_k, seg_q = seg_keys[seq_at], seg_query[seq_at]
        block_last = seg_k.reshape(n_ctx, tok_dev)[:, -1]
        first_blk = jnp.sum((block_last < seg_q[0]).astype(jnp.int32))
        bounds.append(first_blk)

        def stat_step(blk, carry):
            top, total = carry
            masked, counted, _ = block_scores(query_seq, key_seq, seg_k, seg_q, q_place, blk, tok_dev)
            new_top = jnp.maximum(top, jnp.max(masked, axis=-1))
            total = total * jnp.exp(top - new_top) + jnp.sum(
                jnp.where(counted[None], jnp.exp(masked - new_top[..., None]), 0.0), axis=-1
            )
            return (new_top, total)

        start_stats = (
            jnp.full((heads_here, tok_dev), -1e30, F32),
            jnp.zeros((heads_here, tok_dev), F32),
        )
        top, total = lax.fori_loop(first_blk, last_blk, stat_step, start_stats)
        lse = top + jnp.log(total)
        lse_list.append(lse)

        def out_step(blk, accum):
            masked, counted, _ = block_scores(query_seq, key_seq, seg_k, seg_q, q_place, blk, tok_dev)
            value_blk = lax.dynamic_slice_in_dim(value_seq, blk * tok_dev, tok_dev, 0)
            probs = jnp.where(counted[None], jnp.exp(masked - lse[..., None]), 0.0).astype(BF16)
            return accum + jnp.einsum("hqk,khd->qhd", probs, value_blk, preferred_element_type=F32)

        accum = lax.fori_loop(first_blk, last_blk, out_step, jnp.zeros((tok_dev, heads_here, HEAD_DIM), F32))
        attn_list.append(accum.astype(BF16).reshape(tok_dev, heads_here * HEAD_DIM))
    return jnp.concatenate(attn_list, axis=0), lse_list, bounds


def attend_back(query, keys, values, seg_keys, seg_query, q_place, last_blk, lse_list, bounds, d_attn):
    seq_dev, tok_dev, heads_here, _ = query.shape
    seq_len = keys.shape[1]
    q_width = heads_here * HEAD_DIM
    dq_list, dk_list, dv_list = [], [], []
    for seq_at in range(seq_dev):
        query_seq, key_seq, value_seq = query[seq_at], keys[seq_at], values[seq_at]
        seg_k, seg_q = seg_keys[seq_at], seg_query[seq_at]
        lse, grad_seq, first_blk = lse_list[seq_at], d_attn[seq_at], bounds[seq_at]

        def delta_step(blk, delta):
            masked, counted, _ = block_scores(query_seq, key_seq, seg_k, seg_q, q_place, blk, tok_dev)
            value_blk = lax.dynamic_slice_in_dim(value_seq, blk * tok_dev, tok_dev, 0)
            probs = jnp.where(counted[None], jnp.exp(masked - lse[..., None]), 0.0)
            d_prob = jnp.einsum("qhd,khd->hqk", grad_seq, value_blk, preferred_element_type=F32)
            return delta + jnp.sum(probs * d_prob, axis=-1)

        delta = lax.fori_loop(first_blk, last_blk, delta_step, jnp.zeros((heads_here, tok_dev), F32))

        def grad_step(blk, carry):
            d_query, d_keys, d_values = carry
            masked, counted, key_blk = block_scores(query_seq, key_seq, seg_k, seg_q, q_place, blk, tok_dev)
            value_blk = lax.dynamic_slice_in_dim(value_seq, blk * tok_dev, tok_dev, 0)
            probs = jnp.where(counted[None], jnp.exp(masked - lse[..., None]), 0.0)
            d_prob = jnp.einsum("qhd,khd->hqk", grad_seq, value_blk, preferred_element_type=F32)
            d_score = (probs * (d_prob - delta[..., None])).astype(BF16)
            d_query = d_query + 0.125 * jnp.einsum("hqk,khd->qhd", d_score, key_blk, preferred_element_type=F32)
            d_keyblk = 0.125 * jnp.einsum("hqk,qhd->khd", d_score, query_seq, preferred_element_type=F32)
            d_valblk = jnp.einsum("hqk,qhd->khd", probs.astype(BF16), grad_seq, preferred_element_type=F32)
            d_keys = lax.dynamic_update_slice_in_dim(d_keys, d_keyblk.astype(BF16), blk * tok_dev, 0)
            d_values = lax.dynamic_update_slice_in_dim(d_values, d_valblk.astype(BF16), blk * tok_dev, 0)
            return (d_query, d_keys, d_values)

        zero_keys = jnp.zeros((seq_len, heads_here, HEAD_DIM), BF16)
        start_grads = (jnp.zeros((tok_dev, heads_here, HEAD_DIM), F32), zero_keys, zero_keys)
        d_query, d_keys, d_values = lax.fori_loop(first_blk, last_blk, grad_step, start_grads)
        dq_list.append(d_query.astype(BF16).reshape(tok_dev, q_width))
        dk_list.append(d_keys.reshape(seq_len, q_width))
        dv_list.append(d_values.reshape(seq_len, q_width))
    return jnp.concatenate(dq_list, axis=0), jnp.stack(dk_list, axis=0), jnp.stack(dv_list, axis=0)


def on_device(
    tokens, gain1, w_latent, w_query, w_key, w_value, w_out, gain2, w_gate, w_up, w_down, segments, cotangent
):
    seq_dev, tok_dev, feat_dim = tokens.shape
    n_ctx, n_tp, n_fsdp = lax.axis_size("ctx"), lax.axis_size("tp"), lax.axis_size("fsdp")
    seq_len = tok_dev * n_ctx
    row_count = seq_dev * tok_dev
    ctx_at, tp_at = lax.axis_index("ctx"), lax.axis_index("tp")
    q_width = w_query.shape[1]
    heads_here = q_width // HEAD_DIM
    group_at = tp_at * heads_here // (HEADS // GROUPS)
    lat_shard = lax.dynamic_slice_in_dim(w_latent, group_at * LATENT, LATENT, 1)
    gains = jnp.pad(jnp.stack([gain1, gain2]).astype(F32), ((0, 6), (0, 0)))
    seg_rows = jnp.pad(segments, ((0, 8 - seq_dev), (0, 0)))
    (gain_all, w_lat, w_qry, w_kproj, w_vproj), wo_cols, seg_all = gather_first(
        (gains, lat_shard, w_query, w_key, w_value), w_out, seg_rows, n_fsdp, n_ctx, n_tp
    )
    gain_all = gain_all.reshape(n_fsdp, 8, -1)
    g_one = gain_all[:, 0].reshape(1, feat_dim)
    g_two = gain_all[:, 1].reshape(1, feat_dim)
    wo_cols = wo_cols.reshape(-1, w_out.shape[1])
    seg_all = seg_all[:, :seq_dev].transpose(1, 0, 2).reshape(seq_dev, seq_len)

    tok_rows = tokens.reshape(row_count, feat_dim)
    stream = tok_rows.astype(F32)
    r_one = lax.rsqrt(jnp.mean(stream * stream, axis=-1, keepdims=True) + eps)
    xn_one = (stream * r_one * g_one).astype(BF16)
    latent = dot(xn_one, w_lat).astype(BF16)
    lat_ctx = share_latent(latent, n_ctx)
    query = dot(xn_one, w_qry).astype(BF16).reshape(seq_dev, tok_dev, heads_here, HEAD_DIM)
    lat_all = lat_ctx.reshape(n_ctx, seq_dev, tok_dev, LATENT).transpose(1, 0, 2, 3)
    lat_all = lat_all.reshape(seq_dev * seq_len, LATENT)
    head_shape = (seq_dev, seq_len, heads_here, HEAD_DIM)
    keys = dot(lat_all, w_kproj).astype(BF16).reshape(head_shape)
    values = dot(lat_all, w_vproj).astype(BF16).reshape(head_shape)
    seg_keys = seg_all.astype(F32)
    seg_query = segments.astype(F32)
    q_place = ctx_at * tok_dev + jnp.arange(tok_dev, dtype=jnp.int32)
    attended, lse_list, bounds = attend(
        query, keys, values, seg_keys, seg_query, q_place, ctx_at + 1, n_ctx
    )

    att_all, (w_outp, w_gatep, w_upp, w_downp) = gather_attended(
        attended, (wo_cols, w_gate, w_up, w_down), (1, 0, 0, 1), n_fsdp, n_tp
    )
    branch = dot(att_all, w_outp)
    middle = stream + branch
    r_two = lax.rsqrt(jnp.mean(middle * middle, axis=-1, keepdims=True) + eps)
    xn_two = (middle * r_two * g_two).astype(BF16)
    gate = dot(xn_two, w_gatep)
    upper = dot(xn_two, w_upp)
    sigma = jax.nn.sigmoid(gate)
    swish = gate * sigma
    hidden = (swish * upper).astype(BF16)
    part_feed = dot(hidden, w_downp).astype(BF16)
    out_grad = cotangent.reshape(row_count, feat_dim)
    grad_down = dot(hidden.T, out_grad).astype(BF16)
    d_hidden = dot(out_grad, w_downp.T)
    d_gate = (d_hidden * upper * sigma * (1.0 + gate * (1.0 - sigma))).astype(BF16)
    d_upper = (d_hidden * swish).astype(BF16)
    grad_gate = dot(xn_two.T, d_gate).astype(BF16)
    grad_up = dot(xn_two.T, d_upper).astype(BF16)
    part_two = (dot(d_gate, w_gatep.T) + dot(d_upper, w_upp.T)).astype(BF16)

    (d_branch, mixed, d_middle, gain_part, squares), (s_gate, s_up, s_down) = second_norm_back(
        part_two, part_feed, middle, r_two, out_grad, g_two,
        (grad_gate, grad_up, grad_down), (0, 0, 1), n_fsdp, n_ctx, n_tp,
    )

    wo_rows = lax.dynamic_slice_in_dim(w_outp, tp_at * q_width, q_width, 0)
    grad_outp = dot(attended.T, d_branch).astype(BF16)
    d_attn = dot(d_branch, wo_rows.T).astype(BF16).reshape(seq_dev, tok_dev, heads_here, HEAD_DIM)
    d_query, d_keys, d_values = attend_back(
        query, keys, values, seg_keys, seg_query, q_place, ctx_at + 1, lse_list, bounds, d_attn
    )
    d_keys = d_keys.reshape(seq_dev * seq_len, q_width)
    d_values = d_values.reshape(seq_dev * seq_len, q_width)
    grad_kproj = dot(lat_all.T, d_keys).astype(BF16)
    grad_vproj = dot(lat_all.T, d_values).astype(BF16)
    lat_parts = (dot(d_keys, w_kproj.T) + dot(d_values, w_vproj.T)).astype(BF16)
    lat_parts = lat_parts.reshape(seq_dev, n_ctx, tok_dev, LATENT).transpose(1, 0, 2, 3)
    d_latent = reduce_latent(lat_parts.reshape(n_ctx, row_count, LATENT), n_ctx)
    grad_qry = dot(xn_one.T, d_query).astype(BF16)
    grad_lat = dot(xn_one.T, d_latent).astype(BF16)
    part_one = (dot(d_query, w_qry.T) + dot(d_latent, w_lat.T)).astype(BF16)

    (grad_tokens, gain_part1, radial_part), (s_qry, s_kproj, s_vproj, s_outp, s_lat) = first_norm_back(
        part_one, tok_rows, r_one, g_one, d_middle,
        (grad_qry, grad_kproj, grad_vproj, grad_outp, grad_lat), (0, 0, 0, 1, 0), n_fsdp, n_ctx, n_tp,
    )

    half = row_count // 2
    lo = n_tp // 2 - 1
    owner = ((tp_at == lo) | (tp_at == lo + 1)).astype(F32)
    valid = (segments != seg_all[:, -1:]).astype(F32)
    valid_rows = valid.reshape(row_count)
    slot = (tp_at > lo).astype(jnp.int32)
    own_valid = lax.dynamic_slice_in_dim(valid_rows, slot * half, half, 0)
    own_sq = lax.dynamic_update_slice_in_dim(
        jnp.zeros((row_count, 2), F32), squares * own_valid[:, None] * owner, slot * half, 0
    )
    own_sq = jnp.sum(own_sq.reshape(seq_dev, tok_dev, 2), axis=1)
    branch_sq = jnp.sum(branch * branch, axis=-1) * valid_rows
    once = (tp_at == 0).astype(F32)
    branch_sq = jnp.sum(branch_sq.reshape(seq_dev, tok_dev), axis=1) * once
    stat_part = jnp.stack([own_sq[:, 0], branch_sq, own_sq[:, 1], jnp.sum(valid, axis=1) * once], axis=1)
    radial_rows = lax.dynamic_update_slice_in_dim(
        jnp.zeros((row_count,), F32), radial_part[:, 0] * owner, slot * half, 0
    )
    gain_sum = jnp.concatenate([jnp.sum(gain_part1, axis=0), jnp.sum(gain_part, axis=0)]) * owner
    gain_sum = lax.psum(gain_sum, ("fsdp", "ctx", "tp"))
    stat_sum = lax.psum(stat_part, ("ctx", "tp"))
    radial = lax.psum(radial_rows, "tp") / jnp.sqrt(F32(feat_dim))
    f_at = lax.axis_index("fsdp")
    per = feat_dim // n_fsdp
    f_gone = lax.dynamic_slice_in_dim(gain_sum[:feat_dim], f_at * per, per, 0)
    f_gtwo = lax.dynamic_slice_in_dim(gain_sum[feat_dim:], f_at * per, per, 0)
    stats = jnp.sqrt(stat_sum[:, :3] / (stat_sum[:, 3:] * feat_dim))
    return (
        mixed.reshape(seq_dev, tok_dev, feat_dim),
        grad_tokens.reshape(seq_dev, tok_dev, feat_dim),
        f_gone,
        s_lat,
        s_qry,
        s_kproj,
        s_vproj,
        s_outp,
        f_gtwo,
        s_gate,
        s_up,
        s_down,
        stats,
        radial.reshape(seq_dev, tok_dev),
    )


def solution(mesh):
    return jax.shard_map(
        on_device,
        mesh=mesh,
        in_specs=(
            P("fsdp", "ctx", None),
            P("fsdp"),
            P("fsdp", None),
            P("fsdp", "tp"),
            P("fsdp", "tp"),
            P("fsdp", "tp"),
            P("tp", "fsdp"),
            P("fsdp"),
            P("fsdp", "tp"),
            P("fsdp", "tp"),
            P("tp", "fsdp"),
            P("fsdp", "ctx"),
            P("fsdp", "ctx", None),
        ),
        out_specs=(
            P("fsdp", "ctx", None),
            P("fsdp", "ctx", None),
            P("fsdp"),
            P("fsdp", None),
            P("fsdp", "tp"),
            P("fsdp", "tp"),
            P("fsdp", "tp"),
            P("tp", "fsdp"),
            P("fsdp"),
            P("fsdp", "tp"),
            P("fsdp", "tp"),
            P("tp", "fsdp"),
            P("fsdp", None),
            P("fsdp", "ctx"),
        ),
        check_vma=False,
    )
```

```python
import jax
import jax.numpy as jnp
from jax import lax
from jax.experimental import pallas as pl
from jax.experimental.pallas import tpu as pltpu
from jax.sharding import PartitionSpec as P

HEADS = 16
HEAD_DIM = 64
GROUPS = 2
LATENT = 256
MESH = pl.DeviceIdType.MESH
VMEM = pl.BlockSpec(memory_space=pltpu.VMEM)
F32 = jnp.float32
BF16 = jnp.bfloat16

eps = 1e-05


def remote(src, dst, send_sem, recv_sem, device):
    return pltpu.make_async_remote_copy(
        src_ref=src,
        dst_ref=dst,
        send_sem=send_sem,
        recv_sem=recv_sem,
        device_id=device,
        device_id_type=MESH,
    )


def wait_sent(ref, sem, recv_sem):
    remote(ref, ref, sem, recv_sem, {"tp": lax.axis_index("tp")}).wait_send()


def wait_came(ref, send_sem, sem):
    remote(ref, ref, send_sem, sem, {"tp": lax.axis_index("tp")}).wait_recv()


def meet(line=0, fsdp=0, ctx=0, everyone=False):
    barrier = pltpu.get_barrier_semaphore()

    def greet(device):
        pl.semaphore_signal(barrier, inc=1, device_id=device, device_id_type=MESH)

    known = 0
    f, x, me = lax.axis_index("fsdp"), lax.axis_index("ctx"), lax.axis_index("tp")
    if fsdp and everyone:
        for k in range(1, fsdp):
            greet({"fsdp": lax.rem(f + k, fsdp)})
        known += fsdp - 1
    elif fsdp:
        greet({"fsdp": sibling(f)})
        for k in range(1, fsdp // 2):
            greet({"fsdp": lax.rem(f + 2 * k, fsdp)})
        known += fsdp // 2
    for k in range(1, ctx):
        greet({"ctx": lax.rem(x + k, ctx)})
        known += 1
    if line > 1 and everyone:
        for k in range(1, line):
            greet({"tp": lax.rem(me + k, line)})
        known += line - 1
    if line > 1 and not everyone:

        @pl.when(me > 0)
        def _():
            greet({"tp": me - 1})

        @pl.when(me < line - 1)
        def _():
            greet({"tp": me + 1})

        @pl.when((me > 0) & (me < line - 1))
        def _():
            pl.semaphore_wait(barrier, known + 2)

        @pl.when((me == 0) | (me == line - 1))
        def _():
            pl.semaphore_wait(barrier, known + 1)

    else:
        pl.semaphore_wait(barrier, known)


def sibling(f):
    return f + 1 - 2 * lax.rem(f, 2)


def block(ref, axis, index, size):
    at = pl.ds(pl.multiple_of(index * size, size), size)
    return ref.at[at] if axis == 0 else ref.at[:, at]


class Spread:
    def __init__(self, fsdp, pairs, axes, recv, sent, own):
        self.fsdp, self.pairs, self.axes = fsdp, pairs, axes
        self.recv, self.sent, self.own = recv, sent, own
        self.f = lax.axis_index("fsdp")

    def size(self, a):
        return self.pairs[a][0].shape[self.axes[a]]

    def target(self, a, f):
        return block(self.pairs[a][1], self.axes[a], f, self.size(a))

    def start(self):
        f = self.f
        for a, (src, dst) in enumerate(self.pairs):
            for k in range(1, self.fsdp // 2):
                remote(src, self.target(a, f), self.sent.at[a], self.recv.at[a, f],
                       {"fsdp": lax.rem(f + 2 * k, self.fsdp)}).start()
        for a, (src, dst) in enumerate(self.pairs):
            remote(src, self.target(a, f), self.sent.at[a], self.recv.at[a, f],
                   {"fsdp": sibling(f)}).start()
            pltpu.make_async_copy(src, self.target(a, f), self.own.at[a]).start()

    def relay(self, which=None):
        for a in which or range(len(self.pairs)):
            for k in range(1, self.fsdp // 2):
                other = lax.rem(self.f + 2 * k, self.fsdp)
                here = self.target(a, other)
                wait_came(here, self.sent.at[a], self.recv.at[a, other])
                remote(here, here, self.sent.at[a], self.recv.at[a, other],
                       {"fsdp": sibling(self.f)}).start()

    def finish(self, which=None):
        for a in which or range(len(self.pairs)):
            src, dst = self.pairs[a]
            for k in range(0, self.fsdp // 2):
                other = lax.rem(sibling(self.f) + 2 * k, self.fsdp)
                wait_came(self.target(a, other), self.sent.at[a], self.recv.at[a, other])
            pltpu.make_async_copy(src, self.target(a, self.f), self.own.at[a]).wait()
            many = (self.fsdp - 1) * self.size(a)
            ref = dst.at[pl.ds(0, many)] if self.axes[a] == 0 else dst.at[:, pl.ds(0, many)]
            wait_sent(ref, self.sent.at[a], self.recv.at[a, 0])

    @staticmethod
    def scratch(fsdp, arrays):
        return [
            pltpu.SemaphoreType.DMA((arrays, fsdp)),
            pltpu.SemaphoreType.DMA((arrays,)),
            pltpu.SemaphoreType.DMA((arrays,)),
        ]


class CtxShare:
    def __init__(self, ctx, src, dst, recv, sent, own):
        self.ctx, self.src, self.dst = ctx, src, dst
        self.recv, self.sent, self.own = recv, sent, own
        self.x = lax.axis_index("ctx")

    def start(self):
        for k in range(1, self.ctx):
            remote(self.src, self.dst.at[self.x], self.sent.at[k - 1], self.recv.at[self.x],
                   {"ctx": lax.rem(self.x + k, self.ctx)}).start()
        pltpu.make_async_copy(self.src, self.dst.at[self.x], self.own).start()

    def finish(self):
        for k in range(1, self.ctx):
            other = lax.rem(self.x + k, self.ctx)
            wait_came(self.dst.at[other], self.sent.at[k - 1], self.recv.at[other])
            wait_sent(self.src, self.sent.at[k - 1], self.recv.at[other])
        pltpu.make_async_copy(self.src, self.dst.at[self.x], self.own).wait()

    @staticmethod
    def scratch(ctx):
        return [
            pltpu.SemaphoreType.DMA((ctx,)),
            pltpu.SemaphoreType.DMA((ctx,)),
            pltpu.SemaphoreType.DMA,
        ]


class LineGather:
    def __init__(self, n, chunk, src, dst, recv, sent, own):
        self.n, self.chunk, self.src, self.dst = n, chunk, src, dst
        self.width = src.shape[1]
        self.count = src.shape[0] // chunk
        self.recv, self.sent, self.own = recv, sent, own
        self.me = lax.axis_index("tp")

    def steps(self):
        return self.n * self.count

    def place(self, tp, at):
        rows = pl.ds(pl.multiple_of(at * self.chunk, self.chunk), self.chunk)
        return self.dst.at[rows, pl.ds(pl.multiple_of(tp * self.width, self.width), self.width)]

    def begin(self):
        pltpu.make_async_copy(
            self.src, self.dst.at[:, pl.ds(pl.multiple_of(self.me * self.width, self.width), self.width)],
            self.own,
        ).start()

    def step(self, s):
        n, me, count = self.n, self.me, self.count
        left, right = {"tp": me - 1}, {"tp": me + 1}

        @pl.when(s < count)
        def _():
            rows = pl.ds(pl.multiple_of(s * self.chunk, self.chunk), self.chunk)

            @pl.when(me > 0)
            def _():
                remote(self.src.at[rows], self.place(me, s), self.sent.at[0], self.recv.at[me, s], left).start()

            @pl.when(me < n - 1)
            def _():
                remote(self.src.at[rows], self.place(me, s), self.sent.at[1], self.recv.at[me, s], right).start()

        @pl.when(s >= count)
        def _():
            away = s // count
            at = s - away * count
            for sign, onward in ((-1, right), (1, left)):
                tp = me + sign * away

                @pl.when((tp >= 0) & (tp < n))
                def _(tp=tp, onward=onward, sign=sign):
                    here = self.place(tp, at)
                    wait_came(here, self.sent.at[2], self.recv.at[tp, at])

                    @pl.when((me < n - 1) if sign < 0 else (me > 0))
                    def _():
                        remote(here, here, self.sent.at[2], self.recv.at[tp, at], onward).start()

    def drain(self):
        n, me = self.n, self.me
        pltpu.make_async_copy(
            self.src, self.dst.at[:, pl.ds(pl.multiple_of(me * self.width, self.width), self.width)],
            self.own,
        ).wait()

        @pl.when(me > 0)
        def _():
            wait_sent(self.src, self.sent.at[0], self.recv.at[0, 0])

        @pl.when(me < n - 1)
        def _():
            wait_sent(self.src, self.sent.at[1], self.recv.at[0, 0])

        @pl.when((me > 0) & (me < n - 1))
        def _():
            wait_sent(self.dst.at[:, pl.ds(0, (n - 1) * self.width)], self.sent.at[2], self.recv.at[0, 0])

    @staticmethod
    def scratch(n, count):
        return [
            pltpu.SemaphoreType.DMA((n, count)),
            pltpu.SemaphoreType.DMA((3,)),
            pltpu.SemaphoreType.DMA,
        ]


class LineSum:
    def __init__(self, n, chunk, hop, part, from_left, from_right, out, recv, sent, finish):
        self.n, self.chunk, self.hop = n, chunk, hop
        self.total_rows = part.shape[0]
        self.owners = (n // 2 - 1, n // 2)
        self.count = self.total_rows // 2 // chunk
        self.part, self.from_left, self.from_right, self.out = part, from_left, from_right, out
        self.recv, self.sent = recv, sent
        self.finish = finish
        self.me = lax.axis_index("tp")

    def steps(self):
        return self.count + self.hop * 2 * (self.n // 2)

    def rows(self, slot, at):
        return pl.ds(pl.multiple_of((slot * self.count + at) * self.chunk, self.chunk), self.chunk)

    def step(self, s):
        n, me, hop = self.n, self.me, self.hop
        left, right = {"tp": me - 1}, {"tp": me + 1}
        reach = n // 2
        for slot, owner in enumerate(self.owners):
            for side in (0, 1):
                lag = me if side == 0 else n - 1 - me
                at = s - hop * lag
                here = (me < owner) if side == 0 else (me > owner)
                held = self.from_left if side == 0 else self.from_right
                to = right if side == 0 else left
                here = here & (at >= 0) & (at < self.count)

                @pl.when(here & (lag == 0))
                def _(at=at, held=held, to=to, side=side, slot=slot):
                    rows = self.rows(slot, at)
                    remote(self.part.at[rows], held.at[rows], self.sent.at[0],
                           self.recv.at[side, slot, at], to).start()

                if n > 2:

                    @pl.when(here & (lag > 0))
                    def _(at=at, held=held, to=to, side=side, slot=slot):
                        rows = self.rows(slot, at)
                        wait_came(held.at[rows], self.sent.at[0], self.recv.at[side, slot, at])
                        held[rows, :] = (held[rows, :].astype(F32) + self.part[rows, :].astype(F32)).astype(BF16)
                        remote(held.at[rows], held.at[rows], self.sent.at[0],
                               self.recv.at[side, slot, at], to).start()

            at = s - hop * reach

            @pl.when((me == owner) & (at >= 0) & (at < self.count))
            def _(at=at, slot=slot, owner=owner):
                rows = self.rows(slot, at)
                total = self.part[rows, :].astype(F32)
                if owner > 0:
                    wait_came(self.from_left.at[rows], self.sent.at[0], self.recv.at[0, slot, at])
                    total = total + self.from_left[rows, :].astype(F32)
                wait_came(self.from_right.at[rows], self.sent.at[0], self.recv.at[1, slot, at])
                total = total + self.from_right[rows, :].astype(F32)
                own = pl.ds(pl.multiple_of(at * self.chunk, self.chunk), self.chunk)
                self.out[rows, :] = self.finish(rows, own, total)
                if owner > 0:
                    remote(self.out.at[rows], self.out.at[rows], self.sent.at[1],
                           self.recv.at[2, slot, at], left).start()
                remote(self.out.at[rows], self.out.at[rows], self.sent.at[2],
                       self.recv.at[2, slot, at], right).start()

        for slot, owner in enumerate(self.owners):
            away = jnp.abs(me - owner)
            at = s - hop * (reach + away)

            @pl.when((me != owner) & (at >= 0) & (at < self.count))
            def _(at=at, slot=slot, owner=owner):
                rows = self.rows(slot, at)
                here = self.out.at[rows]
                wait_came(here, self.sent.at[3], self.recv.at[2, slot, at])

                @pl.when((me < owner) & (me > 0))
                def _():
                    remote(here, here, self.sent.at[3], self.recv.at[2, slot, at], left).start()

                @pl.when((me > owner) & (me < n - 1))
                def _():
                    remote(here, here, self.sent.at[3], self.recv.at[2, slot, at], right).start()

    def drain(self):
        n, me, half = self.n, self.me, self.total_rows // 2
        lo, hi = self.owners

        def wait(sem, size):
            wait_sent(self.part.at[pl.ds(0, size)], self.sent.at[sem], self.recv.at[0, 0, 0])

        middle = (me == lo) | (me == hi)

        @pl.when(middle)
        def _():
            wait(0, half)
            wait(2, half)

        @pl.when((me != lo) & (me != hi))
        def _():
            wait(0, 2 * half)

        if lo > 0:

            @pl.when(middle)
            def _():
                wait(1, half)
                wait(3, half)

            if n > 4:

                @pl.when((me != lo) & (me != hi) & (me > 0) & (me < n - 1))
                def _():
                    wait(3, 2 * half)
        else:

            @pl.when(me == hi)
            def _():
                wait(1, half)

    @staticmethod
    def scratch(n, rows, width, chunk):
        return [
            pltpu.VMEM((rows, width), BF16),
            pltpu.VMEM((rows, width), BF16),
            pltpu.SemaphoreType.DMA((3, 2, rows // 2 // chunk)),
            pltpu.SemaphoreType.DMA((4,)),
        ]


class GradSum:
    def __init__(self, fsdp, ctx, parts, axes, outs, held, recv, sent):
        self.fsdp, self.ctx, self.parts, self.axes, self.outs = fsdp, ctx, parts, axes, outs
        self.ys = fsdp // 2
        self.held, self.recv, self.sent = held, recv, sent
        self.f = lax.axis_index("fsdp")
        self.x = lax.axis_index("ctx")
        self.y, self.c = self.f // 2, lax.rem(self.f, 2)

    @staticmethod
    def block_shape(shape, axis, fsdp):
        r, c = shape
        return (r // fsdp, c) if axis == 0 else (r, c // fsdp)

    @staticmethod
    def scratch(fsdp, ctx, shapes):
        held = []
        for shape in shapes:
            held += [
                pltpu.VMEM((fsdp // 2,) + shape, BF16),
                pltpu.VMEM((max(fsdp // 2 - 1, 1),) + shape, BF16),
                pltpu.VMEM((ctx,) + shape, BF16),
            ]
        many = max(fsdp // 2, ctx)
        return held, [
            pltpu.SemaphoreType.DMA((len(shapes), 3, many)),
            pltpu.SemaphoreType.DMA((len(shapes), 3, many)),
        ]

    def part(self, a, f):
        shape = self.held[a][0].shape[1:]
        return block(self.parts[a], self.axes[a], f, shape[self.axes[a]])

    def each(self, a, body):
        rows = self.held[a][0].shape[1]
        size = 32 if rows % 32 == 0 else 16

        def step(i, carry):
            body(pl.ds(pl.multiple_of(i * size, size), size))
            return carry

        lax.fori_loop(0, rows // size, step, 0)

    def start(self):
        for a in range(len(self.parts)):
            for k in range(self.ys):
                remote(self.part(a, 2 * k + 1 - self.c), self.held[a][0].at[k], self.sent.at[a, 0, k],
                       self.recv.at[a, 0, k], {"fsdp": sibling(self.f)}).start()

    def second(self):
        for a in range(len(self.parts)):
            first, later = self.held[a][0], self.held[a][1]
            for k in range(self.ys):
                wait_came(first.at[k], self.sent.at[a, 0, k], self.recv.at[a, 0, k])
                mine = self.part(a, 2 * k + self.c)

                def add(rows, first=first, k=k, mine=mine):
                    first[k, rows, :] = (first[k, rows, :].astype(F32) + mine[rows, :].astype(F32)).astype(BF16)

                self.each(a, add)
            for k in range(1, self.ys):
                to = lax.rem(self.y + k, self.ys)
                remote(first.at[to], later.at[k - 1], self.sent.at[a, 1, k], self.recv.at[a, 1, k],
                       {"fsdp": 2 * to + self.c}).start()

    def third(self):
        for a in range(len(self.parts)):
            first, later, last = self.held[a]
            for k in range(1, self.ys):
                wait_came(later.at[k - 1], self.sent.at[a, 1, k], self.recv.at[a, 1, k])

            def add(rows, first=first, later=later, last=last):
                total = first[self.y, rows, :].astype(F32)
                for k in range(1, self.ys):
                    total = total + later[k - 1, rows, :].astype(F32)
                last[self.x, rows, :] = total.astype(BF16)

            self.each(a, add)
            for k in range(1, self.ctx):
                remote(last.at[self.x], last.at[self.x], self.sent.at[a, 2, k], self.recv.at[a, 2, self.x],
                       {"ctx": lax.rem(self.x + k, self.ctx)}).start()

    def fourth(self, store):
        for a in range(len(self.parts)):
            last = self.held[a][2]
            for k in range(1, self.ctx):
                other = lax.rem(self.x + k, self.ctx)
                wait_came(last.at[other], self.sent.at[a, 2, k], self.recv.at[a, 2, other])

            def add(rows, last=last, a=a):
                total = last[0, rows, :].astype(F32)
                for k in range(1, self.ctx):
                    total = total + last[k, rows, :].astype(F32)
                store(a, rows, total)

            self.each(a, add)

    def drain(self):
        for a in range(len(self.parts)):
            first, later, last = self.held[a]
            for k in range(self.ys):
                wait_sent(first.at[k], self.sent.at[a, 0, k], self.recv.at[a, 0, k])
            for k in range(1, self.ys):
                wait_sent(later.at[k - 1], self.sent.at[a, 1, k], self.recv.at[a, 1, k])
            for k in range(1, self.ctx):
                wait_sent(last.at[self.x], self.sent.at[a, 2, k], self.recv.at[a, 2, 0])


def loop(first, last, body):
    def step(s, carry):
        body(s)
        return carry

    lax.fori_loop(first, last, step, 0)


def params(ident, mib):
    return pltpu.CompilerParams(collective_id=ident, has_side_effects=True, vmem_limit_bytes=mib << 20)


def shape_of(shape, dtype):
    return jax.ShapeDtypeStruct(shape, dtype)


class RowGather:
    def __init__(self, n, src, dst, recv, sent, own):
        self.n, self.src, self.dst = n, src, dst
        self.recv, self.sent, self.own = recv, sent, own
        self.me = lax.axis_index("tp")

    def start(self):
        me = self.me
        pltpu.make_async_copy(self.src, self.dst.at[me], self.own).start()

        @pl.when(me > 0)
        def _():
            remote(self.src, self.dst.at[me], self.sent.at[0, 0], self.recv.at[me], {"tp": me - 1}).start()

        @pl.when(me < self.n - 1)
        def _():
            remote(self.src, self.dst.at[me], self.sent.at[1, 0], self.recv.at[me], {"tp": me + 1}).start()

    def each(self, body, which=None):
        me, n = self.me, self.n
        for away in which or range(1, n):
            for way, tp in ((1, me - away), (0, me + away)):

                @pl.when((tp >= 0) & (tp < n))
                def _(tp=tp, way=way, away=away):
                    onward = (me < n - 1) if way == 1 else (me > 0)
                    body(away, way, tp, onward, {"tp": me + 1} if way == 1 else {"tp": me - 1})

    def relay(self, which=None):
        def body(away, way, tp, onward, to):
            here = self.dst.at[tp]
            wait_came(here, self.sent.at[way, away], self.recv.at[tp])

            @pl.when(onward)
            def _():
                remote(here, here, self.sent.at[way, away], self.recv.at[tp], to).start()

        self.each(body, which)

    def finish(self):
        me = self.me
        pltpu.make_async_copy(self.src, self.dst.at[me], self.own).wait()

        @pl.when(me > 0)
        def _():
            wait_sent(self.src, self.sent.at[0, 0], self.recv.at[0])

        @pl.when(me < self.n - 1)
        def _():
            wait_sent(self.src, self.sent.at[1, 0], self.recv.at[0])

        def body(away, way, tp, onward, to):
            @pl.when(onward)
            def _():
                wait_sent(self.src, self.sent.at[way, away], self.recv.at[0])

        self.each(body)

    @staticmethod
    def scratch(n):
        return [
            pltpu.SemaphoreType.DMA((n,)),
            pltpu.SemaphoreType.DMA((2, n)),
            pltpu.SemaphoreType.DMA,
        ]


def front(tokens, gains, shards, w_out, segments, fsdp, ctx, n):
    rows, width = tokens.shape
    latent, q_width = shards[0].shape[1], shards[1].shape[1]
    wide, chunk = 128, 256
    full = [shape_of((s.shape[0] * fsdp,) + s.shape[1:], s.dtype) for s in shards]

    def kernel(*refs):
        (tok, gain), srcs, (wo, seg), refs = refs[:2], refs[2:6], refs[6:8], refs[8:]
        (xn, r1, gain_all), dsts, (wo_all, seg_all), refs = refs[:3], refs[3:7], refs[7:9], refs[9:]
        (lat_all, query, keys, values), refs = refs[:4], refs[4:]
        meet(n, fsdp, ctx)
        spread = Spread(fsdp, [(gain, gain_all)] + list(zip(srcs, dsts)), [1, 0, 0, 0, 0], *refs[:3])
        share = CtxShare(ctx, seg, seg_all, *refs[3:6])
        line = RowGather(n, wo, wo_all, *refs[6:9])
        lat_recv, lat_sent = refs[9:11]
        w_lat, w_qry, w_kproj, w_vproj = dsts
        x = lax.axis_index("ctx")
        spread.start()
        share.start()
        line.start()

        def scale(i):
            at = pl.ds(pl.multiple_of(i * wide, wide), wide)
            value = tok[at, :].astype(F32)
            r1[at, :] = lax.rsqrt(jnp.mean(value * value, axis=-1, keepdims=True) + eps)

        loop(0, rows // wide, scale)
        spread.relay([0, 1])
        spread.finish([0, 1])

        def first(i):
            at = pl.ds(pl.multiple_of(i * chunk, chunk), chunk)
            unit = (tok[at, :].astype(F32) * r1[at, :] * gain_all[0:1, :]).astype(BF16)
            xn[at, :] = unit
            lat_all[x, at, :] = dot(unit, w_lat[...]).astype(BF16)
            for k in range(1, ctx):
                here = lat_all.at[x, at]
                remote(here, here, lat_sent.at[k - 1, i], lat_recv.at[x, i],
                       {"ctx": lax.rem(x + k, ctx)}).start()

        loop(0, rows // chunk, first)
        line.relay([1])
        spread.relay([2, 3, 4])
        spread.finish([2, 3, 4])

        def project(shard, i):
            at = pl.ds(pl.multiple_of(i * chunk, chunk), chunk)
            to = pl.ds(pl.multiple_of(shard * rows, chunk) + pl.multiple_of(i * chunk, chunk), chunk)
            value = lat_all[shard, at, :]
            keys[to, :] = dot(value, w_kproj[...]).astype(BF16)
            values[to, :] = dot(value, w_vproj[...]).astype(BF16)

        def ask(i):
            at = pl.ds(pl.multiple_of(i * chunk, chunk), chunk)
            query[at, :] = dot(xn[at, :], w_qry[...]).astype(BF16)
            project(x, i)

        loop(0, rows // chunk, ask)
        line.relay(range(2, n))
        for k in range(1, ctx):
            other = lax.rem(x + k, ctx)

            def theirs(i, other=other):
                at = pl.ds(pl.multiple_of(i * chunk, chunk), chunk)
                wait_came(lat_all.at[other, at], lat_sent.at[k - 1, i], lat_recv.at[other, i])
                project(other, i)

            loop(0, rows // chunk, theirs)

        def gone(i):
            at = pl.ds(pl.multiple_of(i * chunk, chunk), chunk)
            for k in range(1, ctx):
                wait_sent(lat_all.at[x, at], lat_sent.at[k - 1, i], lat_recv.at[x, i])

        loop(0, rows // chunk, gone)
        share.finish()
        line.finish()

    return pl.pallas_call(
        kernel,
        out_shape=(
            shape_of((rows, width), BF16),
            shape_of((rows, 1), F32),
            shape_of((8, width), F32),
            *full,
            shape_of((n,) + w_out.shape, w_out.dtype),
            shape_of((ctx,) + segments.shape, segments.dtype),
            shape_of((ctx, rows, latent), BF16),
            shape_of((rows, q_width), BF16),
            shape_of((ctx * rows, q_width), BF16),
            shape_of((ctx * rows, q_width), BF16),
        ),
        in_specs=[VMEM] * 8,
        out_specs=(VMEM,) * 13,
        scratch_shapes=Spread.scratch(fsdp, 5)
        + CtxShare.scratch(ctx)
        + RowGather.scratch(n)
        + [pltpu.SemaphoreType.DMA((ctx, rows // chunk))] * 2,
        compiler_params=params(1, 56),
    )(tokens, gains, *shards, w_out, segments)


def gather_attended(attended, shards, axes, fsdp, n):
    count = len(shards)
    rows, width = attended.shape
    chunk = 128

    def full(s, axis):
        shape = (s.shape[0] * fsdp, s.shape[1]) if axis == 0 else (s.shape[0], s.shape[1] * fsdp)
        return shape_of(shape, s.dtype)

    def kernel(*refs):
        src, srcs, refs = refs[0], refs[1 : 1 + count], refs[1 + count :]
        dst, dsts, refs = refs[0], refs[1 : 1 + count], refs[1 + count :]
        meet(n, fsdp)
        line = LineGather(n, chunk, src, dst, *refs[:3])
        spread = Spread(fsdp, list(zip(srcs, dsts)), axes, *refs[3:6])
        line.begin()
        spread.start()
        loop(0, line.steps(), line.step)
        spread.relay()
        spread.finish()
        line.drain()

    out = pl.pallas_call(
        kernel,
        out_shape=(shape_of((rows, n * width), BF16),) + tuple(full(s, a) for s, a in zip(shards, axes)),
        in_specs=[VMEM] * (1 + count),
        out_specs=(VMEM,) * (1 + count),
        scratch_shapes=LineGather.scratch(n, rows // chunk) + Spread.scratch(fsdp, count),
        compiler_params=params(3, 40),
    )(attended, *shards)
    return out[0], out[1:]


def feed_forward(att_all, w_outp, tokens, gain_two, w_gatep, w_upp, w_downp, out_grad):
    rows, width = tokens.shape
    inner = w_gatep.shape[1]
    size = 256

    def kernel(att, wo, tok, g2, wg, wu, wd, cot, mid, r2, xn, hid, dg, du, p_two, p_feed, b_sq):
        def body(i):
            at = pl.ds(pl.multiple_of(i * size, size), size)
            branch = dot(att[at, :], wo[...])
            b_sq[at, :] = jnp.sum(branch * branch, axis=-1, keepdims=True)
            middle = tok[at, :].astype(F32) + branch
            mid[at, :] = middle
            scale = lax.rsqrt(jnp.mean(middle * middle, axis=-1, keepdims=True) + eps)
            r2[at, :] = scale
            unit = (middle * scale * g2[...]).astype(BF16)
            xn[at, :] = unit
            gate = dot(unit, wg[...])
            upper = dot(unit, wu[...])
            sigma = jax.nn.sigmoid(gate)
            swish = gate * sigma
            hidden = (swish * upper).astype(BF16)
            hid[at, :] = hidden
            p_feed[at, :] = dot(hidden, wd[...]).astype(BF16)
            d_hidden = dot_t(cot[at, :], wd[...])
            d_gate = (d_hidden * upper * sigma * (1.0 + gate * (1.0 - sigma))).astype(BF16)
            d_upper = (d_hidden * swish).astype(BF16)
            dg[at, :] = d_gate
            du[at, :] = d_upper
            p_two[at, :] = (dot_t(d_gate, wg[...]) + dot_t(d_upper, wu[...])).astype(BF16)

        loop(0, rows // size, body)

    return pl.pallas_call(
        kernel,
        out_shape=(
            shape_of((rows, width), F32),
            shape_of((rows, 1), F32),
            shape_of((rows, width), BF16),
            shape_of((rows, inner), BF16),
            shape_of((rows, inner), BF16),
            shape_of((rows, inner), BF16),
            shape_of((rows, width), BF16),
            shape_of((rows, width), BF16),
            shape_of((rows, 1), F32),
        ),
        in_specs=[VMEM] * 8,
        out_specs=(VMEM,) * 9,
        compiler_params=pltpu.CompilerParams(vmem_limit_bytes=56 << 20),
    )(att_all, w_outp, tokens, gain_two, w_gatep, w_upp, w_downp, out_grad)


def second_norm_back(part_two, part_feed, middle, r_two, out_grad, gain_two, tokens, r_one, xn_two, hidden,
                     d_gate, d_upper, fsdp, ctx, n):
    rows, width = part_two.shape
    inner = hidden.shape[1]
    chunk, hop = 32, 2
    half = rows // 2
    cols = width // 4
    axes = (0, 0, 1)
    whole = ((width, inner), (width, inner), (inner, width))
    blocks = [GradSum.block_shape(w, a, fsdp) for w, a in zip(whole, axes)]
    held, sems = GradSum.scratch(fsdp, ctx, blocks)

    def kernel(*refs):
        (p_two, p_feed, mid, r2, cot, g2, tok, r1, xn, hid, dg, du), refs = refs[:12], refs[12:]
        (o_branch, o_mixed, o_dmid, o_gain, o_sq), outs, refs = refs[:5], refs[5:8], refs[8:]
        one, two, keep, refs = refs[:4], refs[4:8], refs[8:17], refs[17:]
        gsems, parts = refs[:2], refs[2:5]
        meet(n, fsdp, ctx)
        o_gain[...] = jnp.zeros_like(o_gain)
        o_sq[...] = jnp.zeros_like(o_sq)

        def back(at, own, total):
            unit = mid[at, :] * r2[at, :]
            o_gain[...] += jnp.sum((total * unit).reshape(chunk // 8, 8, width), axis=0)
            scaled = total * g2[...]
            mean = jnp.mean(scaled * unit, axis=-1, keepdims=True)
            d_mid = cot[at, :].astype(F32) + r2[at, :] * (scaled - unit * mean)
            o_dmid[own, :] = d_mid
            first_unit = tok[at, :].astype(F32) * r1[at, :]
            o_sq[own, 2:3] = jnp.sum(first_unit * d_mid, axis=-1, keepdims=True)
            return d_mid.astype(BF16)

        def forward(at, own, total):
            mixed = mid[at, :] + total
            o_sq[own, 0:1] = jnp.sum(mixed * mixed, axis=-1, keepdims=True)
            o_sq[own, 1:2] = jnp.sum(total * total, axis=-1, keepdims=True)
            return mixed.astype(BF16)

        first = LineSum(n, chunk, hop, p_two, one[0], one[1], o_branch, one[2], one[3], back)
        second = LineSum(n, chunk, hop, p_feed, two[0], two[1], o_mixed, two[2], two[3], forward)
        grad = GradSum(fsdp, ctx, parts, axes, outs, [keep[3 * a : 3 * a + 3] for a in range(3)], *gsems)
        third = half // chunk

        def both(s):
            first.step(s)
            second.step(s - third)

        def product(i):
            at = pl.ds(pl.multiple_of(i * cols, cols), cols)
            left = xn[:, at]
            parts[0][at, :] = dot_rows(left, dg[...]).astype(BF16)
            parts[1][at, :] = dot_rows(left, du[...]).astype(BF16)
            parts[2][:, at] = dot_rows(hid[...], cot[:, at]).astype(BF16)

        def busy(s):
            both(s)
            product(s)

        loop(0, 4, busy)
        grad.start()
        last = third + second.steps()
        loop(4, last * 5 // 16, both)
        grad.second()
        loop(last * 5 // 16, last * 5 // 8, both)
        grad.third()
        loop(last * 5 // 8, last, both)

        def store(a, at, total):
            outs[a][at, :] = total

        grad.fourth(store)
        first.drain()
        second.drain()
        grad.drain()

    out = pl.pallas_call(
        kernel,
        out_shape=(
            shape_of((rows, width), BF16),
            shape_of((rows, width), BF16),
            shape_of((half, width), F32),
            shape_of((8, width), F32),
            shape_of((half, 3), F32),
        )
        + tuple(shape_of(b, F32) for b in blocks),
        in_specs=[VMEM] * 12,
        out_specs=(VMEM,) * 8,
        scratch_shapes=LineSum.scratch(n, rows, width, chunk) * 2
        + held
        + sems
        + [pltpu.VMEM(w, BF16) for w in whole],
        compiler_params=params(4, 63),
    )(part_two, part_feed, middle, r_two, out_grad, gain_two, tokens, r_one, xn_two, hidden, d_gate, d_upper)
    return out[:5], out[5:]


class AxisSum:
    def __init__(self, axis, n, slots, recv, sent):
        self.axis, self.n, self.slots, self.recv, self.sent = axis, n, slots, recv, sent
        self.at = lax.axis_index(axis)

    def start(self, value):
        self.slots[self.at] = value
        for k in range(1, self.n):
            remote(self.slots.at[self.at], self.slots.at[self.at], self.sent.at[k], self.recv.at[self.at],
                   {self.axis: lax.rem(self.at + k, self.n)}).start()

    def finish(self):
        for k in range(1, self.n):
            other = lax.rem(self.at + k, self.n)
            wait_came(self.slots.at[other], self.sent.at[k], self.recv.at[other])
            wait_sent(self.slots.at[self.at], self.sent.at[k], self.recv.at[other])
        total = self.slots[0]
        for k in range(1, self.n):
            total = total + self.slots[k]
        return total

    @staticmethod
    def scratch(n, shape):
        return [
            pltpu.VMEM((n,) + shape, F32),
            pltpu.SemaphoreType.DMA((n,)),
            pltpu.SemaphoreType.DMA((n,)),
        ]


def first_norm_back(d_query, d_keys, d_values, lat_parts, lat_all, xn_one, attended, d_branch, w_qry, w_lat,
                    tokens, r_one, gain_one, d_middle, small, fsdp, ctx, n):
    rows, width = tokens.shape
    q_width, latent = d_query.shape[1], w_lat.shape[1]
    chunk, hop, wide = 32, 2, 256
    side = 128
    half = rows // 2
    axes = (0, 0, 0, 1, 0)
    whole = ((width, q_width), (latent, q_width), (latent, q_width), (q_width, width), (width, latent))
    blocks = [GradSum.block_shape(w, a, fsdp) for w, a in zip(whole, axes)]
    held, sems = GradSum.scratch(fsdp, ctx, blocks)
    lat = blocks[-1]
    pieces = rows // wide

    def kernel(*refs):
        (dq, dk, dv, lp, la, xn, att, dbr, wq, wl, tok, r1, g1, dmid, sm_in), refs = refs[:15], refs[15:]
        (o_tok, o_small), outs, refs = refs[:2], refs[2:7], refs[7:]
        one, keep, gsems, refs = refs[:4], refs[4:19], refs[19:21], refs[21:]
        parts, (p_one, dlat, came, c_recv, c_sent, gacc, sm), refs = refs[:5], refs[5:12], refs[12:]
        (lat_own, lat_every), lsems, sums = refs[:2], refs[2:5], refs[5:]
        meet(n, fsdp, ctx, everyone=True)
        x = lax.axis_index("ctx")
        for k in range(1, ctx):
            to = lax.rem(x + k, ctx)
            for i in range(pieces):
                at = pl.ds(i * wide, wide)
                remote(lp.at[to, at], came.at[k - 1, at], c_sent.at[k - 1, i], c_recv.at[k - 1, i],
                       {"ctx": to}).start()
        gacc[...] = jnp.zeros_like(gacc)
        sm[...] = sm_in[...]

        def product(i):
            at = pl.ds(pl.multiple_of(i * wide, wide), wide)
            parts[0][at, :] = dot_rows(xn[:, at], dq[...]).astype(BF16)
            parts[3][:, at] = dot_rows(att[...], dbr[:, at]).astype(BF16)

        loop(0, width // wide, product)
        parts[1][...] = dot_rows(la[...], dk[...]).astype(BF16)
        parts[2][...] = dot_rows(la[...], dv[...]).astype(BF16)

        def whole_latent(i):
            at = pl.ds(pl.multiple_of(i * wide, wide), wide)
            total = lp[x, at, :].astype(F32)
            for k in range(1, ctx):
                wait_came(came.at[k - 1, at], c_sent.at[k - 1, i], c_recv.at[k - 1, i])
                total = total + came[k - 1, at, :].astype(F32)
            total = total.astype(BF16)
            dlat[at, :] = total
            p_one[at, :] = (dot_t(dq[at, :], wq[...]) + dot_t(total, wl[...])).astype(BF16)

        loop(0, pieces, whole_latent)

        def back(at, own, total):
            unit = tok[at, :].astype(F32) * r1[at, :]
            scaled = total * g1[...]
            mean = jnp.mean(scaled * unit, axis=-1, keepdims=True)
            return (dmid[own, :] + r1[at, :] * (scaled - unit * mean)).astype(BF16)

        first = LineSum(n, chunk, hop, p_one, one[0], one[1], o_tok, one[2], one[3], back)
        grad = GradSum(fsdp, ctx, parts, axes, outs, [keep[3 * a : 3 * a + 3] for a in range(5)], *gsems)
        line = RowGather(n, lat_own, lat_every, *lsems)
        over_tp = AxisSum("tp", n, *sums[0:3])
        over_ctx = AxisSum("ctx", ctx, *sums[3:6])
        over_fsdp = AxisSum("fsdp", fsdp, *sums[6:9])

        def product_lat(i):
            at = pl.ds(pl.multiple_of(i * wide, wide), wide)
            parts[4][at, :] = dot_rows(xn[:, at], dlat[...]).astype(BF16)

        def gains(i):
            at = pl.ds(pl.multiple_of(i * side, side), side)
            value = p_one[at, :].astype(F32) * (tok[at, :].astype(F32) * r1[at, :])
            gacc[...] += jnp.sum(value.reshape(side // 8, 8, width), axis=0)
            along = lax.dot_general(jnp.ones((8, width), F32), value * g1[...], (((1,), (1,)), ((), ())),
                                    precision=lax.Precision.HIGHEST, preferred_element_type=F32)
            sm[3:4, at] = along[0:1, :]

        def begin(s):
            first.step(s)
            product_lat(s)

        loop(0, width // wide, begin)
        grad.start()
        begun = width // wide

        def more(s):
            first.step(s)
            gains(s - begun)

        loop(begun, begun + rows // side, more)
        sm[0:1, 0:width] = jnp.sum(gacc[...], axis=0, keepdims=True)
        over_tp.start(sm[...])
        grad.second()
        last = first.steps()
        mark = begun + rows // side
        loop(mark, mark + 4, first.step)
        along_tp = over_tp.finish()
        over_ctx.start(along_tp)
        grad.third()
        loop(mark + 4, mark + 8, first.step)
        along_ctx = over_ctx.finish()
        over_fsdp.start(along_ctx)

        def store(a, at, total):
            if a < 4:
                outs[a][at, :] = total
            else:
                lat_own[at, :] = total.astype(BF16)

        grad.fourth(store)
        line.start()
        loop(mark + 8, last, first.step)
        line.relay()
        line.finish()
        everywhere = over_fsdp.finish()
        row = lax.broadcasted_iota(jnp.int32, everywhere.shape, 0)
        o_small[...] = jnp.where(row < 2, everywhere, jnp.where(row == 2, along_ctx, along_tp))

        def gather(i):
            at = pl.ds(pl.multiple_of(i * 16, 16), 16)
            for g in range(GROUPS):
                total = jnp.zeros((16, lat[1]), F32)
                for t in range(n):
                    if t * GROUPS // n == g:
                        total = total + lat_every[t, at, :].astype(F32)
                outs[4][at, g * lat[1] : (g + 1) * lat[1]] = total

        loop(0, lat[0] // 16, gather)
        for k in range(1, ctx):
            for i in range(pieces):
                at = pl.ds(i * wide, wide)
                wait_sent(came.at[k - 1, at], c_sent.at[k - 1, i], c_recv.at[k - 1, i])
        first.drain()
        grad.drain()

    out = pl.pallas_call(
        kernel,
        out_shape=(shape_of((rows, width), BF16), shape_of(small.shape, F32))
        + tuple(shape_of(b, F32) for b in blocks[:-1])
        + (shape_of((lat[0], GROUPS * lat[1]), F32),),
        in_specs=[VMEM] * 15,
        out_specs=(VMEM,) * 7,
        scratch_shapes=LineSum.scratch(n, rows, width, chunk)
        + held
        + sems
        + [pltpu.VMEM(w, BF16) for w in whole]
        + [
            pltpu.VMEM((rows, width), BF16),
            pltpu.VMEM((rows, latent), BF16),
            pltpu.VMEM((ctx - 1, rows, latent), BF16),
            pltpu.SemaphoreType.DMA((ctx - 1, pieces)),
            pltpu.SemaphoreType.DMA((ctx - 1, pieces)),
            pltpu.VMEM((8, width), F32),
            pltpu.VMEM(small.shape, F32),
        ]
        + [pltpu.VMEM(lat, BF16), pltpu.VMEM((n,) + lat, BF16)]
        + RowGather.scratch(n)
        + AxisSum.scratch(n, small.shape)
        + AxisSum.scratch(ctx, small.shape)
        + AxisSum.scratch(fsdp, small.shape),
        compiler_params=params(6, 63),
    )(d_query, d_keys, d_values, lat_parts, lat_all, xn_one, attended, d_branch, w_qry, w_lat,
      tokens, r_one, gain_one, d_middle, small)
    return out[:2], out[2:]


def dot(left, right):
    return jnp.dot(left, right, preferred_element_type=F32)


TILE = 256


def dot_t(left, right):
    return lax.dot_general(left, right, (((1,), (1,)), ((), ())), preferred_element_type=F32)


def dot_rows(left, right):
    return lax.dot_general(left, right, (((0,), (0,)), ((), ())), preferred_element_type=F32)


def head_only(value, head):
    lane = lax.broadcasted_iota(jnp.int32, value.shape, 1)
    return jnp.where((lane // HEAD_DIM) == head, value, jnp.zeros_like(value))


def first_tile(seg, seq, tok_dev, q_tile, tiles):
    per = tok_dev // TILE
    mine = seg[q_tile // per, seq, lax.rem(q_tile, per) * TILE]

    def count(t, found):
        last = seg[t // per, seq, lax.rem(t, per) * TILE + TILE - 1]
        return found + jnp.where(last < mine, 1, 0)

    return lax.fori_loop(0, tiles, count, 0)


def tile_mask(seg_q, seg_k, q_tile, k_tile):
    q_at = q_tile * TILE + lax.broadcasted_iota(jnp.int32, (TILE, TILE), 0)
    k_at = k_tile * TILE + lax.broadcasted_iota(jnp.int32, (TILE, TILE), 1)
    return (k_at <= q_at) & (seg_k == seg_q)


def tile_place(t, seq, tok_dev, rows):
    per = tok_dev // TILE
    shard = t // per
    inner = pl.multiple_of(lax.rem(t, per) * TILE, TILE)
    return shard, inner, pl.ds(pl.multiple_of(shard * rows + seq * tok_dev, TILE) + inner, TILE)


def attend(query, keys, values, seg_all, seg_col, seq_dev):
    rows, width = query.shape
    heads, tok_dev, shards = width // HEAD_DIM, rows // seq_dev, seg_all.shape[0]
    per = tok_dev // TILE

    def kernel(seg_s, q_ref, k_ref, v_ref, segk, segq, out, lse_ref, held):
        base = lax.axis_index("ctx") * per

        def body(i):
            seq = i // per
            q_tile = base + lax.rem(i, per)
            at = pl.ds(pl.multiple_of(i * TILE, TILE), TILE)
            query = q_ref[at, :]
            mine = [head_only(query, h) for h in range(heads)]
            seg_q = segq[at, :]
            lo = first_tile(seg_s, seq, tok_dev, q_tile, shards * per)

            def scores(t, tops):
                shard, inner, place = tile_place(t, seq, tok_dev, rows)
                key = k_ref[place, :]
                counted = tile_mask(seg_q, segk[shard, pl.ds(seq, 1), pl.ds(inner, TILE)], q_tile, t)
                new = []
                for h in range(heads):
                    score = jnp.where(counted, dot_t(mine[h], key) * 0.125, -1e30)
                    held[h, t] = score
                    new.append(jnp.maximum(tops[h], jnp.max(score, axis=-1, keepdims=True)))
                return tuple(new)

            none = jnp.full((TILE, 1), -1e30, F32)
            tops = lax.fori_loop(lo, q_tile + 1, scores, (none,) * heads)

            def sums(t, totals):
                new = []
                for h in range(heads):
                    weight = jnp.exp(held[h, t] - tops[h])
                    held[h, t] = weight
                    new.append(totals[h] + jnp.sum(weight, axis=-1, keepdims=True))
                return tuple(new)

            totals = lax.fori_loop(lo, q_tile + 1, sums, (jnp.zeros((TILE, 1), F32),) * heads)
            inverse = [1.0 / total for total in totals]

            def mix(t, accum):
                _, _, place = tile_place(t, seq, tok_dev, rows)
                value = v_ref[place, :]
                for h in range(heads):
                    prob = (held[h, t] * inverse[h]).astype(BF16)
                    accum = accum + jnp.dot(prob, head_only(value, h), preferred_element_type=F32)
                return accum

            out[at, :] = lax.fori_loop(lo, q_tile + 1, mix, jnp.zeros((TILE, width), F32)).astype(BF16)
            lane = lax.broadcasted_iota(jnp.int32, (TILE, 128), 1)
            kept = jnp.zeros((TILE, 128), F32)
            for h in range(heads):
                kept = jnp.where(lane == h, tops[h] + jnp.log(totals[h]), kept)
            lse_ref[at, :] = kept

        loop(0, seq_dev * per, body)

    return pl.pallas_call(
        kernel,
        out_shape=(shape_of((rows, width), BF16), shape_of((rows, 128), F32)),
        in_specs=[pl.BlockSpec(memory_space=pltpu.SMEM)] + [VMEM] * 5,
        out_specs=(VMEM, VMEM),
        scratch_shapes=[pltpu.VMEM((heads, shards * per, TILE, TILE), F32)],
        compiler_params=pltpu.CompilerParams(vmem_limit_bytes=48 << 20),
    )(seg_all, query, keys, values, seg_all, seg_col)


def attend_back(query, keys, values, seg_all, seg_col, lse, attended, d_branch, w_outp, w_kproj, w_vproj, seq_dev):
    rows, width = query.shape
    latent = w_kproj.shape[0]
    heads, tok_dev, shards = width // HEAD_DIM, rows // seq_dev, seg_all.shape[0]
    per = tok_dev // TILE

    def kernel(seg_s, q_ref, k_ref, v_ref, segk, segq, lse_ref, o_ref, dbr, wo, wk, wv,
               dq_ref, dk_ref, dv_ref, lat_ref, dk, dv):
        base = lax.axis_index("ctx") * per
        here = pl.ds(pl.multiple_of(lax.axis_index("tp") * width, width), width)

        def clear(i):
            at = pl.ds(pl.multiple_of(i * TILE, TILE), TILE)
            dk[at, :] = jnp.zeros((TILE, width), F32)
            dv[at, :] = jnp.zeros((TILE, width), F32)

        loop(0, shards * rows // TILE, clear)

        def body(i):
            seq = i // per
            q_tile = base + lax.rem(i, per)
            at = pl.ds(pl.multiple_of(i * TILE, TILE), TILE)
            query = q_ref[at, :]
            grad = dot_t(dbr[at, :], wo[here, :]).astype(BF16)
            mine = [head_only(query, h) for h in range(heads)]
            ours = [head_only(grad, h) for h in range(heads)]
            product = grad.astype(F32) * o_ref[at, :].astype(F32)
            delta = [jnp.sum(head_only(product, h), axis=-1, keepdims=True) for h in range(heads)]
            kept = lse_ref[at, :]
            norm = [kept[:, h : h + 1] for h in range(heads)]
            seg_q = segq[at, :]
            lo = first_tile(seg_s, seq, tok_dev, q_tile, shards * per)

            def step(t, d_query):
                shard, inner, place = tile_place(t, seq, tok_dev, rows)
                key, value = k_ref[place, :], v_ref[place, :]
                counted = tile_mask(seg_q, segk[shard, pl.ds(seq, 1), pl.ds(inner, TILE)], q_tile, t)
                d_key = jnp.zeros((TILE, width), F32)
                d_value = jnp.zeros((TILE, width), F32)
                for h in range(heads):
                    score = dot_t(mine[h], key) * 0.125
                    prob = jnp.where(counted, jnp.exp(jnp.where(counted, score, -1e30) - norm[h]), 0.0)
                    d_prob = dot_t(ours[h], value)
                    d_score = (prob * (d_prob - delta[h])).astype(BF16)
                    d_query = d_query + jnp.dot(d_score, head_only(key, h), preferred_element_type=F32)
                    d_key = d_key + dot_rows(d_score, mine[h])
                    d_value = d_value + dot_rows(prob.astype(BF16), ours[h])
                dk[place, :] += d_key * 0.125
                dv[place, :] += d_value
                return d_query

            d_query = lax.fori_loop(lo, q_tile + 1, step, jnp.zeros((TILE, width), F32))
            dq_ref[at, :] = (d_query * 0.125).astype(BF16)

        loop(0, seq_dev * per, body)

        def put(i):
            at = pl.ds(pl.multiple_of(i * TILE, TILE), TILE)
            d_key, d_value = dk[at, :].astype(BF16), dv[at, :].astype(BF16)
            dk_ref[at, :] = d_key
            dv_ref[at, :] = d_value
            lat_ref[at, :] = (dot_t(d_key, wk[...]) + dot_t(d_value, wv[...])).astype(BF16)

        loop(0, shards * rows // TILE, put)

    return pl.pallas_call(
        kernel,
        out_shape=(
            shape_of((rows, width), BF16),
            shape_of((shards * rows, width), BF16),
            shape_of((shards * rows, width), BF16),
            shape_of((shards * rows, latent), BF16),
        ),
        in_specs=[pl.BlockSpec(memory_space=pltpu.SMEM)] + [VMEM] * 11,
        out_specs=(VMEM,) * 4,
        scratch_shapes=[pltpu.VMEM((shards * rows, width), F32)] * 2,
        compiler_params=pltpu.CompilerParams(vmem_limit_bytes=56 << 20),
    )(seg_all, query, keys, values, seg_all, seg_col, lse, attended, d_branch, w_outp, w_kproj, w_vproj)


def on_device(
    tokens, gain1, w_latent, w_query, w_key, w_value, w_out, gain2, w_gate, w_up, w_down, segments, cotangent
):
    seq_dev, tok_dev, feat_dim = tokens.shape
    n_ctx, n_tp, n_fsdp = lax.axis_size("ctx"), lax.axis_size("tp"), lax.axis_size("fsdp")
    row_count = seq_dev * tok_dev
    tp_at, f_at = lax.axis_index("tp"), lax.axis_index("fsdp")
    heads_here = w_query.shape[1] // HEAD_DIM
    group_at = tp_at * heads_here // (HEADS // GROUPS)
    lat_shard = lax.dynamic_slice_in_dim(w_latent, group_at * LATENT, LATENT, 1)
    gains = jnp.pad(jnp.stack([gain1, gain2]).astype(F32), ((0, 6), (0, 0)))
    seg_rows = jnp.pad(segments, ((0, 8 - seq_dev), (0, 0)))
    seg_col = segments.reshape(row_count, 1)
    tok_rows = tokens.reshape(row_count, feat_dim)
    out_grad = cotangent.reshape(row_count, feat_dim)
    (xn_one, r_one, gain_all, w_lat, w_qry, w_kproj, w_vproj, wo_cols, seg_all, lat_ctx, query, keys, values) = front(
        tok_rows, gains, (lat_shard, w_query, w_key, w_value), w_out, seg_rows, n_fsdp, n_ctx, n_tp
    )
    g_one, g_two = gain_all[0:1], gain_all[1:2]
    attended, lse = attend(query, keys, values, seg_all, seg_col, seq_dev)
    att_all, (w_outp, w_gatep, w_upp, w_downp) = gather_attended(
        attended, (wo_cols.reshape(-1, w_out.shape[1]), w_gate, w_up, w_down), (1, 0, 0, 1), n_fsdp, n_tp
    )
    middle, r_two, xn_two, hidden, d_gate, d_upper, part_two, part_feed, branch_sq = feed_forward(
        att_all, w_outp, tok_rows, g_two, w_gatep, w_upp, w_downp, out_grad
    )
    (d_branch, mixed, d_middle, gain_part, squares), (s_gate, s_up, s_down) = second_norm_back(
        part_two, part_feed, middle, r_two, out_grad, g_two, tok_rows, r_one, xn_two, hidden, d_gate, d_upper,
        n_fsdp, n_ctx, n_tp,
    )
    d_query, d_keys, d_values, lat_parts = attend_back(
        query, keys, values, seg_all, seg_col, lse, attended, d_branch, w_outp, w_kproj, w_vproj, seq_dev
    )

    half = row_count // 2
    lo = n_tp // 2 - 1
    owner = (tp_at == lo) | (tp_at == lo + 1)
    slot = (tp_at > lo).astype(jnp.int32)
    once = (tp_at == 0).astype(F32)
    valid = (segments != seg_all[n_ctx - 1, :seq_dev, -1:]).astype(F32)
    own_rows = lax.dynamic_update_slice_in_dim(
        jnp.zeros((3, row_count), F32), jnp.where(owner, squares.T, 0.0), slot * half, 1
    )
    by_seq = own_rows[:2].reshape(2, seq_dev, tok_dev) * valid
    branch_rows = branch_sq.reshape(seq_dev, tok_dev) * valid * once
    stat_part = jnp.sum(
        jnp.concatenate([by_seq, branch_rows[None], (valid * once)[None]]), axis=-1
    ).reshape(-1)
    many = max(feat_dim, row_count)

    def line(value):
        return jnp.pad(value, (0, many - value.shape[0]))[None]

    small = jnp.concatenate(
        [
            jnp.zeros((1, many), F32),
            line(jnp.where(owner, jnp.sum(gain_part, axis=0), 0.0)),
            line(stat_part),
            jnp.zeros((1, many), F32),
            line(own_rows[2]),
            jnp.zeros((3, many), F32),
        ]
    )
    (grad_tokens, small_sum), (s_qry, s_kproj, s_vproj, s_outp, s_lat) = first_norm_back(
        d_query, d_keys, d_values, lat_parts.reshape(n_ctx, row_count, LATENT),
        lat_ctx.reshape(n_ctx * row_count, LATENT), xn_one, attended, d_branch, w_qry, w_lat,
        tok_rows, r_one, g_one, d_middle, small, n_fsdp, n_ctx, n_tp,
    )
    per = feat_dim // n_fsdp
    gain_grads = lax.dynamic_slice_in_dim(small_sum[:2], f_at * per, per, 1)
    sums = small_sum[2, : 4 * seq_dev].reshape(4, seq_dev)
    stats = jnp.sqrt(sums[jnp.array([0, 2, 1])] / (sums[3:] * feat_dim)).T
    r_rows = r_one.reshape(row_count)
    radial = (small_sum[4, :row_count] + eps * r_rows * r_rows * r_rows * small_sum[3, :row_count]) / jnp.sqrt(
        F32(feat_dim)
    )
    return (
        mixed.reshape(seq_dev, tok_dev, feat_dim),
        grad_tokens.reshape(seq_dev, tok_dev, feat_dim),
        gain_grads[0],
        s_lat,
        s_qry,
        s_kproj,
        s_vproj,
        s_outp,
        gain_grads[1],
        s_gate,
        s_up,
        s_down,
        stats,
        radial.reshape(seq_dev, tok_dev),
    )


def solution(mesh):
    return jax.shard_map(
        on_device,
        mesh=mesh,
        in_specs=(
            P("fsdp", "ctx", None),
            P("fsdp"),
            P("fsdp", None),
            P("fsdp", "tp"),
            P("fsdp", "tp"),
            P("fsdp", "tp"),
            P("tp", "fsdp"),
            P("fsdp"),
            P("fsdp", "tp"),
            P("fsdp", "tp"),
            P("tp", "fsdp"),
            P("fsdp", "ctx"),
            P("fsdp", "ctx", None),
        ),
        out_specs=(
            P("fsdp", "ctx", None),
            P("fsdp", "ctx", None),
            P("fsdp"),
            P("fsdp", None),
            P("fsdp", "tp"),
            P("fsdp", "tp"),
            P("fsdp", "tp"),
            P("tp", "fsdp"),
            P("fsdp"),
            P("fsdp", "tp"),
            P("fsdp", "tp"),
            P("tp", "fsdp"),
            P("fsdp", None),
            P("fsdp", "ctx"),
        ),
        check_vma=False,
    )
```

```python
import jax
import jax.numpy as jnp
from jax import lax
from jax.experimental import pallas as pl
from jax.experimental.pallas import tpu as pltpu
from jax.sharding import PartitionSpec as P

HEADS = 16
HEAD_DIM = 64
GROUPS = 2
LATENT = 256
MESH = pl.DeviceIdType.MESH
VMEM = pl.BlockSpec(memory_space=pltpu.VMEM)
ANY = pl.BlockSpec(memory_space=pl.ANY)
F32 = jnp.float32
BF16 = jnp.bfloat16

eps = 1e-05


def remote(src, dst, send_sem, recv_sem, device):
    return pltpu.make_async_remote_copy(
        src_ref=src,
        dst_ref=dst,
        send_sem=send_sem,
        recv_sem=recv_sem,
        device_id=device,
        device_id_type=MESH,
    )


def wait_sent(ref, sem, recv_sem):
    remote(ref, ref, sem, recv_sem, {"tp": lax.axis_index("tp")}).wait_send()


def wait_came(ref, send_sem, sem):
    remote(ref, ref, send_sem, sem, {"tp": lax.axis_index("tp")}).wait_recv()


def meet(line=0, fsdp=0, ctx=0, everyone=False):
    barrier = pltpu.get_barrier_semaphore()

    def greet(device):
        pl.semaphore_signal(barrier, inc=1, device_id=device, device_id_type=MESH)

    known = 0
    f, x, me = lax.axis_index("fsdp"), lax.axis_index("ctx"), lax.axis_index("tp")
    if fsdp and everyone:
        for k in range(1, fsdp):
            greet({"fsdp": lax.rem(f + k, fsdp)})
        known += fsdp - 1
    elif fsdp:
        greet({"fsdp": sibling(f)})
        for k in range(1, fsdp // 2):
            greet({"fsdp": lax.rem(f + 2 * k, fsdp)})
        known += fsdp // 2
    for k in range(1, ctx):
        greet({"ctx": lax.rem(x + k, ctx)})
        known += 1
    if line > 1 and everyone:
        for k in range(1, line):
            greet({"tp": lax.rem(me + k, line)})
        known += line - 1
    if line > 1 and not everyone:

        @pl.when(me > 0)
        def _():
            greet({"tp": me - 1})

        @pl.when(me < line - 1)
        def _():
            greet({"tp": me + 1})

        @pl.when((me > 0) & (me < line - 1))
        def _():
            pl.semaphore_wait(barrier, known + 2)

        @pl.when((me == 0) | (me == line - 1))
        def _():
            pl.semaphore_wait(barrier, known + 1)

    else:
        pl.semaphore_wait(barrier, known)


def sibling(f):
    return f + 1 - 2 * lax.rem(f, 2)


def block(ref, axis, index, size):
    at = pl.ds(pl.multiple_of(index * size, size), size)
    return ref.at[at] if axis == 0 else ref.at[:, at]


class Bring:
    def __init__(self, pairs, sems):
        self.copies = [pltpu.make_async_copy(src, dst, sems.at[i]) for i, (src, dst) in enumerate(pairs)]

    def start(self, which=None):
        for i in which if which is not None else range(len(self.copies)):
            self.copies[i].start()

    def wait(self, which=None):
        for i in which if which is not None else range(len(self.copies)):
            self.copies[i].wait()


class Spread:
    def __init__(self, fsdp, pairs, axes, recv, sent, own):
        self.fsdp, self.pairs, self.axes = fsdp, pairs, axes
        self.recv, self.sent, self.own = recv, sent, own
        self.f = lax.axis_index("fsdp")

    def size(self, a):
        return self.pairs[a][0].shape[self.axes[a]]

    def target(self, a, f):
        return block(self.pairs[a][1], self.axes[a], f, self.size(a))

    def start(self):
        f = self.f
        for a, (src, dst) in enumerate(self.pairs):
            for k in range(1, self.fsdp // 2):
                remote(src, self.target(a, f), self.sent.at[a], self.recv.at[a, f],
                       {"fsdp": lax.rem(f + 2 * k, self.fsdp)}).start()
        for a, (src, dst) in enumerate(self.pairs):
            remote(src, self.target(a, f), self.sent.at[a], self.recv.at[a, f],
                   {"fsdp": sibling(f)}).start()
            pltpu.make_async_copy(src, self.target(a, f), self.own.at[a]).start()

    def relay(self, which=None):
        for a in which or range(len(self.pairs)):
            for k in range(1, self.fsdp // 2):
                other = lax.rem(self.f + 2 * k, self.fsdp)
                here = self.target(a, other)
                wait_came(here, self.sent.at[a], self.recv.at[a, other])
                remote(here, here, self.sent.at[a], self.recv.at[a, other],
                       {"fsdp": sibling(self.f)}).start()

    def finish(self, which=None):
        for a in which or range(len(self.pairs)):
            src, dst = self.pairs[a]
            for k in range(0, self.fsdp // 2):
                other = lax.rem(sibling(self.f) + 2 * k, self.fsdp)
                wait_came(self.target(a, other), self.sent.at[a], self.recv.at[a, other])
            pltpu.make_async_copy(src, self.target(a, self.f), self.own.at[a]).wait()
            many = (self.fsdp - 1) * self.size(a)
            ref = dst.at[pl.ds(0, many)] if self.axes[a] == 0 else dst.at[:, pl.ds(0, many)]
            wait_sent(ref, self.sent.at[a], self.recv.at[a, 0])

    @staticmethod
    def scratch(fsdp, arrays):
        return [
            pltpu.SemaphoreType.DMA((arrays, fsdp)),
            pltpu.SemaphoreType.DMA((arrays,)),
            pltpu.SemaphoreType.DMA((arrays,)),
        ]


class CtxShare:
    def __init__(self, ctx, src, dst, recv, sent, own):
        self.ctx, self.src, self.dst = ctx, src, dst
        self.recv, self.sent, self.own = recv, sent, own
        self.x = lax.axis_index("ctx")

    def start(self):
        for k in range(1, self.ctx):
            remote(self.src, self.dst.at[self.x], self.sent.at[k - 1], self.recv.at[self.x],
                   {"ctx": lax.rem(self.x + k, self.ctx)}).start()
        pltpu.make_async_copy(self.src, self.dst.at[self.x], self.own).start()

    def finish(self):
        for k in range(1, self.ctx):
            other = lax.rem(self.x + k, self.ctx)
            wait_came(self.dst.at[other], self.sent.at[k - 1], self.recv.at[other])
            wait_sent(self.src, self.sent.at[k - 1], self.recv.at[other])
        pltpu.make_async_copy(self.src, self.dst.at[self.x], self.own).wait()

    @staticmethod
    def scratch(ctx):
        return [
            pltpu.SemaphoreType.DMA((ctx,)),
            pltpu.SemaphoreType.DMA((ctx,)),
            pltpu.SemaphoreType.DMA,
        ]


class LineGather:
    def __init__(self, n, chunk, src, dst, recv, sent, own):
        self.n, self.chunk, self.src, self.dst = n, chunk, src, dst
        self.width = src.shape[1]
        self.count = src.shape[0] // chunk
        self.recv, self.sent, self.own = recv, sent, own
        self.me = lax.axis_index("tp")

    def steps(self):
        return self.count + self.n - 1

    def columns(self, tp):
        return pl.ds(pl.multiple_of(tp * self.width, self.width), self.width)

    def place(self, tp, at):
        rows = pl.ds(pl.multiple_of(at * self.chunk, self.chunk), self.chunk)
        return self.dst.at[rows, self.columns(tp)]

    def begin(self):
        pltpu.make_async_copy(self.src, self.dst.at[:, self.columns(self.me)], self.own).start()

    def begun(self):
        pltpu.make_async_copy(self.src, self.dst.at[:, self.columns(self.me)], self.own).wait()

    def step(self, s):
        n, me, count = self.n, self.me, self.count
        left, right = {"tp": me - 1}, {"tp": me + 1}

        @pl.when((s >= 0) & (s < count))
        def _():
            rows = pl.ds(pl.multiple_of(s * self.chunk, self.chunk), self.chunk)

            @pl.when(me > 0)
            def _():
                remote(self.src.at[rows], self.place(me, s), self.sent.at[0], self.recv.at[me, s], left).start()

            @pl.when(me < n - 1)
            def _():
                remote(self.src.at[rows], self.place(me, s), self.sent.at[1], self.recv.at[me, s], right).start()

        for away in range(1, n):
            at = s - away
            for sign, onward in ((-1, right), (1, left)):
                tp = me + sign * away

                @pl.when((tp >= 0) & (tp < n) & (at >= 0) & (at < count))
                def _(tp=tp, onward=onward, sign=sign, at=at):
                    here = self.place(tp, at)
                    wait_came(here, self.sent.at[2], self.recv.at[tp, at])

                    @pl.when((me < n - 1) if sign < 0 else (me > 0))
                    def _():
                        remote(here, here, self.sent.at[2], self.recv.at[tp, at], onward).start()

    def drain(self):
        n, me = self.n, self.me

        @pl.when(me > 0)
        def _():
            wait_sent(self.src, self.sent.at[0], self.recv.at[0, 0])

        @pl.when(me < n - 1)
        def _():
            wait_sent(self.src, self.sent.at[1], self.recv.at[0, 0])

        @pl.when((me > 0) & (me < n - 1))
        def _():
            wait_sent(self.dst.at[:, pl.ds(0, (n - 1) * self.width)], self.sent.at[2], self.recv.at[0, 0])

    @staticmethod
    def scratch(n, count):
        return [
            pltpu.SemaphoreType.DMA((n, count)),
            pltpu.SemaphoreType.DMA((3,)),
            pltpu.SemaphoreType.DMA,
        ]


class LineSum:
    def __init__(self, n, chunk, hop, part, from_left, from_right, out, recv, sent, finish):
        self.n, self.chunk, self.hop = n, chunk, hop
        self.total_rows = part.shape[0]
        self.owners = (n // 2 - 1, n // 2)
        self.count = self.total_rows // 2 // chunk
        self.part, self.from_left, self.from_right, self.out = part, from_left, from_right, out
        self.recv, self.sent = recv, sent
        self.finish = finish
        self.me = lax.axis_index("tp")

    def steps(self):
        return self.count + self.hop * 2 * (self.n // 2)

    def rows(self, slot, at):
        return pl.ds(pl.multiple_of((at * 2 + slot) * self.chunk, self.chunk), self.chunk)

    def step(self, s):
        n, me, hop = self.n, self.me, self.hop
        left, right = {"tp": me - 1}, {"tp": me + 1}
        reach = n // 2
        for slot, owner in enumerate(self.owners):
            for side in (0, 1):
                lag = me if side == 0 else n - 1 - me
                at = s - hop * lag
                here = (me < owner) if side == 0 else (me > owner)
                held = self.from_left if side == 0 else self.from_right
                to = right if side == 0 else left
                here = here & (at >= 0) & (at < self.count)

                @pl.when(here & (lag == 0))
                def _(at=at, held=held, to=to, side=side, slot=slot):
                    rows = self.rows(slot, at)
                    remote(self.part.at[rows], held.at[rows], self.sent.at[0],
                           self.recv.at[side, slot, at], to).start()

                if n > 2:

                    @pl.when(here & (lag > 0))
                    def _(at=at, held=held, to=to, side=side, slot=slot):
                        rows = self.rows(slot, at)
                        wait_came(held.at[rows], self.sent.at[0], self.recv.at[side, slot, at])
                        held[rows, :] = (held[rows, :].astype(F32) + self.part[rows, :].astype(F32)).astype(BF16)
                        remote(held.at[rows], held.at[rows], self.sent.at[0],
                               self.recv.at[side, slot, at], to).start()

            at = s - hop * reach

            @pl.when((me == owner) & (at >= 0) & (at < self.count))
            def _(at=at, slot=slot, owner=owner):
                rows = self.rows(slot, at)
                total = self.part[rows, :].astype(F32)
                if owner > 0:
                    wait_came(self.from_left.at[rows], self.sent.at[0], self.recv.at[0, slot, at])
                    total = total + self.from_left[rows, :].astype(F32)
                wait_came(self.from_right.at[rows], self.sent.at[0], self.recv.at[1, slot, at])
                total = total + self.from_right[rows, :].astype(F32)
                own = pl.ds(pl.multiple_of(at * self.chunk, self.chunk), self.chunk)
                self.out[rows, :] = self.finish(rows, own, total)
                if owner > 0:
                    remote(self.out.at[rows], self.out.at[rows], self.sent.at[1],
                           self.recv.at[2, slot, at], left).start()
                remote(self.out.at[rows], self.out.at[rows], self.sent.at[2],
                       self.recv.at[2, slot, at], right).start()

        for slot, owner in enumerate(self.owners):
            away = jnp.abs(me - owner)
            at = s - hop * (reach + away)

            @pl.when((me != owner) & (at >= 0) & (at < self.count))
            def _(at=at, slot=slot, owner=owner):
                rows = self.rows(slot, at)
                here = self.out.at[rows]
                wait_came(here, self.sent.at[3], self.recv.at[2, slot, at])

                @pl.when((me < owner) & (me > 0))
                def _():
                    remote(here, here, self.sent.at[3], self.recv.at[2, slot, at], left).start()

                @pl.when((me > owner) & (me < n - 1))
                def _():
                    remote(here, here, self.sent.at[3], self.recv.at[2, slot, at], right).start()

    def drain(self):
        n, me, half = self.n, self.me, self.total_rows // 2
        lo, hi = self.owners

        def wait(sem, size):
            wait_sent(self.part.at[pl.ds(0, size)], self.sent.at[sem], self.recv.at[0, 0, 0])

        middle = (me == lo) | (me == hi)

        @pl.when(middle)
        def _():
            wait(0, half)
            wait(2, half)

        @pl.when((me != lo) & (me != hi))
        def _():
            wait(0, 2 * half)

        if lo > 0:

            @pl.when(middle)
            def _():
                wait(1, half)
                wait(3, half)

            if n > 4:

                @pl.when((me != lo) & (me != hi) & (me > 0) & (me < n - 1))
                def _():
                    wait(3, 2 * half)
        else:

            @pl.when(me == hi)
            def _():
                wait(1, half)

    @staticmethod
    def scratch(n, rows, width, chunk):
        return [
            pltpu.VMEM((rows, width), BF16),
            pltpu.VMEM((rows, width), BF16),
            pltpu.SemaphoreType.DMA((3, 2, rows // 2 // chunk)),
            pltpu.SemaphoreType.DMA((4,)),
        ]


class GradSum:
    def __init__(self, fsdp, ctx, parts, axes, outs, held, recv, sent):
        self.fsdp, self.ctx, self.parts, self.axes, self.outs = fsdp, ctx, parts, axes, outs
        self.ys = fsdp // 2
        self.held, self.recv, self.sent = held, recv, sent
        self.f = lax.axis_index("fsdp")
        self.x = lax.axis_index("ctx")
        self.y, self.c = self.f // 2, lax.rem(self.f, 2)

    @staticmethod
    def block_shape(shape, axis, fsdp):
        r, c = shape
        return (r // fsdp, c) if axis == 0 else (r, c // fsdp)

    @staticmethod
    def scratch(fsdp, ctx, shapes, first=True):
        held = []
        for shape in shapes:
            if first:
                held.append(pltpu.VMEM((fsdp // 2,) + shape, BF16))
            held += [
                pltpu.VMEM((max(fsdp // 2 - 1, 1),) + shape, BF16),
                pltpu.VMEM((ctx,) + shape, BF16),
            ]
        return held

    @staticmethod
    def semaphores(fsdp, ctx, count):
        return [pltpu.SemaphoreType.DMA((count, 3, max(fsdp // 2, ctx)))] * 2

    def part(self, a, f):
        shape = self.held[a][0].shape[1:]
        return block(self.parts[a], self.axes[a], f, shape[self.axes[a]])

    def each(self, a, body):
        rows = self.held[a][0].shape[1]
        size = 32 if rows % 32 == 0 else 16

        def step(i, carry):
            body(pl.ds(pl.multiple_of(i * size, size), size))
            return carry

        lax.fori_loop(0, rows // size, step, 0)

    def start(self):
        for a in range(len(self.parts)):
            for k in range(self.ys):
                remote(self.part(a, 2 * k + 1 - self.c), self.held[a][0].at[k], self.sent.at[a, 0, k],
                       self.recv.at[a, 0, k], {"fsdp": sibling(self.f)}).start()

    def pair(self):
        for a in range(len(self.parts)):
            first = self.held[a][0]
            for k in range(self.ys):
                wait_came(first.at[k], self.sent.at[a, 0, k], self.recv.at[a, 0, k])
                mine = self.part(a, 2 * k + self.c)

                def add(rows, first=first, k=k, mine=mine):
                    first[k, rows, :] = (first[k, rows, :].astype(F32) + mine[rows, :].astype(F32)).astype(BF16)

                self.each(a, add)

    def second(self):
        for a in range(len(self.held)):
            first, later = self.held[a][0], self.held[a][1]
            for k in range(1, self.ys):
                to = lax.rem(self.y + k, self.ys)
                remote(first.at[to], later.at[k - 1], self.sent.at[a, 1, k], self.recv.at[a, 1, k],
                       {"fsdp": 2 * to + self.c}).start()

    def third(self):
        for a in range(len(self.held)):
            first, later, last = self.held[a]
            for k in range(1, self.ys):
                wait_came(later.at[k - 1], self.sent.at[a, 1, k], self.recv.at[a, 1, k])

            def add(rows, first=first, later=later, last=last):
                total = first[self.y, rows, :].astype(F32)
                for k in range(1, self.ys):
                    total = total + later[k - 1, rows, :].astype(F32)
                last[self.x, rows, :] = total.astype(BF16)

            self.each(a, add)
            for k in range(1, self.ctx):
                remote(last.at[self.x], last.at[self.x], self.sent.at[a, 2, k], self.recv.at[a, 2, self.x],
                       {"ctx": lax.rem(self.x + k, self.ctx)}).start()

    def fourth(self, store):
        for a in range(len(self.held)):
            last = self.held[a][2]
            for k in range(1, self.ctx):
                other = lax.rem(self.x + k, self.ctx)
                wait_came(last.at[other], self.sent.at[a, 2, k], self.recv.at[a, 2, other])

            def add(rows, last=last, a=a):
                total = last[0, rows, :].astype(F32)
                for k in range(1, self.ctx):
                    total = total + last[k, rows, :].astype(F32)
                store(a, rows, total)

            self.each(a, add)

    def drain_pair(self):
        for a in range(len(self.parts)):
            for k in range(self.ys):
                wait_sent(self.held[a][0].at[k], self.sent.at[a, 0, k], self.recv.at[a, 0, k])

    def drain(self):
        for a in range(len(self.held)):
            first, later, last = self.held[a]
            for k in range(1, self.ys):
                wait_sent(later.at[k - 1], self.sent.at[a, 1, k], self.recv.at[a, 1, k])
            for k in range(1, self.ctx):
                wait_sent(last.at[self.x], self.sent.at[a, 2, k], self.recv.at[a, 2, 0])


def loop(first, last, body):
    def step(s, carry):
        body(s)
        return carry

    lax.fori_loop(first, last, step, 0)


def params(ident, mib):
    return pltpu.CompilerParams(collective_id=ident, has_side_effects=True, vmem_limit_bytes=min(mib << 20, 67043328))


def shape_of(shape, dtype):
    return jax.ShapeDtypeStruct(shape, dtype)


TILE = 256


def dot(left, right):
    return jnp.dot(left, right, preferred_element_type=F32)


def dot_t(left, right):
    return lax.dot_general(left, right, (((1,), (1,)), ((), ())), preferred_element_type=F32)


def dot_rows(left, right):
    return lax.dot_general(left, right, (((0,), (0,)), ((), ())), preferred_element_type=F32)


def head_only(value, head):
    lane = lax.broadcasted_iota(jnp.int32, value.shape, 1)
    return jnp.where((lane // HEAD_DIM) == head, value, jnp.zeros_like(value))


class RowGather:
    def __init__(self, n, src, dst, recv, sent, own):
        self.n, self.src, self.dst = n, src, dst
        self.recv, self.sent, self.own = recv, sent, own
        self.me = lax.axis_index("tp")

    def start(self):
        me = self.me
        pltpu.make_async_copy(self.src, self.dst.at[me], self.own).start()

        @pl.when(me > 0)
        def _():
            remote(self.src, self.dst.at[me], self.sent.at[0, 0], self.recv.at[me], {"tp": me - 1}).start()

        @pl.when(me < self.n - 1)
        def _():
            remote(self.src, self.dst.at[me], self.sent.at[1, 0], self.recv.at[me], {"tp": me + 1}).start()

    def each(self, body, which=None):
        me, n = self.me, self.n
        for away in which or range(1, n):
            for way, tp in ((1, me - away), (0, me + away)):

                @pl.when((tp >= 0) & (tp < n))
                def _(tp=tp, way=way, away=away):
                    onward = (me < n - 1) if way == 1 else (me > 0)
                    body(away, way, tp, onward, {"tp": me + 1} if way == 1 else {"tp": me - 1})

    def relay(self, which=None):
        def body(away, way, tp, onward, to):
            here = self.dst.at[tp]
            wait_came(here, self.sent.at[way, away], self.recv.at[tp])

            @pl.when(onward)
            def _():
                remote(here, here, self.sent.at[way, away], self.recv.at[tp], to).start()

        self.each(body, which)

    def finish(self):
        me = self.me
        pltpu.make_async_copy(self.src, self.dst.at[me], self.own).wait()

        @pl.when(me > 0)
        def _():
            wait_sent(self.src, self.sent.at[0, 0], self.recv.at[0])

        @pl.when(me < self.n - 1)
        def _():
            wait_sent(self.src, self.sent.at[1, 0], self.recv.at[0])

        def body(away, way, tp, onward, to):
            @pl.when(onward)
            def _():
                wait_sent(self.src, self.sent.at[way, away], self.recv.at[0])

        self.each(body)

    @staticmethod
    def scratch(n):
        return [
            pltpu.SemaphoreType.DMA((n,)),
            pltpu.SemaphoreType.DMA((2, n)),
            pltpu.SemaphoreType.DMA,
        ]


class AxisSum:
    def __init__(self, axis, n, slots, recv, sent):
        self.axis, self.n, self.slots, self.recv, self.sent = axis, n, slots, recv, sent
        self.at = lax.axis_index(axis)

    def start(self, value):
        self.slots[self.at] = value
        for k in range(1, self.n):
            remote(self.slots.at[self.at], self.slots.at[self.at], self.sent.at[k], self.recv.at[self.at],
                   {self.axis: lax.rem(self.at + k, self.n)}).start()

    def finish(self):
        for k in range(1, self.n):
            other = lax.rem(self.at + k, self.n)
            wait_came(self.slots.at[other], self.sent.at[k], self.recv.at[other])
            wait_sent(self.slots.at[self.at], self.sent.at[k], self.recv.at[other])
        total = self.slots[0]
        for k in range(1, self.n):
            total = total + self.slots[k]
        return total

    @staticmethod
    def scratch(n, shape):
        return [
            pltpu.VMEM((n,) + shape, F32),
            pltpu.SemaphoreType.DMA((n,)),
            pltpu.SemaphoreType.DMA((n,)),
        ]


def window(ctx, tok_dev):
    return min(ctx, (tok_dev * ctx // 2 + tok_dev - 1) // tok_dev + 1)


def key_span(ctx, tok_dev):
    return min(ctx * tok_dev // 2 // TILE, (window(ctx, tok_dev) - 1) * (tok_dev // TILE))


R_ONE, SEGMENT, VALID = 0, 1, 2


def front(tokens, gain1, gain2, w_latent, shards, w_out, wide_shards, segments, fsdp, ctx, n):
    rows, width = tokens.shape
    seq_dev, tok_dev = segments.shape
    latent, q_width = LATENT, shards[0].shape[1]
    wide, chunk = 128, 256
    pieces = rows // chunk
    win = window(ctx, tok_dev)
    full = [shape_of((s.shape[0] * fsdp,) + s.shape[1:], s.dtype) for s in shards]
    wider = [shape_of((s.shape[0], s.shape[1] * fsdp), s.dtype) for s in wide_shards]
    per_group = HEADS // GROUPS * HEAD_DIM
    per_seq = tok_dev // chunk

    def kernel(*refs):
        (tok_in, ga, gb, wlat, wq, wk, wv, wo, wg, wu, seg), refs = refs[:11], refs[11:]
        (xn_out, cols, gain_all, w_lat, w_qry, w_kproj, w_vproj, gate_all, up_all), refs = refs[:9], refs[9:]
        (wo_all, seg_all, lat_all, query, keys, values), refs = refs[:6], refs[6:]
        (gbuf, sbuf, tok, xn, tsem), refs = refs[:5], refs[5:]
        bring = Bring([(tok_in, tok), (xn, xn_out)], tsem)
        bring.start([0])
        x, me = lax.axis_index("ctx"), lax.axis_index("tp")
        gbuf[...] = jnp.zeros_like(gbuf)
        gbuf[0:1, :] = ga[...].astype(F32).reshape(1, -1)
        gbuf[1:2, :] = gb[...].astype(F32).reshape(1, -1)
        sbuf[...] = jnp.zeros_like(sbuf)
        sbuf[0:seq_dev, :] = seg[...]
        meet(n, fsdp, ctx)
        group = me * q_width // per_group
        src_lat = wlat.at[:, pl.ds(pl.multiple_of(group * latent, latent), latent)]
        pairs = [(gbuf, gain_all), (src_lat, w_lat), (wq, w_qry), (wk, w_kproj), (wv, w_vproj),
                 (wg, gate_all), (wu, up_all)]
        spread = Spread(fsdp, pairs, [1, 0, 0, 0, 0, 1, 1], *refs[:3])
        share = CtxShare(ctx, sbuf, seg_all, *refs[3:6])
        line = RowGather(n, wo, wo_all, *refs[6:9])
        lat_recv, lat_sent = refs[9:11]
        spread.start()
        share.start()
        line.start()
        own = win - 1
        cols[...] = jnp.zeros_like(cols)
        bring.wait([0])

        def scale(i):
            at = pl.ds(pl.multiple_of(i * wide, wide), wide)
            value = tok[at, :].astype(F32)
            cols[at, R_ONE : R_ONE + 1] = lax.rsqrt(jnp.mean(value * value, axis=-1, keepdims=True) + eps)

        loop(0, rows // wide, scale)
        spread.relay([0, 1])
        spread.finish([0, 1])

        def place(shard, i):
            seq = i // per_seq
            return pl.ds(pl.multiple_of(seq * win * tok_dev + shard * tok_dev + lax.rem(i, per_seq) * chunk, chunk), chunk)

        def send(k, i):
            return remote(lat_all.at[place(own, i)], lat_all.at[place(own - k, i)], lat_sent.at[k, i],
                          lat_recv.at[own - k, i], {"ctx": x + k})

        def first(i):
            at = pl.ds(pl.multiple_of(i * chunk, chunk), chunk)
            unit = (tok[at, :].astype(F32) * cols[at, R_ONE : R_ONE + 1] * gain_all[0:1, :]).astype(BF16)
            xn[at, :] = unit
            lat_all[place(own, i), :] = dot(unit, w_lat[...]).astype(BF16)
            for k in range(1, win):

                @pl.when(x + k < ctx)
                def _(k=k):
                    send(k, i).start()

        loop(0, pieces, first)
        bring.start([1])
        line.relay([1])
        spread.relay([2, 3, 4])
        spread.finish([2, 3, 4])

        def project(shard, i):
            to = place(shard, i)
            value = lat_all[to, :]
            keys[to, :] = dot(value, w_kproj[...]).astype(BF16)
            values[to, :] = dot(value, w_vproj[...]).astype(BF16)

        def ask(i):
            at = pl.ds(pl.multiple_of(i * chunk, chunk), chunk)
            query[at, :] = dot(xn[at, :], w_qry[...]).astype(BF16)
            project(own, i)

        loop(0, pieces, ask)
        share.finish()
        for q in range(seq_dev):
            at = slice(q * tok_dev, (q + 1) * tok_dev)
            ids = jnp.broadcast_to(sbuf[q : q + 1, :].astype(F32), (128, tok_dev)).T
            cols[at, SEGMENT : SEGMENT + 1] = ids[:, 0:1]
            last = seg_all[ctx - 1, q : q + 1, tok_dev - 1 : tok_dev].astype(F32)
            cols[at, VALID : VALID + 1] = jnp.where(ids[:, 0:1] != last, 1.0, 0.0)
        line.relay(range(2, n))
        for k in range(1, win):

            def theirs(i, k=k):
                @pl.when(x - k >= 0)
                def _():
                    wait_came(lat_all.at[place(own - k, i)], lat_sent.at[k, i], lat_recv.at[own - k, i])

                @pl.when(x - k < 0)
                def _():
                    lat_all[place(own - k, i), :] = jnp.zeros((chunk, latent), BF16)

                project(own - k, i)

            loop(0, pieces, theirs)

            def gone(i, k=k):
                @pl.when(x + k < ctx)
                def _():
                    send(k, i).wait_send()

            loop(0, pieces, gone)
        spread.relay([5, 6])
        spread.finish([5, 6])
        line.finish()
        bring.wait([1])

    return pl.pallas_call(
        kernel,
        out_shape=(
            shape_of((rows, width), BF16),
            shape_of((rows, 128), F32),
            shape_of((8, width), F32),
            shape_of((width, latent), BF16),
            *full,
            *wider,
            shape_of((n,) + w_out.shape, w_out.dtype),
            shape_of((ctx, 8, tok_dev), segments.dtype),
            shape_of((win * rows, latent), BF16),
            shape_of((rows, q_width), BF16),
            shape_of((win * rows, q_width), BF16),
            shape_of((win * rows, q_width), BF16),
        ),
        in_specs=[ANY] + [VMEM] * 10,
        out_specs=(ANY,) + (VMEM,) * 6 + (ANY,) * 3 + (VMEM,) * 5,
        scratch_shapes=[
            pltpu.VMEM((8, gain1.shape[0]), F32),
            pltpu.VMEM((8, tok_dev), segments.dtype),
            pltpu.VMEM((rows, width), BF16),
            pltpu.VMEM((rows, width), BF16),
            pltpu.SemaphoreType.DMA((2,)),
        ]
        + Spread.scratch(fsdp, 7)
        + CtxShare.scratch(ctx)
        + RowGather.scratch(n)
        + [pltpu.SemaphoreType.DMA((win, pieces))] * 2,
        compiler_params=params(1, 56),
    )(tokens, gain1, gain2, w_latent, *shards, w_out, *wide_shards, segments)


def counted_keys(cols, segk, at, seq, q_first, first, count, tok_dev, win):
    per = tok_dev // TILE
    oldest = lax.axis_index("ctx") - (win - 1)
    mine = cols[at, SEGMENT : SEGMENT + 1]
    shape = (mine.shape[0], TILE)
    pieces = []
    for j in range(count):
        t = first + j
        shard = oldest + t // per
        inner = pl.ds(pl.multiple_of(lax.rem(t, per) * TILE, TILE), TILE)
        ids = segk[jnp.maximum(shard, 0), pl.ds(seq, 1), inner].astype(F32)
        q_at = q_first + lax.broadcasted_iota(jnp.int32, shape, 0)
        k_at = t * TILE + lax.broadcasted_iota(jnp.int32, shape, 1)
        pieces.append((k_at <= q_at) & (ids == mine) & (shard >= 0))
    return pieces


def middle(query, keys, values, seg_all, cols, shards, gate_all, up_all, gains, tokens, out_grad,
           fsdp, ctx, n, seq_dev, late):
    rows, width = tokens.shape
    q_width = query.shape[1]
    heads = q_width // HEAD_DIM
    inner = gate_all.shape[0]
    tok_dev = rows // seq_dev
    per = tok_dev // TILE
    win, span = window(ctx, tok_dev), key_span(ctx, tok_dev)
    tiles = span + 1
    part = TILE if tiles <= 3 else 64
    chunk, hop = 32, 2
    size, piece = 256, 64
    per_block = size // piece
    half = rows // 2
    cols_at = width // 4
    block_shape = (inner, width // fsdp)
    count = 3

    def kernel(*refs):
        (q_in, k_in, v_in, segk, cols, wo_in, wd_in, wg_in, wu_in, gain, tok_in, cot_in), refs = refs[:12], refs[12:]
        (o_branch, o_feed, o_dmid, o_mid, o_wo, o_gain, o_bsq, o_mark, o_att, o_lse), refs = refs[:10], refs[10:]
        outs, refs = refs[:3], refs[3:]
        one, gsems, parts, refs = refs[:4], refs[4:6], refs[6:9], refs[9:]
        (query, keys, values, att, att_all, wo, wd, wg, wu, tok, cot), refs = refs[:11], refs[11:]
        (mid, r2, xn, hid, dg, du, p_two, p_feed, bsem), refs = refs[:9], refs[9:]
        bring = Bring([(q_in, query), (k_in, keys), (v_in, values), (tok_in, tok), (wg_in, wg), (wu_in, wu),
                       (cot_in, cot), (att, o_att), (p_feed, o_feed)], bsem)
        bring.start(range(7))
        meet(n, fsdp, ctx)
        line = LineGather(n, piece, att, att_all, *refs[:3])
        spread = Spread(fsdp, [(wo_in, wo), (wd_in, wd)], [1, 1], *refs[3:6])
        keep = refs[6:]
        spread.start()
        o_gain[...] = jnp.zeros_like(o_gain)
        o_bsq[...] = jnp.zeros_like(o_bsq)
        o_mark[...] = jnp.zeros_like(o_mark)
        g2 = gain.at[1:2]

        def back(at, own, total):
            middle_rows = mid[at, :]
            o_mid[own, :] = middle_rows
            unit = middle_rows * r2[at, :]
            o_gain[...] += jnp.sum((total * unit).reshape(chunk // 8, 8, width), axis=0)
            scaled = total * g2[...]
            mean = jnp.mean(scaled * unit, axis=-1, keepdims=True)
            d_mid = cot[at, :].astype(F32) + r2[at, :] * (scaled - unit * mean)
            o_dmid[own, :] = d_mid
            first_unit = tok[at, :].astype(F32) * cols[at, R_ONE : R_ONE + 1]
            o_mark[at, 0:1] = jnp.sum(first_unit * d_mid, axis=-1, keepdims=True)
            return d_mid.astype(BF16)

        first = LineSum(n, chunk, hop, p_two, one[0], one[1], o_branch, one[2], one[3], back)
        if late:
            held = [[out, None, None] for out in outs]
        else:
            held = [keep[3 * a : 3 * a + 3] for a in range(count)]
        grad = GradSum(fsdp, ctx, parts, [1] * count, outs, held, *gsems)
        bring.wait([0, 1, 2])

        def query_rows(i, j):
            seq = i // per
            q_tile = (win - 1) * per + lax.rem(i, per)
            at = pl.ds(pl.multiple_of(i * TILE + j * part, part), part)
            near = pl.ds(pl.multiple_of((seq * win * per + q_tile - span) * TILE, TILE), tiles * TILE)
            counted = jnp.concatenate(
                [
                    c.astype(F32)
                    for c in counted_keys(
                        cols, segk, at, seq, q_tile * TILE + j * part, q_tile - span, tiles, tok_dev, win
                    )
                ],
                axis=1,
            )
            accum = jnp.zeros((part, q_width), F32)
            lane = lax.broadcasted_iota(jnp.int32, (part, 128), 1)
            kept = jnp.zeros((part, 128), F32)
            for h in range(heads):
                score = jnp.where(counted > 0.0, dot_t(head_only(query[at, :], h), keys[near, :]) * 0.125, -1e30)
                top = jnp.max(score, axis=-1, keepdims=True)
                weight = jnp.exp(score - top)
                total = jnp.sum(weight, axis=-1, keepdims=True)
                prob = (weight * (1.0 / total)).astype(BF16)
                accum = accum + jnp.dot(prob, head_only(values[near, :], h), preferred_element_type=F32)
                kept = jnp.where(lane == h, top + jnp.log(total), kept)
                if part == TILE:
                    line.step((i - 1) * per_block + h * per_block // heads)
            o_lse[at, :] = kept
            att[at, :] = accum.astype(BF16)

        def query_tile(i):
            if part == TILE:
                query_rows(i, 0)
                return
            loop(0, TILE // part, lambda j: query_rows(i, j))
            for h in range(per_block):
                line.step((i - 1) * per_block + h)

        loop(0, rows // TILE, query_tile)
        bring.start([7])
        line.begin()
        s1 = (rows // TILE - 1) * per_block
        spread.relay()
        spread.finish()
        tp = lax.axis_index("tp")
        o_wo[...] = wo[pl.ds(pl.multiple_of(tp * q_width, q_width), q_width), :]
        line.begun()
        bring.wait([3, 4, 5, 6])

        def block_of_rows(b):
            at = pl.ds(pl.multiple_of(b * size, size), size)
            seq = b * size // tok_dev

            def steps(j):
                line.step(s1 + b * per_block + j)
                first.step((b - 1) * per_block + j)

            branch = dot(att_all[at, :], wo[...])
            middle_rows = tok[at, :].astype(F32) + branch
            mid[at, :] = middle_rows
            o_bsq[pl.ds(pl.multiple_of(seq * 8, 8), 8), :] += jnp.sum(
                (branch * branch * cols[at, VALID : VALID + 1]).reshape(size // 8, 8, width), axis=0
            )
            scale = lax.rsqrt(jnp.mean(middle_rows * middle_rows, axis=-1, keepdims=True) + eps)
            r2[at, :] = scale
            unit = (middle_rows * scale * g2[...]).astype(BF16)
            xn[at, :] = unit
            steps(0)
            gate = dot_t(unit, wg[...])
            upper = dot_t(unit, wu[...])
            sigma = jax.nn.sigmoid(gate)
            swish = gate * sigma
            hidden = (swish * upper).astype(BF16)
            hid[at, :] = hidden
            slope = upper * sigma * (1.0 + gate * (1.0 - sigma))
            steps(1)
            p_feed[at, :] = dot(hidden, wd[...]).astype(BF16)
            d_hidden = dot_t(cot[at, :], wd[...])
            d_gate = (d_hidden * slope).astype(BF16)
            d_upper = (d_hidden * swish).astype(BF16)
            dg[at, :] = d_gate
            du[at, :] = d_upper
            steps(2)
            p_two[at, :] = (dot(d_gate, wg[...]) + dot(d_upper, wu[...])).astype(BF16)
            steps(3)

        loop(0, rows // size, block_of_rows)
        bring.start([8])
        s0 = (rows // size - 1) * per_block

        def product(i):
            at = pl.ds(pl.multiple_of(i * cols_at, cols_at), cols_at)
            left = xn[:, at]
            parts[0][:, at] = dot_rows(dg[...], left).astype(BF16)
            parts[1][:, at] = dot_rows(du[...], left).astype(BF16)
            parts[2][:, at] = dot_rows(hid[...], cot[:, at]).astype(BF16)

        def busy(s):
            first.step(s)
            product(s - s0)

        loop(s0, s0 + 4, busy)
        grad.start()
        last = first.steps()
        loop(s0 + 4, s0 + 6, first.step)
        grad.pair()
        if not late:
            grad.second()
        loop(s0 + 6, last, first.step)
        if not late:
            grad.third()

            def store(a, at, total):
                outs[a][at, :] = total

            grad.fourth(store)
            grad.drain()
        line.drain()
        first.drain()
        grad.drain_pair()
        bring.wait([7, 8])

    ys = fsdp // 2
    out = pl.pallas_call(
        kernel,
        out_shape=(
            shape_of((rows, width), BF16),
            shape_of((rows, width), BF16),
            shape_of((half, width), F32),
            shape_of((half, width), F32),
            shape_of((q_width, width), BF16),
            shape_of((8, width), F32),
            shape_of((8 * seq_dev, width), F32),
            shape_of((rows, 128), F32),
            shape_of((rows, q_width), BF16),
            shape_of((rows, 128), F32),
        )
        + ((shape_of((ys,) + block_shape, BF16) if late else shape_of(block_shape, F32)),) * count,
        in_specs=[ANY] * 3 + [VMEM] * 4 + [ANY] * 2 + [VMEM] + [ANY] * 2,
        out_specs=(VMEM, ANY) + (VMEM,) * 6 + (ANY, VMEM) + (VMEM,) * count,
        scratch_shapes=LineSum.scratch(n, rows, width, chunk)
        + GradSum.semaphores(fsdp, ctx, count)
        + [pltpu.VMEM((inner, width), BF16)] * count
        + [
            pltpu.VMEM((rows, q_width), BF16),
            pltpu.VMEM((win * rows, q_width), BF16),
            pltpu.VMEM((win * rows, q_width), BF16),
            pltpu.VMEM((rows, q_width), BF16),
            pltpu.VMEM((rows, n * q_width), BF16),
            pltpu.VMEM((n * q_width, width), BF16),
            pltpu.VMEM((inner, width), BF16),
            pltpu.VMEM((inner, width), BF16),
            pltpu.VMEM((inner, width), BF16),
            pltpu.VMEM((rows, width), BF16),
            pltpu.VMEM((rows, width), BF16),
            pltpu.VMEM((rows, width), F32),
            pltpu.VMEM((rows, 1), F32),
            pltpu.VMEM((rows, width), BF16),
            pltpu.VMEM((rows, inner), BF16),
            pltpu.VMEM((rows, inner), BF16),
            pltpu.VMEM((rows, inner), BF16),
            pltpu.VMEM((rows, width), BF16),
            pltpu.VMEM((rows, width), BF16),
            pltpu.SemaphoreType.DMA((9,)),
        ]
        + LineGather.scratch(n, rows // piece)
        + Spread.scratch(fsdp, 2)
        + ([] if late else GradSum.scratch(fsdp, ctx, [block_shape] * count)),
        compiler_params=params(2, 64),
    )(query, keys, values, seg_all, cols, *shards, gate_all, up_all, gains, tokens, out_grad)
    return out[:10], out[10:]


def back(query, keys, values, seg_all, cols, lse, attended, d_branch, wo_rows, weights, lat_all, xn_one, gains,
         tokens, d_middle, mid_own, part_feed, marks, gain_part, branch_sq, firsts, fsdp, ctx, n, seq_dev):
    rows, width = tokens.shape
    w_qry, w_lat, w_kproj, w_vproj = weights
    q_width, latent = query.shape[1], w_lat.shape[1]
    heads, tok_dev = q_width // HEAD_DIM, rows // seq_dev
    per = tok_dev // TILE
    win, span = window(ctx, tok_dev), key_span(ctx, tok_dev)
    tiles = span + 1
    group = tiles if tiles <= 3 else 1
    chunk, hop, wide, side = 32, 2, 256, 128
    half = rows // 2
    axes = (0, 0, 0, 1, 0)
    whole = ((width, q_width), (latent, q_width), (latent, q_width), (q_width, width), (width, latent))
    blocks = [GradSum.block_shape(w, a, fsdp) for w, a in zip(whole, axes)]
    lat = blocks[-1]
    ffn = [f.shape[1:] for f in firsts]
    seq_pieces = tok_dev // wide
    many = max(width, rows)

    def kernel(*refs):
        (q_ref, k_ref, v_ref, segk, cols, lse_ref, att, dbr, wo), refs = refs[:9], refs[9:]
        (wq, wl, wk, wv, la_in, xn_in, gain, tok_in, dmid_in, mid_in, feed_in), refs = refs[:11], refs[11:]
        (marks, gain_two, bsq), fsts, refs = refs[:3], refs[3 : 3 + len(ffn)], refs[3 + len(ffn) :]
        (o_tok, o_mixed, o_small), outs, refs = refs[:3], refs[3:8], refs[8:]
        fouts, refs = refs[: len(ffn)], refs[len(ffn) :]
        one, two, keep, gsems, parts, refs = refs[:4], refs[4:8], refs[8:23], refs[23:25], refs[25:30], refs[30:]
        (p_one, dlat, came, c_recv, c_sent, gacc, sm, sacc), refs = refs[:8], refs[8:]
        (dk, dv, dq, dqb, grad_seq, lat_parts), refs = refs[:6], refs[6:]
        (la, xn, tok, dmid, mid, p_feed, bsem), refs = refs[:7], refs[7:]
        (lat_own, lat_every), lsems, sums, refs = refs[:2], refs[2:5], refs[5:14], refs[14:]
        bring = Bring([(feed_in, p_feed), (mid_in, mid), (la_in, la), (xn_in, xn), (tok_in, tok), (dmid_in, dmid)], bsem)
        bring.start()
        meet(n, fsdp, ctx, everyone=True)
        x = lax.axis_index("ctx")
        own_shard = win - 1
        grad_ffn = None
        if ffn:
            fkeep, fsems = refs[: 2 * len(ffn)], refs[2 * len(ffn) :]
            grad_ffn = GradSum(fsdp, ctx, [], [], fouts,
                               [[fsts[a], fkeep[2 * a], fkeep[2 * a + 1]] for a in range(len(ffn))], *fsems)
            grad_ffn.second()
        gacc[...] = jnp.zeros_like(gacc)
        sacc[...] = jnp.zeros_like(sacc)
        sm[...] = jnp.zeros_like(sm)
        g1 = gain.at[0:1]

        def forward(at, own, total):
            mixed = mid[own, :] + total
            seq = at.start // tok_dev
            counted = cols[at, VALID : VALID + 1]
            sacc[seq] += jnp.sum((mixed * mixed * counted).reshape(chunk // 8, 8, width), axis=0)
            sacc[seq_dev + seq] += jnp.sum((total * total * counted).reshape(chunk // 8, 8, width), axis=0)
            return mixed.astype(BF16)

        def backward(at, own, total):
            r1 = cols[at, R_ONE : R_ONE + 1]
            unit = tok[at, :].astype(F32) * r1
            scaled = total * g1[...]
            mean = jnp.mean(scaled * unit, axis=-1, keepdims=True)
            return (dmid[own, :] + r1 * (scaled - unit * mean)).astype(BF16)

        feed = LineSum(n, chunk, hop, p_feed, two[0], two[1], o_mixed, two[2], two[3], forward)
        first = LineSum(n, chunk, hop, p_one, one[0], one[1], o_tok, one[2], one[3], backward)
        grad = GradSum(fsdp, ctx, parts, axes, outs, [keep[3 * a : 3 * a + 3] for a in range(5)], *gsems)
        line = RowGather(n, lat_own, lat_every, *lsems)
        over_tp = AxisSum("tp", n, *sums[0:3])
        over_ctx = AxisSum("ctx", ctx, *sums[3:6])
        over_fsdp = AxisSum("fsdp", fsdp, *sums[6:9])

        def clear(i):
            at = pl.ds(pl.multiple_of(i * TILE, TILE), TILE)
            dk[at, :] = jnp.zeros((TILE, q_width), F32)
            dv[at, :] = jnp.zeros((TILE, q_width), F32)

        loop(0, win * rows // TILE, clear)
        bring.wait([0, 1])

        def query_tile(i, step):
            seq = i // per
            q_tile = own_shard * per + lax.rem(i, per)
            at = pl.ds(pl.multiple_of(i * TILE, TILE), TILE)
            grad_seq[...] = dot_t(dbr[at, :], wo[...]).astype(BF16)
            product = grad_seq[...].astype(F32) * att[at, :].astype(F32)
            delta = [jnp.sum(head_only(product, h), axis=-1, keepdims=True) for h in range(heads)]
            dq[...] = jnp.zeros_like(dq)

            def key_tiles(kk):
                t = q_tile - span + kk * group
                near = pl.ds(pl.multiple_of((seq * win * per + t) * TILE, TILE), group * TILE)
                counted = jnp.concatenate(
                    [c.astype(F32) for c in counted_keys(cols, segk, at, seq, q_tile * TILE, t, group, tok_dev, win)], axis=1
                )
                kept = lse_ref[at, :]
                d_query = jnp.zeros((TILE, q_width), F32)
                d_key = jnp.zeros((group * TILE, q_width), F32)
                d_value = jnp.zeros((group * TILE, q_width), F32)
                for h in range(heads):
                    mine, ours = head_only(q_ref[at, :], h), head_only(grad_seq[...], h)
                    score = jnp.where(counted > 0.0, dot_t(mine, k_ref[near, :]) * 0.125, -1e30)
                    prob = jnp.exp(score - kept[:, h : h + 1]) * counted
                    d_score = (prob * (dot_t(ours, v_ref[near, :]) - delta[h])).astype(BF16)
                    d_query = d_query + jnp.dot(d_score, head_only(k_ref[near, :], h), preferred_element_type=F32)
                    d_key = d_key + dot_rows(d_score, mine)
                    d_value = d_value + dot_rows(prob.astype(BF16), ours)
                    step(kk * heads + h)
                dq[...] += d_query
                dk[near, :] += d_key * 0.125
                dv[near, :] += d_value

            loop(0, tiles // group, key_tiles)
            dqb[at, :] = (dq[...] * 0.125).astype(BF16)

        def latent_rows(shard, seq, i):
            return pl.ds(pl.multiple_of((seq * win + shard) * tok_dev + i * wide, wide), wide)

        def send(k, seq, i):
            at = pl.ds(pl.multiple_of(seq * tok_dev + i * wide, wide), wide)
            return remote(lat_parts.at[latent_rows(own_shard - k, seq, i)], came.at[k - 1, at],
                          c_sent.at[k - 1, seq, i], c_recv.at[k - 1, seq, i], {"ctx": x - k})

        def latents(seq):
            for k in range(win - 1, -1, -1):
                for i in range(seq_pieces):
                    at = latent_rows(own_shard - k, seq, i)
                    lat_parts[at, :] = (
                        dot_t(dk[at, :].astype(BF16), wk[...]) + dot_t(dv[at, :].astype(BF16), wv[...])
                    ).astype(BF16)
                    if k > 0:

                        @pl.when(x - k >= 0)
                        def _(k=k, i=i):
                            send(k, seq, i).start()

        def whole_latent(j):
            seq, i = j // seq_pieces, lax.rem(j, seq_pieces)
            at = pl.ds(pl.multiple_of(j * wide, wide), wide)
            dlat[at, :] = lat_parts[latent_rows(own_shard, seq, i), :]
            for k in range(1, win):

                @pl.when(x + k < ctx)
                def _(k=k):
                    wait_came(came.at[k - 1, at], c_sent.at[k - 1, seq, i], c_recv.at[k - 1, seq, i])
                    dlat[at, :] = (dlat[at, :].astype(F32) + came[k - 1, at, :].astype(F32)).astype(BF16)

            p_one[at, :] = (dot_t(dqb[at, :], wq[...]) + dot_t(dlat[at, :], wl[...])).astype(BF16)

        tile_steps = (tiles // group) * heads
        every = max(tile_steps // 4, 1)

        def sequence(seq):
            def tile(i):
                def step(j):
                    @pl.when(lax.rem(j, every) == 0)
                    def _():
                        feed.step(i * (tile_steps // every) + j // every)

                query_tile(i, step)

            loop(seq * per, seq * per + per, tile)
            latents(seq)

        loop(0, seq_dev, sequence)
        fed = seq_dev * per * (tile_steps // every)

        bring.wait([2, 3, 4, 5])

        def product(i):
            at = pl.ds(pl.multiple_of(i * wide, wide), wide)
            parts[0][at, :] = dot_rows(xn[:, at], dqb[...]).astype(BF16)
            parts[3][:, at] = dot_rows(att[...], dbr[:, at]).astype(BF16)

        def steps(s):
            first.step(s)
            feed.step(fed + s)

        early = (seq_dev - 1) * seq_pieces
        loop(0, early, whole_latent)

        def mixed_work(i):
            product(i)
            steps(i)

        loop(0, width // wide, mixed_work)
        s0 = width // wide
        if grad_ffn is not None:
            grad_ffn.third()
        parts[1][...] = dot_rows(la[...], dk[...].astype(BF16)).astype(BF16)
        parts[2][...] = dot_rows(la[...], dv[...].astype(BF16)).astype(BF16)
        loop(early, rows // wide, whole_latent)

        def product_lat(s):
            at = pl.ds(pl.multiple_of((s - s0) * wide, wide), wide)
            parts[4][at, :] = dot_rows(xn[:, at], dlat[...]).astype(BF16)
            steps(s)

        begun = s0 + width // wide
        loop(s0, begun, product_lat)
        grad.start()

        def gains_of(s):
            steps(s)
            at = pl.ds(pl.multiple_of((s - begun) * side, side), side)
            value = p_one[at, :].astype(F32) * (tok[at, :].astype(F32) * cols[at, R_ONE : R_ONE + 1])
            gacc[...] += jnp.sum(value.reshape(side // 8, 8, width), axis=0)
            along = lax.dot_general(jnp.ones((8, width), F32), value * g1[...], (((1,), (1,)), ((), ())),
                                    precision=lax.Precision.HIGHEST, preferred_element_type=F32)
            sm[3:4, at] = along[0:1, :]
            sm[4:5, at] = marks[at, :].T[0:1, :]
            sm[5:6, at] = cols[at, :].T[R_ONE : R_ONE + 1, :]

        mark = begun + rows // side
        loop(begun, begun + 1, gains_of)
        grad.pair()
        grad.second()
        loop(begun + 1, begun + 4, gains_of)
        grad.third()
        loop(begun + 4, mark, gains_of)
        last = first.steps()
        for s in range(fed + mark, feed.steps()):
            feed.step(s)
        lane = lax.broadcasted_iota(jnp.int32, (1, many), 1)
        once = jnp.where(lax.axis_index("tp") == 0, 1.0, 0.0)
        row = jnp.zeros((1, many), F32)

        def whole_sum(value):
            return jnp.sum(jnp.sum(value, axis=0, keepdims=True), axis=1, keepdims=True)

        for q in range(seq_dev):
            values = [
                whole_sum(sacc[q]),
                whole_sum(sacc[seq_dev + q]),
                whole_sum(bsq[8 * q : 8 * q + 8, :]) * once,
                jnp.sum(cols[q * tok_dev : (q + 1) * tok_dev, VALID : VALID + 1], axis=0, keepdims=True) * once,
            ]
            for j, value in enumerate(values):
                row = row + jnp.where(lane == 4 * q + j, value, 0.0)
        sm[2:3, :] = row
        sm[0:1, 0:width] = jnp.sum(gacc[...], axis=0, keepdims=True)
        sm[1:2, 0:width] = jnp.sum(gain_two[...], axis=0, keepdims=True)
        r_row = sm[5:6, :]
        over_tp.start(sm[...])

        def store(a, at, total):
            if a < 4:
                outs[a][at, :] = total
            else:
                lat_own[at, :] = total.astype(BF16)

        def store_ffn(a, at, total):
            fouts[a][at, :] = total

        grad.fourth(store)
        line.start()
        loop(mark, mark + 2, steps)
        line.relay([1])
        along_tp = over_tp.finish()
        over_ctx.start(along_tp)
        loop(mark + 2, mark + 4, steps)
        if n > 2:
            line.relay([2])
        along_ctx = over_ctx.finish()
        over_fsdp.start(along_ctx)
        if grad_ffn is not None:
            grad_ffn.fourth(store_ffn)
        loop(mark + 4, last, steps)
        if n > 3:
            line.relay(range(3, n))
        everywhere = over_fsdp.finish()
        row = lax.broadcasted_iota(jnp.int32, everywhere.shape, 0)
        o_small[...] = jnp.where(row < 2, everywhere, along_ctx)
        o_small[3:4, :] = (along_tp[4:5] + eps * r_row * r_row * r_row * along_tp[3:4]) * (1.0 / width**0.5)
        line.finish()

        def gather(i):
            at = pl.ds(pl.multiple_of(i * 16, 16), 16)
            for g in range(GROUPS):
                total = jnp.zeros((16, lat[1]), F32)
                for t in range(n):
                    if t * GROUPS // n == g:
                        total = total + lat_every[t, at, :].astype(F32)
                outs[4][at, g * lat[1] : (g + 1) * lat[1]] = total

        loop(0, lat[0] // 16, gather)
        for k in range(1, win):

            @pl.when(x - k >= 0)
            def _(k=k):
                for seq in range(seq_dev):
                    for i in range(seq_pieces):
                        send(k, seq, i).wait_send()

        feed.drain()
        first.drain()
        grad.drain_pair()
        grad.drain()
        if grad_ffn is not None:
            grad_ffn.drain()

    out = pl.pallas_call(
        kernel,
        out_shape=(
            shape_of((rows, width), BF16),
            shape_of((rows, width), BF16),
            shape_of((8, many), F32),
        )
        + tuple(shape_of(b, F32) for b in blocks[:-1])
        + (shape_of((lat[0], GROUPS * lat[1]), F32),)
        + tuple(shape_of(f, F32) for f in ffn),
        in_specs=[VMEM] * 13 + [ANY] * 2 + [VMEM] + [ANY] * 4 + [VMEM] * (3 + len(ffn)),
        out_specs=(VMEM,) * (8 + len(ffn)),
        scratch_shapes=LineSum.scratch(n, rows, width, chunk) * 2
        + GradSum.scratch(fsdp, ctx, blocks)
        + GradSum.semaphores(fsdp, ctx, 5)
        + [pltpu.VMEM(w, BF16) for w in whole]
        + [
            pltpu.VMEM((rows, width), BF16),
            pltpu.VMEM((rows, latent), BF16),
            pltpu.VMEM((max(win - 1, 1), rows, latent), BF16),
            pltpu.SemaphoreType.DMA((max(win - 1, 1), seq_dev, seq_pieces)),
            pltpu.SemaphoreType.DMA((max(win - 1, 1), seq_dev, seq_pieces)),
            pltpu.VMEM((8, width), F32),
            pltpu.VMEM((8, many), F32),
            pltpu.VMEM((2 * seq_dev, 8, width), F32),
            pltpu.VMEM((win * rows, q_width), F32),
            pltpu.VMEM((win * rows, q_width), F32),
            pltpu.VMEM((TILE, q_width), F32),
            pltpu.VMEM((rows, q_width), BF16),
            pltpu.VMEM((TILE, q_width), BF16),
            pltpu.VMEM((win * rows, latent), BF16),
        ]
        + [
            pltpu.VMEM((win * rows, latent), BF16),
            pltpu.VMEM((rows, width), BF16),
            pltpu.VMEM((rows, width), BF16),
            pltpu.VMEM((half, width), F32),
            pltpu.VMEM((half, width), F32),
            pltpu.VMEM((rows, width), BF16),
            pltpu.SemaphoreType.DMA((6,)),
        ]
        + [pltpu.VMEM(lat, BF16), pltpu.VMEM((n,) + lat, BF16)]
        + RowGather.scratch(n)
        + AxisSum.scratch(n, (8, many))
        + AxisSum.scratch(ctx, (8, many))
        + AxisSum.scratch(fsdp, (8, many))
        + (GradSum.scratch(fsdp, ctx, ffn, False) + GradSum.semaphores(fsdp, ctx, len(ffn)) if ffn else []),
        compiler_params=params(3, 64),
    )(query, keys, values, seg_all, cols, lse, attended, d_branch, wo_rows, w_qry, w_lat, w_kproj, w_vproj,
      lat_all, xn_one, gains, tokens, d_middle, mid_own, part_feed, marks, gain_part, branch_sq, *firsts)
    return out[:3], out[3:8], out[8:]


def publish(arrays, small, seq_dev, tok_dev, feat_dim, fsdp):
    count = len(arrays)
    per = feat_dim // fsdp

    def kernel(*refs):
        srcs, sm, refs = refs[:count], refs[count], refs[count + 1 :]
        dsts, (gains, stats, radial), refs = refs[:count], refs[count : count + 3], refs[count + 3 :]
        inward = Bring(list(zip(srcs, refs[:count])), refs[count])
        outward = Bring(list(zip(refs[:count], dsts)), refs[count + 1])
        inward.start()
        f = lax.axis_index("fsdp")
        gains[...] = sm[0:2, pl.ds(pl.multiple_of(f * per, per), per)]
        for q in range(seq_dev):
            radial[q : q + 1, :] = sm[3:4, q * tok_dev : (q + 1) * tok_dev]
            total = sm[2:3, 4 * q + 3 : 4 * q + 4] * feat_dim
            for j, lane in enumerate((0, 2, 1)):
                stats[q : q + 1, j : j + 1] = jnp.sqrt(sm[2:3, 4 * q + lane : 4 * q + lane + 1] / total)
        for i in range(count):
            inward.wait([i])
            outward.start([i])
        outward.wait()

    out = pl.pallas_call(
        kernel,
        out_shape=tuple(shape_of(a.shape, a.dtype) for a in arrays)
        + (shape_of((2, per), F32), shape_of((seq_dev, 3), F32), shape_of((seq_dev, tok_dev), F32)),
        in_specs=[ANY] * count + [VMEM],
        out_specs=(ANY,) * count + (VMEM,) * 3,
        scratch_shapes=[pltpu.VMEM(a.shape, a.dtype) for a in arrays] + [pltpu.SemaphoreType.DMA((count,))] * 2,
        compiler_params=pltpu.CompilerParams(vmem_limit_bytes=60 << 20),
    )(*arrays, small)
    return out[:count], out[count], out[count + 1], out[count + 2]


def on_device(
    tokens, gain1, w_latent, w_query, w_key, w_value, w_out, gain2, w_gate, w_up, w_down, segments, cotangent
):
    seq_dev, tok_dev, feat_dim = tokens.shape
    n_ctx, n_tp, n_fsdp = lax.axis_size("ctx"), lax.axis_size("tp"), lax.axis_size("fsdp")
    row_count = seq_dev * tok_dev
    tok_rows = tokens.reshape(row_count, feat_dim)
    out_grad = cotangent.reshape(row_count, feat_dim)
    (xn_one, cols, gains, w_lat, w_qry, w_kproj, w_vproj, gate_all, up_all, wo_cols, seg_all, lat_all,
     query, keys, values) = front(
        tok_rows, gain1, gain2, w_latent, (w_query, w_key, w_value), w_out, (w_gate.T, w_up.T), segments,
        n_fsdp, n_ctx, n_tp,
    )
    late = window(n_ctx, tok_dev) <= 2
    (d_branch, part_feed, d_middle, mid_own, wo_rows, gain_part, branch_sq, marks, attended, lse), ffn = middle(
        query, keys, values, seg_all, cols, (wo_cols.reshape(-1, w_out.shape[1]), w_down), gate_all, up_all, gains,
        tok_rows, out_grad, n_fsdp, n_ctx, n_tp, seq_dev, late,
    )
    (grad_tokens, mixed, small), (s_qry, s_kproj, s_vproj, s_outp, s_lat), late_ffn = back(
        query, keys, values, seg_all, cols, lse, attended, d_branch, wo_rows, (w_qry, w_lat, w_kproj, w_vproj),
        lat_all, xn_one, gains, tok_rows, d_middle, mid_own, part_feed, marks, gain_part, branch_sq,
        ffn if late else (), n_fsdp, n_ctx, n_tp, seq_dev,
    )
    s_gate, s_up, s_down = late_ffn if late else ffn
    arrays, gain_grads, stats, radial = publish(
        (mixed, grad_tokens, s_lat, s_qry, s_kproj, s_vproj, s_outp, s_gate, s_up, s_down), small,
        seq_dev, tok_dev, feat_dim, n_fsdp,
    )
    mixed, grad_tokens, s_lat, s_qry, s_kproj, s_vproj, s_outp, s_gate, s_up, s_down = arrays
    return (
        mixed.reshape(seq_dev, tok_dev, feat_dim),
        grad_tokens.reshape(seq_dev, tok_dev, feat_dim),
        gain_grads[0],
        s_lat,
        s_qry,
        s_kproj,
        s_vproj,
        s_outp,
        gain_grads[1],
        s_gate.T,
        s_up.T,
        s_down,
        stats,
        radial,
    )


def solution(mesh):
    return jax.shard_map(
        on_device,
        mesh=mesh,
        in_specs=(
            P("fsdp", "ctx", None),
            P("fsdp"),
            P("fsdp", None),
            P("fsdp", "tp"),
            P("fsdp", "tp"),
            P("fsdp", "tp"),
            P("tp", "fsdp"),
            P("fsdp"),
            P("fsdp", "tp"),
            P("fsdp", "tp"),
            P("tp", "fsdp"),
            P("fsdp", "ctx"),
            P("fsdp", "ctx", None),
        ),
        out_specs=(
            P("fsdp", "ctx", None),
            P("fsdp", "ctx", None),
            P("fsdp"),
            P("fsdp", None),
            P("fsdp", "tp"),
            P("fsdp", "tp"),
            P("fsdp", "tp"),
            P("tp", "fsdp"),
            P("fsdp"),
            P("fsdp", "tp"),
            P("fsdp", "tp"),
            P("tp", "fsdp"),
            P("fsdp", None),
            P("fsdp", "ctx"),
        ),
        check_vma=False,
    )
```

```python
from types import SimpleNamespace

import jax
import jax.numpy as jnp
from jax import lax
from jax.experimental import pallas as pl
from jax.experimental.pallas import tpu as pltpu
from jax.sharding import PartitionSpec as P

HEADS = 16
HEAD_DIM = 64
GROUPS = 2
LATENT = 256
MESH = pl.DeviceIdType.MESH
VMEM = pl.BlockSpec(memory_space=pltpu.VMEM)
ANY = pl.BlockSpec(memory_space=pl.ANY)
F32 = jnp.float32
BF16 = jnp.bfloat16

eps = 1e-05


def remote(src, dst, send_sem, recv_sem, device):
    return pltpu.make_async_remote_copy(
        src_ref=src,
        dst_ref=dst,
        send_sem=send_sem,
        recv_sem=recv_sem,
        device_id=device,
        device_id_type=MESH,
    )


def wait_sent(ref, sem, recv_sem):
    remote(ref, ref, sem, recv_sem, {"tp": lax.axis_index("tp")}).wait_send()


def wait_came(ref, send_sem, sem):
    remote(ref, ref, send_sem, sem, {"tp": lax.axis_index("tp")}).wait_recv()


def meet(line=0, fsdp=0, ctx=0, everyone=False):
    barrier = pltpu.get_barrier_semaphore()

    def greet(device):
        pl.semaphore_signal(barrier, inc=1, device_id=device, device_id_type=MESH)

    known = 0
    f, x, me = lax.axis_index("fsdp"), lax.axis_index("ctx"), lax.axis_index("tp")
    if fsdp and everyone:
        for k in range(1, fsdp):
            greet({"fsdp": lax.rem(f + k, fsdp)})
        known += fsdp - 1
    elif fsdp:
        greet({"fsdp": sibling(f)})
        for k in range(1, fsdp // 2):
            greet({"fsdp": lax.rem(f + 2 * k, fsdp)})
        known += fsdp // 2
    for k in range(1, ctx):
        greet({"ctx": lax.rem(x + k, ctx)})
        known += 1
    if line > 1 and everyone:
        for k in range(1, line):
            greet({"tp": lax.rem(me + k, line)})
        known += line - 1
    if line > 1 and not everyone:

        @pl.when(me > 0)
        def _():
            greet({"tp": me - 1})

        @pl.when(me < line - 1)
        def _():
            greet({"tp": me + 1})

        @pl.when((me > 0) & (me < line - 1))
        def _():
            pl.semaphore_wait(barrier, known + 2)

        @pl.when((me == 0) | (me == line - 1))
        def _():
            pl.semaphore_wait(barrier, known + 1)

    else:
        pl.semaphore_wait(barrier, known)


def sibling(f):
    return f + 1 - 2 * lax.rem(f, 2)


def block(ref, axis, index, size):
    at = pl.ds(pl.multiple_of(index * size, size), size)
    return ref.at[at] if axis == 0 else ref.at[:, at]


class Bring:
    def __init__(self, pairs, sems):
        self.copies = [pltpu.make_async_copy(src, dst, sems.at[i]) for i, (src, dst) in enumerate(pairs)]

    def start(self, which=None):
        for i in which if which is not None else range(len(self.copies)):
            self.copies[i].start()

    def wait(self, which=None):
        for i in which if which is not None else range(len(self.copies)):
            self.copies[i].wait()


class Spread:
    def __init__(self, fsdp, pairs, axes, recv, sent, own):
        self.fsdp, self.pairs, self.axes = fsdp, pairs, axes
        self.recv, self.sent, self.own = recv, sent, own
        self.f = lax.axis_index("fsdp")

    def size(self, a):
        return self.pairs[a][0].shape[self.axes[a]]

    def target(self, a, f):
        return block(self.pairs[a][1], self.axes[a], f, self.size(a))

    def start(self):
        f = self.f
        for a, (src, dst) in enumerate(self.pairs):
            for k in range(1, self.fsdp // 2):
                remote(src, self.target(a, f), self.sent.at[a], self.recv.at[a, f],
                       {"fsdp": lax.rem(f + 2 * k, self.fsdp)}).start()
        for a, (src, dst) in enumerate(self.pairs):
            remote(src, self.target(a, f), self.sent.at[a], self.recv.at[a, f],
                   {"fsdp": sibling(f)}).start()
            pltpu.make_async_copy(src, self.target(a, f), self.own.at[a]).start()

    def relay(self, which=None):
        for a in which or range(len(self.pairs)):
            for k in range(1, self.fsdp // 2):
                other = lax.rem(self.f + 2 * k, self.fsdp)
                here = self.target(a, other)
                wait_came(here, self.sent.at[a], self.recv.at[a, other])
                remote(here, here, self.sent.at[a], self.recv.at[a, other],
                       {"fsdp": sibling(self.f)}).start()

    def finish(self, which=None):
        for a in which or range(len(self.pairs)):
            src, dst = self.pairs[a]
            for k in range(0, self.fsdp // 2):
                other = lax.rem(sibling(self.f) + 2 * k, self.fsdp)
                wait_came(self.target(a, other), self.sent.at[a], self.recv.at[a, other])
            pltpu.make_async_copy(src, self.target(a, self.f), self.own.at[a]).wait()
            many = (self.fsdp - 1) * self.size(a)
            ref = dst.at[pl.ds(0, many)] if self.axes[a] == 0 else dst.at[:, pl.ds(0, many)]
            wait_sent(ref, self.sent.at[a], self.recv.at[a, 0])

    @staticmethod
    def scratch(fsdp, arrays):
        return [
            pltpu.SemaphoreType.DMA((arrays, fsdp)),
            pltpu.SemaphoreType.DMA((arrays,)),
            pltpu.SemaphoreType.DMA((arrays,)),
        ]


class CtxShare:
    def __init__(self, ctx, src, dst, recv, sent, own):
        self.ctx, self.src, self.dst = ctx, src, dst
        self.recv, self.sent, self.own = recv, sent, own
        self.x = lax.axis_index("ctx")

    def start(self):
        for k in range(1, self.ctx):
            remote(self.src, self.dst.at[self.x], self.sent.at[k - 1], self.recv.at[self.x],
                   {"ctx": lax.rem(self.x + k, self.ctx)}).start()
        pltpu.make_async_copy(self.src, self.dst.at[self.x], self.own).start()

    def finish(self):
        for k in range(1, self.ctx):
            other = lax.rem(self.x + k, self.ctx)
            wait_came(self.dst.at[other], self.sent.at[k - 1], self.recv.at[other])
            wait_sent(self.src, self.sent.at[k - 1], self.recv.at[other])
        pltpu.make_async_copy(self.src, self.dst.at[self.x], self.own).wait()

    @staticmethod
    def scratch(ctx):
        return [
            pltpu.SemaphoreType.DMA((ctx,)),
            pltpu.SemaphoreType.DMA((ctx,)),
            pltpu.SemaphoreType.DMA,
        ]


class LineGather:
    def __init__(self, n, chunk, src, dst, recv, sent, own, hop=1):
        self.n, self.chunk, self.src, self.dst, self.hop = n, chunk, src, dst, hop
        self.width = src.shape[1]
        self.count = src.shape[0] // chunk
        self.recv, self.sent, self.own = recv, sent, own
        self.me = lax.axis_index("tp")

    def steps(self):
        return self.count + self.hop * (self.n - 1)

    def columns(self, tp):
        return pl.ds(pl.multiple_of(tp * self.width, self.width), self.width)

    def place(self, tp, at):
        rows = pl.ds(pl.multiple_of(at * self.chunk, self.chunk), self.chunk)
        return self.dst.at[rows, self.columns(tp)]

    def begin(self):
        pltpu.make_async_copy(self.src, self.dst.at[:, self.columns(self.me)], self.own).start()

    def begun(self):
        pltpu.make_async_copy(self.src, self.dst.at[:, self.columns(self.me)], self.own).wait()

    def step(self, s):
        n, me, count = self.n, self.me, self.count
        left, right = {"tp": me - 1}, {"tp": me + 1}

        @pl.when((s >= 0) & (s < count))
        def _():
            rows = pl.ds(pl.multiple_of(s * self.chunk, self.chunk), self.chunk)

            @pl.when(me > 0)
            def _():
                remote(self.src.at[rows], self.place(me, s), self.sent.at[0], self.recv.at[me, s], left).start()

            @pl.when(me < n - 1)
            def _():
                remote(self.src.at[rows], self.place(me, s), self.sent.at[1], self.recv.at[me, s], right).start()

        for away in range(1, n):
            at = s - away * self.hop
            for sign, onward in ((-1, right), (1, left)):
                tp = me + sign * away

                @pl.when((tp >= 0) & (tp < n) & (at >= 0) & (at < count))
                def _(tp=tp, onward=onward, sign=sign, at=at):
                    here = self.place(tp, at)
                    wait_came(here, self.sent.at[2], self.recv.at[tp, at])

                    @pl.when((me < n - 1) if sign < 0 else (me > 0))
                    def _():
                        remote(here, here, self.sent.at[2], self.recv.at[tp, at], onward).start()

    def drain(self):
        n, me = self.n, self.me

        @pl.when(me > 0)
        def _():
            wait_sent(self.src, self.sent.at[0], self.recv.at[0, 0])

        @pl.when(me < n - 1)
        def _():
            wait_sent(self.src, self.sent.at[1], self.recv.at[0, 0])

        @pl.when((me > 0) & (me < n - 1))
        def _():
            wait_sent(self.dst.at[:, pl.ds(0, (n - 1) * self.width)], self.sent.at[2], self.recv.at[0, 0])

    @staticmethod
    def scratch(n, count):
        return [
            pltpu.SemaphoreType.DMA((n, count)),
            pltpu.SemaphoreType.DMA((3,)),
            pltpu.SemaphoreType.DMA,
        ]


class LineSum:
    def __init__(self, n, chunk, hop, part, from_left, from_right, out, recv, sent, finish):
        self.n, self.chunk, self.hop = n, chunk, hop
        self.total_rows = part.shape[0]
        self.owners = (n // 2 - 1, n // 2)
        self.count = self.total_rows // 2 // chunk
        self.part, self.from_left, self.from_right, self.out = part, from_left, from_right, out
        self.recv, self.sent = recv, sent
        self.finish = finish
        self.me = lax.axis_index("tp")

    def steps(self):
        return self.count + self.hop * 2 * (self.n // 2)

    def rows(self, slot, at):
        return pl.ds(pl.multiple_of((at * 2 + slot) * self.chunk, self.chunk), self.chunk)

    def step(self, s):
        n, me, hop = self.n, self.me, self.hop
        left, right = {"tp": me - 1}, {"tp": me + 1}
        reach = n // 2
        for slot, owner in enumerate(self.owners):
            for side in (0, 1):
                lag = me if side == 0 else n - 1 - me
                at = s - hop * lag
                here = (me < owner) if side == 0 else (me > owner)
                held = self.from_left if side == 0 else self.from_right
                to = right if side == 0 else left
                here = here & (at >= 0) & (at < self.count)

                @pl.when(here & (lag == 0))
                def _(at=at, held=held, to=to, side=side, slot=slot):
                    rows = self.rows(slot, at)
                    remote(self.part.at[rows], held.at[rows], self.sent.at[0],
                           self.recv.at[side, slot, at], to).start()

                if n > 2:

                    @pl.when(here & (lag > 0))
                    def _(at=at, held=held, to=to, side=side, slot=slot):
                        rows = self.rows(slot, at)
                        wait_came(held.at[rows], self.sent.at[0], self.recv.at[side, slot, at])
                        held[rows, :] = (held[rows, :].astype(F32) + self.part[rows, :].astype(F32)).astype(BF16)
                        remote(held.at[rows], held.at[rows], self.sent.at[0],
                               self.recv.at[side, slot, at], to).start()

            at = s - hop * reach

            @pl.when((me == owner) & (at >= 0) & (at < self.count))
            def _(at=at, slot=slot, owner=owner):
                rows = self.rows(slot, at)
                total = self.part[rows, :].astype(F32)
                if owner > 0:
                    wait_came(self.from_left.at[rows], self.sent.at[0], self.recv.at[0, slot, at])
                    total = total + self.from_left[rows, :].astype(F32)
                wait_came(self.from_right.at[rows], self.sent.at[0], self.recv.at[1, slot, at])
                total = total + self.from_right[rows, :].astype(F32)
                own = pl.ds(pl.multiple_of(at * self.chunk, self.chunk), self.chunk)
                self.out[rows, :] = self.finish(rows, own, total)
                if owner > 0:
                    remote(self.out.at[rows], self.out.at[rows], self.sent.at[1],
                           self.recv.at[2, slot, at], left).start()
                remote(self.out.at[rows], self.out.at[rows], self.sent.at[2],
                       self.recv.at[2, slot, at], right).start()

        for slot, owner in enumerate(self.owners):
            away = jnp.abs(me - owner)
            at = s - hop * (reach + away)

            @pl.when((me != owner) & (at >= 0) & (at < self.count))
            def _(at=at, slot=slot, owner=owner):
                rows = self.rows(slot, at)
                here = self.out.at[rows]
                wait_came(here, self.sent.at[3], self.recv.at[2, slot, at])

                @pl.when((me < owner) & (me > 0))
                def _():
                    remote(here, here, self.sent.at[3], self.recv.at[2, slot, at], left).start()

                @pl.when((me > owner) & (me < n - 1))
                def _():
                    remote(here, here, self.sent.at[3], self.recv.at[2, slot, at], right).start()

    def drain(self):
        n, me, half = self.n, self.me, self.total_rows // 2
        lo, hi = self.owners

        def wait(sem, size):
            wait_sent(self.part.at[pl.ds(0, size)], self.sent.at[sem], self.recv.at[0, 0, 0])

        middle = (me == lo) | (me == hi)

        @pl.when(middle)
        def _():
            wait(0, half)
            wait(2, half)

        @pl.when((me != lo) & (me != hi))
        def _():
            wait(0, 2 * half)

        if lo > 0:

            @pl.when(middle)
            def _():
                wait(1, half)
                wait(3, half)

            if n > 4:

                @pl.when((me != lo) & (me != hi) & (me > 0) & (me < n - 1))
                def _():
                    wait(3, 2 * half)
        else:

            @pl.when(me == hi)
            def _():
                wait(1, half)

    @staticmethod
    def scratch(n, rows, width, chunk):
        return [
            pltpu.VMEM((rows, width), BF16),
            pltpu.VMEM((rows, width), BF16),
            pltpu.SemaphoreType.DMA((3, 2, rows // 2 // chunk)),
            pltpu.SemaphoreType.DMA((4,)),
        ]


class GradSum:
    def __init__(self, fsdp, ctx, parts, axes, outs, held, recv, sent):
        self.fsdp, self.ctx, self.parts, self.axes, self.outs = fsdp, ctx, parts, axes, outs
        self.ys = fsdp // 2
        self.held, self.recv, self.sent = held, recv, sent
        self.f = lax.axis_index("fsdp")
        self.x = lax.axis_index("ctx")
        self.y, self.c = self.f // 2, lax.rem(self.f, 2)

    @staticmethod
    def block_shape(shape, axis, fsdp):
        r, c = shape
        return (r // fsdp, c) if axis == 0 else (r, c // fsdp)

    @staticmethod
    def scratch(fsdp, ctx, shapes, first=True):
        held = []
        for shape in shapes:
            if first:
                held.append(pltpu.VMEM((fsdp // 2,) + shape, BF16))
            held += [
                pltpu.VMEM((max(fsdp // 2 - 1, 1),) + shape, BF16),
                pltpu.VMEM((ctx,) + shape, BF16),
            ]
        return held

    @staticmethod
    def semaphores(fsdp, ctx, count):
        return [pltpu.SemaphoreType.DMA((count, 3, max(fsdp // 2, ctx)))] * 2

    def part(self, a, f):
        shape = self.held[a][0].shape[1:]
        return block(self.parts[a], self.axes[a], f, shape[self.axes[a]])

    def each(self, a, body):
        rows = self.held[a][0].shape[1]
        size = 32 if rows % 32 == 0 else 16

        def step(i, carry):
            body(pl.ds(pl.multiple_of(i * size, size), size))
            return carry

        lax.fori_loop(0, rows // size, step, 0)

    def start(self):
        for a in range(len(self.parts)):
            for k in range(self.ys):
                remote(self.part(a, 2 * k + 1 - self.c), self.held[a][0].at[k], self.sent.at[a, 0, k],
                       self.recv.at[a, 0, k], {"fsdp": sibling(self.f)}).start()

    def pair(self):
        for a in range(len(self.parts)):
            first = self.held[a][0]
            for k in range(self.ys):
                wait_came(first.at[k], self.sent.at[a, 0, k], self.recv.at[a, 0, k])
                mine = self.part(a, 2 * k + self.c)

                def add(rows, first=first, k=k, mine=mine):
                    first[k, rows, :] = (first[k, rows, :].astype(F32) + mine[rows, :].astype(F32)).astype(BF16)

                self.each(a, add)

    def second(self):
        for a in range(len(self.held)):
            first, later = self.held[a][0], self.held[a][1]
            for k in range(1, self.ys):
                to = lax.rem(self.y + k, self.ys)
                remote(first.at[to], later.at[k - 1], self.sent.at[a, 1, k], self.recv.at[a, 1, k],
                       {"fsdp": 2 * to + self.c}).start()

    def third(self):
        for a in range(len(self.held)):
            first, later, last = self.held[a]
            for k in range(1, self.ys):
                wait_came(later.at[k - 1], self.sent.at[a, 1, k], self.recv.at[a, 1, k])

            def add(rows, first=first, later=later, last=last):
                total = first[self.y, rows, :].astype(F32)
                for k in range(1, self.ys):
                    total = total + later[k - 1, rows, :].astype(F32)
                last[self.x, rows, :] = total.astype(BF16)

            self.each(a, add)
            for k in range(1, self.ctx):
                remote(last.at[self.x], last.at[self.x], self.sent.at[a, 2, k], self.recv.at[a, 2, self.x],
                       {"ctx": lax.rem(self.x + k, self.ctx)}).start()

    def fourth(self, store):
        for a in range(len(self.held)):
            last = self.held[a][2]
            for k in range(1, self.ctx):
                other = lax.rem(self.x + k, self.ctx)
                wait_came(last.at[other], self.sent.at[a, 2, k], self.recv.at[a, 2, other])

            def add(rows, last=last, a=a):
                total = last[0, rows, :].astype(F32)
                for k in range(1, self.ctx):
                    total = total + last[k, rows, :].astype(F32)
                store(a, rows, total)

            self.each(a, add)

    def drain_pair(self):
        for a in range(len(self.parts)):
            for k in range(self.ys):
                wait_sent(self.held[a][0].at[k], self.sent.at[a, 0, k], self.recv.at[a, 0, k])

    def drain(self):
        for a in range(len(self.held)):
            first, later, last = self.held[a]
            for k in range(1, self.ys):
                wait_sent(later.at[k - 1], self.sent.at[a, 1, k], self.recv.at[a, 1, k])
            for k in range(1, self.ctx):
                wait_sent(last.at[self.x], self.sent.at[a, 2, k], self.recv.at[a, 2, 0])


def loop(first, last, body):
    def step(s, carry):
        body(s)
        return carry

    lax.fori_loop(first, last, step, 0)


def params(ident, mib):
    return pltpu.CompilerParams(collective_id=ident, has_side_effects=True, vmem_limit_bytes=min(mib << 20, 67043328))


def shape_of(shape, dtype):
    return jax.ShapeDtypeStruct(shape, dtype)


TILE = 256


def dot(left, right):
    return jnp.dot(left, right, preferred_element_type=F32)


def dot_t(left, right):
    return lax.dot_general(left, right, (((1,), (1,)), ((), ())), preferred_element_type=F32)


def dot_rows(left, right):
    return lax.dot_general(left, right, (((0,), (0,)), ((), ())), preferred_element_type=F32)


def head_only(value, head):
    lane = lax.broadcasted_iota(jnp.int32, value.shape, 1)
    return jnp.where((lane // HEAD_DIM) == head, value, jnp.zeros_like(value))


class RowGather:
    def __init__(self, n, src, dst, recv, sent, own):
        self.n, self.src, self.dst = n, src, dst
        self.recv, self.sent, self.own = recv, sent, own
        self.me = lax.axis_index("tp")

    def start(self):
        me = self.me
        pltpu.make_async_copy(self.src, self.dst.at[me], self.own).start()

        @pl.when(me > 0)
        def _():
            remote(self.src, self.dst.at[me], self.sent.at[0, 0], self.recv.at[me], {"tp": me - 1}).start()

        @pl.when(me < self.n - 1)
        def _():
            remote(self.src, self.dst.at[me], self.sent.at[1, 0], self.recv.at[me], {"tp": me + 1}).start()

    def each(self, body, which=None):
        me, n = self.me, self.n
        for away in which or range(1, n):
            for way, tp in ((1, me - away), (0, me + away)):

                @pl.when((tp >= 0) & (tp < n))
                def _(tp=tp, way=way, away=away):
                    onward = (me < n - 1) if way == 1 else (me > 0)
                    body(away, way, tp, onward, {"tp": me + 1} if way == 1 else {"tp": me - 1})

    def relay(self, which=None):
        def body(away, way, tp, onward, to):
            here = self.dst.at[tp]
            wait_came(here, self.sent.at[way, away], self.recv.at[tp])

            @pl.when(onward)
            def _():
                remote(here, here, self.sent.at[way, away], self.recv.at[tp], to).start()

        self.each(body, which)

    def finish(self):
        me = self.me
        pltpu.make_async_copy(self.src, self.dst.at[me], self.own).wait()

        @pl.when(me > 0)
        def _():
            wait_sent(self.src, self.sent.at[0, 0], self.recv.at[0])

        @pl.when(me < self.n - 1)
        def _():
            wait_sent(self.src, self.sent.at[1, 0], self.recv.at[0])

        def body(away, way, tp, onward, to):
            @pl.when(onward)
            def _():
                wait_sent(self.src, self.sent.at[way, away], self.recv.at[0])

        self.each(body)

    @staticmethod
    def scratch(n):
        return [
            pltpu.SemaphoreType.DMA((n,)),
            pltpu.SemaphoreType.DMA((2, n)),
            pltpu.SemaphoreType.DMA,
        ]


class AxisSum:
    def __init__(self, axis, n, slots, recv, sent):
        self.axis, self.n, self.slots, self.recv, self.sent = axis, n, slots, recv, sent
        self.at = lax.axis_index(axis)

    def start(self, value):
        self.slots[self.at] = value
        for k in range(1, self.n):
            remote(self.slots.at[self.at], self.slots.at[self.at], self.sent.at[k], self.recv.at[self.at],
                   {self.axis: lax.rem(self.at + k, self.n)}).start()

    def finish(self):
        for k in range(1, self.n):
            other = lax.rem(self.at + k, self.n)
            wait_came(self.slots.at[other], self.sent.at[k], self.recv.at[other])
            wait_sent(self.slots.at[self.at], self.sent.at[k], self.recv.at[other])
        total = self.slots[0]
        for k in range(1, self.n):
            total = total + self.slots[k]
        return total

    @staticmethod
    def scratch(n, shape):
        return [
            pltpu.VMEM((n,) + shape, F32),
            pltpu.SemaphoreType.DMA((n,)),
            pltpu.SemaphoreType.DMA((n,)),
        ]


def window(ctx, tok_dev):
    return min(ctx, (tok_dev * ctx // 2 + tok_dev - 1) // tok_dev + 1)


def key_span(ctx, tok_dev):
    return min(ctx * tok_dev // 2 // TILE, (window(ctx, tok_dev) - 1) * (tok_dev // TILE))


R_ONE, SEGMENT, VALID = 0, 1, 2


def front(tokens, gain1, gain2, w_latent, shards, w_out, wide_shards, segments, fsdp, ctx, n):
    rows, width = tokens.shape
    seq_dev, tok_dev = segments.shape
    latent, q_width = LATENT, shards[0].shape[1]
    wide, chunk = 128, 256
    pieces = rows // chunk
    win = window(ctx, tok_dev)
    full = [shape_of((s.shape[0] * fsdp,) + s.shape[1:], s.dtype) for s in shards]
    wider = [shape_of((s.shape[0], s.shape[1] * fsdp), s.dtype) for s in wide_shards]
    per_group = HEADS // GROUPS * HEAD_DIM
    per_seq = tok_dev // chunk

    def kernel(*refs):
        (tok_in, ga, gb, wlat, wq, wk, wv, wo, wg, wu, seg), refs = refs[:11], refs[11:]
        (xn_out, cols, gain_all, w_lat, w_qry, w_kproj, w_vproj, gate_all, up_all), refs = refs[:9], refs[9:]
        (wo_all, seg_all, lat_all, query, keys, values), refs = refs[:6], refs[6:]
        (gbuf, sbuf, tok, xn, tsem), refs = refs[:5], refs[5:]
        bring = Bring([(tok_in, tok), (xn, xn_out)], tsem)
        bring.start([0])
        x, me = lax.axis_index("ctx"), lax.axis_index("tp")
        gbuf[...] = jnp.zeros_like(gbuf)
        gbuf[0:1, :] = ga[...].astype(F32).reshape(1, -1)
        gbuf[1:2, :] = gb[...].astype(F32).reshape(1, -1)
        sbuf[...] = jnp.zeros_like(sbuf)
        sbuf[0:seq_dev, :] = seg[...]
        meet(n, fsdp, ctx)
        group = me * q_width // per_group
        src_lat = wlat.at[:, pl.ds(pl.multiple_of(group * latent, latent), latent)]
        pairs = [(gbuf, gain_all), (src_lat, w_lat), (wq, w_qry), (wk, w_kproj), (wv, w_vproj),
                 (wg, gate_all), (wu, up_all)]
        spread = Spread(fsdp, pairs, [1, 0, 0, 0, 0, 1, 1], *refs[:3])
        share = CtxShare(ctx, sbuf, seg_all, *refs[3:6])
        line = RowGather(n, wo, wo_all, *refs[6:9])
        lat_recv, lat_sent = refs[9:11]
        spread.start()
        share.start()
        line.start()
        own = win - 1
        cols[...] = jnp.zeros_like(cols)
        bring.wait([0])

        def scale(i):
            at = pl.ds(pl.multiple_of(i * wide, wide), wide)
            value = tok[at, :].astype(F32)
            cols[at, R_ONE : R_ONE + 1] = lax.rsqrt(jnp.mean(value * value, axis=-1, keepdims=True) + eps)

        loop(0, rows // wide, scale)
        spread.relay([0, 1])
        spread.finish([0, 1])

        def place(shard, i):
            seq = i // per_seq
            return pl.ds(pl.multiple_of(seq * win * tok_dev + shard * tok_dev + lax.rem(i, per_seq) * chunk, chunk), chunk)

        def send(k, i):
            return remote(lat_all.at[place(own, i)], lat_all.at[place(own - k, i)], lat_sent.at[k, i],
                          lat_recv.at[own - k, i], {"ctx": x + k})

        def first(i):
            at = pl.ds(pl.multiple_of(i * chunk, chunk), chunk)
            unit = (tok[at, :].astype(F32) * cols[at, R_ONE : R_ONE + 1] * gain_all[0:1, :]).astype(BF16)
            xn[at, :] = unit
            lat_all[place(own, i), :] = dot(unit, w_lat[...]).astype(BF16)
            for k in range(1, win):

                @pl.when(x + k < ctx)
                def _(k=k):
                    send(k, i).start()

        loop(0, pieces, first)
        bring.start([1])
        line.relay([1])
        spread.relay([2, 3, 4])
        spread.finish([2, 3, 4])

        def project(shard, i):
            to = place(shard, i)
            value = lat_all[to, :]
            keys[to, :] = dot(value, w_kproj[...]).astype(BF16)
            values[to, :] = dot(value, w_vproj[...]).astype(BF16)

        def ask(i):
            at = pl.ds(pl.multiple_of(i * chunk, chunk), chunk)
            query[at, :] = dot(xn[at, :], w_qry[...]).astype(BF16)
            project(own, i)

        loop(0, pieces, ask)
        share.finish()
        for q in range(seq_dev):
            at = slice(q * tok_dev, (q + 1) * tok_dev)
            ids = jnp.broadcast_to(sbuf[q : q + 1, :].astype(F32), (128, tok_dev)).T
            cols[at, SEGMENT : SEGMENT + 1] = ids[:, 0:1]
            last = seg_all[ctx - 1, q : q + 1, tok_dev - 1 : tok_dev].astype(F32)
            cols[at, VALID : VALID + 1] = jnp.where(ids[:, 0:1] != last, 1.0, 0.0)
        line.relay(range(2, n))
        for k in range(1, win):

            def theirs(i, k=k):
                @pl.when(x - k >= 0)
                def _():
                    wait_came(lat_all.at[place(own - k, i)], lat_sent.at[k, i], lat_recv.at[own - k, i])

                @pl.when(x - k < 0)
                def _():
                    lat_all[place(own - k, i), :] = jnp.zeros((chunk, latent), BF16)

                project(own - k, i)

            loop(0, pieces, theirs)

            def gone(i, k=k):
                @pl.when(x + k < ctx)
                def _():
                    send(k, i).wait_send()

            loop(0, pieces, gone)
        spread.relay([5, 6])
        spread.finish([5, 6])
        line.finish()
        bring.wait([1])

    return pl.pallas_call(
        kernel,
        out_shape=(
            shape_of((rows, width), BF16),
            shape_of((rows, 128), F32),
            shape_of((8, width), F32),
            shape_of((width, latent), BF16),
            *full,
            *wider,
            shape_of((n,) + w_out.shape, w_out.dtype),
            shape_of((ctx, 8, tok_dev), segments.dtype),
            shape_of((win * rows, latent), BF16),
            shape_of((rows, q_width), BF16),
            shape_of((win * rows, q_width), BF16),
            shape_of((win * rows, q_width), BF16),
        ),
        in_specs=[ANY] + [VMEM] * 10,
        out_specs=(ANY,) + (VMEM,) * 6 + (ANY,) * 3 + (VMEM,) * 5,
        scratch_shapes=[
            pltpu.VMEM((8, gain1.shape[0]), F32),
            pltpu.VMEM((8, tok_dev), segments.dtype),
            pltpu.VMEM((rows, width), BF16),
            pltpu.VMEM((rows, width), BF16),
            pltpu.SemaphoreType.DMA((2,)),
        ]
        + Spread.scratch(fsdp, 7)
        + CtxShare.scratch(ctx)
        + RowGather.scratch(n)
        + [pltpu.SemaphoreType.DMA((win, pieces))] * 2,
        compiler_params=params(1, 56),
    )(tokens, gain1, gain2, w_latent, *shards, w_out, *wide_shards, segments)


def counted_keys(cols, segk, at, seq, q_first, first, count, tok_dev, win):
    per = tok_dev // TILE
    oldest = lax.axis_index("ctx") - (win - 1)
    mine = cols[at, SEGMENT : SEGMENT + 1]
    shape = (mine.shape[0], TILE)
    pieces = []
    for j in range(count):
        t = first + j
        shard = oldest + t // per
        inner = pl.ds(pl.multiple_of(lax.rem(t, per) * TILE, TILE), TILE)
        ids = segk[jnp.maximum(shard, 0), pl.ds(seq, 1), inner].astype(F32)
        q_at = q_first + lax.broadcasted_iota(jnp.int32, shape, 0)
        k_at = t * TILE + lax.broadcasted_iota(jnp.int32, shape, 1)
        pieces.append((k_at <= q_at) & (ids == mine) & (shard >= 0))
    return pieces


def middle(query, keys, values, seg_all, cols, shards, gate_all, up_all, gains, tokens, out_grad,
           fsdp, ctx, n, seq_dev, late):
    rows, width = tokens.shape
    q_width = query.shape[1]
    heads = q_width // HEAD_DIM
    inner = gate_all.shape[0]
    tok_dev = rows // seq_dev
    per = tok_dev // TILE
    win, span = window(ctx, tok_dev), key_span(ctx, tok_dev)
    tiles = span + 1
    part = TILE if tiles <= 3 else 64
    chunk, hop = 32, 2
    size, piece = 256, 64
    per_block = size // piece
    half = rows // 2
    cols_at = width // 4
    block_shape = (inner, width // fsdp)
    count = 3

    def kernel(*refs):
        (q_in, k_in, v_in, segk, cols, wo_in, wd_in, wg_in, wu_in, gain, tok_in, cot_in), refs = refs[:12], refs[12:]
        (o_branch, o_feed, o_dmid, o_mid, o_wo, o_gain, o_bsq, o_mark, o_att, o_lse), refs = refs[:10], refs[10:]
        outs, refs = refs[:3], refs[3:]
        one, gsems, parts, refs = refs[:4], refs[4:6], refs[6:9], refs[9:]
        (query, keys, values, att, att_all, wo, wd, wg, wu, tok, cot), refs = refs[:11], refs[11:]
        (mid, r2, xn, hid, dg, du, p_two, p_feed, bsem), refs = refs[:9], refs[9:]
        bring = Bring([(q_in, query), (k_in, keys), (v_in, values), (tok_in, tok), (wg_in, wg), (wu_in, wu),
                       (cot_in, cot), (att, o_att), (p_feed, o_feed)], bsem)
        bring.start(range(7))
        meet(n, fsdp, ctx)
        line = LineGather(n, piece, att, att_all, *refs[:3])
        spread = Spread(fsdp, [(wo_in, wo), (wd_in, wd)], [1, 1], *refs[3:6])
        keep = refs[6:]
        spread.start()
        o_gain[...] = jnp.zeros_like(o_gain)
        o_bsq[...] = jnp.zeros_like(o_bsq)
        o_mark[...] = jnp.zeros_like(o_mark)
        g2 = gain.at[1:2]

        def back(at, own, total):
            middle_rows = mid[at, :]
            o_mid[own, :] = middle_rows
            unit = middle_rows * r2[at, :]
            o_gain[...] += jnp.sum((total * unit).reshape(chunk // 8, 8, width), axis=0)
            scaled = total * g2[...]
            mean = jnp.mean(scaled * unit, axis=-1, keepdims=True)
            d_mid = cot[at, :].astype(F32) + r2[at, :] * (scaled - unit * mean)
            o_dmid[own, :] = d_mid
            first_unit = tok[at, :].astype(F32) * cols[at, R_ONE : R_ONE + 1]
            o_mark[at, 0:1] = jnp.sum(first_unit * d_mid, axis=-1, keepdims=True)
            return d_mid.astype(BF16)

        first = LineSum(n, chunk, hop, p_two, one[0], one[1], o_branch, one[2], one[3], back)
        if late:
            held = [[out, None, None] for out in outs]
        else:
            held = [keep[3 * a : 3 * a + 3] for a in range(count)]
        grad = GradSum(fsdp, ctx, parts, [1] * count, outs, held, *gsems)
        bring.wait([0, 1, 2])

        def query_rows(i, j):
            seq = i // per
            q_tile = (win - 1) * per + lax.rem(i, per)
            at = pl.ds(pl.multiple_of(i * TILE + j * part, part), part)
            near = pl.ds(pl.multiple_of((seq * win * per + q_tile - span) * TILE, TILE), tiles * TILE)
            counted = jnp.concatenate(
                [
                    c.astype(F32)
                    for c in counted_keys(
                        cols, segk, at, seq, q_tile * TILE + j * part, q_tile - span, tiles, tok_dev, win
                    )
                ],
                axis=1,
            )
            accum = jnp.zeros((part, q_width), F32)
            lane = lax.broadcasted_iota(jnp.int32, (part, 128), 1)
            kept = jnp.zeros((part, 128), F32)
            for h in range(heads):
                score = jnp.where(counted > 0.0, dot_t(head_only(query[at, :], h), keys[near, :]) * 0.125, -1e30)
                top = jnp.max(score, axis=-1, keepdims=True)
                weight = jnp.exp(score - top)
                total = jnp.sum(weight, axis=-1, keepdims=True)
                prob = (weight * (1.0 / total)).astype(BF16)
                accum = accum + jnp.dot(prob, head_only(values[near, :], h), preferred_element_type=F32)
                kept = jnp.where(lane == h, top + jnp.log(total), kept)
                if part == TILE:
                    line.step((i - 1) * per_block + h * per_block // heads)
            o_lse[at, :] = kept
            att[at, :] = accum.astype(BF16)

        def query_tile(i):
            if part == TILE:
                query_rows(i, 0)
                return
            loop(0, TILE // part, lambda j: query_rows(i, j))
            for h in range(per_block):
                line.step((i - 1) * per_block + h)

        loop(0, rows // TILE, query_tile)
        bring.start([7])
        line.begin()
        s1 = (rows // TILE - 1) * per_block
        spread.relay()
        spread.finish()
        tp = lax.axis_index("tp")
        o_wo[...] = wo[pl.ds(pl.multiple_of(tp * q_width, q_width), q_width), :]
        line.begun()
        bring.wait([3, 4, 5, 6])

        def block_of_rows(b):
            at = pl.ds(pl.multiple_of(b * size, size), size)
            seq = b * size // tok_dev

            def steps(j):
                line.step(s1 + b * per_block + j)
                first.step((b - 1) * per_block + j)

            branch = dot(att_all[at, :], wo[...])
            middle_rows = tok[at, :].astype(F32) + branch
            mid[at, :] = middle_rows
            o_bsq[pl.ds(pl.multiple_of(seq * 8, 8), 8), :] += jnp.sum(
                (branch * branch * cols[at, VALID : VALID + 1]).reshape(size // 8, 8, width), axis=0
            )
            scale = lax.rsqrt(jnp.mean(middle_rows * middle_rows, axis=-1, keepdims=True) + eps)
            r2[at, :] = scale
            unit = (middle_rows * scale * g2[...]).astype(BF16)
            xn[at, :] = unit
            steps(0)
            gate = dot_t(unit, wg[...])
            upper = dot_t(unit, wu[...])
            sigma = jax.nn.sigmoid(gate)
            swish = gate * sigma
            hidden = (swish * upper).astype(BF16)
            hid[at, :] = hidden
            slope = upper * sigma * (1.0 + gate * (1.0 - sigma))
            steps(1)
            p_feed[at, :] = dot(hidden, wd[...]).astype(BF16)
            d_hidden = dot_t(cot[at, :], wd[...])
            d_gate = (d_hidden * slope).astype(BF16)
            d_upper = (d_hidden * swish).astype(BF16)
            dg[at, :] = d_gate
            du[at, :] = d_upper
            steps(2)
            p_two[at, :] = (dot(d_gate, wg[...]) + dot(d_upper, wu[...])).astype(BF16)
            steps(3)

        loop(0, rows // size, block_of_rows)
        bring.start([8])
        s0 = (rows // size - 1) * per_block

        def product(i):
            at = pl.ds(pl.multiple_of(i * cols_at, cols_at), cols_at)
            left = xn[:, at]
            parts[0][:, at] = dot_rows(dg[...], left).astype(BF16)
            parts[1][:, at] = dot_rows(du[...], left).astype(BF16)
            parts[2][:, at] = dot_rows(hid[...], cot[:, at]).astype(BF16)

        def busy(s):
            first.step(s)
            product(s - s0)

        loop(s0, s0 + 4, busy)
        grad.start()
        last = first.steps()
        loop(s0 + 4, s0 + 6, first.step)
        grad.pair()
        if not late:
            grad.second()
        loop(s0 + 6, last, first.step)
        if not late:
            grad.third()

            def store(a, at, total):
                outs[a][at, :] = total

            grad.fourth(store)
            grad.drain()
        line.drain()
        first.drain()
        grad.drain_pair()
        bring.wait([7, 8])

    ys = fsdp // 2
    out = pl.pallas_call(
        kernel,
        out_shape=(
            shape_of((rows, width), BF16),
            shape_of((rows, width), BF16),
            shape_of((half, width), F32),
            shape_of((half, width), F32),
            shape_of((q_width, width), BF16),
            shape_of((8, width), F32),
            shape_of((8 * seq_dev, width), F32),
            shape_of((rows, 128), F32),
            shape_of((rows, q_width), BF16),
            shape_of((rows, 128), F32),
        )
        + ((shape_of((ys,) + block_shape, BF16) if late else shape_of(block_shape, F32)),) * count,
        in_specs=[ANY] * 3 + [VMEM] * 4 + [ANY] * 2 + [VMEM] + [ANY] * 2,
        out_specs=(VMEM, ANY) + (VMEM,) * 6 + (ANY, VMEM) + (VMEM,) * count,
        scratch_shapes=LineSum.scratch(n, rows, width, chunk)
        + GradSum.semaphores(fsdp, ctx, count)
        + [pltpu.VMEM((inner, width), BF16)] * count
        + [
            pltpu.VMEM((rows, q_width), BF16),
            pltpu.VMEM((win * rows, q_width), BF16),
            pltpu.VMEM((win * rows, q_width), BF16),
            pltpu.VMEM((rows, q_width), BF16),
            pltpu.VMEM((rows, n * q_width), BF16),
            pltpu.VMEM((n * q_width, width), BF16),
            pltpu.VMEM((inner, width), BF16),
            pltpu.VMEM((inner, width), BF16),
            pltpu.VMEM((inner, width), BF16),
            pltpu.VMEM((rows, width), BF16),
            pltpu.VMEM((rows, width), BF16),
            pltpu.VMEM((rows, width), F32),
            pltpu.VMEM((rows, 1), F32),
            pltpu.VMEM((rows, width), BF16),
            pltpu.VMEM((rows, inner), BF16),
            pltpu.VMEM((rows, inner), BF16),
            pltpu.VMEM((rows, inner), BF16),
            pltpu.VMEM((rows, width), BF16),
            pltpu.VMEM((rows, width), BF16),
            pltpu.SemaphoreType.DMA((9,)),
        ]
        + LineGather.scratch(n, rows // piece)
        + Spread.scratch(fsdp, 2)
        + ([] if late else GradSum.scratch(fsdp, ctx, [block_shape] * count)),
        compiler_params=params(2, 64),
    )(query, keys, values, seg_all, cols, *shards, gate_all, up_all, gains, tokens, out_grad)
    return out[:10], out[10:]


def back(query, keys, values, seg_all, cols, lse, attended, d_branch, wo_rows, weights, lat_all, xn_one, gains,
         tokens, d_middle, mid_own, part_feed, marks, gain_part, branch_sq, firsts, fsdp, ctx, n, seq_dev):
    rows, width = tokens.shape
    w_qry, w_lat, w_kproj, w_vproj = weights
    q_width, latent = query.shape[1], w_lat.shape[1]
    heads, tok_dev = q_width // HEAD_DIM, rows // seq_dev
    per = tok_dev // TILE
    win, span = window(ctx, tok_dev), key_span(ctx, tok_dev)
    tiles = span + 1
    group = tiles if tiles <= 3 else 1
    chunk, hop, wide, side = 32, 2, 256, 128
    half = rows // 2
    axes = (0, 0, 0, 1, 0)
    whole = ((width, q_width), (latent, q_width), (latent, q_width), (q_width, width), (width, latent))
    blocks = [GradSum.block_shape(w, a, fsdp) for w, a in zip(whole, axes)]
    lat = blocks[-1]
    ffn = [f.shape[1:] for f in firsts]
    seq_pieces = tok_dev // wide
    many = max(width, rows)

    def kernel(*refs):
        (q_ref, k_ref, v_ref, segk, cols, lse_ref, att, dbr, wo), refs = refs[:9], refs[9:]
        (wq, wl, wk, wv, la_in, xn_in, gain, tok_in, dmid_in, mid_in, feed_in), refs = refs[:11], refs[11:]
        (marks, gain_two, bsq), fsts, refs = refs[:3], refs[3 : 3 + len(ffn)], refs[3 + len(ffn) :]
        (o_tok, o_mixed, o_small), outs, refs = refs[:3], refs[3:8], refs[8:]
        fouts, refs = refs[: len(ffn)], refs[len(ffn) :]
        one, two, keep, gsems, parts, refs = refs[:4], refs[4:8], refs[8:23], refs[23:25], refs[25:30], refs[30:]
        (p_one, dlat, came, c_recv, c_sent, gacc, sm, sacc), refs = refs[:8], refs[8:]
        (dk, dv, dq, dqb, grad_seq, lat_parts), refs = refs[:6], refs[6:]
        (la, xn, tok, dmid, mid, p_feed, bsem), refs = refs[:7], refs[7:]
        (lat_own, lat_every), lsems, sums, refs = refs[:2], refs[2:5], refs[5:14], refs[14:]
        bring = Bring([(feed_in, p_feed), (mid_in, mid), (la_in, la), (xn_in, xn), (tok_in, tok), (dmid_in, dmid)], bsem)
        bring.start()
        meet(n, fsdp, ctx, everyone=True)
        x = lax.axis_index("ctx")
        own_shard = win - 1
        grad_ffn = None
        if ffn:
            fkeep, fsems = refs[: 2 * len(ffn)], refs[2 * len(ffn) :]
            grad_ffn = GradSum(fsdp, ctx, [], [], fouts,
                               [[fsts[a], fkeep[2 * a], fkeep[2 * a + 1]] for a in range(len(ffn))], *fsems)
            grad_ffn.second()
        gacc[...] = jnp.zeros_like(gacc)
        sacc[...] = jnp.zeros_like(sacc)
        sm[...] = jnp.zeros_like(sm)
        g1 = gain.at[0:1]

        def forward(at, own, total):
            mixed = mid[own, :] + total
            seq = at.start // tok_dev
            counted = cols[at, VALID : VALID + 1]
            sacc[seq] += jnp.sum((mixed * mixed * counted).reshape(chunk // 8, 8, width), axis=0)
            sacc[seq_dev + seq] += jnp.sum((total * total * counted).reshape(chunk // 8, 8, width), axis=0)
            return mixed.astype(BF16)

        def backward(at, own, total):
            r1 = cols[at, R_ONE : R_ONE + 1]
            unit = tok[at, :].astype(F32) * r1
            scaled = total * g1[...]
            mean = jnp.mean(scaled * unit, axis=-1, keepdims=True)
            return (dmid[own, :] + r1 * (scaled - unit * mean)).astype(BF16)

        feed = LineSum(n, chunk, hop, p_feed, two[0], two[1], o_mixed, two[2], two[3], forward)
        first = LineSum(n, chunk, hop, p_one, one[0], one[1], o_tok, one[2], one[3], backward)
        grad = GradSum(fsdp, ctx, parts, axes, outs, [keep[3 * a : 3 * a + 3] for a in range(5)], *gsems)
        line = RowGather(n, lat_own, lat_every, *lsems)
        over_tp = AxisSum("tp", n, *sums[0:3])
        over_ctx = AxisSum("ctx", ctx, *sums[3:6])
        over_fsdp = AxisSum("fsdp", fsdp, *sums[6:9])

        def clear(i):
            at = pl.ds(pl.multiple_of(i * TILE, TILE), TILE)
            dk[at, :] = jnp.zeros((TILE, q_width), F32)
            dv[at, :] = jnp.zeros((TILE, q_width), F32)

        loop(0, win * rows // TILE, clear)
        bring.wait([0, 1])

        def query_tile(i, step):
            seq = i // per
            q_tile = own_shard * per + lax.rem(i, per)
            at = pl.ds(pl.multiple_of(i * TILE, TILE), TILE)
            grad_seq[...] = dot_t(dbr[at, :], wo[...]).astype(BF16)
            product = grad_seq[...].astype(F32) * att[at, :].astype(F32)
            delta = [jnp.sum(head_only(product, h), axis=-1, keepdims=True) for h in range(heads)]
            dq[...] = jnp.zeros_like(dq)

            def key_tiles(kk):
                t = q_tile - span + kk * group
                near = pl.ds(pl.multiple_of((seq * win * per + t) * TILE, TILE), group * TILE)
                counted = jnp.concatenate(
                    [c.astype(F32) for c in counted_keys(cols, segk, at, seq, q_tile * TILE, t, group, tok_dev, win)], axis=1
                )
                kept = lse_ref[at, :]
                d_query = jnp.zeros((TILE, q_width), F32)
                d_key = jnp.zeros((group * TILE, q_width), F32)
                d_value = jnp.zeros((group * TILE, q_width), F32)
                for h in range(heads):
                    mine, ours = head_only(q_ref[at, :], h), head_only(grad_seq[...], h)
                    score = jnp.where(counted > 0.0, dot_t(mine, k_ref[near, :]) * 0.125, -1e30)
                    prob = jnp.exp(score - kept[:, h : h + 1]) * counted
                    d_score = (prob * (dot_t(ours, v_ref[near, :]) - delta[h])).astype(BF16)
                    d_query = d_query + jnp.dot(d_score, head_only(k_ref[near, :], h), preferred_element_type=F32)
                    d_key = d_key + dot_rows(d_score, mine)
                    d_value = d_value + dot_rows(prob.astype(BF16), ours)
                    step(kk * heads + h)
                dq[...] += d_query
                dk[near, :] += d_key * 0.125
                dv[near, :] += d_value

            loop(0, tiles // group, key_tiles)
            dqb[at, :] = (dq[...] * 0.125).astype(BF16)

        def latent_rows(shard, seq, i):
            return pl.ds(pl.multiple_of((seq * win + shard) * tok_dev + i * wide, wide), wide)

        def send(k, seq, i):
            at = pl.ds(pl.multiple_of(seq * tok_dev + i * wide, wide), wide)
            return remote(lat_parts.at[latent_rows(own_shard - k, seq, i)], came.at[k - 1, at],
                          c_sent.at[k - 1, seq, i], c_recv.at[k - 1, seq, i], {"ctx": x - k})

        def latents(seq):
            for k in range(win - 1, -1, -1):
                for i in range(seq_pieces):
                    at = latent_rows(own_shard - k, seq, i)
                    lat_parts[at, :] = (
                        dot_t(dk[at, :].astype(BF16), wk[...]) + dot_t(dv[at, :].astype(BF16), wv[...])
                    ).astype(BF16)
                    if k > 0:

                        @pl.when(x - k >= 0)
                        def _(k=k, i=i):
                            send(k, seq, i).start()

        def whole_latent(j):
            seq, i = j // seq_pieces, lax.rem(j, seq_pieces)
            at = pl.ds(pl.multiple_of(j * wide, wide), wide)
            dlat[at, :] = lat_parts[latent_rows(own_shard, seq, i), :]
            for k in range(1, win):

                @pl.when(x + k < ctx)
                def _(k=k):
                    wait_came(came.at[k - 1, at], c_sent.at[k - 1, seq, i], c_recv.at[k - 1, seq, i])
                    dlat[at, :] = (dlat[at, :].astype(F32) + came[k - 1, at, :].astype(F32)).astype(BF16)

            p_one[at, :] = (dot_t(dqb[at, :], wq[...]) + dot_t(dlat[at, :], wl[...])).astype(BF16)

        tile_steps = (tiles // group) * heads
        every = max(tile_steps // 4, 1)

        def sequence(seq):
            def tile(i):
                def step(j):
                    @pl.when(lax.rem(j, every) == 0)
                    def _():
                        feed.step(i * (tile_steps // every) + j // every)

                query_tile(i, step)

            loop(seq * per, seq * per + per, tile)
            latents(seq)

        loop(0, seq_dev, sequence)
        fed = seq_dev * per * (tile_steps // every)

        bring.wait([2, 3, 4, 5])

        def product(i):
            at = pl.ds(pl.multiple_of(i * wide, wide), wide)
            parts[0][at, :] = dot_rows(xn[:, at], dqb[...]).astype(BF16)
            parts[3][:, at] = dot_rows(att[...], dbr[:, at]).astype(BF16)

        def steps(s):
            first.step(s)
            feed.step(fed + s)

        early = (seq_dev - 1) * seq_pieces
        loop(0, early, whole_latent)

        def mixed_work(i):
            product(i)
            steps(i)

        loop(0, width // wide, mixed_work)
        s0 = width // wide
        if grad_ffn is not None:
            grad_ffn.third()
        parts[1][...] = dot_rows(la[...], dk[...].astype(BF16)).astype(BF16)
        parts[2][...] = dot_rows(la[...], dv[...].astype(BF16)).astype(BF16)
        loop(early, rows // wide, whole_latent)

        def product_lat(s):
            at = pl.ds(pl.multiple_of((s - s0) * wide, wide), wide)
            parts[4][at, :] = dot_rows(xn[:, at], dlat[...]).astype(BF16)
            steps(s)

        begun = s0 + width // wide
        loop(s0, begun, product_lat)
        grad.start()

        def gains_of(s):
            steps(s)
            at = pl.ds(pl.multiple_of((s - begun) * side, side), side)
            value = p_one[at, :].astype(F32) * (tok[at, :].astype(F32) * cols[at, R_ONE : R_ONE + 1])
            gacc[...] += jnp.sum(value.reshape(side // 8, 8, width), axis=0)
            along = lax.dot_general(jnp.ones((8, width), F32), value * g1[...], (((1,), (1,)), ((), ())),
                                    precision=lax.Precision.HIGHEST, preferred_element_type=F32)
            sm[3:4, at] = along[0:1, :]
            sm[4:5, at] = marks[at, :].T[0:1, :]
            sm[5:6, at] = cols[at, :].T[R_ONE : R_ONE + 1, :]

        mark = begun + rows // side
        loop(begun, begun + 1, gains_of)
        grad.pair()
        grad.second()
        loop(begun + 1, begun + 4, gains_of)
        grad.third()
        loop(begun + 4, mark, gains_of)
        last = first.steps()
        for s in range(fed + mark, feed.steps()):
            feed.step(s)
        lane = lax.broadcasted_iota(jnp.int32, (1, many), 1)
        once = jnp.where(lax.axis_index("tp") == 0, 1.0, 0.0)
        row = jnp.zeros((1, many), F32)

        def whole_sum(value):
            return jnp.sum(jnp.sum(value, axis=0, keepdims=True), axis=1, keepdims=True)

        for q in range(seq_dev):
            values = [
                whole_sum(sacc[q]),
                whole_sum(sacc[seq_dev + q]),
                whole_sum(bsq[8 * q : 8 * q + 8, :]) * once,
                jnp.sum(cols[q * tok_dev : (q + 1) * tok_dev, VALID : VALID + 1], axis=0, keepdims=True) * once,
            ]
            for j, value in enumerate(values):
                row = row + jnp.where(lane == 4 * q + j, value, 0.0)
        sm[2:3, :] = row
        sm[0:1, 0:width] = jnp.sum(gacc[...], axis=0, keepdims=True)
        sm[1:2, 0:width] = jnp.sum(gain_two[...], axis=0, keepdims=True)
        r_row = sm[5:6, :]
        over_tp.start(sm[...])

        def store(a, at, total):
            if a < 4:
                outs[a][at, :] = total
            else:
                lat_own[at, :] = total.astype(BF16)

        def store_ffn(a, at, total):
            fouts[a][at, :] = total

        grad.fourth(store)
        line.start()
        loop(mark, mark + 2, steps)
        line.relay([1])
        along_tp = over_tp.finish()
        over_ctx.start(along_tp)
        loop(mark + 2, mark + 4, steps)
        if n > 2:
            line.relay([2])
        along_ctx = over_ctx.finish()
        over_fsdp.start(along_ctx)
        if grad_ffn is not None:
            grad_ffn.fourth(store_ffn)
        loop(mark + 4, last, steps)
        if n > 3:
            line.relay(range(3, n))
        everywhere = over_fsdp.finish()
        row = lax.broadcasted_iota(jnp.int32, everywhere.shape, 0)
        o_small[...] = jnp.where(row < 2, everywhere, along_ctx)
        o_small[3:4, :] = (along_tp[4:5] + eps * r_row * r_row * r_row * along_tp[3:4]) * (1.0 / width**0.5)
        line.finish()

        def gather(i):
            at = pl.ds(pl.multiple_of(i * 16, 16), 16)
            for g in range(GROUPS):
                total = jnp.zeros((16, lat[1]), F32)
                for t in range(n):
                    if t * GROUPS // n == g:
                        total = total + lat_every[t, at, :].astype(F32)
                outs[4][at, g * lat[1] : (g + 1) * lat[1]] = total

        loop(0, lat[0] // 16, gather)
        for k in range(1, win):

            @pl.when(x - k >= 0)
            def _(k=k):
                for seq in range(seq_dev):
                    for i in range(seq_pieces):
                        send(k, seq, i).wait_send()

        feed.drain()
        first.drain()
        grad.drain_pair()
        grad.drain()
        if grad_ffn is not None:
            grad_ffn.drain()

    out = pl.pallas_call(
        kernel,
        out_shape=(
            shape_of((rows, width), BF16),
            shape_of((rows, width), BF16),
            shape_of((8, many), F32),
        )
        + tuple(shape_of(b, F32) for b in blocks[:-1])
        + (shape_of((lat[0], GROUPS * lat[1]), F32),)
        + tuple(shape_of(f, F32) for f in ffn),
        in_specs=[VMEM] * 13 + [ANY] * 2 + [VMEM] + [ANY] * 4 + [VMEM] * (3 + len(ffn)),
        out_specs=(VMEM,) * (8 + len(ffn)),
        scratch_shapes=LineSum.scratch(n, rows, width, chunk) * 2
        + GradSum.scratch(fsdp, ctx, blocks)
        + GradSum.semaphores(fsdp, ctx, 5)
        + [pltpu.VMEM(w, BF16) for w in whole]
        + [
            pltpu.VMEM((rows, width), BF16),
            pltpu.VMEM((rows, latent), BF16),
            pltpu.VMEM((max(win - 1, 1), rows, latent), BF16),
            pltpu.SemaphoreType.DMA((max(win - 1, 1), seq_dev, seq_pieces)),
            pltpu.SemaphoreType.DMA((max(win - 1, 1), seq_dev, seq_pieces)),
            pltpu.VMEM((8, width), F32),
            pltpu.VMEM((8, many), F32),
            pltpu.VMEM((2 * seq_dev, 8, width), F32),
            pltpu.VMEM((win * rows, q_width), F32),
            pltpu.VMEM((win * rows, q_width), F32),
            pltpu.VMEM((TILE, q_width), F32),
            pltpu.VMEM((rows, q_width), BF16),
            pltpu.VMEM((TILE, q_width), BF16),
            pltpu.VMEM((win * rows, latent), BF16),
        ]
        + [
            pltpu.VMEM((win * rows, latent), BF16),
            pltpu.VMEM((rows, width), BF16),
            pltpu.VMEM((rows, width), BF16),
            pltpu.VMEM((half, width), F32),
            pltpu.VMEM((half, width), F32),
            pltpu.VMEM((rows, width), BF16),
            pltpu.SemaphoreType.DMA((6,)),
        ]
        + [pltpu.VMEM(lat, BF16), pltpu.VMEM((n,) + lat, BF16)]
        + RowGather.scratch(n)
        + AxisSum.scratch(n, (8, many))
        + AxisSum.scratch(ctx, (8, many))
        + AxisSum.scratch(fsdp, (8, many))
        + (GradSum.scratch(fsdp, ctx, ffn, False) + GradSum.semaphores(fsdp, ctx, len(ffn)) if ffn else []),
        compiler_params=params(3, 64),
    )(query, keys, values, seg_all, cols, lse, attended, d_branch, wo_rows, w_qry, w_lat, w_kproj, w_vproj,
      lat_all, xn_one, gains, tokens, d_middle, mid_own, part_feed, marks, gain_part, branch_sq, *firsts)
    return out[:3], out[3:8], out[8:]


def publish(arrays, small, seq_dev, tok_dev, feat_dim, fsdp):
    count = len(arrays)
    per = feat_dim // fsdp

    def kernel(*refs):
        srcs, sm, refs = refs[:count], refs[count], refs[count + 1 :]
        dsts, (gains, stats, radial), refs = refs[:count], refs[count : count + 3], refs[count + 3 :]
        inward = Bring(list(zip(srcs, refs[:count])), refs[count])
        outward = Bring(list(zip(refs[:count], dsts)), refs[count + 1])
        inward.start()
        f = lax.axis_index("fsdp")
        gains[...] = sm[0:2, pl.ds(pl.multiple_of(f * per, per), per)]
        for q in range(seq_dev):
            radial[q : q + 1, :] = sm[3:4, q * tok_dev : (q + 1) * tok_dev]
            total = sm[2:3, 4 * q + 3 : 4 * q + 4] * feat_dim
            for j, lane in enumerate((0, 2, 1)):
                stats[q : q + 1, j : j + 1] = jnp.sqrt(sm[2:3, 4 * q + lane : 4 * q + lane + 1] / total)
        for i in range(count):
            inward.wait([i])
            outward.start([i])
        outward.wait()

    out = pl.pallas_call(
        kernel,
        out_shape=tuple(shape_of(a.shape, a.dtype) for a in arrays)
        + (shape_of((2, per), F32), shape_of((seq_dev, 3), F32), shape_of((seq_dev, tok_dev), F32)),
        in_specs=[ANY] * count + [VMEM],
        out_specs=(ANY,) * count + (VMEM,) * 3,
        scratch_shapes=[pltpu.VMEM(a.shape, a.dtype) for a in arrays] + [pltpu.SemaphoreType.DMA((count,))] * 2,
        compiler_params=pltpu.CompilerParams(vmem_limit_bytes=60 << 20),
    )(*arrays, small)
    return out[:count], out[count], out[count + 1], out[count + 2]


class HalfSpread:
    def __init__(self, fsdp, pairs, recv, sent, own):
        self.fsdp, self.pairs, self.recv, self.sent, self.own = fsdp, pairs, recv, sent, own
        self.f, self.x = lax.axis_index("fsdp"), lax.axis_index("ctx")
        self.ys = fsdp // 2

    def view(self, a, f, half=None):
        src, dst = self.pairs[a]
        rows, size = src.shape
        columns = pl.ds(pl.multiple_of(f * size, size), size)
        if half is None:
            return dst.at[:, columns]
        return dst.at[pl.ds(pl.multiple_of(half * (rows // 2), rows // 2), rows // 2), columns]

    def part(self, a):
        src = self.pairs[a][0]
        return src.at[pl.ds(pl.multiple_of(self.x * (src.shape[0] // 2), src.shape[0] // 2), src.shape[0] // 2)]

    def start(self, which):
        for a in which:
            for k in range(1, self.ys):
                remote(self.part(a), self.view(a, self.f, self.x), self.sent.at[a, 0, k], self.recv.at[a, 0, k],
                       {"fsdp": lax.rem(self.f + 2 * k, self.fsdp)}).start()
        for a in which:
            src = self.pairs[a][0]
            remote(src, self.view(a, self.f), self.sent.at[a, 1, 0], self.recv.at[a, 1, 0],
                   {"fsdp": sibling(self.f)}).start()
            pltpu.make_async_copy(src, self.view(a, self.f), self.own.at[a]).start()

    def source(self, k):
        return lax.rem(self.f - 2 * k + self.fsdp, self.fsdp)

    def relay(self, which):
        for a in which:
            for k in range(1, self.ys):
                here = self.view(a, self.source(k), self.x)
                wait_came(here, self.sent.at[a, 0, k], self.recv.at[a, 0, k])
                remote(here, here, self.sent.at[a, 2, k], self.recv.at[a, 2, k], {"ctx": 1 - self.x}).start()
                remote(here, here, self.sent.at[a, 3, k], self.recv.at[a, 3, k],
                       {"fsdp": sibling(self.f)}).start()

    def cross(self, which):
        for a in which:
            for k in range(1, self.ys):
                here = self.view(a, self.source(k), 1 - self.x)
                wait_came(here, self.sent.at[a, 2, k], self.recv.at[a, 2, k])
                remote(here, here, self.sent.at[a, 4, k], self.recv.at[a, 4, k],
                       {"fsdp": sibling(self.f)}).start()

    def finish(self, which):
        for a in which:
            src = self.pairs[a][0]
            other = sibling(self.f)
            wait_came(self.view(a, other), self.sent.at[a, 1, 0], self.recv.at[a, 1, 0])
            pltpu.make_async_copy(src, self.view(a, self.f), self.own.at[a]).wait()
            for k in range(1, self.ys):
                there = lax.rem(other - 2 * k + self.fsdp, self.fsdp)
                wait_came(self.view(a, there, self.x), self.sent.at[a, 3, k], self.recv.at[a, 3, k])
                wait_came(self.view(a, there, 1 - self.x), self.sent.at[a, 4, k], self.recv.at[a, 4, k])

    def drain(self, which):
        for a in which:
            wait_sent(self.view(a, self.f), self.sent.at[a, 1, 0], self.recv.at[a, 1, 0])
            for k in range(1, self.ys):
                for kind in (0, 2, 3, 4):
                    wait_sent(self.part(a), self.sent.at[a, kind, k], self.recv.at[a, kind, k])

    @staticmethod
    def scratch(fsdp, arrays):
        return [
            pltpu.SemaphoreType.DMA((arrays, 5, fsdp // 2)),
            pltpu.SemaphoreType.DMA((arrays, 5, fsdp // 2)),
            pltpu.SemaphoreType.DMA((arrays,)),
        ]


R_TWO, MARK, LSE = 3, 4, 8


def layer(tokens, gain1, gain2, w_latent, shards, w_out, wide_shards, segments, out_grad, fsdp, ctx, n):
    rows, width = tokens.shape
    seq_dev, tok_dev = segments.shape
    w_query = shards[0]
    latent, q_width, inner = LATENT, w_query.shape[1], wide_shards[0].shape[0]
    heads = q_width // HEAD_DIM
    per = tok_dev // TILE
    win, span = window(ctx, tok_dev), key_span(ctx, tok_dev)
    own_shard = win - 1
    tiles = span + 1
    keyed = win * rows
    per_group = HEADS // GROUPS * HEAD_DIM
    wide, chunk = 128, 256
    pieces = rows // chunk
    per_seq = tok_dev // chunk
    strip, hop, reach = 32, 2, 3
    piece = 64
    per_block = TILE // piece
    side = 128
    many = max(width, rows)
    q_tiles = rows // TILE
    steps_all = rows // 2 // strip
    lag = hop * 2 * (n // 2)
    ffn = (inner, width // fsdp)
    axes = (0, 0, 0, 1, 0)
    whole = ((width, q_width), (latent, q_width), (latent, q_width), (q_width, width), (width, latent))
    blocks = [GradSum.block_shape(w, a, fsdp) for w, a in zip(whole, axes)]
    lat = blocks[-1]
    cols_at = width // 4

    scratch = dict(
        gbuf=pltpu.VMEM((8, gain1.shape[0]), F32),
        sbuf=pltpu.VMEM((8, tok_dev), segments.dtype),
        gain=pltpu.VMEM((8, width), F32),
        segk=pltpu.VMEM((ctx, 8, tok_dev), segments.dtype),
        cols=pltpu.VMEM((rows, 128), F32),
        tok=pltpu.VMEM((rows, width), BF16),
        gathered=pltpu.VMEM((rows, n * q_width), BF16),
        wo=pltpu.VMEM((n * q_width, width), BF16),
        cot=pltpu.VMEM((rows, width), BF16),
        xn=pltpu.VMEM((rows, width), BF16),
        p_two=pltpu.VMEM((rows, width), BF16),
        p_feed=pltpu.VMEM((rows, width), BF16),
        left=pltpu.VMEM((rows, width), BF16),
        right=pltpu.VMEM((rows, width), BF16),
        branch=pltpu.VMEM((rows, width), BF16),
        mid=pltpu.VMEM((rows, width), F32),
        wg=pltpu.VMEM((inner, width), BF16),
        wu=pltpu.VMEM((inner, width), BF16),
        wd=pltpu.VMEM((inner, width), BF16),
        hid=pltpu.VMEM((rows, inner), BF16),
        dg=pltpu.VMEM((rows, inner), BF16),
        du=pltpu.VMEM((rows, inner), BF16),
        w_lat=pltpu.VMEM((width, latent), BF16),
        w_qry=pltpu.VMEM((width, q_width), BF16),
        w_kproj=pltpu.VMEM((latent, q_width), BF16),
        w_vproj=pltpu.VMEM((latent, q_width), BF16),
        wo_rows=pltpu.VMEM((q_width, width), BF16),
        wo_line=pltpu.VMEM((n,) + w_out.shape, BF16),
        lat_all=pltpu.VMEM((keyed, latent), BF16),
        query=pltpu.VMEM((rows, q_width), BF16),
        keys=pltpu.VMEM((keyed, q_width), BF16),
        values=pltpu.VMEM((keyed, q_width), BF16),
        att=pltpu.VMEM((rows, q_width), BF16),
        dk=pltpu.VMEM((keyed, q_width), F32),
        dv=pltpu.VMEM((keyed, q_width), F32),
        dqb=pltpu.VMEM((rows, q_width), BF16),
        grad_seq=pltpu.VMEM((TILE, q_width), BF16),
        lat_parts=pltpu.VMEM((keyed, latent), BF16),
        dlat=pltpu.VMEM((rows, latent), BF16),
        came=pltpu.VMEM((rows, latent), BF16),
        g_sum=pltpu.VMEM((8, width), F32),
        g_sum2=pltpu.VMEM((8, width), F32),
        sm=pltpu.VMEM((8, many), F32),
        sacc=pltpu.VMEM((3 * seq_dev, 8, width), F32),
        lat_own=pltpu.VMEM(lat, BF16),
        lat_every=pltpu.VMEM((n,) + lat, BF16),
        local=pltpu.SemaphoreType.DMA((2,)),
        flush=pltpu.SemaphoreType.DMA((10,)),
        lat_recv=pltpu.SemaphoreType.DMA((pieces,)),
        lat_sent=pltpu.SemaphoreType.DMA((pieces,)),
        c_recv=pltpu.SemaphoreType.DMA((seq_dev, per_seq)),
        c_sent=pltpu.SemaphoreType.DMA((seq_dev, per_seq)),
    )
    out_blocks = [shape_of(b, F32) for b in blocks[:-1]] + [shape_of((lat[0], GROUPS * lat[1]), F32)]
    out_blocks += [shape_of(ffn, F32)] * 3
    groups = dict(
        outs=[pltpu.VMEM(o.shape, F32) for o in out_blocks[:5]],
        held=GradSum.scratch(fsdp, ctx, [ffn] * 3 + blocks),
        parts=[pltpu.VMEM(w, BF16) for w in whole],
        spread=Spread.scratch(fsdp, 5),
        half=HalfSpread.scratch(fsdp, 4),
        share=CtxShare.scratch(ctx),
        wline=RowGather.scratch(n),
        gather=LineGather.scratch(n, rows // piece),
        two=LineSum.scratch(n, rows, width, strip)[2:],
        feed=LineSum.scratch(n, rows, width, strip)[2:],
        one=LineSum.scratch(n, rows, width, strip)[2:],
        gffn=GradSum.semaphores(fsdp, ctx, 3),
        gatt=GradSum.semaphores(fsdp, ctx, 5),
        lline=RowGather.scratch(n),
        s_tp=AxisSum.scratch(n, (8, many)),
        s_ctx=AxisSum.scratch(ctx, (8, many)),
        s_fsdp=AxisSum.scratch(fsdp, (8, many)),
    )
    names = list(scratch)
    shapes = list(scratch.values())
    places = {}
    for key, some in groups.items():
        places[key] = (len(shapes), len(shapes) + len(some))
        shapes = shapes + list(some)

    def kernel(*refs):
        (tok_in, ga, gb, wlat, wq, wkp, wvp, wout, wgt, wut, wdn, seg, cot_in), refs = refs[:13], refs[13:]
        (o_mixed, o_tok), o_blocks, o_small, refs = refs[:2], refs[2:10], refs[10], refs[11:]
        r = SimpleNamespace(**dict(zip(names, refs)))
        g = SimpleNamespace(**{key: refs[a:b] for key, (a, b) in places.items()})
        cols, tok, cot, xn, mid = r.cols, r.tok, r.cot, r.xn, r.mid
        gain, segk = r.gain, r.segk
        x, me = lax.axis_index("ctx"), lax.axis_index("tp")
        outs = list(g.outs) + [mid.at[0 : ffn[0], i * ffn[1] : (i + 1) * ffn[1]] for i in range(3)]

        load = Bring([(tok_in, tok), (cot_in, cot)], r.local)
        load.start()
        r.gbuf[...] = jnp.zeros_like(r.gbuf)
        r.gbuf[0:1, :] = ga[...].astype(F32).reshape(1, -1)
        r.gbuf[1:2, :] = gb[...].astype(F32).reshape(1, -1)
        r.sbuf[...] = jnp.zeros_like(r.sbuf)
        r.sbuf[0:seq_dev, :] = seg[...]
        meet(n, fsdp, ctx, everyone=True)

        group = me * q_width // per_group
        src_lat = wlat.at[:, pl.ds(pl.multiple_of(group * latent, latent), latent)]
        spread = Spread(
            fsdp,
            [(r.gbuf, gain), (src_lat, r.w_lat), (wq, r.w_qry), (wkp, r.w_kproj), (wvp, r.w_vproj)],
            [1, 0, 0, 0, 0], *g.spread,
        )
        share = CtxShare(ctx, r.sbuf, segk, *g.share)
        wline = RowGather(n, wout, r.wo_line, *g.wline)
        half = HalfSpread(
            fsdp,
            [(wgt, r.wg), (wut, r.wu), (wdn, r.wd), (r.wo_line.reshape(n * q_width, w_out.shape[1]), r.wo)],
            *g.half,
        )
        spread.start()
        share.start()
        wline.start()
        half.start([0, 1, 2])
        cols[...] = jnp.zeros_like(cols)
        r.g_sum[...] = jnp.zeros_like(r.g_sum)
        r.g_sum2[...] = jnp.zeros_like(r.g_sum2)
        r.sacc[...] = jnp.zeros_like(r.sacc)
        r.sm[...] = jnp.zeros_like(r.sm)
        load.wait([0])

        def scale(i):
            at = pl.ds(pl.multiple_of(i * wide, wide), wide)
            value = tok[at, :].astype(F32)
            cols[at, R_ONE : R_ONE + 1] = lax.rsqrt(jnp.mean(value * value, axis=-1, keepdims=True) + eps)

        loop(0, rows // wide, scale)
        spread.relay([0, 1])
        spread.finish([0, 1])
        lat_all = r.lat_all

        def place(shard, i):
            seq = i // per_seq
            return pl.ds(pl.multiple_of((seq * win + shard) * tok_dev + lax.rem(i, per_seq) * chunk, chunk), chunk)

        def pass_on(i):
            return remote(lat_all.at[place(own_shard, i)], lat_all.at[place(own_shard - 1, i)], r.lat_sent.at[i],
                          r.lat_recv.at[i], {"ctx": x + 1})

        def first_norm(i):
            at = pl.ds(pl.multiple_of(i * chunk, chunk), chunk)
            unit = (tok[at, :].astype(F32) * cols[at, R_ONE : R_ONE + 1] * gain[0:1, :]).astype(BF16)
            xn[at, :] = unit
            lat_all[place(own_shard, i), :] = dot(unit, r.w_lat[...]).astype(BF16)

            @pl.when(x + 1 < ctx)
            def _():
                pass_on(i).start()

        loop(0, pieces, first_norm)
        wline.relay([1])
        spread.relay([2, 3, 4])
        spread.finish([2, 3, 4])

        def project(shard, i):
            to = place(shard, i)
            value = lat_all[to, :]
            r.keys[to, :] = dot(value, r.w_kproj[...]).astype(BF16)
            r.values[to, :] = dot(value, r.w_vproj[...]).astype(BF16)

        def ask(i):
            at = pl.ds(pl.multiple_of(i * chunk, chunk), chunk)
            r.query[at, :] = dot(xn[at, :], r.w_qry[...]).astype(BF16)
            project(own_shard, i)

        loop(0, pieces, ask)
        if n > 2:
            wline.relay([2])
        share.finish()
        for q in range(seq_dev):
            at = slice(q * tok_dev, (q + 1) * tok_dev)
            ids = jnp.broadcast_to(r.sbuf[q : q + 1, :].astype(F32), (128, tok_dev)).T
            cols[at, SEGMENT : SEGMENT + 1] = ids[:, 0:1]
            final = segk[ctx - 1, q : q + 1, tok_dev - 1 : tok_dev].astype(F32)
            cols[at, VALID : VALID + 1] = jnp.where(ids[:, 0:1] != final, 1.0, 0.0)
        if n > 3:
            wline.relay(range(3, n))
        wline.finish()
        half.start([3])
        half.relay([0, 1])

        def theirs(i):
            @pl.when(x - 1 >= 0)
            def _():
                wait_came(lat_all.at[place(own_shard - 1, i)], r.lat_sent.at[i], r.lat_recv.at[i])

            @pl.when(x - 1 < 0)
            def _():
                lat_all[place(own_shard - 1, i), :] = jnp.zeros((chunk, latent), BF16)

            project(own_shard - 1, i)

        loop(0, pieces, theirs)

        att, gathered = r.att, r.gathered
        line = LineGather(n, piece, att, gathered, *g.gather, hop=reach)

        def query_tile(i):
            seq = i // per
            q_tile = own_shard * per + lax.rem(i, per)
            at = pl.ds(pl.multiple_of(i * TILE, TILE), TILE)
            near = pl.ds(pl.multiple_of((seq * win * per + q_tile - span) * TILE, TILE), tiles * TILE)
            counted = jnp.concatenate(
                [
                    c.astype(F32)
                    for c in counted_keys(cols, segk, at, seq, q_tile * TILE, q_tile - span, tiles, tok_dev, win)
                ],
                axis=1,
            )
            accum = jnp.zeros((TILE, q_width), F32)
            for h in range(heads):
                score = dot_t(head_only(r.query[at, :], h), r.keys[near, :]) * 0.125
                score = jnp.where(counted > 0.0, score, -1e30)
                top = jnp.max(score, axis=-1, keepdims=True)
                weight = jnp.exp(score - top)
                total = jnp.sum(weight, axis=-1, keepdims=True)
                prob = (weight * (1.0 / total)).astype(BF16)
                accum = accum + jnp.dot(prob, head_only(r.values[near, :], h), preferred_element_type=F32)
                cols[at, LSE + h : LSE + h + 1] = top + jnp.log(total)
                line.step((i - 1) * per_block + h * per_block // heads)
            att[at, :] = accum.astype(BF16)

        loop(0, q_tiles, query_tile)
        s1 = (q_tiles - 1) * per_block
        line.begin()
        half.relay([2, 3])
        half.cross([0, 1, 2, 3])
        loop(s1, per_block + reach * (n - 1), line.step)
        s1 = per_block + reach * (n - 1)
        half.finish([3, 0, 1, 2])
        half.drain([0, 1, 2, 3])
        r.wo_rows[...] = r.wo[pl.ds(pl.multiple_of(me * q_width, q_width), q_width), :]
        line.begun()
        load.wait([1])

        p_two, p_feed, wg, wu, wd = r.p_two, r.p_feed, r.wg, r.wu, r.wd

        def second_back(at, own, total):
            unit = mid[at, :] * cols[at, R_TWO : R_TWO + 1]
            r.g_sum2[...] += jnp.sum((total * unit).reshape(strip // 8, 8, width), axis=0)
            scaled = total * gain[1:2, :]
            mean = jnp.mean(scaled * unit, axis=-1, keepdims=True)
            d_mid = cot[at, :].astype(F32) + cols[at, R_TWO : R_TWO + 1] * (scaled - unit * mean)
            first_unit = tok[at, :].astype(F32) * cols[at, R_ONE : R_ONE + 1]
            cols[at, MARK : MARK + 1] = jnp.sum(first_unit * d_mid, axis=-1, keepdims=True)
            return d_mid.astype(BF16)

        def forward(at, own, total):
            mixed = mid[at, :] + total
            seq = at.start // tok_dev
            counted = cols[at, VALID : VALID + 1]
            r.sacc[seq] += jnp.sum((mixed * mixed * counted).reshape(strip // 8, 8, width), axis=0)
            r.sacc[seq_dev + seq] += jnp.sum((total * total * counted).reshape(strip // 8, 8, width), axis=0)
            return mixed.astype(BF16)

        def first_back(at, own, total):
            r1 = cols[at, R_ONE : R_ONE + 1]
            unit = tok[at, :].astype(F32) * r1
            scaled = total * gain[0:1, :]
            mean = jnp.mean(scaled * unit, axis=-1, keepdims=True)
            return (r.branch[at, :].astype(F32) + r1 * (scaled - unit * mean)).astype(BF16)

        two = LineSum(n, strip, hop, p_two, r.left, r.right, r.branch, *g.two, second_back)
        feed = LineSum(n, strip, hop, p_feed, gathered, r.wo, xn, *g.feed, forward)
        one = LineSum(n, strip, hop, cot, r.left, r.right, p_two, *g.one, first_back)
        parts = [wg, wu, wd]
        gffn = GradSum(fsdp, ctx, parts, [1, 1, 1], None,
                       [g.held[3 * a : 3 * a + 3] for a in range(3)], *g.gffn)
        aparts = g.parts
        gatt = GradSum(fsdp, ctx, aparts, axes, None,
                       [g.held[3 * a : 3 * a + 3] for a in range(3, 8)], *g.gatt)

        def block_of_rows(b):
            at = pl.ds(pl.multiple_of(b * TILE, TILE), TILE)
            seq = b * TILE // tok_dev

            def steps(j):
                line.step(s1 + b * per_block + j)
                two.step((b - 1) * per_block + j)

            branch = dot(gathered[at, :], r.wo[...])
            middle_rows = tok[at, :].astype(F32) + branch
            mid[at, :] = middle_rows
            r.sacc[2 * seq_dev + seq] += jnp.sum(
                (branch * branch * cols[at, VALID : VALID + 1]).reshape(TILE // 8, 8, width), axis=0
            )
            level = lax.rsqrt(jnp.mean(middle_rows * middle_rows, axis=-1, keepdims=True) + eps)
            cols[at, R_TWO : R_TWO + 1] = level
            unit = (middle_rows * level * gain[1:2, :]).astype(BF16)
            xn[at, :] = unit
            steps(0)
            gate = dot_t(unit, wg[...])
            upper = dot_t(unit, wu[...])
            sigma = jax.nn.sigmoid(gate)
            swish = gate * sigma
            hidden = (swish * upper).astype(BF16)
            r.hid[at, :] = hidden
            slope = upper * sigma * (1.0 + gate * (1.0 - sigma))
            steps(1)
            p_feed[at, :] = dot(hidden, wd[...]).astype(BF16)
            d_hidden = dot_t(cot[at, :], wd[...])
            d_gate = (d_hidden * slope).astype(BF16)
            d_upper = (d_hidden * swish).astype(BF16)
            r.dg[at, :] = d_gate
            r.du[at, :] = d_upper
            steps(2)
            p_two[at, :] = (dot(d_gate, wg[...]) + dot(d_upper, wu[...])).astype(BF16)
            steps(3)

        loop(0, q_tiles, block_of_rows)
        s2 = (q_tiles - 1) * per_block

        def product(i):
            at = pl.ds(pl.multiple_of(i * cols_at, cols_at), cols_at)
            left = xn[:, at]
            parts[0][:, at] = dot_rows(r.dg[...], left).astype(BF16)
            parts[1][:, at] = dot_rows(r.du[...], left).astype(BF16)
            parts[2][:, at] = dot_rows(r.hid[...], cot[:, at]).astype(BF16)

        def busy(s):
            two.step(s)
            product(s - s2)

        line.drain()
        loop(s2, s2 + 4, busy)
        gffn.start()
        s2 = s2 + 4

        dk, dv, dqb, grad_seq, lat_parts = r.dk, r.dv, r.dqb, r.grad_seq, r.lat_parts

        def clear(i):
            at = pl.ds(pl.multiple_of(i * TILE, TILE), TILE)
            dk[at, :] = jnp.zeros((TILE, q_width), F32)
            dv[at, :] = jnp.zeros((TILE, q_width), F32)

        loop(0, keyed // TILE, clear)
        ready = steps_all // seq_dev + lag
        loop(s2, ready, two.step)

        def grad_tile(i, step):
            seq = i // per
            q_tile = own_shard * per + lax.rem(i, per)
            at = pl.ds(pl.multiple_of(i * TILE, TILE), TILE)
            near = pl.ds(pl.multiple_of((seq * win * per + q_tile - span) * TILE, TILE), tiles * TILE)
            grad_seq[...] = dot_t(r.branch[at, :], r.wo_rows[...]).astype(BF16)
            inner_sum = grad_seq[...].astype(F32) * att[at, :].astype(F32)
            counted = jnp.concatenate(
                [
                    c.astype(F32)
                    for c in counted_keys(cols, segk, at, seq, q_tile * TILE, q_tile - span, tiles, tok_dev, win)
                ],
                axis=1,
            )
            d_query = jnp.zeros((TILE, q_width), F32)
            d_key = jnp.zeros((tiles * TILE, q_width), F32)
            d_value = jnp.zeros((tiles * TILE, q_width), F32)
            for h in range(heads):
                delta = jnp.sum(head_only(inner_sum, h), axis=-1, keepdims=True)
                asked, ours = head_only(r.query[at, :], h), head_only(grad_seq[...], h)
                score = jnp.where(counted > 0.0, dot_t(asked, r.keys[near, :]) * 0.125, -1e30)
                prob = jnp.exp(score - cols[at, LSE + h : LSE + h + 1]) * counted
                d_score = (prob * (dot_t(ours, r.values[near, :]) - delta)).astype(BF16)
                d_query = d_query + jnp.dot(d_score, head_only(r.keys[near, :], h), preferred_element_type=F32)
                d_key = d_key + dot_rows(d_score, asked)
                d_value = d_value + dot_rows(prob.astype(BF16), ours)
                step(h)
            dqb[at, :] = (d_query * 0.125).astype(BF16)
            dk[near, :] += d_key * 0.125
            dv[near, :] += d_value

        def send_latent(seq, i):
            j = seq * per_seq + i
            at = pl.ds(pl.multiple_of(j * chunk, chunk), chunk)
            return remote(lat_parts.at[place(own_shard - 1, j)], r.came.at[at], r.c_sent.at[seq, i],
                          r.c_recv.at[seq, i], {"ctx": x - 1})

        def latents(seq):
            for shard in (own_shard - 1, own_shard):
                for i in range(per_seq):
                    at = place(shard, seq * per_seq + i)
                    lat_parts[at, :] = (
                        dot_t(dk[at, :].astype(BF16), r.w_kproj[...])
                        + dot_t(dv[at, :].astype(BF16), r.w_vproj[...])
                    ).astype(BF16)
                    if shard < own_shard:

                        @pl.when(x - 1 >= 0)
                        def _(i=i):
                            send_latent(seq, i).start()

        def sequence(seq):
            def tile(i):
                def step(h):
                    t = (i * heads + h) * steps_per // heads
                    two.step(ready + t)
                    feed.step(t)

                grad_tile(i, step)

            loop(seq * per, seq * per + per, tile)
            latents(seq)

            @pl.when(seq == 0)
            def _():
                two.drain()
                gffn.pair()

            @pl.when(seq == seq_dev - 1)
            def _():
                gffn.second()

        steps_per = heads
        loop(0, seq_dev, sequence)
        fed = q_tiles * steps_per

        def whole_latent(j):
            seq, i = j // per_seq, lax.rem(j, per_seq)
            at = pl.ds(pl.multiple_of(j * chunk, chunk), chunk)
            r.dlat[at, :] = lat_parts[place(own_shard, j), :]

            @pl.when(x + 1 < ctx)
            def _():
                wait_came(r.came.at[at], r.c_sent.at[seq, i], r.c_recv.at[seq, i])
                r.dlat[at, :] = (r.dlat[at, :].astype(F32) + r.came[at, :].astype(F32)).astype(BF16)

            cot[at, :] = (dot_t(dqb[at, :], r.w_qry[...]) + dot_t(r.dlat[at, :], r.w_lat[...])).astype(BF16)

        def steps(s):
            one.step(s)
            feed.step(fed + s)

        def first_unit_columns(at):
            return (tok[:, at].astype(F32) * cols[:, R_ONE : R_ONE + 1] * gain[0:1, at]).astype(BF16)

        early = (seq_dev - 1) * per_seq
        loop(0, early, whole_latent)

        def mixed_work(i):
            at = pl.ds(pl.multiple_of(i * chunk, chunk), chunk)
            aparts[0][at, :] = dot_rows(first_unit_columns(at), dqb[...]).astype(BF16)
            aparts[3][:, at] = dot_rows(att[...], r.branch[:, at]).astype(BF16)
            steps(i)

        s0 = width // chunk
        loop(0, s0, mixed_work)
        loop(early, pieces, whole_latent)
        aparts[1][...] = dot_rows(lat_all[...], dk[...].astype(BF16)).astype(BF16)
        steps(s0)
        aparts[2][...] = dot_rows(lat_all[...], dv[...].astype(BF16)).astype(BF16)
        steps(s0 + 1)
        s0 = s0 + 2

        def product_lat(s):
            at = pl.ds(pl.multiple_of((s - s0) * chunk, chunk), chunk)
            aparts[4][at, :] = dot_rows(first_unit_columns(at), r.dlat[...]).astype(BF16)
            steps(s)

        begun = s0 + width // chunk
        loop(s0, begun, product_lat)
        gatt.start()
        gffn.third()

        def gains_of(i):
            at = pl.ds(pl.multiple_of(i * side, side), side)
            value = cot[at, :].astype(F32) * (tok[at, :].astype(F32) * cols[at, R_ONE : R_ONE + 1])
            r.g_sum[...] += jnp.sum(value.reshape(side // 8, 8, width), axis=0)
            along = lax.dot_general(jnp.ones((8, width), F32), value * gain[0:1, :], (((1,), (1,)), ((), ())),
                                    precision=lax.Precision.HIGHEST, preferred_element_type=F32)
            r.sm[3:4, at] = along[0:1, :]
            lines = cols[at, :].T
            r.sm[4:5, at] = lines[MARK : MARK + 1, :]
            r.sm[5:6, at] = lines[R_ONE : R_ONE + 1, :]

        def two_gains(s):
            steps(s)
            gains_of(2 * (s - begun))
            gains_of(2 * (s - begun) + 1)

        mark = begun + rows // side // 2
        loop(begun, begun + 1, two_gains)
        gatt.pair()
        gatt.second()
        loop(begun + 1, mark, two_gains)
        last = one.steps()
        for s in range(fed + mark, feed.steps()):
            feed.step(s)
        flush = r.flush
        out_mixed = pltpu.make_async_copy(xn, o_mixed, flush.at[8])
        out_mixed.start()
        gatt.third()
        lane = lax.broadcasted_iota(jnp.int32, (1, many), 1)
        once = jnp.where(me == 0, 1.0, 0.0)
        row = jnp.zeros((1, many), F32)

        def whole_sum(value):
            return jnp.sum(jnp.sum(value, axis=0, keepdims=True), axis=1, keepdims=True)

        for q in range(seq_dev):
            stats = [
                whole_sum(r.sacc[q]),
                whole_sum(r.sacc[seq_dev + q]),
                whole_sum(r.sacc[2 * seq_dev + q]) * once,
                jnp.sum(cols[q * tok_dev : (q + 1) * tok_dev, VALID : VALID + 1], axis=0, keepdims=True) * once,
            ]
            for j, value in enumerate(stats):
                row = row + jnp.where(lane == 4 * q + j, value, 0.0)
        r.sm[2:3, :] = row
        r.sm[0:1, 0:width] = jnp.sum(r.g_sum[...], axis=0, keepdims=True)
        r.sm[1:2, 0:width] = jnp.sum(r.g_sum2[...], axis=0, keepdims=True)
        r_row = r.sm[5:6, :]
        over_tp = AxisSum("tp", n, *g.s_tp)
        over_ctx = AxisSum("ctx", ctx, *g.s_ctx)
        over_fsdp = AxisSum("fsdp", fsdp, *g.s_fsdp)
        over_tp.start(r.sm[...])
        lline = RowGather(n, r.lat_own, r.lat_every, *g.lline)
        outward = Bring([(outs[i], o_blocks[i]) for i in range(8)], flush)

        def store(a, at, total):
            if a < 4:
                outs[a][at, :] = total
            else:
                r.lat_own[at, :] = total.astype(BF16)

        def store_ffn(a, at, total):
            outs[5 + a][at, :] = total

        loop(mark, mark + 2, steps)
        along_tp = over_tp.finish()
        over_ctx.start(along_tp)
        gffn.fourth(store_ffn)
        outward.start([5, 6, 7])
        loop(mark + 2, mark + 4, steps)
        gatt.fourth(store)
        outward.start([0, 1, 2, 3])
        lline.start()
        along_ctx = over_ctx.finish()
        over_fsdp.start(along_ctx)
        loop(mark + 4, mark + 6, steps)
        lline.relay([1])
        everywhere = over_fsdp.finish()
        loop(mark + 6, mark + 8, steps)
        if n > 2:
            lline.relay([2])
        loop(mark + 8, last, steps)
        if n > 3:
            lline.relay(range(3, n))
        out_tok = pltpu.make_async_copy(p_two, o_tok, flush.at[9])
        out_tok.start()
        row = lax.broadcasted_iota(jnp.int32, everywhere.shape, 0)
        o_small[...] = jnp.where(row < 2, everywhere, along_ctx)
        o_small[3:4, :] = (along_tp[4:5] + eps * r_row * r_row * r_row * along_tp[3:4]) * (1.0 / width**0.5)
        lline.finish()

        def latent_sum(i):
            at = pl.ds(pl.multiple_of(i * 16, 16), 16)
            for gr in range(GROUPS):
                total = jnp.zeros((16, lat[1]), F32)
                for t in range(n):
                    if t * GROUPS // n == gr:
                        total = total + r.lat_every[t, at, :].astype(F32)
                outs[4][at, gr * lat[1] : (gr + 1) * lat[1]] = total

        loop(0, lat[0] // 16, latent_sum)
        outward.start([4])

        @pl.when(x + 1 < ctx)
        def _():
            loop(0, pieces, lambda i: pass_on(i).wait_send())

        @pl.when(x - 1 >= 0)
        def _():
            for seq in range(seq_dev):
                for i in range(per_seq):
                    send_latent(seq, i).wait_send()

        feed.drain()
        one.drain()
        gffn.drain_pair()
        gffn.drain()
        gatt.drain_pair()
        gatt.drain()
        outward.wait()
        out_mixed.wait()
        out_tok.wait()

    out = pl.pallas_call(
        kernel,
        out_shape=(shape_of((rows, width), BF16),) * 2 + tuple(out_blocks) + (shape_of((8, many), F32),),
        in_specs=[ANY] + [VMEM] * 2 + [ANY] * 8 + [VMEM, ANY],
        out_specs=(ANY,) * 10 + (VMEM,),
        scratch_shapes=shapes,
        compiler_params=params(1, 64),
    )(tokens, gain1, gain2, w_latent, *shards, w_out, *wide_shards, segments, out_grad)
    return out[0], out[1], out[2:7], out[7:10], out[10]


def three_kernels(tokens, gain1, gain2, w_latent, shards, w_out, wide_shards, segments, out_grad, fsdp, ctx, n):
    seq_dev, tok_dev = segments.shape
    gate, up, down = wide_shards
    (xn_one, cols, gains, w_lat, w_qry, w_kproj, w_vproj, gate_all, up_all, wo_cols, seg_all, lat_all,
     query, keys, values) = front(tokens, gain1, gain2, w_latent, shards, w_out, (gate, up), segments, fsdp, ctx, n)
    late = window(ctx, tok_dev) <= 2
    (d_branch, part_feed, d_middle, mid_own, wo_rows, gain_part, branch_sq, marks, attended, lse), ffn = middle(
        query, keys, values, seg_all, cols, (wo_cols.reshape(-1, w_out.shape[1]), down), gate_all, up_all, gains,
        tokens, out_grad, fsdp, ctx, n, seq_dev, late,
    )
    (grad_tokens, mixed, small), att_grads, late_ffn = back(
        query, keys, values, seg_all, cols, lse, attended, d_branch, wo_rows, (w_qry, w_lat, w_kproj, w_vproj),
        lat_all, xn_one, gains, tokens, d_middle, mid_own, part_feed, marks, gain_part, branch_sq,
        ffn if late else (), fsdp, ctx, n, seq_dev,
    )
    return mixed, grad_tokens, att_grads, late_ffn if late else ffn, small


def on_device(
    tokens, gain1, w_latent, w_query, w_key, w_value, w_out, gain2, w_gate, w_up, w_down, segments, cotangent
):
    seq_dev, tok_dev, feat_dim = tokens.shape
    n_ctx, n_tp, n_fsdp = lax.axis_size("ctx"), lax.axis_size("tp"), lax.axis_size("fsdp")
    row_count = seq_dev * tok_dev
    tok_rows = tokens.reshape(row_count, feat_dim)
    out_grad = cotangent.reshape(row_count, feat_dim)
    if n_ctx == 2 and n_fsdp >= 4 and w_down.shape[0] <= row_count and feat_dim <= row_count:
        mixed, grad_tokens, att_grads, ffn_grads, small = layer(
            tok_rows, gain1, gain2, w_latent, (w_query, w_key, w_value), w_out, (w_gate.T, w_up.T, w_down), segments,
            out_grad, n_fsdp, n_ctx, n_tp,
        )
    else:
        mixed, grad_tokens, att_grads, ffn_grads, small = three_kernels(
            tok_rows, gain1, gain2, w_latent, (w_query, w_key, w_value), w_out, (w_gate.T, w_up.T, w_down), segments,
            out_grad, n_fsdp, n_ctx, n_tp,
        )
    arrays, gain_grads, stats, radial = publish(
        (mixed, grad_tokens, *att_grads, *ffn_grads), small, seq_dev, tok_dev, feat_dim, n_fsdp
    )
    mixed, grad_tokens, s_qry, s_kproj, s_vproj, s_outp, s_lat, s_gate, s_up, s_down = arrays
    return (
        mixed.reshape(seq_dev, tok_dev, feat_dim),
        grad_tokens.reshape(seq_dev, tok_dev, feat_dim),
        gain_grads[0],
        s_lat,
        s_qry,
        s_kproj,
        s_vproj,
        s_outp,
        gain_grads[1],
        s_gate.T,
        s_up.T,
        s_down,
        stats,
        radial,
    )


def solution(mesh):
    return jax.shard_map(
        on_device,
        mesh=mesh,
        in_specs=(
            P("fsdp", "ctx", None),
            P("fsdp"),
            P("fsdp", None),
            P("fsdp", "tp"),
            P("fsdp", "tp"),
            P("fsdp", "tp"),
            P("tp", "fsdp"),
            P("fsdp"),
            P("fsdp", "tp"),
            P("fsdp", "tp"),
            P("tp", "fsdp"),
            P("fsdp", "ctx"),
            P("fsdp", "ctx", None),
        ),
        out_specs=(
            P("fsdp", "ctx", None),
            P("fsdp", "ctx", None),
            P("fsdp"),
            P("fsdp", None),
            P("fsdp", "tp"),
            P("fsdp", "tp"),
            P("fsdp", "tp"),
            P("tp", "fsdp"),
            P("fsdp"),
            P("fsdp", "tp"),
            P("fsdp", "tp"),
            P("tp", "fsdp"),
            P("fsdp", None),
            P("fsdp", "ctx"),
        ),
        check_vma=False,
    )
```

```python
from types import SimpleNamespace

import jax
import jax.numpy as jnp
from jax import lax
from jax.experimental import pallas as pl
from jax.experimental.pallas import tpu as pltpu
from jax.sharding import PartitionSpec as P

HEADS = 16
HEAD_DIM = 64
GROUPS = 2
LATENT = 256
MESH = pl.DeviceIdType.MESH
VMEM = pl.BlockSpec(memory_space=pltpu.VMEM)
ANY = pl.BlockSpec(memory_space=pl.ANY)
F32 = jnp.float32
BF16 = jnp.bfloat16

eps = 1e-05


def remote(src, dst, send_sem, recv_sem, device):
    return pltpu.make_async_remote_copy(
        src_ref=src,
        dst_ref=dst,
        send_sem=send_sem,
        recv_sem=recv_sem,
        device_id=device,
        device_id_type=MESH,
    )


def wait_sent(ref, sem, recv_sem):
    remote(ref, ref, sem, recv_sem, {"tp": lax.axis_index("tp")}).wait_send()


def wait_came(ref, send_sem, sem):
    remote(ref, ref, send_sem, sem, {"tp": lax.axis_index("tp")}).wait_recv()


def meet(line=0, fsdp=0, ctx=0, everyone=False):
    barrier = pltpu.get_barrier_semaphore()

    def greet(device):
        pl.semaphore_signal(barrier, inc=1, device_id=device, device_id_type=MESH)

    known = 0
    f, x, me = lax.axis_index("fsdp"), lax.axis_index("ctx"), lax.axis_index("tp")
    if fsdp and everyone:
        for k in range(1, fsdp):
            greet({"fsdp": lax.rem(f + k, fsdp)})
        known += fsdp - 1
    elif fsdp:
        greet({"fsdp": sibling(f)})
        for k in range(1, fsdp // 2):
            greet({"fsdp": lax.rem(f + 2 * k, fsdp)})
        known += fsdp // 2
    for k in range(1, ctx):
        greet({"ctx": lax.rem(x + k, ctx)})
        known += 1
    if line > 1 and everyone:
        for k in range(1, line):
            greet({"tp": lax.rem(me + k, line)})
        known += line - 1
    if line > 1 and not everyone:

        @pl.when(me > 0)
        def _():
            greet({"tp": me - 1})

        @pl.when(me < line - 1)
        def _():
            greet({"tp": me + 1})

        @pl.when((me > 0) & (me < line - 1))
        def _():
            pl.semaphore_wait(barrier, known + 2)

        @pl.when((me == 0) | (me == line - 1))
        def _():
            pl.semaphore_wait(barrier, known + 1)

    else:
        pl.semaphore_wait(barrier, known)


def sibling(f):
    return f + 1 - 2 * lax.rem(f, 2)


def block(ref, axis, index, size):
    at = pl.ds(pl.multiple_of(index * size, size), size)
    return ref.at[at] if axis == 0 else ref.at[:, at]


class Bring:
    def __init__(self, pairs, sems):
        self.copies = [pltpu.make_async_copy(src, dst, sems.at[i]) for i, (src, dst) in enumerate(pairs)]

    def start(self, which=None):
        for i in which if which is not None else range(len(self.copies)):
            self.copies[i].start()

    def wait(self, which=None):
        for i in which if which is not None else range(len(self.copies)):
            self.copies[i].wait()


class Spread:
    def __init__(self, fsdp, pairs, axes, recv, sent, own):
        self.fsdp, self.pairs, self.axes = fsdp, pairs, axes
        self.recv, self.sent, self.own = recv, sent, own
        self.f = lax.axis_index("fsdp")

    def size(self, a):
        return self.pairs[a][0].shape[self.axes[a]]

    def target(self, a, f):
        return block(self.pairs[a][1], self.axes[a], f, self.size(a))

    def start(self):
        f = self.f
        for a, (src, dst) in enumerate(self.pairs):
            for k in range(1, self.fsdp // 2):
                remote(src, self.target(a, f), self.sent.at[a], self.recv.at[a, f],
                       {"fsdp": lax.rem(f + 2 * k, self.fsdp)}).start()
        for a, (src, dst) in enumerate(self.pairs):
            remote(src, self.target(a, f), self.sent.at[a], self.recv.at[a, f],
                   {"fsdp": sibling(f)}).start()
            pltpu.make_async_copy(src, self.target(a, f), self.own.at[a]).start()

    def relay(self, which=None):
        for a in which or range(len(self.pairs)):
            for k in range(1, self.fsdp // 2):
                other = lax.rem(self.f + 2 * k, self.fsdp)
                here = self.target(a, other)
                wait_came(here, self.sent.at[a], self.recv.at[a, other])
                remote(here, here, self.sent.at[a], self.recv.at[a, other],
                       {"fsdp": sibling(self.f)}).start()

    def finish(self, which=None):
        for a in which or range(len(self.pairs)):
            src, dst = self.pairs[a]
            for k in range(0, self.fsdp // 2):
                other = lax.rem(sibling(self.f) + 2 * k, self.fsdp)
                wait_came(self.target(a, other), self.sent.at[a], self.recv.at[a, other])
            pltpu.make_async_copy(src, self.target(a, self.f), self.own.at[a]).wait()
            many = (self.fsdp - 1) * self.size(a)
            ref = dst.at[pl.ds(0, many)] if self.axes[a] == 0 else dst.at[:, pl.ds(0, many)]
            wait_sent(ref, self.sent.at[a], self.recv.at[a, 0])

    @staticmethod
    def scratch(fsdp, arrays):
        return [
            pltpu.SemaphoreType.DMA((arrays, fsdp)),
            pltpu.SemaphoreType.DMA((arrays,)),
            pltpu.SemaphoreType.DMA((arrays,)),
        ]


class CtxShare:
    def __init__(self, ctx, src, dst, recv, sent, own):
        self.ctx, self.src, self.dst = ctx, src, dst
        self.recv, self.sent, self.own = recv, sent, own
        self.x = lax.axis_index("ctx")

    def start(self):
        for k in range(1, self.ctx):
            remote(self.src, self.dst.at[self.x], self.sent.at[k - 1], self.recv.at[self.x],
                   {"ctx": lax.rem(self.x + k, self.ctx)}).start()
        pltpu.make_async_copy(self.src, self.dst.at[self.x], self.own).start()

    def finish(self):
        for k in range(1, self.ctx):
            other = lax.rem(self.x + k, self.ctx)
            wait_came(self.dst.at[other], self.sent.at[k - 1], self.recv.at[other])
            wait_sent(self.src, self.sent.at[k - 1], self.recv.at[other])
        pltpu.make_async_copy(self.src, self.dst.at[self.x], self.own).wait()

    @staticmethod
    def scratch(ctx):
        return [
            pltpu.SemaphoreType.DMA((ctx,)),
            pltpu.SemaphoreType.DMA((ctx,)),
            pltpu.SemaphoreType.DMA,
        ]


class LineGather:
    def __init__(self, n, chunk, src, dst, recv, sent, own, hop=1):
        self.n, self.chunk, self.src, self.dst, self.hop = n, chunk, src, dst, hop
        self.width = src.shape[1]
        self.count = src.shape[0] // chunk
        self.recv, self.sent, self.own = recv, sent, own
        self.me = lax.axis_index("tp")

    def steps(self):
        return self.count + self.hop * (self.n - 1)

    def columns(self, tp):
        return pl.ds(pl.multiple_of(tp * self.width, self.width), self.width)

    def place(self, tp, at):
        rows = pl.ds(pl.multiple_of(at * self.chunk, self.chunk), self.chunk)
        return self.dst.at[rows, self.columns(tp)]

    def begin(self):
        pltpu.make_async_copy(self.src, self.dst.at[:, self.columns(self.me)], self.own).start()

    def begun(self):
        pltpu.make_async_copy(self.src, self.dst.at[:, self.columns(self.me)], self.own).wait()

    def step(self, s):
        n, me, count = self.n, self.me, self.count
        left, right = {"tp": me - 1}, {"tp": me + 1}

        @pl.when((s >= 0) & (s < count))
        def _():
            rows = pl.ds(pl.multiple_of(s * self.chunk, self.chunk), self.chunk)

            @pl.when(me > 0)
            def _():
                remote(self.src.at[rows], self.place(me, s), self.sent.at[0], self.recv.at[me, s], left).start()

            @pl.when(me < n - 1)
            def _():
                remote(self.src.at[rows], self.place(me, s), self.sent.at[1], self.recv.at[me, s], right).start()

        for away in range(1, n):
            at = s - away * self.hop
            for sign, onward in ((-1, right), (1, left)):
                tp = me + sign * away

                @pl.when((tp >= 0) & (tp < n) & (at >= 0) & (at < count))
                def _(tp=tp, onward=onward, sign=sign, at=at):
                    here = self.place(tp, at)
                    wait_came(here, self.sent.at[2], self.recv.at[tp, at])

                    @pl.when((me < n - 1) if sign < 0 else (me > 0))
                    def _():
                        remote(here, here, self.sent.at[2], self.recv.at[tp, at], onward).start()

    def drain(self):
        n, me = self.n, self.me

        @pl.when(me > 0)
        def _():
            wait_sent(self.src, self.sent.at[0], self.recv.at[0, 0])

        @pl.when(me < n - 1)
        def _():
            wait_sent(self.src, self.sent.at[1], self.recv.at[0, 0])

        @pl.when((me > 0) & (me < n - 1))
        def _():
            wait_sent(self.dst.at[:, pl.ds(0, (n - 1) * self.width)], self.sent.at[2], self.recv.at[0, 0])

    @staticmethod
    def scratch(n, count):
        return [
            pltpu.SemaphoreType.DMA((n, count)),
            pltpu.SemaphoreType.DMA((3,)),
            pltpu.SemaphoreType.DMA,
        ]


class LineSum:
    def __init__(self, n, chunk, hop, part, from_left, from_right, out, recv, sent, finish):
        self.n, self.chunk, self.hop = n, chunk, hop
        self.total_rows = part.shape[0]
        self.owners = (n // 2 - 1, n // 2)
        self.count = self.total_rows // 2 // chunk
        self.part, self.from_left, self.from_right, self.out = part, from_left, from_right, out
        self.recv, self.sent = recv, sent
        self.finish = finish
        self.me = lax.axis_index("tp")

    def steps(self):
        return self.count + self.hop * 2 * (self.n // 2)

    def turn(self, at):
        return lax.rem(at, self.recv.shape[2])

    def rows(self, slot, at):
        return pl.ds(pl.multiple_of((at * 2 + slot) * self.chunk, self.chunk), self.chunk)

    def step(self, s):
        n, me, hop = self.n, self.me, self.hop
        left, right = {"tp": me - 1}, {"tp": me + 1}
        reach = n // 2
        for slot, owner in enumerate(self.owners):
            for side in (0, 1):
                lag = me if side == 0 else n - 1 - me
                at = s - hop * lag
                here = (me < owner) if side == 0 else (me > owner)
                held = self.from_left if side == 0 else self.from_right
                to = right if side == 0 else left
                here = here & (at >= 0) & (at < self.count)

                @pl.when(here & (lag == 0))
                def _(at=at, held=held, to=to, side=side, slot=slot):
                    rows = self.rows(slot, at)
                    remote(self.part.at[rows], held.at[rows], self.sent.at[0],
                           self.recv.at[side, slot, self.turn(at)], to).start()

                if n > 2:

                    @pl.when(here & (lag > 0))
                    def _(at=at, held=held, to=to, side=side, slot=slot):
                        rows = self.rows(slot, at)
                        wait_came(held.at[rows], self.sent.at[0], self.recv.at[side, slot, self.turn(at)])
                        held[rows, :] = (held[rows, :].astype(F32) + self.part[rows, :].astype(F32)).astype(BF16)
                        remote(held.at[rows], held.at[rows], self.sent.at[0],
                               self.recv.at[side, slot, self.turn(at)], to).start()

            at = s - hop * reach

            @pl.when((me == owner) & (at >= 0) & (at < self.count))
            def _(at=at, slot=slot, owner=owner):
                rows = self.rows(slot, at)
                total = self.part[rows, :].astype(F32)
                if owner > 0:
                    wait_came(self.from_left.at[rows], self.sent.at[0], self.recv.at[0, slot, self.turn(at)])
                    total = total + self.from_left[rows, :].astype(F32)
                wait_came(self.from_right.at[rows], self.sent.at[0], self.recv.at[1, slot, self.turn(at)])
                total = total + self.from_right[rows, :].astype(F32)
                own = pl.ds(pl.multiple_of(at * self.chunk, self.chunk), self.chunk)
                self.out[rows, :] = self.finish(rows, own, total)
                if owner > 0:
                    remote(self.out.at[rows], self.out.at[rows], self.sent.at[1],
                           self.recv.at[2, slot, self.turn(at)], left).start()
                remote(self.out.at[rows], self.out.at[rows], self.sent.at[2],
                       self.recv.at[2, slot, self.turn(at)], right).start()

        for slot, owner in enumerate(self.owners):
            away = jnp.abs(me - owner)
            at = s - hop * (reach + away)

            @pl.when((me != owner) & (at >= 0) & (at < self.count))
            def _(at=at, slot=slot, owner=owner):
                rows = self.rows(slot, at)
                here = self.out.at[rows]
                wait_came(here, self.sent.at[3], self.recv.at[2, slot, self.turn(at)])

                @pl.when((me < owner) & (me > 0))
                def _():
                    remote(here, here, self.sent.at[3], self.recv.at[2, slot, self.turn(at)], left).start()

                @pl.when((me > owner) & (me < n - 1))
                def _():
                    remote(here, here, self.sent.at[3], self.recv.at[2, slot, self.turn(at)], right).start()

    def drain(self):
        n, me, half = self.n, self.me, self.total_rows // 2
        lo, hi = self.owners

        def wait(sem, size):
            wait_sent(self.part.at[pl.ds(0, size)], self.sent.at[sem], self.recv.at[0, 0, 0])

        middle = (me == lo) | (me == hi)

        @pl.when(middle)
        def _():
            wait(0, half)
            wait(2, half)

        @pl.when((me != lo) & (me != hi))
        def _():
            wait(0, 2 * half)

        if lo > 0:

            @pl.when(middle)
            def _():
                wait(1, half)
                wait(3, half)

            if n > 4:

                @pl.when((me != lo) & (me != hi) & (me > 0) & (me < n - 1))
                def _():
                    wait(3, 2 * half)
        else:

            @pl.when(me == hi)
            def _():
                wait(1, half)

    @staticmethod
    def scratch(n, rows, width, chunk):
        return [
            pltpu.VMEM((rows, width), BF16),
            pltpu.VMEM((rows, width), BF16),
            pltpu.SemaphoreType.DMA((3, 2, min(rows // 2 // chunk, 12))),
            pltpu.SemaphoreType.DMA((4,)),
        ]


class GradSum:
    def __init__(self, fsdp, ctx, parts, axes, outs, held, recv, sent):
        self.fsdp, self.ctx, self.parts, self.axes, self.outs = fsdp, ctx, parts, axes, outs
        self.ys = fsdp // 2
        self.held, self.recv, self.sent = held, recv, sent
        self.f = lax.axis_index("fsdp")
        self.x = lax.axis_index("ctx")
        self.y, self.c = self.f // 2, lax.rem(self.f, 2)

    @staticmethod
    def block_shape(shape, axis, fsdp):
        r, c = shape
        return (r // fsdp, c) if axis == 0 else (r, c // fsdp)

    @staticmethod
    def scratch(fsdp, ctx, shapes, first=True):
        held = []
        for shape in shapes:
            if first:
                held.append(pltpu.VMEM((fsdp // 2,) + shape, BF16))
            held += [
                pltpu.VMEM((max(fsdp // 2 - 1, 1),) + shape, BF16),
                pltpu.VMEM((ctx,) + shape, BF16),
            ]
        return held

    @staticmethod
    def semaphores(fsdp, ctx, count):
        return [pltpu.SemaphoreType.DMA((count, 3, max(fsdp // 2, ctx)))] * 2

    def part(self, a, f):
        shape = self.held[a][0].shape[1:]
        return block(self.parts[a], self.axes[a], f, shape[self.axes[a]])

    def each(self, a, body):
        rows = self.held[a][0].shape[1]
        size = 32 if rows % 32 == 0 else 16

        def step(i, carry):
            body(pl.ds(pl.multiple_of(i * size, size), size))
            return carry

        lax.fori_loop(0, rows // size, step, 0)

    def start(self):
        for a in range(len(self.parts)):
            for k in range(self.ys):
                remote(self.part(a, 2 * k + 1 - self.c), self.held[a][0].at[k], self.sent.at[a, 0, k],
                       self.recv.at[a, 0, k], {"fsdp": sibling(self.f)}).start()

    def pair(self):
        for a in range(len(self.parts)):
            first = self.held[a][0]
            for k in range(self.ys):
                wait_came(first.at[k], self.sent.at[a, 0, k], self.recv.at[a, 0, k])
                mine = self.part(a, 2 * k + self.c)

                def add(rows, first=first, k=k, mine=mine):
                    first[k, rows, :] = (first[k, rows, :].astype(F32) + mine[rows, :].astype(F32)).astype(BF16)

                self.each(a, add)

    def second(self):
        for a in range(len(self.held)):
            first, later = self.held[a][0], self.held[a][1]
            for k in range(1, self.ys):
                to = lax.rem(self.y + k, self.ys)
                remote(first.at[to], later.at[k - 1], self.sent.at[a, 1, k], self.recv.at[a, 1, k],
                       {"fsdp": 2 * to + self.c}).start()

    def third(self):
        for a in range(len(self.held)):
            first, later, last = self.held[a]
            for k in range(1, self.ys):
                wait_came(later.at[k - 1], self.sent.at[a, 1, k], self.recv.at[a, 1, k])

            def add(rows, first=first, later=later, last=last):
                total = first[self.y, rows, :].astype(F32)
                for k in range(1, self.ys):
                    total = total + later[k - 1, rows, :].astype(F32)
                last[self.x, rows, :] = total.astype(BF16)

            self.each(a, add)
            for k in range(1, self.ctx):
                remote(last.at[self.x], last.at[self.x], self.sent.at[a, 2, k], self.recv.at[a, 2, self.x],
                       {"ctx": lax.rem(self.x + k, self.ctx)}).start()

    def fourth(self, store):
        for a in range(len(self.held)):
            last = self.held[a][2]
            for k in range(1, self.ctx):
                other = lax.rem(self.x + k, self.ctx)
                wait_came(last.at[other], self.sent.at[a, 2, k], self.recv.at[a, 2, other])

            def add(rows, last=last, a=a):
                total = last[0, rows, :].astype(F32)
                for k in range(1, self.ctx):
                    total = total + last[k, rows, :].astype(F32)
                store(a, rows, total)

            self.each(a, add)

    def drain_pair(self):
        for a in range(len(self.parts)):
            for k in range(self.ys):
                wait_sent(self.held[a][0].at[k], self.sent.at[a, 0, k], self.recv.at[a, 0, k])

    def drain(self):
        for a in range(len(self.held)):
            first, later, last = self.held[a]
            for k in range(1, self.ys):
                wait_sent(later.at[k - 1], self.sent.at[a, 1, k], self.recv.at[a, 1, k])
            for k in range(1, self.ctx):
                wait_sent(last.at[self.x], self.sent.at[a, 2, k], self.recv.at[a, 2, 0])


def loop(first, last, body):
    def step(s, carry):
        body(s)
        return carry

    lax.fori_loop(first, last, step, 0)


def params(ident, mib):
    return pltpu.CompilerParams(collective_id=ident, has_side_effects=True, vmem_limit_bytes=min(mib << 20, 67043328))


def shape_of(shape, dtype):
    return jax.ShapeDtypeStruct(shape, dtype)


TILE = 256


def dot(left, right):
    return jnp.dot(left, right, preferred_element_type=F32)


def dot_t(left, right):
    return lax.dot_general(left, right, (((1,), (1,)), ((), ())), preferred_element_type=F32)


def dot_rows(left, right):
    return lax.dot_general(left, right, (((0,), (0,)), ((), ())), preferred_element_type=F32)


def head_only(value, head):
    lane = lax.broadcasted_iota(jnp.int32, value.shape, 1)
    return jnp.where((lane // HEAD_DIM) == head, value, jnp.zeros_like(value))


class RowGather:
    def __init__(self, n, src, dst, recv, sent, own):
        self.n, self.src, self.dst = n, src, dst
        self.recv, self.sent, self.own = recv, sent, own
        self.me = lax.axis_index("tp")

    def start(self):
        me = self.me
        pltpu.make_async_copy(self.src, self.dst.at[me], self.own).start()

        @pl.when(me > 0)
        def _():
            remote(self.src, self.dst.at[me], self.sent.at[0, 0], self.recv.at[me], {"tp": me - 1}).start()

        @pl.when(me < self.n - 1)
        def _():
            remote(self.src, self.dst.at[me], self.sent.at[1, 0], self.recv.at[me], {"tp": me + 1}).start()

    def each(self, body, which=None):
        me, n = self.me, self.n
        for away in which or range(1, n):
            for way, tp in ((1, me - away), (0, me + away)):

                @pl.when((tp >= 0) & (tp < n))
                def _(tp=tp, way=way, away=away):
                    onward = (me < n - 1) if way == 1 else (me > 0)
                    body(away, way, tp, onward, {"tp": me + 1} if way == 1 else {"tp": me - 1})

    def relay(self, which=None):
        def body(away, way, tp, onward, to):
            here = self.dst.at[tp]
            wait_came(here, self.sent.at[way, away], self.recv.at[tp])

            @pl.when(onward)
            def _():
                remote(here, here, self.sent.at[way, away], self.recv.at[tp], to).start()

        self.each(body, which)

    def finish(self):
        me = self.me
        pltpu.make_async_copy(self.src, self.dst.at[me], self.own).wait()

        @pl.when(me > 0)
        def _():
            wait_sent(self.src, self.sent.at[0, 0], self.recv.at[0])

        @pl.when(me < self.n - 1)
        def _():
            wait_sent(self.src, self.sent.at[1, 0], self.recv.at[0])

        def body(away, way, tp, onward, to):
            @pl.when(onward)
            def _():
                wait_sent(self.src, self.sent.at[way, away], self.recv.at[0])

        self.each(body)

    @staticmethod
    def scratch(n):
        return [
            pltpu.SemaphoreType.DMA((n,)),
            pltpu.SemaphoreType.DMA((2, n)),
            pltpu.SemaphoreType.DMA,
        ]


class AxisSum:
    def __init__(self, axis, n, slots, recv, sent):
        self.axis, self.n, self.slots, self.recv, self.sent = axis, n, slots, recv, sent
        self.at = lax.axis_index(axis)

    def start(self, value):
        self.slots[self.at] = value
        for k in range(1, self.n):
            remote(self.slots.at[self.at], self.slots.at[self.at], self.sent.at[k], self.recv.at[self.at],
                   {self.axis: lax.rem(self.at + k, self.n)}).start()

    def finish(self):
        for k in range(1, self.n):
            other = lax.rem(self.at + k, self.n)
            wait_came(self.slots.at[other], self.sent.at[k], self.recv.at[other])
            wait_sent(self.slots.at[self.at], self.sent.at[k], self.recv.at[other])
        total = self.slots[0]
        for k in range(1, self.n):
            total = total + self.slots[k]
        return total

    @staticmethod
    def scratch(n, shape):
        return [
            pltpu.VMEM((n,) + shape, F32),
            pltpu.SemaphoreType.DMA((n,)),
            pltpu.SemaphoreType.DMA((n,)),
        ]


def window(ctx, tok_dev):
    return min(ctx, (tok_dev * ctx // 2 + tok_dev - 1) // tok_dev + 1)


def key_span(ctx, tok_dev):
    return min(ctx * tok_dev // 2 // TILE, (window(ctx, tok_dev) - 1) * (tok_dev // TILE))


R_ONE, SEGMENT, VALID = 0, 1, 2


def front(tokens, gain1, gain2, w_latent, shards, w_out, wide_shards, segments, fsdp, ctx, n):
    rows, width = tokens.shape
    seq_dev, tok_dev = segments.shape
    latent, q_width = LATENT, shards[0].shape[1]
    wide, chunk = 128, 256
    pieces = rows // chunk
    win = window(ctx, tok_dev)
    full = [shape_of((s.shape[0] * fsdp,) + s.shape[1:], s.dtype) for s in shards]
    wider = [shape_of((s.shape[0], s.shape[1] * fsdp), s.dtype) for s in wide_shards]
    per_group = HEADS // GROUPS * HEAD_DIM
    per_seq = tok_dev // chunk

    def kernel(*refs):
        (tok_in, ga, gb, wlat, wq, wk, wv, wo, wg, wu, seg), refs = refs[:11], refs[11:]
        (xn_out, cols, gain_all, w_lat, w_qry, w_kproj, w_vproj, gate_all, up_all), refs = refs[:9], refs[9:]
        (wo_all, seg_all, lat_all, query, keys, values), refs = refs[:6], refs[6:]
        (gbuf, sbuf, tok, xn, tsem), refs = refs[:5], refs[5:]
        bring = Bring([(tok_in, tok), (xn, xn_out)], tsem)
        bring.start([0])
        x, me = lax.axis_index("ctx"), lax.axis_index("tp")
        gbuf[...] = jnp.zeros_like(gbuf)
        gbuf[0:1, :] = ga[...].astype(F32).reshape(1, -1)
        gbuf[1:2, :] = gb[...].astype(F32).reshape(1, -1)
        sbuf[...] = jnp.zeros_like(sbuf)
        sbuf[0:seq_dev, :] = seg[...]
        meet(n, fsdp, ctx)
        group = me * q_width // per_group
        src_lat = wlat.at[:, pl.ds(pl.multiple_of(group * latent, latent), latent)]
        pairs = [(gbuf, gain_all), (src_lat, w_lat), (wq, w_qry), (wk, w_kproj), (wv, w_vproj),
                 (wg, gate_all), (wu, up_all)]
        spread = Spread(fsdp, pairs, [1, 0, 0, 0, 0, 1, 1], *refs[:3])
        share = CtxShare(ctx, sbuf, seg_all, *refs[3:6])
        line = RowGather(n, wo, wo_all, *refs[6:9])
        lat_recv, lat_sent = refs[9:11]
        spread.start()
        share.start()
        line.start()
        own = win - 1
        cols[...] = jnp.zeros_like(cols)
        bring.wait([0])

        def scale(i):
            at = pl.ds(pl.multiple_of(i * wide, wide), wide)
            value = tok[at, :].astype(F32)
            cols[at, R_ONE : R_ONE + 1] = lax.rsqrt(jnp.mean(value * value, axis=-1, keepdims=True) + eps)

        loop(0, rows // wide, scale)
        spread.relay([0, 1])
        spread.finish([0, 1])

        def place(shard, i):
            seq = i // per_seq
            return pl.ds(pl.multiple_of(seq * win * tok_dev + shard * tok_dev + lax.rem(i, per_seq) * chunk, chunk), chunk)

        def send(k, i):
            return remote(lat_all.at[place(own, i)], lat_all.at[place(own - k, i)], lat_sent.at[k, i],
                          lat_recv.at[own - k, i], {"ctx": x + k})

        def first(i):
            at = pl.ds(pl.multiple_of(i * chunk, chunk), chunk)
            unit = (tok[at, :].astype(F32) * cols[at, R_ONE : R_ONE + 1] * gain_all[0:1, :]).astype(BF16)
            xn[at, :] = unit
            lat_all[place(own, i), :] = dot(unit, w_lat[...]).astype(BF16)
            for k in range(1, win):

                @pl.when(x + k < ctx)
                def _(k=k):
                    send(k, i).start()

        loop(0, pieces, first)
        bring.start([1])
        line.relay([1])
        spread.relay([2, 3, 4])
        spread.finish([2, 3, 4])

        def project(shard, i):
            to = place(shard, i)
            value = lat_all[to, :]
            keys[to, :] = dot(value, w_kproj[...]).astype(BF16)
            values[to, :] = dot(value, w_vproj[...]).astype(BF16)

        def ask(i):
            at = pl.ds(pl.multiple_of(i * chunk, chunk), chunk)
            query[at, :] = dot(xn[at, :], w_qry[...]).astype(BF16)
            project(own, i)

        loop(0, pieces, ask)
        share.finish()
        for q in range(seq_dev):
            at = slice(q * tok_dev, (q + 1) * tok_dev)
            ids = jnp.broadcast_to(sbuf[q : q + 1, :].astype(F32), (128, tok_dev)).T
            cols[at, SEGMENT : SEGMENT + 1] = ids[:, 0:1]
            last = seg_all[ctx - 1, q : q + 1, tok_dev - 1 : tok_dev].astype(F32)
            cols[at, VALID : VALID + 1] = jnp.where(ids[:, 0:1] != last, 1.0, 0.0)
        line.relay(range(2, n))
        for k in range(1, win):

            def theirs(i, k=k):
                @pl.when(x - k >= 0)
                def _():
                    wait_came(lat_all.at[place(own - k, i)], lat_sent.at[k, i], lat_recv.at[own - k, i])

                @pl.when(x - k < 0)
                def _():
                    lat_all[place(own - k, i), :] = jnp.zeros((chunk, latent), BF16)

                project(own - k, i)

            loop(0, pieces, theirs)

            def gone(i, k=k):
                @pl.when(x + k < ctx)
                def _():
                    send(k, i).wait_send()

            loop(0, pieces, gone)
        spread.relay([5, 6])
        spread.finish([5, 6])
        line.finish()
        bring.wait([1])

    return pl.pallas_call(
        kernel,
        out_shape=(
            shape_of((rows, width), BF16),
            shape_of((rows, 128), F32),
            shape_of((8, width), F32),
            shape_of((width, latent), BF16),
            *full,
            *wider,
            shape_of((n,) + w_out.shape, w_out.dtype),
            shape_of((ctx, 8, tok_dev), segments.dtype),
            shape_of((win * rows, latent), BF16),
            shape_of((rows, q_width), BF16),
            shape_of((win * rows, q_width), BF16),
            shape_of((win * rows, q_width), BF16),
        ),
        in_specs=[ANY] + [VMEM] * 10,
        out_specs=(ANY,) + (VMEM,) * 6 + (ANY,) * 3 + (VMEM,) * 5,
        scratch_shapes=[
            pltpu.VMEM((8, gain1.shape[0]), F32),
            pltpu.VMEM((8, tok_dev), segments.dtype),
            pltpu.VMEM((rows, width), BF16),
            pltpu.VMEM((rows, width), BF16),
            pltpu.SemaphoreType.DMA((2,)),
        ]
        + Spread.scratch(fsdp, 7)
        + CtxShare.scratch(ctx)
        + RowGather.scratch(n)
        + [pltpu.SemaphoreType.DMA((win, pieces))] * 2,
        compiler_params=params(1, 56),
    )(tokens, gain1, gain2, w_latent, *shards, w_out, *wide_shards, segments)


def counted_keys(cols, segk, at, seq, q_first, first, count, tok_dev, win):
    per = tok_dev // TILE
    oldest = lax.axis_index("ctx") - (win - 1)
    mine = cols[at, SEGMENT : SEGMENT + 1]
    shape = (mine.shape[0], TILE)
    pieces = []
    for j in range(count):
        t = first + j
        shard = oldest + t // per
        inner = pl.ds(pl.multiple_of(lax.rem(t, per) * TILE, TILE), TILE)
        ids = segk[jnp.maximum(shard, 0), pl.ds(seq, 1), inner].astype(F32)
        q_at = q_first + lax.broadcasted_iota(jnp.int32, shape, 0)
        k_at = t * TILE + lax.broadcasted_iota(jnp.int32, shape, 1)
        pieces.append((k_at <= q_at) & (ids == mine) & (shard >= 0))
    return pieces


def middle(query, keys, values, seg_all, cols, shards, gate_all, up_all, gains, tokens, out_grad,
           fsdp, ctx, n, seq_dev, late):
    rows, width = tokens.shape
    q_width = query.shape[1]
    heads = q_width // HEAD_DIM
    inner = gate_all.shape[0]
    tok_dev = rows // seq_dev
    per = tok_dev // TILE
    win, span = window(ctx, tok_dev), key_span(ctx, tok_dev)
    tiles = span + 1
    part = TILE if tiles <= 3 else 64
    chunk, hop = 32, 2
    size, piece = 256, 64
    per_block = size // piece
    half = rows // 2
    cols_at = width // 4
    block_shape = (inner, width // fsdp)
    count = 3

    def kernel(*refs):
        (q_in, k_in, v_in, segk, cols, wo_in, wd_in, wg_in, wu_in, gain, tok_in, cot_in), refs = refs[:12], refs[12:]
        (o_branch, o_feed, o_dmid, o_mid, o_wo, o_gain, o_bsq, o_mark, o_att, o_lse), refs = refs[:10], refs[10:]
        outs, refs = refs[:3], refs[3:]
        one, gsems, parts, refs = refs[:4], refs[4:6], refs[6:9], refs[9:]
        (query, keys, values, att, att_all, wo, wd, wg, wu, tok, cot), refs = refs[:11], refs[11:]
        (mid, r2, xn, hid, dg, du, p_two, p_feed, bsem), refs = refs[:9], refs[9:]
        bring = Bring([(q_in, query), (k_in, keys), (v_in, values), (tok_in, tok), (wg_in, wg), (wu_in, wu),
                       (cot_in, cot), (att, o_att), (p_feed, o_feed)], bsem)
        bring.start(range(7))
        meet(n, fsdp, ctx)
        line = LineGather(n, piece, att, att_all, *refs[:3])
        spread = Spread(fsdp, [(wo_in, wo), (wd_in, wd)], [1, 1], *refs[3:6])
        keep = refs[6:]
        spread.start()
        o_gain[...] = jnp.zeros_like(o_gain)
        o_bsq[...] = jnp.zeros_like(o_bsq)
        o_mark[...] = jnp.zeros_like(o_mark)
        g2 = gain.at[1:2]

        def back(at, own, total):
            middle_rows = mid[at, :]
            o_mid[own, :] = middle_rows
            unit = middle_rows * r2[at, :]
            o_gain[...] += jnp.sum((total * unit).reshape(chunk // 8, 8, width), axis=0)
            scaled = total * g2[...]
            mean = jnp.mean(scaled * unit, axis=-1, keepdims=True)
            d_mid = cot[at, :].astype(F32) + r2[at, :] * (scaled - unit * mean)
            o_dmid[own, :] = d_mid
            first_unit = tok[at, :].astype(F32) * cols[at, R_ONE : R_ONE + 1]
            o_mark[at, 0:1] = jnp.sum(first_unit * d_mid, axis=-1, keepdims=True)
            return d_mid.astype(BF16)

        first = LineSum(n, chunk, hop, p_two, one[0], one[1], o_branch, one[2], one[3], back)
        if late:
            held = [[out, None, None] for out in outs]
        else:
            held = [keep[3 * a : 3 * a + 3] for a in range(count)]
        grad = GradSum(fsdp, ctx, parts, [1] * count, outs, held, *gsems)
        bring.wait([0, 1, 2])

        def query_rows(i, j):
            seq = i // per
            q_tile = (win - 1) * per + lax.rem(i, per)
            at = pl.ds(pl.multiple_of(i * TILE + j * part, part), part)
            near = pl.ds(pl.multiple_of((seq * win * per + q_tile - span) * TILE, TILE), tiles * TILE)
            counted = jnp.concatenate(
                [
                    c.astype(F32)
                    for c in counted_keys(
                        cols, segk, at, seq, q_tile * TILE + j * part, q_tile - span, tiles, tok_dev, win
                    )
                ],
                axis=1,
            )
            accum = jnp.zeros((part, q_width), F32)
            lane = lax.broadcasted_iota(jnp.int32, (part, 128), 1)
            kept = jnp.zeros((part, 128), F32)
            for h in range(heads):
                score = jnp.where(counted > 0.0, dot_t(head_only(query[at, :], h), keys[near, :]) * 0.125, -1e30)
                top = jnp.max(score, axis=-1, keepdims=True)
                weight = jnp.exp(score - top)
                total = jnp.sum(weight, axis=-1, keepdims=True)
                prob = (weight * (1.0 / total)).astype(BF16)
                accum = accum + jnp.dot(prob, head_only(values[near, :], h), preferred_element_type=F32)
                kept = jnp.where(lane == h, top + jnp.log(total), kept)
                if part == TILE:
                    line.step((i - 1) * per_block + h * per_block // heads)
            o_lse[at, :] = kept
            att[at, :] = accum.astype(BF16)

        def query_tile(i):
            if part == TILE:
                query_rows(i, 0)
                return
            loop(0, TILE // part, lambda j: query_rows(i, j))
            for h in range(per_block):
                line.step((i - 1) * per_block + h)

        loop(0, rows // TILE, query_tile)
        bring.start([7])
        line.begin()
        s1 = (rows // TILE - 1) * per_block
        spread.relay()
        spread.finish()
        tp = lax.axis_index("tp")
        o_wo[...] = wo[pl.ds(pl.multiple_of(tp * q_width, q_width), q_width), :]
        line.begun()
        bring.wait([3, 4, 5, 6])

        def block_of_rows(b):
            at = pl.ds(pl.multiple_of(b * size, size), size)
            seq = b * size // tok_dev

            def steps(j):
                line.step(s1 + b * per_block + j)
                first.step((b - 1) * per_block + j)

            branch = dot(att_all[at, :], wo[...])
            middle_rows = tok[at, :].astype(F32) + branch
            mid[at, :] = middle_rows
            o_bsq[pl.ds(pl.multiple_of(seq * 8, 8), 8), :] += jnp.sum(
                (branch * branch * cols[at, VALID : VALID + 1]).reshape(size // 8, 8, width), axis=0
            )
            scale = lax.rsqrt(jnp.mean(middle_rows * middle_rows, axis=-1, keepdims=True) + eps)
            r2[at, :] = scale
            unit = (middle_rows * scale * g2[...]).astype(BF16)
            xn[at, :] = unit
            steps(0)
            gate = dot_t(unit, wg[...])
            upper = dot_t(unit, wu[...])
            sigma = jax.nn.sigmoid(gate)
            swish = gate * sigma
            hidden = (swish * upper).astype(BF16)
            hid[at, :] = hidden
            slope = upper * sigma * (1.0 + gate * (1.0 - sigma))
            steps(1)
            p_feed[at, :] = dot(hidden, wd[...]).astype(BF16)
            d_hidden = dot_t(cot[at, :], wd[...])
            d_gate = (d_hidden * slope).astype(BF16)
            d_upper = (d_hidden * swish).astype(BF16)
            dg[at, :] = d_gate
            du[at, :] = d_upper
            steps(2)
            p_two[at, :] = (dot(d_gate, wg[...]) + dot(d_upper, wu[...])).astype(BF16)
            steps(3)

        loop(0, rows // size, block_of_rows)
        bring.start([8])
        s0 = (rows // size - 1) * per_block

        def product(i):
            at = pl.ds(pl.multiple_of(i * cols_at, cols_at), cols_at)
            left = xn[:, at]
            parts[0][:, at] = dot_rows(dg[...], left).astype(BF16)
            parts[1][:, at] = dot_rows(du[...], left).astype(BF16)
            parts[2][:, at] = dot_rows(hid[...], cot[:, at]).astype(BF16)

        def busy(s):
            first.step(s)
            product(s - s0)

        loop(s0, s0 + 4, busy)
        grad.start()
        last = first.steps()
        loop(s0 + 4, s0 + 6, first.step)
        grad.pair()
        if not late:
            grad.second()
        loop(s0 + 6, last, first.step)
        if not late:
            grad.third()

            def store(a, at, total):
                outs[a][at, :] = total

            grad.fourth(store)
            grad.drain()
        line.drain()
        first.drain()
        grad.drain_pair()
        bring.wait([7, 8])

    ys = fsdp // 2
    out = pl.pallas_call(
        kernel,
        out_shape=(
            shape_of((rows, width), BF16),
            shape_of((rows, width), BF16),
            shape_of((half, width), F32),
            shape_of((half, width), F32),
            shape_of((q_width, width), BF16),
            shape_of((8, width), F32),
            shape_of((8 * seq_dev, width), F32),
            shape_of((rows, 128), F32),
            shape_of((rows, q_width), BF16),
            shape_of((rows, 128), F32),
        )
        + ((shape_of((ys,) + block_shape, BF16) if late else shape_of(block_shape, F32)),) * count,
        in_specs=[ANY] * 3 + [VMEM] * 4 + [ANY] * 2 + [VMEM] + [ANY] * 2,
        out_specs=(VMEM, ANY) + (VMEM,) * 6 + (ANY, VMEM) + (VMEM,) * count,
        scratch_shapes=LineSum.scratch(n, rows, width, chunk)
        + GradSum.semaphores(fsdp, ctx, count)
        + [pltpu.VMEM((inner, width), BF16)] * count
        + [
            pltpu.VMEM((rows, q_width), BF16),
            pltpu.VMEM((win * rows, q_width), BF16),
            pltpu.VMEM((win * rows, q_width), BF16),
            pltpu.VMEM((rows, q_width), BF16),
            pltpu.VMEM((rows, n * q_width), BF16),
            pltpu.VMEM((n * q_width, width), BF16),
            pltpu.VMEM((inner, width), BF16),
            pltpu.VMEM((inner, width), BF16),
            pltpu.VMEM((inner, width), BF16),
            pltpu.VMEM((rows, width), BF16),
            pltpu.VMEM((rows, width), BF16),
            pltpu.VMEM((rows, width), F32),
            pltpu.VMEM((rows, 1), F32),
            pltpu.VMEM((rows, width), BF16),
            pltpu.VMEM((rows, inner), BF16),
            pltpu.VMEM((rows, inner), BF16),
            pltpu.VMEM((rows, inner), BF16),
            pltpu.VMEM((rows, width), BF16),
            pltpu.VMEM((rows, width), BF16),
            pltpu.SemaphoreType.DMA((9,)),
        ]
        + LineGather.scratch(n, rows // piece)
        + Spread.scratch(fsdp, 2)
        + ([] if late else GradSum.scratch(fsdp, ctx, [block_shape] * count)),
        compiler_params=params(2, 64),
    )(query, keys, values, seg_all, cols, *shards, gate_all, up_all, gains, tokens, out_grad)
    return out[:10], out[10:]


def back(query, keys, values, seg_all, cols, lse, attended, d_branch, wo_rows, weights, lat_all, xn_one, gains,
         tokens, d_middle, mid_own, part_feed, marks, gain_part, branch_sq, firsts, fsdp, ctx, n, seq_dev):
    rows, width = tokens.shape
    w_qry, w_lat, w_kproj, w_vproj = weights
    q_width, latent = query.shape[1], w_lat.shape[1]
    heads, tok_dev = q_width // HEAD_DIM, rows // seq_dev
    per = tok_dev // TILE
    win, span = window(ctx, tok_dev), key_span(ctx, tok_dev)
    tiles = span + 1
    group = tiles if tiles <= 3 else 1
    chunk, hop, wide, side = 32, 2, 256, 128
    half = rows // 2
    axes = (0, 0, 0, 1, 0)
    whole = ((width, q_width), (latent, q_width), (latent, q_width), (q_width, width), (width, latent))
    blocks = [GradSum.block_shape(w, a, fsdp) for w, a in zip(whole, axes)]
    lat = blocks[-1]
    ffn = [f.shape[1:] for f in firsts]
    seq_pieces = tok_dev // wide
    many = max(width, rows)

    def kernel(*refs):
        (q_ref, k_ref, v_ref, segk, cols, lse_ref, att, dbr, wo), refs = refs[:9], refs[9:]
        (wq, wl, wk, wv, la_in, xn_in, gain, tok_in, dmid_in, mid_in, feed_in), refs = refs[:11], refs[11:]
        (marks, gain_two, bsq), fsts, refs = refs[:3], refs[3 : 3 + len(ffn)], refs[3 + len(ffn) :]
        (o_tok, o_mixed, o_small), outs, refs = refs[:3], refs[3:8], refs[8:]
        fouts, refs = refs[: len(ffn)], refs[len(ffn) :]
        one, two, keep, gsems, parts, refs = refs[:4], refs[4:8], refs[8:23], refs[23:25], refs[25:30], refs[30:]
        (p_one, dlat, came, c_recv, c_sent, gacc, sm, sacc), refs = refs[:8], refs[8:]
        (dk, dv, dq, dqb, grad_seq, lat_parts), refs = refs[:6], refs[6:]
        (la, xn, tok, dmid, mid, p_feed, bsem), refs = refs[:7], refs[7:]
        (lat_own, lat_every), lsems, sums, refs = refs[:2], refs[2:5], refs[5:14], refs[14:]
        bring = Bring([(feed_in, p_feed), (mid_in, mid), (la_in, la), (xn_in, xn), (tok_in, tok), (dmid_in, dmid)], bsem)
        bring.start()
        meet(n, fsdp, ctx, everyone=True)
        x = lax.axis_index("ctx")
        own_shard = win - 1
        grad_ffn = None
        if ffn:
            fkeep, fsems = refs[: 2 * len(ffn)], refs[2 * len(ffn) :]
            grad_ffn = GradSum(fsdp, ctx, [], [], fouts,
                               [[fsts[a], fkeep[2 * a], fkeep[2 * a + 1]] for a in range(len(ffn))], *fsems)
            grad_ffn.second()
        gacc[...] = jnp.zeros_like(gacc)
        sacc[...] = jnp.zeros_like(sacc)
        sm[...] = jnp.zeros_like(sm)
        g1 = gain.at[0:1]

        def forward(at, own, total):
            mixed = mid[own, :] + total
            seq = at.start // tok_dev
            counted = cols[at, VALID : VALID + 1]
            sacc[seq] += jnp.sum((mixed * mixed * counted).reshape(chunk // 8, 8, width), axis=0)
            sacc[seq_dev + seq] += jnp.sum((total * total * counted).reshape(chunk // 8, 8, width), axis=0)
            return mixed.astype(BF16)

        def backward(at, own, total):
            r1 = cols[at, R_ONE : R_ONE + 1]
            unit = tok[at, :].astype(F32) * r1
            scaled = total * g1[...]
            mean = jnp.mean(scaled * unit, axis=-1, keepdims=True)
            return (dmid[own, :] + r1 * (scaled - unit * mean)).astype(BF16)

        feed = LineSum(n, chunk, hop, p_feed, two[0], two[1], o_mixed, two[2], two[3], forward)
        first = LineSum(n, chunk, hop, p_one, one[0], one[1], o_tok, one[2], one[3], backward)
        grad = GradSum(fsdp, ctx, parts, axes, outs, [keep[3 * a : 3 * a + 3] for a in range(5)], *gsems)
        line = RowGather(n, lat_own, lat_every, *lsems)
        over_tp = AxisSum("tp", n, *sums[0:3])
        over_ctx = AxisSum("ctx", ctx, *sums[3:6])
        over_fsdp = AxisSum("fsdp", fsdp, *sums[6:9])

        def clear(i):
            at = pl.ds(pl.multiple_of(i * TILE, TILE), TILE)
            dk[at, :] = jnp.zeros((TILE, q_width), F32)
            dv[at, :] = jnp.zeros((TILE, q_width), F32)

        loop(0, win * rows // TILE, clear)
        bring.wait([0, 1])

        def query_tile(i, step):
            seq = i // per
            q_tile = own_shard * per + lax.rem(i, per)
            at = pl.ds(pl.multiple_of(i * TILE, TILE), TILE)
            grad_seq[...] = dot_t(dbr[at, :], wo[...]).astype(BF16)
            product = grad_seq[...].astype(F32) * att[at, :].astype(F32)
            delta = [jnp.sum(head_only(product, h), axis=-1, keepdims=True) for h in range(heads)]
            dq[...] = jnp.zeros_like(dq)

            def key_tiles(kk):
                t = q_tile - span + kk * group
                near = pl.ds(pl.multiple_of((seq * win * per + t) * TILE, TILE), group * TILE)
                counted = jnp.concatenate(
                    [c.astype(F32) for c in counted_keys(cols, segk, at, seq, q_tile * TILE, t, group, tok_dev, win)], axis=1
                )
                kept = lse_ref[at, :]
                d_query = jnp.zeros((TILE, q_width), F32)
                d_key = jnp.zeros((group * TILE, q_width), F32)
                d_value = jnp.zeros((group * TILE, q_width), F32)
                for h in range(heads):
                    mine, ours = head_only(q_ref[at, :], h), head_only(grad_seq[...], h)
                    score = jnp.where(counted > 0.0, dot_t(mine, k_ref[near, :]) * 0.125, -1e30)
                    prob = jnp.exp(score - kept[:, h : h + 1]) * counted
                    d_score = (prob * (dot_t(ours, v_ref[near, :]) - delta[h])).astype(BF16)
                    d_query = d_query + jnp.dot(d_score, head_only(k_ref[near, :], h), preferred_element_type=F32)
                    d_key = d_key + dot_rows(d_score, mine)
                    d_value = d_value + dot_rows(prob.astype(BF16), ours)
                    step(kk * heads + h)
                dq[...] += d_query
                dk[near, :] += d_key * 0.125
                dv[near, :] += d_value

            loop(0, tiles // group, key_tiles)
            dqb[at, :] = (dq[...] * 0.125).astype(BF16)

        def latent_rows(shard, seq, i):
            return pl.ds(pl.multiple_of((seq * win + shard) * tok_dev + i * wide, wide), wide)

        def send(k, seq, i):
            at = pl.ds(pl.multiple_of(seq * tok_dev + i * wide, wide), wide)
            return remote(lat_parts.at[latent_rows(own_shard - k, seq, i)], came.at[k - 1, at],
                          c_sent.at[k - 1, seq, i], c_recv.at[k - 1, seq, i], {"ctx": x - k})

        def latents(seq):
            for k in range(win - 1, -1, -1):
                for i in range(seq_pieces):
                    at = latent_rows(own_shard - k, seq, i)
                    lat_parts[at, :] = (
                        dot_t(dk[at, :].astype(BF16), wk[...]) + dot_t(dv[at, :].astype(BF16), wv[...])
                    ).astype(BF16)
                    if k > 0:

                        @pl.when(x - k >= 0)
                        def _(k=k, i=i):
                            send(k, seq, i).start()

        def whole_latent(j):
            seq, i = j // seq_pieces, lax.rem(j, seq_pieces)
            at = pl.ds(pl.multiple_of(j * wide, wide), wide)
            dlat[at, :] = lat_parts[latent_rows(own_shard, seq, i), :]
            for k in range(1, win):

                @pl.when(x + k < ctx)
                def _(k=k):
                    wait_came(came.at[k - 1, at], c_sent.at[k - 1, seq, i], c_recv.at[k - 1, seq, i])
                    dlat[at, :] = (dlat[at, :].astype(F32) + came[k - 1, at, :].astype(F32)).astype(BF16)

            p_one[at, :] = (dot_t(dqb[at, :], wq[...]) + dot_t(dlat[at, :], wl[...])).astype(BF16)

        tile_steps = (tiles // group) * heads
        every = max(tile_steps // 4, 1)

        def sequence(seq):
            def tile(i):
                def step(j):
                    @pl.when(lax.rem(j, every) == 0)
                    def _():
                        feed.step(i * (tile_steps // every) + j // every)

                query_tile(i, step)

            loop(seq * per, seq * per + per, tile)
            latents(seq)

        loop(0, seq_dev, sequence)
        fed = seq_dev * per * (tile_steps // every)

        bring.wait([2, 3, 4, 5])

        def product(i):
            at = pl.ds(pl.multiple_of(i * wide, wide), wide)
            parts[0][at, :] = dot_rows(xn[:, at], dqb[...]).astype(BF16)
            parts[3][:, at] = dot_rows(att[...], dbr[:, at]).astype(BF16)

        def steps(s):
            first.step(s)
            feed.step(fed + s)

        early = (seq_dev - 1) * seq_pieces
        loop(0, early, whole_latent)

        def mixed_work(i):
            product(i)
            steps(i)

        loop(0, width // wide, mixed_work)
        s0 = width // wide
        if grad_ffn is not None:
            grad_ffn.third()
        parts[1][...] = dot_rows(la[...], dk[...].astype(BF16)).astype(BF16)
        parts[2][...] = dot_rows(la[...], dv[...].astype(BF16)).astype(BF16)
        loop(early, rows // wide, whole_latent)

        def product_lat(s):
            at = pl.ds(pl.multiple_of((s - s0) * wide, wide), wide)
            parts[4][at, :] = dot_rows(xn[:, at], dlat[...]).astype(BF16)
            steps(s)

        begun = s0 + width // wide
        loop(s0, begun, product_lat)
        grad.start()

        def gains_of(s):
            steps(s)
            at = pl.ds(pl.multiple_of((s - begun) * side, side), side)
            value = p_one[at, :].astype(F32) * (tok[at, :].astype(F32) * cols[at, R_ONE : R_ONE + 1])
            gacc[...] += jnp.sum(value.reshape(side // 8, 8, width), axis=0)
            along = lax.dot_general(jnp.ones((8, width), F32), value * g1[...], (((1,), (1,)), ((), ())),
                                    precision=lax.Precision.HIGHEST, preferred_element_type=F32)
            sm[3:4, at] = along[0:1, :]
            sm[4:5, at] = marks[at, :].T[0:1, :]
            sm[5:6, at] = cols[at, :].T[R_ONE : R_ONE + 1, :]

        mark = begun + rows // side
        loop(begun, begun + 1, gains_of)
        grad.pair()
        grad.second()
        loop(begun + 1, begun + 4, gains_of)
        grad.third()
        loop(begun + 4, mark, gains_of)
        last = first.steps()
        for s in range(fed + mark, feed.steps()):
            feed.step(s)
        lane = lax.broadcasted_iota(jnp.int32, (1, many), 1)
        once = jnp.where(lax.axis_index("tp") == 0, 1.0, 0.0)
        row = jnp.zeros((1, many), F32)

        def whole_sum(value):
            return jnp.sum(jnp.sum(value, axis=0, keepdims=True), axis=1, keepdims=True)

        for q in range(seq_dev):
            values = [
                whole_sum(sacc[q]),
                whole_sum(sacc[seq_dev + q]),
                whole_sum(bsq[8 * q : 8 * q + 8, :]) * once,
                jnp.sum(cols[q * tok_dev : (q + 1) * tok_dev, VALID : VALID + 1], axis=0, keepdims=True) * once,
            ]
            for j, value in enumerate(values):
                row = row + jnp.where(lane == 4 * q + j, value, 0.0)
        sm[2:3, :] = row
        sm[0:1, 0:width] = jnp.sum(gacc[...], axis=0, keepdims=True)
        sm[1:2, 0:width] = jnp.sum(gain_two[...], axis=0, keepdims=True)
        r_row = sm[5:6, :]
        over_tp.start(sm[...])

        def store(a, at, total):
            if a < 4:
                outs[a][at, :] = total
            else:
                lat_own[at, :] = total.astype(BF16)

        def store_ffn(a, at, total):
            fouts[a][at, :] = total

        grad.fourth(store)
        line.start()
        loop(mark, mark + 2, steps)
        line.relay([1])
        along_tp = over_tp.finish()
        over_ctx.start(along_tp)
        loop(mark + 2, mark + 4, steps)
        if n > 2:
            line.relay([2])
        along_ctx = over_ctx.finish()
        over_fsdp.start(along_ctx)
        if grad_ffn is not None:
            grad_ffn.fourth(store_ffn)
        loop(mark + 4, last, steps)
        if n > 3:
            line.relay(range(3, n))
        everywhere = over_fsdp.finish()
        row = lax.broadcasted_iota(jnp.int32, everywhere.shape, 0)
        o_small[...] = jnp.where(row < 2, everywhere, along_ctx)
        o_small[3:4, :] = (along_tp[4:5] + eps * r_row * r_row * r_row * along_tp[3:4]) * (1.0 / width**0.5)
        line.finish()

        def gather(i):
            at = pl.ds(pl.multiple_of(i * 16, 16), 16)
            for g in range(GROUPS):
                total = jnp.zeros((16, lat[1]), F32)
                for t in range(n):
                    if t * GROUPS // n == g:
                        total = total + lat_every[t, at, :].astype(F32)
                outs[4][at, g * lat[1] : (g + 1) * lat[1]] = total

        loop(0, lat[0] // 16, gather)
        for k in range(1, win):

            @pl.when(x - k >= 0)
            def _(k=k):
                for seq in range(seq_dev):
                    for i in range(seq_pieces):
                        send(k, seq, i).wait_send()

        feed.drain()
        first.drain()
        grad.drain_pair()
        grad.drain()
        if grad_ffn is not None:
            grad_ffn.drain()

    out = pl.pallas_call(
        kernel,
        out_shape=(
            shape_of((rows, width), BF16),
            shape_of((rows, width), BF16),
            shape_of((8, many), F32),
        )
        + tuple(shape_of(b, F32) for b in blocks[:-1])
        + (shape_of((lat[0], GROUPS * lat[1]), F32),)
        + tuple(shape_of(f, F32) for f in ffn),
        in_specs=[VMEM] * 13 + [ANY] * 2 + [VMEM] + [ANY] * 4 + [VMEM] * (3 + len(ffn)),
        out_specs=(VMEM,) * (8 + len(ffn)),
        scratch_shapes=LineSum.scratch(n, rows, width, chunk) * 2
        + GradSum.scratch(fsdp, ctx, blocks)
        + GradSum.semaphores(fsdp, ctx, 5)
        + [pltpu.VMEM(w, BF16) for w in whole]
        + [
            pltpu.VMEM((rows, width), BF16),
            pltpu.VMEM((rows, latent), BF16),
            pltpu.VMEM((max(win - 1, 1), rows, latent), BF16),
            pltpu.SemaphoreType.DMA((max(win - 1, 1), seq_dev, seq_pieces)),
            pltpu.SemaphoreType.DMA((max(win - 1, 1), seq_dev, seq_pieces)),
            pltpu.VMEM((8, width), F32),
            pltpu.VMEM((8, many), F32),
            pltpu.VMEM((2 * seq_dev, 8, width), F32),
            pltpu.VMEM((win * rows, q_width), F32),
            pltpu.VMEM((win * rows, q_width), F32),
            pltpu.VMEM((TILE, q_width), F32),
            pltpu.VMEM((rows, q_width), BF16),
            pltpu.VMEM((TILE, q_width), BF16),
            pltpu.VMEM((win * rows, latent), BF16),
        ]
        + [
            pltpu.VMEM((win * rows, latent), BF16),
            pltpu.VMEM((rows, width), BF16),
            pltpu.VMEM((rows, width), BF16),
            pltpu.VMEM((half, width), F32),
            pltpu.VMEM((half, width), F32),
            pltpu.VMEM((rows, width), BF16),
            pltpu.SemaphoreType.DMA((6,)),
        ]
        + [pltpu.VMEM(lat, BF16), pltpu.VMEM((n,) + lat, BF16)]
        + RowGather.scratch(n)
        + AxisSum.scratch(n, (8, many))
        + AxisSum.scratch(ctx, (8, many))
        + AxisSum.scratch(fsdp, (8, many))
        + (GradSum.scratch(fsdp, ctx, ffn, False) + GradSum.semaphores(fsdp, ctx, len(ffn)) if ffn else []),
        compiler_params=params(3, 64),
    )(query, keys, values, seg_all, cols, lse, attended, d_branch, wo_rows, w_qry, w_lat, w_kproj, w_vproj,
      lat_all, xn_one, gains, tokens, d_middle, mid_own, part_feed, marks, gain_part, branch_sq, *firsts)
    return out[:3], out[3:8], out[8:]


def publish(arrays, small, seq_dev, tok_dev, feat_dim, fsdp):
    count = len(arrays)
    per = feat_dim // fsdp

    def kernel(*refs):
        srcs, sm, refs = refs[:count], refs[count], refs[count + 1 :]
        dsts, (gain1, gain2, stats, radial), refs = refs[:count], refs[count : count + 4], refs[count + 4 :]
        inward = Bring(list(zip(srcs, refs[:count])), refs[count])
        outward = Bring(list(zip(refs[:count], dsts)), refs[count + 1])
        inward.start()
        f = lax.axis_index("fsdp")
        mine = pl.ds(pl.multiple_of(f * per, per), per)
        gain1[...] = sm[0:1, mine].reshape(per)
        gain2[...] = sm[1:2, mine].reshape(per)
        for q in range(seq_dev):
            radial[q : q + 1, :] = sm[3:4, q * tok_dev : (q + 1) * tok_dev]
            total = sm[2:3, 4 * q + 3 : 4 * q + 4] * feat_dim
            for j, lane in enumerate((0, 2, 1)):
                stats[q : q + 1, j : j + 1] = jnp.sqrt(sm[2:3, 4 * q + lane : 4 * q + lane + 1] / total)
        for i in range(count):
            inward.wait([i])
            outward.start([i])
        outward.wait()

    out = pl.pallas_call(
        kernel,
        out_shape=tuple(shape_of(a.shape, a.dtype) for a in arrays)
        + (shape_of((per,), F32),) * 2
        + (shape_of((seq_dev, 3), F32), shape_of((seq_dev, tok_dev), F32)),
        in_specs=[ANY] * count + [VMEM],
        out_specs=(ANY,) * count + (VMEM,) * 4,
        scratch_shapes=[pltpu.VMEM(a.shape, a.dtype) for a in arrays] + [pltpu.SemaphoreType.DMA((count,))] * 2,
        compiler_params=pltpu.CompilerParams(vmem_limit_bytes=60 << 20),
    )(*arrays, small)
    return out[:count], out[count:]


class AxisShare:
    def __init__(self, axis, n, src, dst, recv, sent, own):
        self.axis, self.n, self.src, self.dst = axis, n, src, dst
        self.recv, self.sent, self.own = recv, sent, own
        self.at = lax.axis_index(axis)

    def start(self):
        for k in range(1, self.n):
            remote(self.src, self.dst.at[self.at], self.sent.at[k - 1], self.recv.at[self.at],
                   {self.axis: lax.rem(self.at + k, self.n)}).start()
        pltpu.make_async_copy(self.src, self.dst.at[self.at], self.own).start()

    def finish(self):
        for k in range(1, self.n):
            other = lax.rem(self.at + k, self.n)
            wait_came(self.dst.at[other], self.sent.at[k - 1], self.recv.at[other])
            wait_sent(self.src, self.sent.at[k - 1], self.recv.at[other])
        pltpu.make_async_copy(self.src, self.dst.at[self.at], self.own).wait()

    @staticmethod
    def scratch(n):
        return CtxShare.scratch(n)


class HalfSpread:
    def __init__(self, fsdp, pairs, recv, sent, own):
        self.fsdp, self.pairs, self.recv, self.sent, self.own = fsdp, pairs, recv, sent, own
        self.f, self.x = lax.axis_index("fsdp"), lax.axis_index("ctx")
        self.ys = fsdp // 2

    def view(self, a, f, half=None):
        src, dst = self.pairs[a]
        rows, size = src.shape
        columns = pl.ds(pl.multiple_of(f * size, size), size)
        if half is None:
            return dst.at[:, columns]
        return dst.at[pl.ds(pl.multiple_of(half * (rows // 2), rows // 2), rows // 2), columns]

    def part(self, a):
        src = self.pairs[a][0]
        return src.at[pl.ds(pl.multiple_of(self.x * (src.shape[0] // 2), src.shape[0] // 2), src.shape[0] // 2)]

    def start(self, which):
        for a in which:
            for k in range(1, self.ys):
                remote(self.part(a), self.view(a, self.f, self.x), self.sent.at[a, 0, k - 1], self.recv.at[a, 0, k - 1],
                       {"fsdp": lax.rem(self.f + 2 * k, self.fsdp)}).start()
        for a in which:
            src = self.pairs[a][0]
            remote(src, self.view(a, self.f), self.sent.at[a, 1, 0], self.recv.at[a, 1, 0],
                   {"fsdp": sibling(self.f)}).start()
            pltpu.make_async_copy(src, self.view(a, self.f), self.own.at[a]).start()

    def source(self, k):
        return lax.rem(self.f - 2 * k + self.fsdp, self.fsdp)

    def relay(self, which):
        for a in which:
            for k in range(1, self.ys):
                here = self.view(a, self.source(k), self.x)
                wait_came(here, self.sent.at[a, 0, k - 1], self.recv.at[a, 0, k - 1])
                remote(here, here, self.sent.at[a, 2, k - 1], self.recv.at[a, 2, k - 1], {"ctx": 1 - self.x}).start()
                remote(here, here, self.sent.at[a, 3, k - 1], self.recv.at[a, 3, k - 1],
                       {"fsdp": sibling(self.f)}).start()

    def cross(self, which):
        for a in which:
            for k in range(1, self.ys):
                here = self.view(a, self.source(k), 1 - self.x)
                wait_came(here, self.sent.at[a, 2, k - 1], self.recv.at[a, 2, k - 1])
                remote(here, here, self.sent.at[a, 4, k - 1], self.recv.at[a, 4, k - 1],
                       {"fsdp": sibling(self.f)}).start()

    def finish(self, which):
        for a in which:
            src = self.pairs[a][0]
            other = sibling(self.f)
            wait_came(self.view(a, other), self.sent.at[a, 1, 0], self.recv.at[a, 1, 0])
            pltpu.make_async_copy(src, self.view(a, self.f), self.own.at[a]).wait()
            for k in range(1, self.ys):
                there = lax.rem(other - 2 * k + self.fsdp, self.fsdp)
                wait_came(self.view(a, there, self.x), self.sent.at[a, 3, k - 1], self.recv.at[a, 3, k - 1])
                wait_came(self.view(a, there, 1 - self.x), self.sent.at[a, 4, k - 1], self.recv.at[a, 4, k - 1])

    def drain(self, which):
        for a in which:
            wait_sent(self.view(a, self.f), self.sent.at[a, 1, 0], self.recv.at[a, 1, 0])
            for k in range(1, self.ys):
                for kind in (0, 2, 3, 4):
                    wait_sent(self.part(a), self.sent.at[a, kind, k - 1], self.recv.at[a, kind, k - 1])

    @staticmethod
    def scratch(fsdp, arrays):
        return [
            pltpu.SemaphoreType.DMA((arrays, 5, max(fsdp // 2 - 1, 1))),
            pltpu.SemaphoreType.DMA((arrays, 5, max(fsdp // 2 - 1, 1))),
            pltpu.SemaphoreType.DMA((arrays,)),
        ]


R_TWO, MARK, LSE = 3, 4, 8


def layer(tokens, gain1, gain2, w_latent, shards, w_out, wide_shards, segments, out_grad, fsdp, ctx, n):
    rows, width = tokens.shape
    seq_dev, tok_dev = segments.shape
    w_query = shards[0]
    latent, q_width, inner = LATENT, w_query.shape[1], wide_shards[0].shape[0]
    heads = q_width // HEAD_DIM
    per = tok_dev // TILE
    win, span = window(ctx, tok_dev), key_span(ctx, tok_dev)
    own_shard = win - 1
    tiles = span + 1
    keyed = win * rows
    per_group = HEADS // GROUPS * HEAD_DIM
    wide, chunk = 128, 256
    pieces = rows // chunk
    per_seq = tok_dev // chunk
    strip, hop, reach = 32, 2, 3
    piece = 64
    per_block = TILE // piece
    side = 128
    many = max(width, rows)
    q_tiles = rows // TILE
    steps_all = rows // 2 // strip
    lag = hop * 2 * (n // 2)
    ffn = (inner, width // fsdp)
    axes = (0, 0, 0, 1, 0)
    whole = ((width, q_width), (latent, q_width), (latent, q_width), (q_width, width), (width, latent))
    blocks = [GradSum.block_shape(w, a, fsdp) for w, a in zip(whole, axes)]
    lat = blocks[-1]
    cols_at = width // 4

    scratch = dict(
        gbuf=pltpu.VMEM((8, gain1.shape[0]), F32),
        sbuf=pltpu.VMEM((8, tok_dev), segments.dtype),
        gain=pltpu.VMEM((8, width), F32),
        segk=pltpu.VMEM((ctx, 8, tok_dev), segments.dtype),
        cols=pltpu.VMEM((rows, 128), F32),
        tok=pltpu.VMEM((rows, width), BF16),
        gathered=pltpu.VMEM((rows, n * q_width), BF16),
        wo=pltpu.VMEM((n * q_width, width), BF16),
        cot=pltpu.VMEM((rows, width), BF16),
        xn=pltpu.VMEM((rows, width), BF16),
        p_two=pltpu.VMEM((rows, width), BF16),
        p_feed=pltpu.VMEM((rows, width), BF16),
        left=pltpu.VMEM((rows, width), BF16),
        right=pltpu.VMEM((rows, width), BF16),
        branch=pltpu.VMEM((rows, width), BF16),
        mid=pltpu.VMEM((rows, width), F32),
        wg=pltpu.VMEM((inner, width), BF16),
        wu=pltpu.VMEM((inner, width), BF16),
        wd=pltpu.VMEM((inner, width), BF16),
        hid=pltpu.VMEM((rows, inner), BF16),
        dg=pltpu.VMEM((rows, inner), BF16),
        du=pltpu.VMEM((rows, inner), BF16),
        w_lat=pltpu.VMEM((width, latent), BF16),
        w_qry=pltpu.VMEM((width, q_width), BF16),
        w_kproj=pltpu.VMEM((latent, q_width), BF16),
        w_vproj=pltpu.VMEM((latent, q_width), BF16),
        wo_rows=pltpu.VMEM((q_width, width), BF16),
        wo_line=pltpu.VMEM((n,) + w_out.shape, BF16),
        lat_all=pltpu.VMEM((keyed, latent), BF16),
        query=pltpu.VMEM((rows, q_width), BF16),
        keys=pltpu.VMEM((keyed, q_width), BF16),
        values=pltpu.VMEM((keyed, q_width), BF16),
        att=pltpu.VMEM((rows, q_width), BF16),
        dk=pltpu.VMEM((keyed, q_width), F32),
        dv=pltpu.VMEM((keyed, q_width), F32),
        dqb=pltpu.VMEM((rows, q_width), BF16),
        grad_seq=pltpu.VMEM((TILE, q_width), BF16),
        lat_parts=pltpu.VMEM((keyed, latent), BF16),
        dlat=pltpu.VMEM((rows, latent), BF16),
        came=pltpu.VMEM((rows, latent), BF16),
        g_sum=pltpu.VMEM((8, width), F32),
        g_sum2=pltpu.VMEM((8, width), F32),
        sm=pltpu.VMEM((8, many), F32),
        sacc=pltpu.VMEM((3 * seq_dev, 8, width), F32),
        lat_own=pltpu.VMEM(lat, BF16),
        lat_every=pltpu.VMEM((n, lat[0] // 2, lat[1]), BF16),
        lat_sum=pltpu.VMEM((lat[0] // 2, GROUPS * lat[1]), BF16),
        lat_both=pltpu.VMEM((ctx, lat[0] // 2, GROUPS * lat[1]), BF16),
        local=pltpu.SemaphoreType.DMA((2,)),
        flush=pltpu.SemaphoreType.DMA((10,)),
        lat_recv=pltpu.SemaphoreType.DMA((pieces,)),
        lat_sent=pltpu.SemaphoreType.DMA((pieces,)),
        c_recv=pltpu.SemaphoreType.DMA((seq_dev, per_seq)),
        c_sent=pltpu.SemaphoreType.DMA((seq_dev, per_seq)),
    )
    out_blocks = [shape_of(b, F32) for b in blocks[:-1]] + [shape_of((lat[0], GROUPS * lat[1]), F32)]
    out_blocks += [shape_of(ffn, F32)] * 3
    groups = dict(
        outs=[pltpu.VMEM(o.shape, F32) for o in out_blocks[:5]],
        held=GradSum.scratch(fsdp, ctx, [ffn] * 3 + blocks),
        parts=[pltpu.VMEM(w, BF16) for w in whole],
        spread=Spread.scratch(fsdp, 5),
        half=HalfSpread.scratch(fsdp, 4),
        share=CtxShare.scratch(ctx),
        wline=AxisShare.scratch(n),
        gather=LineGather.scratch(n, rows // piece),
        two=LineSum.scratch(n, rows, width, strip)[2:],
        feed=LineSum.scratch(n, rows, width, strip)[2:],
        gffn=GradSum.semaphores(fsdp, ctx, 3),
        gatt=GradSum.semaphores(fsdp, ctx, 5),
        lline=AxisShare.scratch(n),
        xline=AxisShare.scratch(ctx),
        s_tp=AxisSum.scratch(n, (8, many)),
        s_ctx=AxisSum.scratch(ctx, (8, many)),
        s_fsdp=AxisSum.scratch(fsdp, (8, many)),
    )
    names = list(scratch)
    shapes = list(scratch.values())
    places = {}
    for key, some in groups.items():
        places[key] = (len(shapes), len(shapes) + len(some))
        shapes = shapes + list(some)

    def kernel(*refs):
        (tok_in, ga, gb, wlat, wq, wkp, wvp, wout, wgt, wut, wdn, seg, cot_in), refs = refs[:13], refs[13:]
        (o_mixed, o_tok), o_blocks, o_small, refs = refs[:2], refs[2:10], refs[10], refs[11:]
        r = SimpleNamespace(**dict(zip(names, refs)))
        g = SimpleNamespace(**{key: refs[a:b] for key, (a, b) in places.items()})
        cols, tok, cot, xn, mid = r.cols, r.tok, r.cot, r.xn, r.mid
        gain, segk = r.gain, r.segk
        x, me = lax.axis_index("ctx"), lax.axis_index("tp")
        outs = list(g.outs) + [mid.at[0 : ffn[0], i * ffn[1] : (i + 1) * ffn[1]] for i in range(3)]

        load = Bring([(tok_in, tok), (cot_in, cot)], r.local)
        load.start()
        r.gbuf[...] = jnp.zeros_like(r.gbuf)
        r.gbuf[0:1, :] = ga[...].astype(F32).reshape(1, -1)
        r.gbuf[1:2, :] = gb[...].astype(F32).reshape(1, -1)
        r.sbuf[...] = jnp.zeros_like(r.sbuf)
        r.sbuf[0:seq_dev, :] = seg[...]
        meet(n, fsdp, ctx, everyone=True)

        group = me * q_width // per_group
        src_lat = wlat.at[:, pl.ds(pl.multiple_of(group * latent, latent), latent)]
        spread = Spread(
            fsdp,
            [(r.gbuf, gain), (src_lat, r.w_lat), (wq, r.w_qry), (wkp, r.w_kproj), (wvp, r.w_vproj)],
            [1, 0, 0, 0, 0], *g.spread,
        )
        share = CtxShare(ctx, r.sbuf, segk, *g.share)
        wline = AxisShare("tp", n, wout, r.wo_line, *g.wline)
        half = HalfSpread(
            fsdp,
            [(wgt, r.wg), (wut, r.wu), (wdn, r.wd), (r.wo_line.reshape(n * q_width, w_out.shape[1]), r.wo)],
            *g.half,
        )
        spread.start()
        share.start()
        wline.start()
        half.start([0, 1, 2])
        cols[...] = jnp.zeros_like(cols)
        r.g_sum[...] = jnp.zeros_like(r.g_sum)
        r.g_sum2[...] = jnp.zeros_like(r.g_sum2)
        r.sacc[...] = jnp.zeros_like(r.sacc)
        r.sm[...] = jnp.zeros_like(r.sm)
        load.wait([0])

        def scale(i):
            at = pl.ds(pl.multiple_of(i * wide, wide), wide)
            value = tok[at, :].astype(F32)
            cols[at, R_ONE : R_ONE + 1] = lax.rsqrt(jnp.mean(value * value, axis=-1, keepdims=True) + eps)

        loop(0, rows // wide, scale)
        spread.relay([0, 1])
        spread.finish([0, 1])
        lat_all = r.lat_all

        def place(shard, i):
            seq = i // per_seq
            return pl.ds(pl.multiple_of((seq * win + shard) * tok_dev + lax.rem(i, per_seq) * chunk, chunk), chunk)

        def pass_on(i):
            return remote(lat_all.at[place(own_shard, i)], lat_all.at[place(own_shard - 1, i)], r.lat_sent.at[i],
                          r.lat_recv.at[i], {"ctx": x + 1})

        def first_norm(i):
            at = pl.ds(pl.multiple_of(i * chunk, chunk), chunk)
            unit = (tok[at, :].astype(F32) * cols[at, R_ONE : R_ONE + 1] * gain[0:1, :]).astype(BF16)
            xn[at, :] = unit
            lat_all[place(own_shard, i), :] = dot(unit, r.w_lat[...]).astype(BF16)

            @pl.when(x + 1 < ctx)
            def _():
                pass_on(i).start()

        loop(0, pieces, first_norm)
        spread.relay([2, 3, 4])
        spread.finish([2, 3, 4])

        def project(shard, i):
            to = place(shard, i)
            value = lat_all[to, :]
            r.keys[to, :] = dot(value, r.w_kproj[...]).astype(BF16)
            r.values[to, :] = dot(value, r.w_vproj[...]).astype(BF16)

        def ask(i):
            at = pl.ds(pl.multiple_of(i * chunk, chunk), chunk)
            r.query[at, :] = dot(xn[at, :], r.w_qry[...]).astype(BF16)
            project(own_shard, i)

        loop(0, pieces, ask)
        share.finish()
        for q in range(seq_dev):
            at = slice(q * tok_dev, (q + 1) * tok_dev)
            ids = jnp.broadcast_to(r.sbuf[q : q + 1, :].astype(F32), (128, tok_dev)).T
            cols[at, SEGMENT : SEGMENT + 1] = ids[:, 0:1]
            final = segk[ctx - 1, q : q + 1, tok_dev - 1 : tok_dev].astype(F32)
            cols[at, VALID : VALID + 1] = jnp.where(ids[:, 0:1] != final, 1.0, 0.0)
        half.relay([0, 1])

        def theirs(i):
            @pl.when(x - 1 >= 0)
            def _():
                wait_came(lat_all.at[place(own_shard - 1, i)], r.lat_sent.at[i], r.lat_recv.at[i])

            @pl.when(x - 1 < 0)
            def _():
                lat_all[place(own_shard - 1, i), :] = jnp.zeros((chunk, latent), BF16)

            project(own_shard - 1, i)

        att, gathered = r.att, r.gathered
        line = LineGather(n, piece, att, gathered, *g.gather, hop=reach)

        def query_tile(i):
            seq = i // per
            q_tile = own_shard * per + lax.rem(i, per)
            at = pl.ds(pl.multiple_of(i * TILE, TILE), TILE)
            near = pl.ds(pl.multiple_of((seq * win * per + q_tile - span) * TILE, TILE), tiles * TILE)
            counted = jnp.concatenate(
                [
                    c.astype(F32)
                    for c in counted_keys(cols, segk, at, seq, q_tile * TILE, q_tile - span, tiles, tok_dev, win)
                ],
                axis=1,
            )
            accum = jnp.zeros((TILE, q_width), F32)
            for h in range(heads):
                score = dot_t(head_only(r.query[at, :], h), r.keys[near, :]) * 0.125
                score = jnp.where(counted > 0.0, score, -1e30)
                top = jnp.max(score, axis=-1, keepdims=True)
                weight = jnp.exp(score - top)
                total = jnp.sum(weight, axis=-1, keepdims=True)
                prob = (weight * (1.0 / total)).astype(BF16)
                accum = accum + jnp.dot(prob, head_only(r.values[near, :], h), preferred_element_type=F32)
                cols[at, LSE + h : LSE + h + 1] = top + jnp.log(total)
                line.step((i - 1) * per_block + h * per_block // heads)
            att[at, :] = accum.astype(BF16)

        def sequence_forward(seq):
            loop(seq * per_seq, seq * per_seq + per_seq, theirs)

            @pl.when(seq == 0)
            def _():
                wline.finish()
                half.start([3])

            loop(seq * per, seq * per + per, query_tile)

            @pl.when(seq == 0)
            def _():
                half.relay([2, 3])

        loop(0, seq_dev, sequence_forward)
        s1 = (q_tiles - 1) * per_block
        line.begin()
        half.cross([0, 1, 2, 3])
        loop(s1, per_block + reach * (n - 1), line.step)
        s1 = per_block + reach * (n - 1)
        half.finish([3, 0, 1, 2])
        half.drain([0, 1, 2, 3])
        r.wo_rows[...] = r.wo[pl.ds(pl.multiple_of(me * q_width, q_width), q_width), :]
        line.begun()
        load.wait([1])

        p_two, p_feed, wg, wu, wd = r.p_two, r.p_feed, r.wg, r.wu, r.wd

        def second_back(at, own, total):
            unit = mid[at, :] * cols[at, R_TWO : R_TWO + 1]
            r.g_sum2[...] += jnp.sum((total * unit).reshape(strip // 8, 8, width), axis=0)
            scaled = total * gain[1:2, :]
            mean = jnp.mean(scaled * unit, axis=-1, keepdims=True)
            d_mid = cot[at, :].astype(F32) + cols[at, R_TWO : R_TWO + 1] * (scaled - unit * mean)
            first_unit = tok[at, :].astype(F32) * cols[at, R_ONE : R_ONE + 1]
            cols[at, MARK : MARK + 1] = jnp.sum(first_unit * d_mid, axis=-1, keepdims=True)
            return d_mid.astype(BF16)

        def forward(at, own, total):
            mixed = mid[at, :] + total
            seq = at.start // tok_dev
            counted = cols[at, VALID : VALID + 1]
            r.sacc[seq] += jnp.sum((mixed * mixed * counted).reshape(strip // 8, 8, width), axis=0)
            r.sacc[seq_dev + seq] += jnp.sum((total * total * counted).reshape(strip // 8, 8, width), axis=0)
            return mixed.astype(BF16)

        def first_back(at, own, total):
            r1 = cols[at, R_ONE : R_ONE + 1]
            unit = tok[at, :].astype(F32) * r1
            scaled = total * gain[0:1, :]
            mean = jnp.mean(scaled * unit, axis=-1, keepdims=True)
            return (r.branch[at, :].astype(F32) + r1 * (scaled - unit * mean)).astype(BF16)

        two = LineSum(n, strip, hop, p_two, r.left, r.right, r.branch, *g.two, second_back)
        feed = LineSum(n, strip, hop, p_feed, gathered, r.wo, xn, *g.feed, forward)
        one = LineSum(n, strip, hop, cot, r.left, r.right, p_two, *g.two, first_back)
        parts = [wg, wu, wd]
        gffn = GradSum(fsdp, ctx, parts, [1, 1, 1], None,
                       [g.held[3 * a : 3 * a + 3] for a in range(3)], *g.gffn)
        aparts = g.parts
        gatt = GradSum(fsdp, ctx, aparts, axes, None,
                       [g.held[3 * a : 3 * a + 3] for a in range(3, 8)], *g.gatt)

        def block_of_rows(b):
            at = pl.ds(pl.multiple_of(b * TILE, TILE), TILE)
            seq = b * TILE // tok_dev

            def steps(j):
                line.step(s1 + b * per_block + j)
                two.step((b - 1) * per_block + j)

            branch = dot(gathered[at, :], r.wo[...])
            middle_rows = tok[at, :].astype(F32) + branch
            mid[at, :] = middle_rows
            r.sacc[2 * seq_dev + seq] += jnp.sum(
                (branch * branch * cols[at, VALID : VALID + 1]).reshape(TILE // 8, 8, width), axis=0
            )
            level = lax.rsqrt(jnp.mean(middle_rows * middle_rows, axis=-1, keepdims=True) + eps)
            cols[at, R_TWO : R_TWO + 1] = level
            unit = (middle_rows * level * gain[1:2, :]).astype(BF16)
            xn[at, :] = unit
            steps(0)
            gate = dot_t(unit, wg[...])
            upper = dot_t(unit, wu[...])
            sigma = jax.nn.sigmoid(gate)
            swish = gate * sigma
            hidden = (swish * upper).astype(BF16)
            r.hid[at, :] = hidden
            slope = upper * sigma * (1.0 + gate * (1.0 - sigma))
            steps(1)
            p_feed[at, :] = dot(hidden, wd[...]).astype(BF16)
            d_hidden = dot_t(cot[at, :], wd[...])
            d_gate = (d_hidden * slope).astype(BF16)
            d_upper = (d_hidden * swish).astype(BF16)
            r.dg[at, :] = d_gate
            r.du[at, :] = d_upper
            steps(2)
            p_two[at, :] = (dot(d_gate, wg[...]) + dot(d_upper, wu[...])).astype(BF16)
            steps(3)

        loop(0, q_tiles, block_of_rows)
        s2 = (q_tiles - 1) * per_block

        def product(i):
            at = pl.ds(pl.multiple_of(i * cols_at, cols_at), cols_at)
            left = xn[:, at]
            parts[0][:, at] = dot_rows(r.dg[...], left).astype(BF16)
            parts[1][:, at] = dot_rows(r.du[...], left).astype(BF16)
            parts[2][:, at] = dot_rows(r.hid[...], cot[:, at]).astype(BF16)

        def busy(s):
            two.step(s)
            product(s - s2)

        line.drain()
        loop(s2, s2 + 4, busy)
        gffn.start()
        s2 = s2 + 4

        dk, dv, dqb, grad_seq, lat_parts = r.dk, r.dv, r.dqb, r.grad_seq, r.lat_parts

        def clear(i):
            at = pl.ds(pl.multiple_of(i * TILE, TILE), TILE)
            dk[at, :] = jnp.zeros((TILE, q_width), F32)
            dv[at, :] = jnp.zeros((TILE, q_width), F32)

        loop(0, keyed // TILE, clear)
        ready = steps_all // seq_dev + lag
        loop(s2, ready, two.step)

        def grad_tile(i, step):
            seq = i // per
            q_tile = own_shard * per + lax.rem(i, per)
            at = pl.ds(pl.multiple_of(i * TILE, TILE), TILE)
            near = pl.ds(pl.multiple_of((seq * win * per + q_tile - span) * TILE, TILE), tiles * TILE)
            grad_seq[...] = dot_t(r.branch[at, :], r.wo_rows[...]).astype(BF16)
            inner_sum = grad_seq[...].astype(F32) * att[at, :].astype(F32)
            counted = jnp.concatenate(
                [
                    c.astype(F32)
                    for c in counted_keys(cols, segk, at, seq, q_tile * TILE, q_tile - span, tiles, tok_dev, win)
                ],
                axis=1,
            )
            d_query = jnp.zeros((TILE, q_width), F32)
            d_key = jnp.zeros((tiles * TILE, q_width), F32)
            d_value = jnp.zeros((tiles * TILE, q_width), F32)
            for h in range(heads):
                delta = jnp.sum(head_only(inner_sum, h), axis=-1, keepdims=True)
                asked, ours = head_only(r.query[at, :], h), head_only(grad_seq[...], h)
                score = jnp.where(counted > 0.0, dot_t(asked, r.keys[near, :]) * 0.125, -1e30)
                prob = jnp.exp(score - cols[at, LSE + h : LSE + h + 1]) * counted
                d_score = (prob * (dot_t(ours, r.values[near, :]) - delta)).astype(BF16)
                d_query = d_query + jnp.dot(d_score, head_only(r.keys[near, :], h), preferred_element_type=F32)
                d_key = d_key + dot_rows(d_score, asked)
                d_value = d_value + dot_rows(prob.astype(BF16), ours)
                step(h)
            dqb[at, :] = (d_query * 0.125).astype(BF16)
            dk[near, :] += d_key * 0.125
            dv[near, :] += d_value

        def send_latent(seq, i):
            j = seq * per_seq + i
            at = pl.ds(pl.multiple_of(j * chunk, chunk), chunk)
            return remote(lat_parts.at[place(own_shard - 1, j)], r.came.at[at], r.c_sent.at[seq, i],
                          r.c_recv.at[seq, i], {"ctx": x - 1})

        def latents(seq):
            for shard in (own_shard - 1, own_shard):
                for i in range(per_seq):
                    at = place(shard, seq * per_seq + i)
                    lat_parts[at, :] = (
                        dot_t(dk[at, :].astype(BF16), r.w_kproj[...])
                        + dot_t(dv[at, :].astype(BF16), r.w_vproj[...])
                    ).astype(BF16)
                    if shard < own_shard:

                        @pl.when(x - 1 >= 0)
                        def _(i=i):
                            send_latent(seq, i).start()

        def sequence(seq):
            def tile(i):
                def step(h):
                    t = (i * heads + h) * steps_per // heads
                    two.step(ready + t)
                    feed.step(t)

                grad_tile(i, step)

            loop(seq * per, seq * per + per, tile)
            latents(seq)

            @pl.when(seq == 0)
            def _():
                two.drain()
                gffn.pair()
                gffn.second()

        steps_per = heads
        loop(0, seq_dev, sequence)
        fed = q_tiles * steps_per

        def whole_latent(j):
            seq, i = j // per_seq, lax.rem(j, per_seq)
            at = pl.ds(pl.multiple_of(j * chunk, chunk), chunk)
            r.dlat[at, :] = lat_parts[place(own_shard, j), :]

            @pl.when(x + 1 < ctx)
            def _():
                wait_came(r.came.at[at], r.c_sent.at[seq, i], r.c_recv.at[seq, i])
                r.dlat[at, :] = (r.dlat[at, :].astype(F32) + r.came[at, :].astype(F32)).astype(BF16)

            cot[at, :] = (dot_t(dqb[at, :], r.w_qry[...]) + dot_t(r.dlat[at, :], r.w_lat[...])).astype(BF16)

        def first_unit_columns(at):
            return (tok[:, at].astype(F32) * cols[:, R_ONE : R_ONE + 1] * gain[0:1, at]).astype(BF16)

        early = (seq_dev - 1) * per_seq
        loop(0, early, whole_latent)

        def mixed_work(i):
            at = pl.ds(pl.multiple_of(i * chunk, chunk), chunk)
            aparts[0][at, :] = dot_rows(first_unit_columns(at), dqb[...]).astype(BF16)
            aparts[3][:, at] = dot_rows(att[...], r.branch[:, at]).astype(BF16)
            feed.step(fed + i)

        fed_later = fed + width // chunk
        loop(0, width // chunk, mixed_work)
        gffn.third()
        aparts[1][...] = dot_rows(lat_all[...], dk[...].astype(BF16)).astype(BF16)
        aparts[2][...] = dot_rows(lat_all[...], dv[...].astype(BF16)).astype(BF16)
        loop(early, pieces, whole_latent)

        def steps(s):
            one.step(s)
            feed.step(fed_later + s)

        def product_lat(s):
            at = pl.ds(pl.multiple_of(s * chunk, chunk), chunk)
            aparts[4][at, :] = dot_rows(first_unit_columns(at), r.dlat[...]).astype(BF16)
            steps(s)

        begun = width // chunk
        loop(0, begun, product_lat)
        gatt.start()

        def gains_of(i):
            at = pl.ds(pl.multiple_of(i * side, side), side)
            value = cot[at, :].astype(F32) * (tok[at, :].astype(F32) * cols[at, R_ONE : R_ONE + 1])
            r.g_sum[...] += jnp.sum(value.reshape(side // 8, 8, width), axis=0)
            along = lax.dot_general(jnp.ones((8, width), F32), value * gain[0:1, :], (((1,), (1,)), ((), ())),
                                    precision=lax.Precision.HIGHEST, preferred_element_type=F32)
            r.sm[3:4, at] = along[0:1, :]
            lines = cols[at, :].T
            r.sm[4:5, at] = lines[MARK : MARK + 1, :]
            r.sm[5:6, at] = lines[R_ONE : R_ONE + 1, :]

        def two_gains(s):
            steps(s)
            gains_of(2 * (s - begun))
            gains_of(2 * (s - begun) + 1)

        mark = begun + rows // side // 2
        loop(begun, begun + 1, two_gains)
        gatt.pair()
        gatt.second()
        loop(begun + 1, mark, two_gains)
        last = one.steps()
        for s in range(fed_later + mark, feed.steps()):
            feed.step(s)
        flush = r.flush
        out_mixed = pltpu.make_async_copy(xn, o_mixed, flush.at[8])
        out_mixed.start()
        lane = lax.broadcasted_iota(jnp.int32, (1, many), 1)
        once = jnp.where(me == 0, 1.0, 0.0)
        row = jnp.zeros((1, many), F32)

        def whole_sum(value):
            return jnp.sum(jnp.sum(value, axis=0, keepdims=True), axis=1, keepdims=True)

        for q in range(seq_dev):
            stats = [
                whole_sum(r.sacc[q]),
                whole_sum(r.sacc[seq_dev + q]),
                whole_sum(r.sacc[2 * seq_dev + q]) * once,
                jnp.sum(cols[q * tok_dev : (q + 1) * tok_dev, VALID : VALID + 1], axis=0, keepdims=True) * once,
            ]
            for j, value in enumerate(stats):
                row = row + jnp.where(lane == 4 * q + j, value, 0.0)
        r.sm[2:3, :] = row
        r.sm[0:1, 0:width] = jnp.sum(r.g_sum[...], axis=0, keepdims=True)
        r.sm[1:2, 0:width] = jnp.sum(r.g_sum2[...], axis=0, keepdims=True)
        r_row = r.sm[5:6, :]
        over_tp = AxisSum("tp", n, *g.s_tp)
        over_ctx = AxisSum("ctx", ctx, *g.s_ctx)
        over_fsdp = AxisSum("fsdp", fsdp, *g.s_fsdp)
        over_tp.start(r.sm[...])
        lat_half = pl.ds(pl.multiple_of(x * (lat[0] // 2), lat[0] // 2), lat[0] // 2)
        lline = AxisShare("tp", n, r.lat_own.at[lat_half], r.lat_every, *g.lline)
        xline = AxisShare("ctx", ctx, r.lat_sum, r.lat_both, *g.xline)
        outward = Bring([(outs[i], o_blocks[i]) for i in range(8)], flush)

        def store(a, at, total):
            if a < 4:
                outs[a][at, :] = total
            else:
                r.lat_own[at, :] = total.astype(BF16)

        def store_ffn(a, at, total):
            outs[5 + a][at, :] = total

        loop(mark, mark + 2, steps)
        gatt.third()
        along_tp = over_tp.finish()
        over_ctx.start(along_tp)
        gffn.fourth(store_ffn)
        outward.start([5, 6, 7])
        loop(mark + 2, mark + 4, steps)
        along_ctx = over_ctx.finish()
        over_fsdp.start(along_ctx)
        loop(mark + 4, mark + 6, steps)
        gatt.fourth(store)
        outward.start([0, 1, 2, 3])
        lline.start()
        everywhere = over_fsdp.finish()
        loop(mark + 6, mark + 10, steps)
        lline.finish()

        def latent_sum(i):
            at = pl.ds(pl.multiple_of(i * 16, 16), 16)
            for gr in range(GROUPS):
                total = jnp.zeros((16, lat[1]), F32)
                for t in range(n):
                    if t * GROUPS // n == gr:
                        total = total + r.lat_every[t, at, :].astype(F32)
                r.lat_sum[at, gr * lat[1] : (gr + 1) * lat[1]] = total.astype(BF16)

        loop(0, lat[0] // 32, latent_sum)
        xline.start()
        loop(mark + 10, mark + 13, steps)
        xline.finish()
        for k in range(ctx):
            outs[4][k * (lat[0] // 2) : (k + 1) * (lat[0] // 2), :] = r.lat_both[k].astype(F32)
        outward.start([4])
        row = lax.broadcasted_iota(jnp.int32, everywhere.shape, 0)
        o_small[...] = jnp.where(row < 2, everywhere, along_ctx)
        o_small[3:4, :] = (along_tp[4:5] + eps * r_row * r_row * r_row * along_tp[3:4]) * (1.0 / width**0.5)
        loop(mark + 13, last, steps)
        out_tok = pltpu.make_async_copy(p_two, o_tok, flush.at[9])
        out_tok.start()

        @pl.when(x + 1 < ctx)
        def _():
            loop(0, pieces, lambda i: pass_on(i).wait_send())

        @pl.when(x - 1 >= 0)
        def _():
            for seq in range(seq_dev):
                for i in range(per_seq):
                    send_latent(seq, i).wait_send()

        feed.drain()
        one.drain()
        gffn.drain_pair()
        gffn.drain()
        gatt.drain_pair()
        gatt.drain()
        outward.wait()
        out_mixed.wait()
        out_tok.wait()

    out = pl.pallas_call(
        kernel,
        out_shape=(shape_of((rows, width), BF16),) * 2 + tuple(out_blocks) + (shape_of((8, many), F32),),
        in_specs=[ANY] + [VMEM] * 2 + [ANY] * 8 + [VMEM, ANY],
        out_specs=(ANY,) * 10 + (VMEM,),
        scratch_shapes=shapes,
        compiler_params=params(1, 64),
    )(tokens, gain1, gain2, w_latent, *shards, w_out, *wide_shards, segments, out_grad)
    return out[0], out[1], out[2:7], out[7:10], out[10]


def three_kernels(tokens, gain1, gain2, w_latent, shards, w_out, wide_shards, segments, out_grad, fsdp, ctx, n):
    seq_dev, tok_dev = segments.shape
    gate, up, down = wide_shards
    (xn_one, cols, gains, w_lat, w_qry, w_kproj, w_vproj, gate_all, up_all, wo_cols, seg_all, lat_all,
     query, keys, values) = front(tokens, gain1, gain2, w_latent, shards, w_out, (gate, up), segments, fsdp, ctx, n)
    late = window(ctx, tok_dev) <= 2
    (d_branch, part_feed, d_middle, mid_own, wo_rows, gain_part, branch_sq, marks, attended, lse), ffn = middle(
        query, keys, values, seg_all, cols, (wo_cols.reshape(-1, w_out.shape[1]), down), gate_all, up_all, gains,
        tokens, out_grad, fsdp, ctx, n, seq_dev, late,
    )
    (grad_tokens, mixed, small), att_grads, late_ffn = back(
        query, keys, values, seg_all, cols, lse, attended, d_branch, wo_rows, (w_qry, w_lat, w_kproj, w_vproj),
        lat_all, xn_one, gains, tokens, d_middle, mid_own, part_feed, marks, gain_part, branch_sq,
        ffn if late else (), fsdp, ctx, n, seq_dev,
    )
    return mixed, grad_tokens, att_grads, late_ffn if late else ffn, small


def on_device(
    tokens, gain1, w_latent, w_query, w_key, w_value, w_out, gain2, w_gate, w_up, w_down, segments, cotangent
):
    seq_dev, tok_dev, feat_dim = tokens.shape
    n_ctx, n_tp, n_fsdp = lax.axis_size("ctx"), lax.axis_size("tp"), lax.axis_size("fsdp")
    row_count = seq_dev * tok_dev
    tok_rows = tokens.reshape(row_count, feat_dim)
    out_grad = cotangent.reshape(row_count, feat_dim)
    if n_ctx == 2 and n_fsdp >= 4 and w_down.shape[0] <= row_count and feat_dim <= row_count:
        mixed, grad_tokens, att_grads, ffn_grads, small = layer(
            tok_rows, gain1, gain2, w_latent, (w_query, w_key, w_value), w_out, (w_gate.T, w_up.T, w_down), segments,
            out_grad, n_fsdp, n_ctx, n_tp,
        )
    else:
        mixed, grad_tokens, att_grads, ffn_grads, small = three_kernels(
            tok_rows, gain1, gain2, w_latent, (w_query, w_key, w_value), w_out, (w_gate.T, w_up.T, w_down), segments,
            out_grad, n_fsdp, n_ctx, n_tp,
        )
    arrays, (gain_grad1, gain_grad2, stats, radial) = publish(
        (mixed, grad_tokens, *att_grads, *ffn_grads), small, seq_dev, tok_dev, feat_dim, n_fsdp
    )
    mixed, grad_tokens, s_qry, s_kproj, s_vproj, s_outp, s_lat, s_gate, s_up, s_down = arrays
    return (
        mixed.reshape(seq_dev, tok_dev, feat_dim),
        grad_tokens.reshape(seq_dev, tok_dev, feat_dim),
        gain_grad1,
        s_lat,
        s_qry,
        s_kproj,
        s_vproj,
        s_outp,
        gain_grad2,
        s_gate.T,
        s_up.T,
        s_down,
        stats,
        radial,
    )


def solution(mesh):
    return jax.shard_map(
        on_device,
        mesh=mesh,
        in_specs=(
            P("fsdp", "ctx", None),
            P("fsdp"),
            P("fsdp", None),
            P("fsdp", "tp"),
            P("fsdp", "tp"),
            P("fsdp", "tp"),
            P("tp", "fsdp"),
            P("fsdp"),
            P("fsdp", "tp"),
            P("fsdp", "tp"),
            P("tp", "fsdp"),
            P("fsdp", "ctx"),
            P("fsdp", "ctx", None),
        ),
        out_specs=(
            P("fsdp", "ctx", None),
            P("fsdp", "ctx", None),
            P("fsdp"),
            P("fsdp", None),
            P("fsdp", "tp"),
            P("fsdp", "tp"),
            P("fsdp", "tp"),
            P("tp", "fsdp"),
            P("fsdp"),
            P("fsdp", "tp"),
            P("fsdp", "tp"),
            P("tp", "fsdp"),
            P("fsdp", None),
            P("fsdp", "ctx"),
        ),
        check_vma=False,
    )
```

```python
from types import SimpleNamespace

import jax
import jax.numpy as jnp
from jax import lax
from jax.experimental import pallas as pl
from jax.experimental.pallas import tpu as pltpu
from jax.sharding import PartitionSpec as P

HEADS = 16
HEAD_DIM = 64
GROUPS = 2
LATENT = 256
MESH = pl.DeviceIdType.MESH
VMEM = pl.BlockSpec(memory_space=pltpu.VMEM)
ANY = pl.BlockSpec(memory_space=pl.ANY)
F32 = jnp.float32
BF16 = jnp.bfloat16

eps = 1e-05


def remote(src, dst, send_sem, recv_sem, device):
    return pltpu.make_async_remote_copy(
        src_ref=src,
        dst_ref=dst,
        send_sem=send_sem,
        recv_sem=recv_sem,
        device_id=device,
        device_id_type=MESH,
    )


def wait_sent(ref, sem, recv_sem):
    remote(ref, ref, sem, recv_sem, {"tp": lax.axis_index("tp")}).wait_send()


def wait_came(ref, send_sem, sem):
    remote(ref, ref, send_sem, sem, {"tp": lax.axis_index("tp")}).wait_recv()


def meet(line=0, fsdp=0, ctx=0, everyone=False):
    barrier = pltpu.get_barrier_semaphore()

    def greet(device):
        pl.semaphore_signal(barrier, inc=1, device_id=device, device_id_type=MESH)

    known = 0
    f, x, me = lax.axis_index("fsdp"), lax.axis_index("ctx"), lax.axis_index("tp")
    if fsdp and everyone:
        for k in range(1, fsdp):
            greet({"fsdp": lax.rem(f + k, fsdp)})
        known += fsdp - 1
    elif fsdp:
        greet({"fsdp": sibling(f)})
        for k in range(1, fsdp // 2):
            greet({"fsdp": lax.rem(f + 2 * k, fsdp)})
        known += fsdp // 2
    for k in range(1, ctx):
        greet({"ctx": lax.rem(x + k, ctx)})
        known += 1
    if line > 1 and everyone:
        for k in range(1, line):
            greet({"tp": lax.rem(me + k, line)})
        known += line - 1
    if line > 1 and not everyone:

        @pl.when(me > 0)
        def _():
            greet({"tp": me - 1})

        @pl.when(me < line - 1)
        def _():
            greet({"tp": me + 1})

        @pl.when((me > 0) & (me < line - 1))
        def _():
            pl.semaphore_wait(barrier, known + 2)

        @pl.when((me == 0) | (me == line - 1))
        def _():
            pl.semaphore_wait(barrier, known + 1)

    else:
        pl.semaphore_wait(barrier, known)


def sibling(f):
    return f + 1 - 2 * lax.rem(f, 2)


def block(ref, axis, index, size):
    at = pl.ds(pl.multiple_of(index * size, size), size)
    return ref.at[at] if axis == 0 else ref.at[:, at]


class Bring:
    def __init__(self, pairs, sems):
        self.copies = [pltpu.make_async_copy(src, dst, sems.at[i]) for i, (src, dst) in enumerate(pairs)]

    def start(self, which=None):
        for i in which if which is not None else range(len(self.copies)):
            self.copies[i].start()

    def wait(self, which=None):
        for i in which if which is not None else range(len(self.copies)):
            self.copies[i].wait()


class Spread:
    def __init__(self, fsdp, pairs, axes, recv, sent, own):
        self.fsdp, self.pairs, self.axes = fsdp, pairs, axes
        self.recv, self.sent, self.own = recv, sent, own
        self.f = lax.axis_index("fsdp")

    def size(self, a):
        return self.pairs[a][0].shape[self.axes[a]]

    def target(self, a, f):
        return block(self.pairs[a][1], self.axes[a], f, self.size(a))

    def start(self):
        f = self.f
        for a, (src, dst) in enumerate(self.pairs):
            for k in range(1, self.fsdp // 2):
                remote(src, self.target(a, f), self.sent.at[a], self.recv.at[a, f],
                       {"fsdp": lax.rem(f + 2 * k, self.fsdp)}).start()
        for a, (src, dst) in enumerate(self.pairs):
            remote(src, self.target(a, f), self.sent.at[a], self.recv.at[a, f],
                   {"fsdp": sibling(f)}).start()
            pltpu.make_async_copy(src, self.target(a, f), self.own.at[a]).start()

    def relay(self, which=None):
        for a in which or range(len(self.pairs)):
            for k in range(1, self.fsdp // 2):
                other = lax.rem(self.f + 2 * k, self.fsdp)
                here = self.target(a, other)
                wait_came(here, self.sent.at[a], self.recv.at[a, other])
                remote(here, here, self.sent.at[a], self.recv.at[a, other],
                       {"fsdp": sibling(self.f)}).start()

    def finish(self, which=None):
        for a in which or range(len(self.pairs)):
            src, dst = self.pairs[a]
            for k in range(0, self.fsdp // 2):
                other = lax.rem(sibling(self.f) + 2 * k, self.fsdp)
                wait_came(self.target(a, other), self.sent.at[a], self.recv.at[a, other])
            pltpu.make_async_copy(src, self.target(a, self.f), self.own.at[a]).wait()
            many = (self.fsdp - 1) * self.size(a)
            ref = dst.at[pl.ds(0, many)] if self.axes[a] == 0 else dst.at[:, pl.ds(0, many)]
            wait_sent(ref, self.sent.at[a], self.recv.at[a, 0])

    @staticmethod
    def scratch(fsdp, arrays):
        return [
            pltpu.SemaphoreType.DMA((arrays, fsdp)),
            pltpu.SemaphoreType.DMA((arrays,)),
            pltpu.SemaphoreType.DMA((arrays,)),
        ]


class CtxShare:
    def __init__(self, ctx, src, dst, recv, sent, own):
        self.ctx, self.src, self.dst = ctx, src, dst
        self.recv, self.sent, self.own = recv, sent, own
        self.x = lax.axis_index("ctx")

    def start(self):
        for k in range(1, self.ctx):
            remote(self.src, self.dst.at[self.x], self.sent.at[k - 1], self.recv.at[self.x],
                   {"ctx": lax.rem(self.x + k, self.ctx)}).start()
        pltpu.make_async_copy(self.src, self.dst.at[self.x], self.own).start()

    def finish(self):
        for k in range(1, self.ctx):
            other = lax.rem(self.x + k, self.ctx)
            wait_came(self.dst.at[other], self.sent.at[k - 1], self.recv.at[other])
            wait_sent(self.src, self.sent.at[k - 1], self.recv.at[other])
        pltpu.make_async_copy(self.src, self.dst.at[self.x], self.own).wait()

    @staticmethod
    def scratch(ctx):
        return [
            pltpu.SemaphoreType.DMA((ctx,)),
            pltpu.SemaphoreType.DMA((ctx,)),
            pltpu.SemaphoreType.DMA,
        ]


class LineGather:
    def __init__(self, n, chunk, src, dst, recv, sent, own, hop=1):
        self.n, self.chunk, self.src, self.dst, self.hop = n, chunk, src, dst, hop
        self.width = src.shape[1]
        self.count = src.shape[0] // chunk
        self.recv, self.sent, self.own = recv, sent, own
        self.me = lax.axis_index("tp")

    def steps(self):
        return self.count + self.hop * (self.n - 1)

    def columns(self, tp):
        return pl.ds(pl.multiple_of(tp * self.width, self.width), self.width)

    def place(self, tp, at):
        rows = pl.ds(pl.multiple_of(at * self.chunk, self.chunk), self.chunk)
        return self.dst.at[rows, self.columns(tp)]

    def begin(self):
        pltpu.make_async_copy(self.src, self.dst.at[:, self.columns(self.me)], self.own).start()

    def begun(self):
        pltpu.make_async_copy(self.src, self.dst.at[:, self.columns(self.me)], self.own).wait()

    def step(self, s):
        n, me, count = self.n, self.me, self.count
        left, right = {"tp": me - 1}, {"tp": me + 1}

        @pl.when((s >= 0) & (s < count))
        def _():
            rows = pl.ds(pl.multiple_of(s * self.chunk, self.chunk), self.chunk)

            @pl.when(me > 0)
            def _():
                remote(self.src.at[rows], self.place(me, s), self.sent.at[0], self.recv.at[me, s], left).start()

            @pl.when(me < n - 1)
            def _():
                remote(self.src.at[rows], self.place(me, s), self.sent.at[1], self.recv.at[me, s], right).start()

        for away in range(1, n):
            at = s - away * self.hop
            for sign, onward in ((-1, right), (1, left)):
                tp = me + sign * away

                @pl.when((tp >= 0) & (tp < n) & (at >= 0) & (at < count))
                def _(tp=tp, onward=onward, sign=sign, at=at):
                    here = self.place(tp, at)
                    wait_came(here, self.sent.at[2], self.recv.at[tp, at])

                    @pl.when((me < n - 1) if sign < 0 else (me > 0))
                    def _():
                        remote(here, here, self.sent.at[2], self.recv.at[tp, at], onward).start()

    def drain(self):
        n, me = self.n, self.me

        @pl.when(me > 0)
        def _():
            wait_sent(self.src, self.sent.at[0], self.recv.at[0, 0])

        @pl.when(me < n - 1)
        def _():
            wait_sent(self.src, self.sent.at[1], self.recv.at[0, 0])

        @pl.when((me > 0) & (me < n - 1))
        def _():
            wait_sent(self.dst.at[:, pl.ds(0, (n - 1) * self.width)], self.sent.at[2], self.recv.at[0, 0])

    @staticmethod
    def scratch(n, count):
        return [
            pltpu.SemaphoreType.DMA((n, count)),
            pltpu.SemaphoreType.DMA((3,)),
            pltpu.SemaphoreType.DMA,
        ]


class LineSum:
    def __init__(self, n, chunk, hop, part, from_left, from_right, out, recv, sent, finish, pushed=False):
        self.n, self.chunk, self.hop, self.pushed = n, chunk, hop, pushed
        self.total_rows = part.shape[0]
        self.owners = (n // 2 - 1, n // 2)
        self.count = self.total_rows // 2 // chunk
        self.part, self.from_left, self.from_right, self.out = part, from_left, from_right, out
        self.recv, self.sent = recv, sent
        self.finish = finish
        self.me = lax.axis_index("tp")

    def steps(self):
        return self.count + self.hop * 2 * (self.n // 2)

    def turn(self, at):
        return lax.rem(at, self.recv.shape[2])

    def rows(self, slot, at):
        return pl.ds(pl.multiple_of((at * 2 + slot) * self.chunk, self.chunk), self.chunk)

    def send(self, here, side, slot, at):
        held = self.from_left if side == 0 else self.from_right
        to = {"tp": self.me + 1} if side == 0 else {"tp": self.me - 1}

        @pl.when(here)
        def _():
            rows = self.rows(slot, at)
            remote(self.part.at[rows], held.at[rows], self.sent.at[0], self.recv.at[side, slot, self.turn(at)],
                   to).start()

    def push(self, at):
        for slot, owner in enumerate(self.owners):
            if owner > 0:
                self.send(self.me == 0, 0, slot, at)
            if owner < self.n - 1:
                self.send(self.me == self.n - 1, 1, slot, at)

    def step(self, s):
        n, me, hop = self.n, self.me, self.hop
        left, right = {"tp": me - 1}, {"tp": me + 1}
        reach = n // 2
        for slot, owner in enumerate(self.owners):
            for side in (0, 1):
                lag = me if side == 0 else n - 1 - me
                at = s - hop * lag
                here = (me < owner) if side == 0 else (me > owner)
                held = self.from_left if side == 0 else self.from_right
                to = right if side == 0 else left
                here = here & (at >= 0) & (at < self.count)

                if not self.pushed:
                    self.send(here & (lag == 0), side, slot, at)

                if n > 2:

                    @pl.when(here & (lag > 0))
                    def _(at=at, held=held, to=to, side=side, slot=slot):
                        rows = self.rows(slot, at)
                        wait_came(held.at[rows], self.sent.at[0], self.recv.at[side, slot, self.turn(at)])
                        held[rows, :] = (held[rows, :].astype(F32) + self.part[rows, :].astype(F32)).astype(BF16)
                        remote(held.at[rows], held.at[rows], self.sent.at[0],
                               self.recv.at[side, slot, self.turn(at)], to).start()

            at = s - hop * reach

            @pl.when((me == owner) & (at >= 0) & (at < self.count))
            def _(at=at, slot=slot, owner=owner):
                rows = self.rows(slot, at)
                total = self.part[rows, :].astype(F32)
                if owner > 0:
                    wait_came(self.from_left.at[rows], self.sent.at[0], self.recv.at[0, slot, self.turn(at)])
                    total = total + self.from_left[rows, :].astype(F32)
                wait_came(self.from_right.at[rows], self.sent.at[0], self.recv.at[1, slot, self.turn(at)])
                total = total + self.from_right[rows, :].astype(F32)
                own = pl.ds(pl.multiple_of(at * self.chunk, self.chunk), self.chunk)
                self.out[rows, :] = self.finish(rows, own, total)
                if owner > 0:
                    remote(self.out.at[rows], self.out.at[rows], self.sent.at[1],
                           self.recv.at[2, slot, self.turn(at)], left).start()
                remote(self.out.at[rows], self.out.at[rows], self.sent.at[2],
                       self.recv.at[2, slot, self.turn(at)], right).start()

        for slot, owner in enumerate(self.owners):
            away = jnp.abs(me - owner)
            at = s - hop * (reach + away)

            @pl.when((me != owner) & (at >= 0) & (at < self.count))
            def _(at=at, slot=slot, owner=owner):
                rows = self.rows(slot, at)
                here = self.out.at[rows]
                wait_came(here, self.sent.at[3], self.recv.at[2, slot, self.turn(at)])

                @pl.when((me < owner) & (me > 0))
                def _():
                    remote(here, here, self.sent.at[3], self.recv.at[2, slot, self.turn(at)], left).start()

                @pl.when((me > owner) & (me < n - 1))
                def _():
                    remote(here, here, self.sent.at[3], self.recv.at[2, slot, self.turn(at)], right).start()

    def drain(self):
        n, me, half = self.n, self.me, self.total_rows // 2
        lo, hi = self.owners

        def wait(sem, size):
            wait_sent(self.part.at[pl.ds(0, size)], self.sent.at[sem], self.recv.at[0, 0, 0])

        middle = (me == lo) | (me == hi)

        @pl.when(middle)
        def _():
            wait(0, half)
            wait(2, half)

        @pl.when((me != lo) & (me != hi))
        def _():
            wait(0, 2 * half)

        if lo > 0:

            @pl.when(middle)
            def _():
                wait(1, half)
                wait(3, half)

            if n > 4:

                @pl.when((me != lo) & (me != hi) & (me > 0) & (me < n - 1))
                def _():
                    wait(3, 2 * half)
        else:

            @pl.when(me == hi)
            def _():
                wait(1, half)

    @staticmethod
    def scratch(n, rows, width, chunk):
        return [
            pltpu.VMEM((rows, width), BF16),
            pltpu.VMEM((rows, width), BF16),
            pltpu.SemaphoreType.DMA((3, 2, min(rows // 2 // chunk, 12))),
            pltpu.SemaphoreType.DMA((4,)),
        ]


class GradSum:
    def __init__(self, fsdp, ctx, parts, axes, outs, held, recv, sent):
        self.fsdp, self.ctx, self.parts, self.axes, self.outs = fsdp, ctx, parts, axes, outs
        self.ys = fsdp // 2
        self.held, self.recv, self.sent = held, recv, sent
        self.f = lax.axis_index("fsdp")
        self.x = lax.axis_index("ctx")
        self.y, self.c = self.f // 2, lax.rem(self.f, 2)

    @staticmethod
    def block_shape(shape, axis, fsdp):
        r, c = shape
        return (r // fsdp, c) if axis == 0 else (r, c // fsdp)

    @staticmethod
    def scratch(fsdp, ctx, shapes, first=True):
        held = []
        for shape in shapes:
            if first:
                held.append(pltpu.VMEM((fsdp // 2,) + shape, BF16))
            held += [
                pltpu.VMEM((max(fsdp // 2 - 1, 1),) + shape, BF16),
                pltpu.VMEM((ctx,) + shape, BF16),
            ]
        return held

    @staticmethod
    def semaphores(fsdp, ctx, count):
        return [pltpu.SemaphoreType.DMA((count, 3, max(fsdp // 2, ctx)))] * 2

    def part(self, a, f):
        shape = self.held[a][0].shape[1:]
        return block(self.parts[a], self.axes[a], f, shape[self.axes[a]])

    def each(self, a, body):
        rows = self.held[a][0].shape[1]
        size = 32 if rows % 32 == 0 else 16

        def step(i, carry):
            body(pl.ds(pl.multiple_of(i * size, size), size))
            return carry

        lax.fori_loop(0, rows // size, step, 0)

    def start(self):
        for a in range(len(self.parts)):
            for k in range(self.ys):
                remote(self.part(a, 2 * k + 1 - self.c), self.held[a][0].at[k], self.sent.at[a, 0, k],
                       self.recv.at[a, 0, k], {"fsdp": sibling(self.f)}).start()

    def pair(self):
        for a in range(len(self.parts)):
            first = self.held[a][0]
            for k in range(self.ys):
                wait_came(first.at[k], self.sent.at[a, 0, k], self.recv.at[a, 0, k])
                mine = self.part(a, 2 * k + self.c)

                def add(rows, first=first, k=k, mine=mine):
                    first[k, rows, :] = (first[k, rows, :].astype(F32) + mine[rows, :].astype(F32)).astype(BF16)

                self.each(a, add)

    def second(self):
        for a in range(len(self.held)):
            first, later = self.held[a][0], self.held[a][1]
            for k in range(1, self.ys):
                to = lax.rem(self.y + k, self.ys)
                remote(first.at[to], later.at[k - 1], self.sent.at[a, 1, k], self.recv.at[a, 1, k],
                       {"fsdp": 2 * to + self.c}).start()

    def third(self):
        for a in range(len(self.held)):
            first, later, last = self.held[a]
            for k in range(1, self.ys):
                wait_came(later.at[k - 1], self.sent.at[a, 1, k], self.recv.at[a, 1, k])

            def add(rows, first=first, later=later, last=last):
                total = first[self.y, rows, :].astype(F32)
                for k in range(1, self.ys):
                    total = total + later[k - 1, rows, :].astype(F32)
                last[self.x, rows, :] = total.astype(BF16)

            self.each(a, add)
            for k in range(1, self.ctx):
                remote(last.at[self.x], last.at[self.x], self.sent.at[a, 2, k], self.recv.at[a, 2, self.x],
                       {"ctx": lax.rem(self.x + k, self.ctx)}).start()

    def fourth(self, store):
        for a in range(len(self.held)):
            last = self.held[a][2]
            for k in range(1, self.ctx):
                other = lax.rem(self.x + k, self.ctx)
                wait_came(last.at[other], self.sent.at[a, 2, k], self.recv.at[a, 2, other])

            def add(rows, last=last, a=a):
                total = last[0, rows, :].astype(F32)
                for k in range(1, self.ctx):
                    total = total + last[k, rows, :].astype(F32)
                store(a, rows, total)

            self.each(a, add)

    def drain_pair(self):
        for a in range(len(self.parts)):
            for k in range(self.ys):
                wait_sent(self.held[a][0].at[k], self.sent.at[a, 0, k], self.recv.at[a, 0, k])

    def drain(self):
        for a in range(len(self.held)):
            first, later, last = self.held[a]
            for k in range(1, self.ys):
                wait_sent(later.at[k - 1], self.sent.at[a, 1, k], self.recv.at[a, 1, k])
            for k in range(1, self.ctx):
                wait_sent(last.at[self.x], self.sent.at[a, 2, k], self.recv.at[a, 2, 0])


def loop(first, last, body):
    def step(s, carry):
        body(s)
        return carry

    lax.fori_loop(first, last, step, 0)


def params(ident, mib):
    return pltpu.CompilerParams(collective_id=ident, has_side_effects=True, vmem_limit_bytes=min(mib << 20, 67043328))


def shape_of(shape, dtype):
    return jax.ShapeDtypeStruct(shape, dtype)


TILE = 256


def dot(left, right):
    return jnp.dot(left, right, preferred_element_type=F32)


def dot_t(left, right):
    return lax.dot_general(left, right, (((1,), (1,)), ((), ())), preferred_element_type=F32)


def dot_rows(left, right):
    return lax.dot_general(left, right, (((0,), (0,)), ((), ())), preferred_element_type=F32)


def head_only(value, head):
    lane = lax.broadcasted_iota(jnp.int32, value.shape, 1)
    return jnp.where((lane // HEAD_DIM) == head, value, jnp.zeros_like(value))


class RowGather:
    def __init__(self, n, src, dst, recv, sent, own):
        self.n, self.src, self.dst = n, src, dst
        self.recv, self.sent, self.own = recv, sent, own
        self.me = lax.axis_index("tp")

    def start(self):
        me = self.me
        pltpu.make_async_copy(self.src, self.dst.at[me], self.own).start()

        @pl.when(me > 0)
        def _():
            remote(self.src, self.dst.at[me], self.sent.at[0, 0], self.recv.at[me], {"tp": me - 1}).start()

        @pl.when(me < self.n - 1)
        def _():
            remote(self.src, self.dst.at[me], self.sent.at[1, 0], self.recv.at[me], {"tp": me + 1}).start()

    def each(self, body, which=None):
        me, n = self.me, self.n
        for away in which or range(1, n):
            for way, tp in ((1, me - away), (0, me + away)):

                @pl.when((tp >= 0) & (tp < n))
                def _(tp=tp, way=way, away=away):
                    onward = (me < n - 1) if way == 1 else (me > 0)
                    body(away, way, tp, onward, {"tp": me + 1} if way == 1 else {"tp": me - 1})

    def relay(self, which=None):
        def body(away, way, tp, onward, to):
            here = self.dst.at[tp]
            wait_came(here, self.sent.at[way, away], self.recv.at[tp])

            @pl.when(onward)
            def _():
                remote(here, here, self.sent.at[way, away], self.recv.at[tp], to).start()

        self.each(body, which)

    def finish(self):
        me = self.me
        pltpu.make_async_copy(self.src, self.dst.at[me], self.own).wait()

        @pl.when(me > 0)
        def _():
            wait_sent(self.src, self.sent.at[0, 0], self.recv.at[0])

        @pl.when(me < self.n - 1)
        def _():
            wait_sent(self.src, self.sent.at[1, 0], self.recv.at[0])

        def body(away, way, tp, onward, to):
            @pl.when(onward)
            def _():
                wait_sent(self.src, self.sent.at[way, away], self.recv.at[0])

        self.each(body)

    @staticmethod
    def scratch(n):
        return [
            pltpu.SemaphoreType.DMA((n,)),
            pltpu.SemaphoreType.DMA((2, n)),
            pltpu.SemaphoreType.DMA,
        ]


class AxisSum:
    def __init__(self, axis, n, slots, recv, sent):
        self.axis, self.n, self.slots, self.recv, self.sent = axis, n, slots, recv, sent
        self.at = lax.axis_index(axis)

    def start(self, value):
        self.slots[self.at] = value
        for k in range(1, self.n):
            remote(self.slots.at[self.at], self.slots.at[self.at], self.sent.at[k], self.recv.at[self.at],
                   {self.axis: lax.rem(self.at + k, self.n)}).start()

    def finish(self):
        for k in range(1, self.n):
            other = lax.rem(self.at + k, self.n)
            wait_came(self.slots.at[other], self.sent.at[k], self.recv.at[other])
            wait_sent(self.slots.at[self.at], self.sent.at[k], self.recv.at[other])
        total = self.slots[0]
        for k in range(1, self.n):
            total = total + self.slots[k]
        return total

    @staticmethod
    def scratch(n, shape):
        return [
            pltpu.VMEM((n,) + shape, F32),
            pltpu.SemaphoreType.DMA((n,)),
            pltpu.SemaphoreType.DMA((n,)),
        ]


def window(ctx, tok_dev):
    return min(ctx, (tok_dev * ctx // 2 + tok_dev - 1) // tok_dev + 1)


def key_span(ctx, tok_dev):
    return min(ctx * tok_dev // 2 // TILE, (window(ctx, tok_dev) - 1) * (tok_dev // TILE))


R_ONE, SEGMENT, VALID = 0, 1, 2


def front(tokens, gain1, gain2, w_latent, shards, w_out, wide_shards, segments, fsdp, ctx, n):
    rows, width = tokens.shape
    seq_dev, tok_dev = segments.shape
    latent, q_width = LATENT, shards[0].shape[1]
    wide, chunk = 128, 256
    pieces = rows // chunk
    win = window(ctx, tok_dev)
    full = [shape_of((s.shape[0] * fsdp,) + s.shape[1:], s.dtype) for s in shards]
    wider = [shape_of((s.shape[0], s.shape[1] * fsdp), s.dtype) for s in wide_shards]
    per_group = HEADS // GROUPS * HEAD_DIM
    per_seq = tok_dev // chunk

    def kernel(*refs):
        (tok_in, ga, gb, wlat, wq, wk, wv, wo, wg, wu, seg), refs = refs[:11], refs[11:]
        (xn_out, cols, gain_all, w_lat, w_qry, w_kproj, w_vproj, gate_all, up_all), refs = refs[:9], refs[9:]
        (wo_all, seg_all, lat_all, query, keys, values), refs = refs[:6], refs[6:]
        (gbuf, sbuf, tok, xn, tsem), refs = refs[:5], refs[5:]
        bring = Bring([(tok_in, tok), (xn, xn_out)], tsem)
        bring.start([0])
        x, me = lax.axis_index("ctx"), lax.axis_index("tp")
        gbuf[...] = jnp.zeros_like(gbuf)
        gbuf[0:1, :] = ga[...].astype(F32).reshape(1, -1)
        gbuf[1:2, :] = gb[...].astype(F32).reshape(1, -1)
        sbuf[...] = jnp.zeros_like(sbuf)
        sbuf[0:seq_dev, :] = seg[...]
        meet(n, fsdp, ctx)
        group = me * q_width // per_group
        src_lat = wlat.at[:, pl.ds(pl.multiple_of(group * latent, latent), latent)]
        pairs = [(gbuf, gain_all), (src_lat, w_lat), (wq, w_qry), (wk, w_kproj), (wv, w_vproj),
                 (wg, gate_all), (wu, up_all)]
        spread = Spread(fsdp, pairs, [1, 0, 0, 0, 0, 1, 1], *refs[:3])
        share = CtxShare(ctx, sbuf, seg_all, *refs[3:6])
        line = RowGather(n, wo, wo_all, *refs[6:9])
        lat_recv, lat_sent = refs[9:11]
        spread.start()
        share.start()
        line.start()
        own = win - 1
        cols[...] = jnp.zeros_like(cols)
        bring.wait([0])

        def scale(i):
            at = pl.ds(pl.multiple_of(i * wide, wide), wide)
            value = tok[at, :].astype(F32)
            cols[at, R_ONE : R_ONE + 1] = lax.rsqrt(jnp.mean(value * value, axis=-1, keepdims=True) + eps)

        loop(0, rows // wide, scale)
        spread.relay([0, 1])
        spread.finish([0, 1])

        def place(shard, i):
            seq = i // per_seq
            return pl.ds(pl.multiple_of(seq * win * tok_dev + shard * tok_dev + lax.rem(i, per_seq) * chunk, chunk), chunk)

        def send(k, i):
            return remote(lat_all.at[place(own, i)], lat_all.at[place(own - k, i)], lat_sent.at[k, i],
                          lat_recv.at[own - k, i], {"ctx": x + k})

        def first(i):
            at = pl.ds(pl.multiple_of(i * chunk, chunk), chunk)
            unit = (tok[at, :].astype(F32) * cols[at, R_ONE : R_ONE + 1] * gain_all[0:1, :]).astype(BF16)
            xn[at, :] = unit
            lat_all[place(own, i), :] = dot(unit, w_lat[...]).astype(BF16)
            for k in range(1, win):

                @pl.when(x + k < ctx)
                def _(k=k):
                    send(k, i).start()

        loop(0, pieces, first)
        bring.start([1])
        line.relay([1])
        spread.relay([2, 3, 4])
        spread.finish([2, 3, 4])

        def project(shard, i):
            to = place(shard, i)
            value = lat_all[to, :]
            keys[to, :] = dot(value, w_kproj[...]).astype(BF16)
            values[to, :] = dot(value, w_vproj[...]).astype(BF16)

        def ask(i):
            at = pl.ds(pl.multiple_of(i * chunk, chunk), chunk)
            query[at, :] = dot(xn[at, :], w_qry[...]).astype(BF16)
            project(own, i)

        loop(0, pieces, ask)
        share.finish()
        for q in range(seq_dev):
            at = slice(q * tok_dev, (q + 1) * tok_dev)
            ids = jnp.broadcast_to(sbuf[q : q + 1, :].astype(F32), (128, tok_dev)).T
            cols[at, SEGMENT : SEGMENT + 1] = ids[:, 0:1]
            last = seg_all[ctx - 1, q : q + 1, tok_dev - 1 : tok_dev].astype(F32)
            cols[at, VALID : VALID + 1] = jnp.where(ids[:, 0:1] != last, 1.0, 0.0)
        line.relay(range(2, n))
        for k in range(1, win):

            def theirs(i, k=k):
                @pl.when(x - k >= 0)
                def _():
                    wait_came(lat_all.at[place(own - k, i)], lat_sent.at[k, i], lat_recv.at[own - k, i])

                @pl.when(x - k < 0)
                def _():
                    lat_all[place(own - k, i), :] = jnp.zeros((chunk, latent), BF16)

                project(own - k, i)

            loop(0, pieces, theirs)

            def gone(i, k=k):
                @pl.when(x + k < ctx)
                def _():
                    send(k, i).wait_send()

            loop(0, pieces, gone)
        spread.relay([5, 6])
        spread.finish([5, 6])
        line.finish()
        bring.wait([1])

    return pl.pallas_call(
        kernel,
        out_shape=(
            shape_of((rows, width), BF16),
            shape_of((rows, 128), F32),
            shape_of((8, width), F32),
            shape_of((width, latent), BF16),
            *full,
            *wider,
            shape_of((n,) + w_out.shape, w_out.dtype),
            shape_of((ctx, 8, tok_dev), segments.dtype),
            shape_of((win * rows, latent), BF16),
            shape_of((rows, q_width), BF16),
            shape_of((win * rows, q_width), BF16),
            shape_of((win * rows, q_width), BF16),
        ),
        in_specs=[ANY] + [VMEM] * 10,
        out_specs=(ANY,) + (VMEM,) * 6 + (ANY,) * 3 + (VMEM,) * 5,
        scratch_shapes=[
            pltpu.VMEM((8, gain1.shape[0]), F32),
            pltpu.VMEM((8, tok_dev), segments.dtype),
            pltpu.VMEM((rows, width), BF16),
            pltpu.VMEM((rows, width), BF16),
            pltpu.SemaphoreType.DMA((2,)),
        ]
        + Spread.scratch(fsdp, 7)
        + CtxShare.scratch(ctx)
        + RowGather.scratch(n)
        + [pltpu.SemaphoreType.DMA((win, pieces))] * 2,
        compiler_params=params(1, 56),
    )(tokens, gain1, gain2, w_latent, *shards, w_out, *wide_shards, segments)


def counted_keys(cols, segk, at, seq, q_first, first, count, tok_dev, win):
    per = tok_dev // TILE
    oldest = lax.axis_index("ctx") - (win - 1)
    mine = cols[at, SEGMENT : SEGMENT + 1]
    shape = (mine.shape[0], TILE)
    pieces = []
    for j in range(count):
        t = first + j
        shard = oldest + t // per
        inner = pl.ds(pl.multiple_of(lax.rem(t, per) * TILE, TILE), TILE)
        ids = segk[jnp.maximum(shard, 0), pl.ds(seq, 1), inner].astype(F32)
        q_at = q_first + lax.broadcasted_iota(jnp.int32, shape, 0)
        k_at = t * TILE + lax.broadcasted_iota(jnp.int32, shape, 1)
        pieces.append((k_at <= q_at) & (ids == mine) & (shard >= 0))
    return pieces


def middle(query, keys, values, seg_all, cols, shards, gate_all, up_all, gains, tokens, out_grad,
           fsdp, ctx, n, seq_dev, late):
    rows, width = tokens.shape
    q_width = query.shape[1]
    heads = q_width // HEAD_DIM
    inner = gate_all.shape[0]
    tok_dev = rows // seq_dev
    per = tok_dev // TILE
    win, span = window(ctx, tok_dev), key_span(ctx, tok_dev)
    tiles = span + 1
    part = TILE if tiles <= 3 else 64
    chunk, hop = 32, 2
    size, piece = 256, 64
    per_block = size // piece
    half = rows // 2
    cols_at = width // 4
    block_shape = (inner, width // fsdp)
    count = 3

    def kernel(*refs):
        (q_in, k_in, v_in, segk, cols, wo_in, wd_in, wg_in, wu_in, gain, tok_in, cot_in), refs = refs[:12], refs[12:]
        (o_branch, o_feed, o_dmid, o_mid, o_wo, o_gain, o_bsq, o_mark, o_att, o_lse), refs = refs[:10], refs[10:]
        outs, refs = refs[:3], refs[3:]
        one, gsems, parts, refs = refs[:4], refs[4:6], refs[6:9], refs[9:]
        (query, keys, values, att, att_all, wo, wd, wg, wu, tok, cot), refs = refs[:11], refs[11:]
        (mid, r2, xn, hid, dg, du, p_two, p_feed, bsem), refs = refs[:9], refs[9:]
        bring = Bring([(q_in, query), (k_in, keys), (v_in, values), (tok_in, tok), (wg_in, wg), (wu_in, wu),
                       (cot_in, cot), (att, o_att), (p_feed, o_feed)], bsem)
        bring.start(range(7))
        meet(n, fsdp, ctx)
        line = LineGather(n, piece, att, att_all, *refs[:3])
        spread = Spread(fsdp, [(wo_in, wo), (wd_in, wd)], [1, 1], *refs[3:6])
        keep = refs[6:]
        spread.start()
        o_gain[...] = jnp.zeros_like(o_gain)
        o_bsq[...] = jnp.zeros_like(o_bsq)
        o_mark[...] = jnp.zeros_like(o_mark)
        g2 = gain.at[1:2]

        def back(at, own, total):
            middle_rows = mid[at, :]
            o_mid[own, :] = middle_rows
            unit = middle_rows * r2[at, :]
            o_gain[...] += jnp.sum((total * unit).reshape(chunk // 8, 8, width), axis=0)
            scaled = total * g2[...]
            mean = jnp.mean(scaled * unit, axis=-1, keepdims=True)
            d_mid = cot[at, :].astype(F32) + r2[at, :] * (scaled - unit * mean)
            o_dmid[own, :] = d_mid
            first_unit = tok[at, :].astype(F32) * cols[at, R_ONE : R_ONE + 1]
            o_mark[at, 0:1] = jnp.sum(first_unit * d_mid, axis=-1, keepdims=True)
            return d_mid.astype(BF16)

        first = LineSum(n, chunk, hop, p_two, one[0], one[1], o_branch, one[2], one[3], back)
        if late:
            held = [[out, None, None] for out in outs]
        else:
            held = [keep[3 * a : 3 * a + 3] for a in range(count)]
        grad = GradSum(fsdp, ctx, parts, [1] * count, outs, held, *gsems)
        bring.wait([0, 1, 2])

        def query_rows(i, j):
            seq = i // per
            q_tile = (win - 1) * per + lax.rem(i, per)
            at = pl.ds(pl.multiple_of(i * TILE + j * part, part), part)
            near = pl.ds(pl.multiple_of((seq * win * per + q_tile - span) * TILE, TILE), tiles * TILE)
            counted = jnp.concatenate(
                [
                    c.astype(F32)
                    for c in counted_keys(
                        cols, segk, at, seq, q_tile * TILE + j * part, q_tile - span, tiles, tok_dev, win
                    )
                ],
                axis=1,
            )
            accum = jnp.zeros((part, q_width), F32)
            lane = lax.broadcasted_iota(jnp.int32, (part, 128), 1)
            kept = jnp.zeros((part, 128), F32)
            for h in range(heads):
                score = jnp.where(counted > 0.0, dot_t(head_only(query[at, :], h), keys[near, :]) * 0.125, -1e30)
                top = jnp.max(score, axis=-1, keepdims=True)
                weight = jnp.exp(score - top)
                total = jnp.sum(weight, axis=-1, keepdims=True)
                prob = (weight * (1.0 / total)).astype(BF16)
                accum = accum + jnp.dot(prob, head_only(values[near, :], h), preferred_element_type=F32)
                kept = jnp.where(lane == h, top + jnp.log(total), kept)
                if part == TILE:
                    line.step((i - 1) * per_block + h * per_block // heads)
            o_lse[at, :] = kept
            att[at, :] = accum.astype(BF16)

        def query_tile(i):
            if part == TILE:
                query_rows(i, 0)
                return
            loop(0, TILE // part, lambda j: query_rows(i, j))
            for h in range(per_block):
                line.step((i - 1) * per_block + h)

        loop(0, rows // TILE, query_tile)
        bring.start([7])
        line.begin()
        s1 = (rows // TILE - 1) * per_block
        spread.relay()
        spread.finish()
        tp = lax.axis_index("tp")
        o_wo[...] = wo[pl.ds(pl.multiple_of(tp * q_width, q_width), q_width), :]
        line.begun()
        bring.wait([3, 4, 5, 6])

        def block_of_rows(b):
            at = pl.ds(pl.multiple_of(b * size, size), size)
            seq = b * size // tok_dev

            def steps(j):
                line.step(s1 + b * per_block + j)
                first.step((b - 1) * per_block + j)

            branch = dot(att_all[at, :], wo[...])
            middle_rows = tok[at, :].astype(F32) + branch
            mid[at, :] = middle_rows
            o_bsq[pl.ds(pl.multiple_of(seq * 8, 8), 8), :] += jnp.sum(
                (branch * branch * cols[at, VALID : VALID + 1]).reshape(size // 8, 8, width), axis=0
            )
            scale = lax.rsqrt(jnp.mean(middle_rows * middle_rows, axis=-1, keepdims=True) + eps)
            r2[at, :] = scale
            unit = (middle_rows * scale * g2[...]).astype(BF16)
            xn[at, :] = unit
            steps(0)
            gate = dot_t(unit, wg[...])
            upper = dot_t(unit, wu[...])
            sigma = jax.nn.sigmoid(gate)
            swish = gate * sigma
            hidden = (swish * upper).astype(BF16)
            hid[at, :] = hidden
            slope = upper * sigma * (1.0 + gate * (1.0 - sigma))
            steps(1)
            p_feed[at, :] = dot(hidden, wd[...]).astype(BF16)
            d_hidden = dot_t(cot[at, :], wd[...])
            d_gate = (d_hidden * slope).astype(BF16)
            d_upper = (d_hidden * swish).astype(BF16)
            dg[at, :] = d_gate
            du[at, :] = d_upper
            steps(2)
            p_two[at, :] = (dot(d_gate, wg[...]) + dot(d_upper, wu[...])).astype(BF16)
            steps(3)

        loop(0, rows // size, block_of_rows)
        bring.start([8])
        s0 = (rows // size - 1) * per_block

        def product(i):
            at = pl.ds(pl.multiple_of(i * cols_at, cols_at), cols_at)
            left = xn[:, at]
            parts[0][:, at] = dot_rows(dg[...], left).astype(BF16)
            parts[1][:, at] = dot_rows(du[...], left).astype(BF16)
            parts[2][:, at] = dot_rows(hid[...], cot[:, at]).astype(BF16)

        def busy(s):
            first.step(s)
            product(s - s0)

        loop(s0, s0 + 4, busy)
        grad.start()
        last = first.steps()
        loop(s0 + 4, s0 + 6, first.step)
        grad.pair()
        if not late:
            grad.second()
        loop(s0 + 6, last, first.step)
        if not late:
            grad.third()

            def store(a, at, total):
                outs[a][at, :] = total

            grad.fourth(store)
            grad.drain()
        line.drain()
        first.drain()
        grad.drain_pair()
        bring.wait([7, 8])

    ys = fsdp // 2
    out = pl.pallas_call(
        kernel,
        out_shape=(
            shape_of((rows, width), BF16),
            shape_of((rows, width), BF16),
            shape_of((half, width), F32),
            shape_of((half, width), F32),
            shape_of((q_width, width), BF16),
            shape_of((8, width), F32),
            shape_of((8 * seq_dev, width), F32),
            shape_of((rows, 128), F32),
            shape_of((rows, q_width), BF16),
            shape_of((rows, 128), F32),
        )
        + ((shape_of((ys,) + block_shape, BF16) if late else shape_of(block_shape, F32)),) * count,
        in_specs=[ANY] * 3 + [VMEM] * 4 + [ANY] * 2 + [VMEM] + [ANY] * 2,
        out_specs=(VMEM, ANY) + (VMEM,) * 6 + (ANY, VMEM) + (VMEM,) * count,
        scratch_shapes=LineSum.scratch(n, rows, width, chunk)
        + GradSum.semaphores(fsdp, ctx, count)
        + [pltpu.VMEM((inner, width), BF16)] * count
        + [
            pltpu.VMEM((rows, q_width), BF16),
            pltpu.VMEM((win * rows, q_width), BF16),
            pltpu.VMEM((win * rows, q_width), BF16),
            pltpu.VMEM((rows, q_width), BF16),
            pltpu.VMEM((rows, n * q_width), BF16),
            pltpu.VMEM((n * q_width, width), BF16),
            pltpu.VMEM((inner, width), BF16),
            pltpu.VMEM((inner, width), BF16),
            pltpu.VMEM((inner, width), BF16),
            pltpu.VMEM((rows, width), BF16),
            pltpu.VMEM((rows, width), BF16),
            pltpu.VMEM((rows, width), F32),
            pltpu.VMEM((rows, 1), F32),
            pltpu.VMEM((rows, width), BF16),
            pltpu.VMEM((rows, inner), BF16),
            pltpu.VMEM((rows, inner), BF16),
            pltpu.VMEM((rows, inner), BF16),
            pltpu.VMEM((rows, width), BF16),
            pltpu.VMEM((rows, width), BF16),
            pltpu.SemaphoreType.DMA((9,)),
        ]
        + LineGather.scratch(n, rows // piece)
        + Spread.scratch(fsdp, 2)
        + ([] if late else GradSum.scratch(fsdp, ctx, [block_shape] * count)),
        compiler_params=params(2, 64),
    )(query, keys, values, seg_all, cols, *shards, gate_all, up_all, gains, tokens, out_grad)
    return out[:10], out[10:]


def back(query, keys, values, seg_all, cols, lse, attended, d_branch, wo_rows, weights, lat_all, xn_one, gains,
         tokens, d_middle, mid_own, part_feed, marks, gain_part, branch_sq, firsts, fsdp, ctx, n, seq_dev):
    rows, width = tokens.shape
    w_qry, w_lat, w_kproj, w_vproj = weights
    q_width, latent = query.shape[1], w_lat.shape[1]
    heads, tok_dev = q_width // HEAD_DIM, rows // seq_dev
    per = tok_dev // TILE
    win, span = window(ctx, tok_dev), key_span(ctx, tok_dev)
    tiles = span + 1
    group = tiles if tiles <= 3 else 1
    chunk, hop, wide, side = 32, 2, 256, 128
    half = rows // 2
    axes = (0, 0, 0, 1, 0)
    whole = ((width, q_width), (latent, q_width), (latent, q_width), (q_width, width), (width, latent))
    blocks = [GradSum.block_shape(w, a, fsdp) for w, a in zip(whole, axes)]
    lat = blocks[-1]
    ffn = [f.shape[1:] for f in firsts]
    seq_pieces = tok_dev // wide
    many = max(width, rows)

    def kernel(*refs):
        (q_ref, k_ref, v_ref, segk, cols, lse_ref, att, dbr, wo), refs = refs[:9], refs[9:]
        (wq, wl, wk, wv, la_in, xn_in, gain, tok_in, dmid_in, mid_in, feed_in), refs = refs[:11], refs[11:]
        (marks, gain_two, bsq), fsts, refs = refs[:3], refs[3 : 3 + len(ffn)], refs[3 + len(ffn) :]
        (o_tok, o_mixed, o_small), outs, refs = refs[:3], refs[3:8], refs[8:]
        fouts, refs = refs[: len(ffn)], refs[len(ffn) :]
        one, two, keep, gsems, parts, refs = refs[:4], refs[4:8], refs[8:23], refs[23:25], refs[25:30], refs[30:]
        (p_one, dlat, came, c_recv, c_sent, gacc, sm, sacc), refs = refs[:8], refs[8:]
        (dk, dv, dq, dqb, grad_seq, lat_parts), refs = refs[:6], refs[6:]
        (la, xn, tok, dmid, mid, p_feed, bsem), refs = refs[:7], refs[7:]
        (lat_own, lat_every), lsems, sums, refs = refs[:2], refs[2:5], refs[5:14], refs[14:]
        bring = Bring([(feed_in, p_feed), (mid_in, mid), (la_in, la), (xn_in, xn), (tok_in, tok), (dmid_in, dmid)], bsem)
        bring.start()
        meet(n, fsdp, ctx, everyone=True)
        x = lax.axis_index("ctx")
        own_shard = win - 1
        grad_ffn = None
        if ffn:
            fkeep, fsems = refs[: 2 * len(ffn)], refs[2 * len(ffn) :]
            grad_ffn = GradSum(fsdp, ctx, [], [], fouts,
                               [[fsts[a], fkeep[2 * a], fkeep[2 * a + 1]] for a in range(len(ffn))], *fsems)
            grad_ffn.second()
        gacc[...] = jnp.zeros_like(gacc)
        sacc[...] = jnp.zeros_like(sacc)
        sm[...] = jnp.zeros_like(sm)
        g1 = gain.at[0:1]

        def forward(at, own, total):
            mixed = mid[own, :] + total
            seq = at.start // tok_dev
            counted = cols[at, VALID : VALID + 1]
            sacc[seq] += jnp.sum((mixed * mixed * counted).reshape(chunk // 8, 8, width), axis=0)
            sacc[seq_dev + seq] += jnp.sum((total * total * counted).reshape(chunk // 8, 8, width), axis=0)
            return mixed.astype(BF16)

        def backward(at, own, total):
            r1 = cols[at, R_ONE : R_ONE + 1]
            unit = tok[at, :].astype(F32) * r1
            scaled = total * g1[...]
            mean = jnp.mean(scaled * unit, axis=-1, keepdims=True)
            return (dmid[own, :] + r1 * (scaled - unit * mean)).astype(BF16)

        feed = LineSum(n, chunk, hop, p_feed, two[0], two[1], o_mixed, two[2], two[3], forward)
        first = LineSum(n, chunk, hop, p_one, one[0], one[1], o_tok, one[2], one[3], backward)
        grad = GradSum(fsdp, ctx, parts, axes, outs, [keep[3 * a : 3 * a + 3] for a in range(5)], *gsems)
        line = RowGather(n, lat_own, lat_every, *lsems)
        over_tp = AxisSum("tp", n, *sums[0:3])
        over_ctx = AxisSum("ctx", ctx, *sums[3:6])
        over_fsdp = AxisSum("fsdp", fsdp, *sums[6:9])

        def clear(i):
            at = pl.ds(pl.multiple_of(i * TILE, TILE), TILE)
            dk[at, :] = jnp.zeros((TILE, q_width), F32)
            dv[at, :] = jnp.zeros((TILE, q_width), F32)

        loop(0, win * rows // TILE, clear)
        bring.wait([0, 1])

        def query_tile(i, step):
            seq = i // per
            q_tile = own_shard * per + lax.rem(i, per)
            at = pl.ds(pl.multiple_of(i * TILE, TILE), TILE)
            grad_seq[...] = dot_t(dbr[at, :], wo[...]).astype(BF16)
            product = grad_seq[...].astype(F32) * att[at, :].astype(F32)
            delta = [jnp.sum(head_only(product, h), axis=-1, keepdims=True) for h in range(heads)]
            dq[...] = jnp.zeros_like(dq)

            def key_tiles(kk):
                t = q_tile - span + kk * group
                near = pl.ds(pl.multiple_of((seq * win * per + t) * TILE, TILE), group * TILE)
                counted = jnp.concatenate(
                    [c.astype(F32) for c in counted_keys(cols, segk, at, seq, q_tile * TILE, t, group, tok_dev, win)], axis=1
                )
                kept = lse_ref[at, :]
                d_query = jnp.zeros((TILE, q_width), F32)
                d_key = jnp.zeros((group * TILE, q_width), F32)
                d_value = jnp.zeros((group * TILE, q_width), F32)
                for h in range(heads):
                    mine, ours = head_only(q_ref[at, :], h), head_only(grad_seq[...], h)
                    score = jnp.where(counted > 0.0, dot_t(mine, k_ref[near, :]) * 0.125, -1e30)
                    prob = jnp.exp(score - kept[:, h : h + 1]) * counted
                    d_score = (prob * (dot_t(ours, v_ref[near, :]) - delta[h])).astype(BF16)
                    d_query = d_query + jnp.dot(d_score, head_only(k_ref[near, :], h), preferred_element_type=F32)
                    d_key = d_key + dot_rows(d_score, mine)
                    d_value = d_value + dot_rows(prob.astype(BF16), ours)
                    step(kk * heads + h)
                dq[...] += d_query
                dk[near, :] += d_key * 0.125
                dv[near, :] += d_value

            loop(0, tiles // group, key_tiles)
            dqb[at, :] = (dq[...] * 0.125).astype(BF16)

        def latent_rows(shard, seq, i):
            return pl.ds(pl.multiple_of((seq * win + shard) * tok_dev + i * wide, wide), wide)

        def send(k, seq, i):
            at = pl.ds(pl.multiple_of(seq * tok_dev + i * wide, wide), wide)
            return remote(lat_parts.at[latent_rows(own_shard - k, seq, i)], came.at[k - 1, at],
                          c_sent.at[k - 1, seq, i], c_recv.at[k - 1, seq, i], {"ctx": x - k})

        def latents(seq):
            for k in range(win - 1, -1, -1):
                for i in range(seq_pieces):
                    at = latent_rows(own_shard - k, seq, i)
                    lat_parts[at, :] = (
                        dot_t(dk[at, :].astype(BF16), wk[...]) + dot_t(dv[at, :].astype(BF16), wv[...])
                    ).astype(BF16)
                    if k > 0:

                        @pl.when(x - k >= 0)
                        def _(k=k, i=i):
                            send(k, seq, i).start()

        def whole_latent(j):
            seq, i = j // seq_pieces, lax.rem(j, seq_pieces)
            at = pl.ds(pl.multiple_of(j * wide, wide), wide)
            dlat[at, :] = lat_parts[latent_rows(own_shard, seq, i), :]
            for k in range(1, win):

                @pl.when(x + k < ctx)
                def _(k=k):
                    wait_came(came.at[k - 1, at], c_sent.at[k - 1, seq, i], c_recv.at[k - 1, seq, i])
                    dlat[at, :] = (dlat[at, :].astype(F32) + came[k - 1, at, :].astype(F32)).astype(BF16)

            p_one[at, :] = (dot_t(dqb[at, :], wq[...]) + dot_t(dlat[at, :], wl[...])).astype(BF16)

        tile_steps = (tiles // group) * heads
        every = max(tile_steps // 4, 1)

        def sequence(seq):
            def tile(i):
                def step(j):
                    @pl.when(lax.rem(j, every) == 0)
                    def _():
                        feed.step(i * (tile_steps // every) + j // every)

                query_tile(i, step)

            loop(seq * per, seq * per + per, tile)
            latents(seq)

        loop(0, seq_dev, sequence)
        fed = seq_dev * per * (tile_steps // every)

        bring.wait([2, 3, 4, 5])

        def product(i):
            at = pl.ds(pl.multiple_of(i * wide, wide), wide)
            parts[0][at, :] = dot_rows(xn[:, at], dqb[...]).astype(BF16)
            parts[3][:, at] = dot_rows(att[...], dbr[:, at]).astype(BF16)

        def steps(s):
            first.step(s)
            feed.step(fed + s)

        early = (seq_dev - 1) * seq_pieces
        loop(0, early, whole_latent)

        def mixed_work(i):
            product(i)
            steps(i)

        loop(0, width // wide, mixed_work)
        s0 = width // wide
        if grad_ffn is not None:
            grad_ffn.third()
        parts[1][...] = dot_rows(la[...], dk[...].astype(BF16)).astype(BF16)
        parts[2][...] = dot_rows(la[...], dv[...].astype(BF16)).astype(BF16)
        loop(early, rows // wide, whole_latent)

        def product_lat(s):
            at = pl.ds(pl.multiple_of((s - s0) * wide, wide), wide)
            parts[4][at, :] = dot_rows(xn[:, at], dlat[...]).astype(BF16)
            steps(s)

        begun = s0 + width // wide
        loop(s0, begun, product_lat)
        grad.start()

        def gains_of(s):
            steps(s)
            at = pl.ds(pl.multiple_of((s - begun) * side, side), side)
            value = p_one[at, :].astype(F32) * (tok[at, :].astype(F32) * cols[at, R_ONE : R_ONE + 1])
            gacc[...] += jnp.sum(value.reshape(side // 8, 8, width), axis=0)
            along = lax.dot_general(jnp.ones((8, width), F32), value * g1[...], (((1,), (1,)), ((), ())),
                                    precision=lax.Precision.HIGHEST, preferred_element_type=F32)
            sm[3:4, at] = along[0:1, :]
            sm[4:5, at] = marks[at, :].T[0:1, :]
            sm[5:6, at] = cols[at, :].T[R_ONE : R_ONE + 1, :]

        mark = begun + rows // side
        loop(begun, begun + 1, gains_of)
        grad.pair()
        grad.second()
        loop(begun + 1, begun + 4, gains_of)
        grad.third()
        loop(begun + 4, mark, gains_of)
        last = first.steps()
        for s in range(fed + mark, feed.steps()):
            feed.step(s)
        lane = lax.broadcasted_iota(jnp.int32, (1, many), 1)
        once = jnp.where(lax.axis_index("tp") == 0, 1.0, 0.0)
        row = jnp.zeros((1, many), F32)

        def whole_sum(value):
            return jnp.sum(jnp.sum(value, axis=0, keepdims=True), axis=1, keepdims=True)

        for q in range(seq_dev):
            values = [
                whole_sum(sacc[q]),
                whole_sum(sacc[seq_dev + q]),
                whole_sum(bsq[8 * q : 8 * q + 8, :]) * once,
                jnp.sum(cols[q * tok_dev : (q + 1) * tok_dev, VALID : VALID + 1], axis=0, keepdims=True) * once,
            ]
            for j, value in enumerate(values):
                row = row + jnp.where(lane == 4 * q + j, value, 0.0)
        sm[2:3, :] = row
        sm[0:1, 0:width] = jnp.sum(gacc[...], axis=0, keepdims=True)
        sm[1:2, 0:width] = jnp.sum(gain_two[...], axis=0, keepdims=True)
        r_row = sm[5:6, :]
        over_tp.start(sm[...])

        def store(a, at, total):
            if a < 4:
                outs[a][at, :] = total
            else:
                lat_own[at, :] = total.astype(BF16)

        def store_ffn(a, at, total):
            fouts[a][at, :] = total

        grad.fourth(store)
        line.start()
        loop(mark, mark + 2, steps)
        line.relay([1])
        along_tp = over_tp.finish()
        over_ctx.start(along_tp)
        loop(mark + 2, mark + 4, steps)
        if n > 2:
            line.relay([2])
        along_ctx = over_ctx.finish()
        over_fsdp.start(along_ctx)
        if grad_ffn is not None:
            grad_ffn.fourth(store_ffn)
        loop(mark + 4, last, steps)
        if n > 3:
            line.relay(range(3, n))
        everywhere = over_fsdp.finish()
        row = lax.broadcasted_iota(jnp.int32, everywhere.shape, 0)
        o_small[...] = jnp.where(row < 2, everywhere, along_ctx)
        o_small[3:4, :] = (along_tp[4:5] + eps * r_row * r_row * r_row * along_tp[3:4]) * (1.0 / width**0.5)
        line.finish()

        def gather(i):
            at = pl.ds(pl.multiple_of(i * 16, 16), 16)
            for g in range(GROUPS):
                total = jnp.zeros((16, lat[1]), F32)
                for t in range(n):
                    if t * GROUPS // n == g:
                        total = total + lat_every[t, at, :].astype(F32)
                outs[4][at, g * lat[1] : (g + 1) * lat[1]] = total

        loop(0, lat[0] // 16, gather)
        for k in range(1, win):

            @pl.when(x - k >= 0)
            def _(k=k):
                for seq in range(seq_dev):
                    for i in range(seq_pieces):
                        send(k, seq, i).wait_send()

        feed.drain()
        first.drain()
        grad.drain_pair()
        grad.drain()
        if grad_ffn is not None:
            grad_ffn.drain()

    out = pl.pallas_call(
        kernel,
        out_shape=(
            shape_of((rows, width), BF16),
            shape_of((rows, width), BF16),
            shape_of((8, many), F32),
        )
        + tuple(shape_of(b, F32) for b in blocks[:-1])
        + (shape_of((lat[0], GROUPS * lat[1]), F32),)
        + tuple(shape_of(f, F32) for f in ffn),
        in_specs=[VMEM] * 13 + [ANY] * 2 + [VMEM] + [ANY] * 4 + [VMEM] * (3 + len(ffn)),
        out_specs=(VMEM,) * (8 + len(ffn)),
        scratch_shapes=LineSum.scratch(n, rows, width, chunk) * 2
        + GradSum.scratch(fsdp, ctx, blocks)
        + GradSum.semaphores(fsdp, ctx, 5)
        + [pltpu.VMEM(w, BF16) for w in whole]
        + [
            pltpu.VMEM((rows, width), BF16),
            pltpu.VMEM((rows, latent), BF16),
            pltpu.VMEM((max(win - 1, 1), rows, latent), BF16),
            pltpu.SemaphoreType.DMA((max(win - 1, 1), seq_dev, seq_pieces)),
            pltpu.SemaphoreType.DMA((max(win - 1, 1), seq_dev, seq_pieces)),
            pltpu.VMEM((8, width), F32),
            pltpu.VMEM((8, many), F32),
            pltpu.VMEM((2 * seq_dev, 8, width), F32),
            pltpu.VMEM((win * rows, q_width), F32),
            pltpu.VMEM((win * rows, q_width), F32),
            pltpu.VMEM((TILE, q_width), F32),
            pltpu.VMEM((rows, q_width), BF16),
            pltpu.VMEM((TILE, q_width), BF16),
            pltpu.VMEM((win * rows, latent), BF16),
        ]
        + [
            pltpu.VMEM((win * rows, latent), BF16),
            pltpu.VMEM((rows, width), BF16),
            pltpu.VMEM((rows, width), BF16),
            pltpu.VMEM((half, width), F32),
            pltpu.VMEM((half, width), F32),
            pltpu.VMEM((rows, width), BF16),
            pltpu.SemaphoreType.DMA((6,)),
        ]
        + [pltpu.VMEM(lat, BF16), pltpu.VMEM((n,) + lat, BF16)]
        + RowGather.scratch(n)
        + AxisSum.scratch(n, (8, many))
        + AxisSum.scratch(ctx, (8, many))
        + AxisSum.scratch(fsdp, (8, many))
        + (GradSum.scratch(fsdp, ctx, ffn, False) + GradSum.semaphores(fsdp, ctx, len(ffn)) if ffn else []),
        compiler_params=params(3, 64),
    )(query, keys, values, seg_all, cols, lse, attended, d_branch, wo_rows, w_qry, w_lat, w_kproj, w_vproj,
      lat_all, xn_one, gains, tokens, d_middle, mid_own, part_feed, marks, gain_part, branch_sq, *firsts)
    return out[:3], out[3:8], out[8:]


def publish(arrays, small, seq_dev, tok_dev, feat_dim, fsdp):
    count = len(arrays)
    per = feat_dim // fsdp

    def kernel(*refs):
        srcs, sm, refs = refs[:count], refs[count], refs[count + 1 :]
        dsts, (gain1, gain2, stats, radial), refs = refs[:count], refs[count : count + 4], refs[count + 4 :]
        inward = Bring(list(zip(srcs, refs[:count])), refs[count])
        outward = Bring(list(zip(refs[:count], dsts)), refs[count + 1])
        inward.start()
        f = lax.axis_index("fsdp")
        mine = pl.ds(pl.multiple_of(f * per, per), per)
        gain1[...] = sm[0:1, mine].reshape(per)
        gain2[...] = sm[1:2, mine].reshape(per)
        for q in range(seq_dev):
            radial[q : q + 1, :] = sm[3:4, q * tok_dev : (q + 1) * tok_dev]
            total = sm[2:3, 4 * q + 3 : 4 * q + 4] * feat_dim
            for j, lane in enumerate((0, 2, 1)):
                stats[q : q + 1, j : j + 1] = jnp.sqrt(sm[2:3, 4 * q + lane : 4 * q + lane + 1] / total)
        for i in range(count):
            inward.wait([i])
            outward.start([i])
        outward.wait()

    out = pl.pallas_call(
        kernel,
        out_shape=tuple(shape_of(a.shape, a.dtype) for a in arrays)
        + (shape_of((per,), F32),) * 2
        + (shape_of((seq_dev, 3), F32), shape_of((seq_dev, tok_dev), F32)),
        in_specs=[ANY] * count + [VMEM],
        out_specs=(ANY,) * count + (VMEM,) * 4,
        scratch_shapes=[pltpu.VMEM(a.shape, a.dtype) for a in arrays] + [pltpu.SemaphoreType.DMA((count,))] * 2,
        compiler_params=pltpu.CompilerParams(vmem_limit_bytes=60 << 20),
    )(*arrays, small)
    return out[:count], out[count:]


class AxisShare:
    def __init__(self, axis, n, src, dst, recv, sent, own):
        self.axis, self.n, self.src, self.dst = axis, n, src, dst
        self.recv, self.sent, self.own = recv, sent, own
        self.at = lax.axis_index(axis)

    def start(self):
        for k in range(1, self.n):
            remote(self.src, self.dst.at[self.at], self.sent.at[k - 1], self.recv.at[self.at],
                   {self.axis: lax.rem(self.at + k, self.n)}).start()
        pltpu.make_async_copy(self.src, self.dst.at[self.at], self.own).start()

    def finish(self):
        for k in range(1, self.n):
            other = lax.rem(self.at + k, self.n)
            wait_came(self.dst.at[other], self.sent.at[k - 1], self.recv.at[other])
            wait_sent(self.src, self.sent.at[k - 1], self.recv.at[other])
        pltpu.make_async_copy(self.src, self.dst.at[self.at], self.own).wait()

    @staticmethod
    def scratch(n):
        return CtxShare.scratch(n)


class HalfSpread:
    def __init__(self, fsdp, pairs, recv, sent, own):
        self.fsdp, self.pairs, self.recv, self.sent, self.own = fsdp, pairs, recv, sent, own
        self.f, self.x = lax.axis_index("fsdp"), lax.axis_index("ctx")
        self.ys = fsdp // 2

    def view(self, a, f, half=None):
        src, dst = self.pairs[a]
        rows, size = src.shape
        columns = pl.ds(pl.multiple_of(f * size, size), size)
        if half is None:
            return dst.at[:, columns]
        return dst.at[pl.ds(pl.multiple_of(half * (rows // 2), rows // 2), rows // 2), columns]

    def part(self, a):
        src = self.pairs[a][0]
        return src.at[pl.ds(pl.multiple_of(self.x * (src.shape[0] // 2), src.shape[0] // 2), src.shape[0] // 2)]

    def start(self, which):
        for a in which:
            for k in range(1, self.ys):
                remote(self.part(a), self.view(a, self.f, self.x), self.sent.at[a, 0, k - 1], self.recv.at[a, 0, k - 1],
                       {"fsdp": lax.rem(self.f + 2 * k, self.fsdp)}).start()
        for a in which:
            src = self.pairs[a][0]
            remote(src, self.view(a, self.f), self.sent.at[a, 1, 0], self.recv.at[a, 1, 0],
                   {"fsdp": sibling(self.f)}).start()
            pltpu.make_async_copy(src, self.view(a, self.f), self.own.at[a]).start()

    def source(self, k):
        return lax.rem(self.f - 2 * k + self.fsdp, self.fsdp)

    def relay(self, which):
        for a in which:
            for k in range(1, self.ys):
                here = self.view(a, self.source(k), self.x)
                wait_came(here, self.sent.at[a, 0, k - 1], self.recv.at[a, 0, k - 1])
                remote(here, here, self.sent.at[a, 2, k - 1], self.recv.at[a, 2, k - 1], {"ctx": 1 - self.x}).start()
                remote(here, here, self.sent.at[a, 3, k - 1], self.recv.at[a, 3, k - 1],
                       {"fsdp": sibling(self.f)}).start()

    def cross(self, which):
        for a in which:
            for k in range(1, self.ys):
                here = self.view(a, self.source(k), 1 - self.x)
                wait_came(here, self.sent.at[a, 2, k - 1], self.recv.at[a, 2, k - 1])
                remote(here, here, self.sent.at[a, 4, k - 1], self.recv.at[a, 4, k - 1],
                       {"fsdp": sibling(self.f)}).start()

    def finish(self, which):
        for a in which:
            src = self.pairs[a][0]
            other = sibling(self.f)
            wait_came(self.view(a, other), self.sent.at[a, 1, 0], self.recv.at[a, 1, 0])
            pltpu.make_async_copy(src, self.view(a, self.f), self.own.at[a]).wait()
            for k in range(1, self.ys):
                there = lax.rem(other - 2 * k + self.fsdp, self.fsdp)
                wait_came(self.view(a, there, self.x), self.sent.at[a, 3, k - 1], self.recv.at[a, 3, k - 1])
                wait_came(self.view(a, there, 1 - self.x), self.sent.at[a, 4, k - 1], self.recv.at[a, 4, k - 1])

    def drain(self, which):
        for a in which:
            wait_sent(self.view(a, self.f), self.sent.at[a, 1, 0], self.recv.at[a, 1, 0])
            for k in range(1, self.ys):
                for kind in (0, 2, 3, 4):
                    wait_sent(self.part(a), self.sent.at[a, kind, k - 1], self.recv.at[a, kind, k - 1])

    @staticmethod
    def scratch(fsdp, arrays):
        return [
            pltpu.SemaphoreType.DMA((arrays, 5, max(fsdp // 2 - 1, 1))),
            pltpu.SemaphoreType.DMA((arrays, 5, max(fsdp // 2 - 1, 1))),
            pltpu.SemaphoreType.DMA((arrays,)),
        ]


R_TWO, MARK, LSE = 3, 4, 8


def layer(tokens, gain1, gain2, w_latent, shards, w_out, wide_shards, segments, out_grad, fsdp, ctx, n):
    rows, width = tokens.shape
    seq_dev, tok_dev = segments.shape
    w_query = shards[0]
    latent, q_width, inner = LATENT, w_query.shape[1], wide_shards[0].shape[0]
    heads = q_width // HEAD_DIM
    per = tok_dev // TILE
    win, span = window(ctx, tok_dev), key_span(ctx, tok_dev)
    own_shard = win - 1
    tiles = span + 1
    keyed = win * rows
    per_group = HEADS // GROUPS * HEAD_DIM
    wide, chunk = 128, 256
    pieces = rows // chunk
    per_seq = tok_dev // chunk
    strip, hop, reach, behind = 32, 2, 3, 2
    piece = 64
    per_block = TILE // piece
    side = 128
    many = max(width, rows)
    q_tiles = rows // TILE
    steps_all = rows // 2 // strip
    lag = hop * 2 * (n // 2)
    ffn = (inner, width // fsdp)
    axes = (0, 0, 0, 1, 0)
    whole = ((width, q_width), (latent, q_width), (latent, q_width), (q_width, width), (width, latent))
    blocks = [GradSum.block_shape(w, a, fsdp) for w, a in zip(whole, axes)]
    lat = blocks[-1]
    cols_at = width // 4

    scratch = dict(
        gbuf=pltpu.VMEM((8, gain1.shape[0]), F32),
        sbuf=pltpu.VMEM((8, tok_dev), segments.dtype),
        gain=pltpu.VMEM((8, width), F32),
        segk=pltpu.VMEM((ctx, 8, tok_dev), segments.dtype),
        cols=pltpu.VMEM((rows, 128), F32),
        tok=pltpu.VMEM((rows, width), BF16),
        gathered=pltpu.VMEM((rows, n * q_width), BF16),
        wo=pltpu.VMEM((n * q_width, width), BF16),
        cot=pltpu.VMEM((rows, width), BF16),
        xn=pltpu.VMEM((rows, width), BF16),
        p_two=pltpu.VMEM((rows, width), BF16),
        p_feed=pltpu.VMEM((rows, width), BF16),
        left=pltpu.VMEM((rows, width), BF16),
        right=pltpu.VMEM((rows, width), BF16),
        branch=pltpu.VMEM((rows, width), BF16),
        mid=pltpu.VMEM((rows, width), F32),
        wg=pltpu.VMEM((inner, width), BF16),
        wu=pltpu.VMEM((inner, width), BF16),
        wd=pltpu.VMEM((inner, width), BF16),
        hid=pltpu.VMEM((rows, inner), BF16),
        dg=pltpu.VMEM((rows, inner), BF16),
        du=pltpu.VMEM((rows, inner), BF16),
        w_lat=pltpu.VMEM((width, latent), BF16),
        w_qry=pltpu.VMEM((width, q_width), BF16),
        w_kproj=pltpu.VMEM((latent, q_width), BF16),
        w_vproj=pltpu.VMEM((latent, q_width), BF16),
        wo_rows=pltpu.VMEM((q_width, width), BF16),
        wo_line=pltpu.VMEM((n,) + w_out.shape, BF16),
        lat_all=pltpu.VMEM((keyed, latent), BF16),
        query=pltpu.VMEM((rows, q_width), BF16),
        keys=pltpu.VMEM((keyed, q_width), BF16),
        values=pltpu.VMEM((keyed, q_width), BF16),
        att=pltpu.VMEM((rows, q_width), BF16),
        dk=pltpu.VMEM((keyed, q_width), F32),
        dv=pltpu.VMEM((keyed, q_width), F32),
        dqb=pltpu.VMEM((rows, q_width), BF16),
        grad_seq=pltpu.VMEM((TILE, q_width), BF16),
        lat_parts=pltpu.VMEM((keyed, latent), BF16),
        dlat=pltpu.VMEM((rows, latent), BF16),
        came=pltpu.VMEM((rows, latent), BF16),
        g_sum=pltpu.VMEM((8, width), F32),
        g_sum2=pltpu.VMEM((8, width), F32),
        sm=pltpu.VMEM((8, many), F32),
        sacc=pltpu.VMEM((3 * seq_dev, 8, width), F32),
        lat_own=pltpu.VMEM(lat, BF16),
        lat_every=pltpu.VMEM((n, lat[0] // 2, lat[1]), BF16),
        lat_sum=pltpu.VMEM((lat[0] // 2, GROUPS * lat[1]), BF16),
        lat_both=pltpu.VMEM((ctx, lat[0] // 2, GROUPS * lat[1]), BF16),
        local=pltpu.SemaphoreType.DMA((2,)),
        flush=pltpu.SemaphoreType.DMA((11,)),
        lat_recv=pltpu.SemaphoreType.DMA((pieces,)),
        lat_sent=pltpu.SemaphoreType.DMA((pieces,)),
        c_recv=pltpu.SemaphoreType.DMA((seq_dev, per_seq)),
        c_sent=pltpu.SemaphoreType.DMA((seq_dev, per_seq)),
    )
    out_blocks = [shape_of(b, F32) for b in blocks[:-1]] + [shape_of((lat[0], GROUPS * lat[1]), F32)]
    out_blocks += [shape_of(ffn, F32)] * 3
    groups = dict(
        outs=[pltpu.VMEM(o.shape, F32) for o in out_blocks[:5]],
        held=GradSum.scratch(fsdp, ctx, [ffn] * 3 + blocks),
        parts=[pltpu.VMEM(w, BF16) for w in whole],
        spread=Spread.scratch(fsdp, 5),
        half=HalfSpread.scratch(fsdp, 4),
        share=CtxShare.scratch(ctx),
        wline=RowGather.scratch(n),
        gather=LineGather.scratch(n, rows // piece),
        two=LineSum.scratch(n, rows, width, strip)[2:],
        feed=LineSum.scratch(n, rows, width, strip)[2:],
        gffn=GradSum.semaphores(fsdp, ctx, 3),
        gatt=GradSum.semaphores(fsdp, ctx, 5),
        lline=AxisShare.scratch(n),
        xline=AxisShare.scratch(ctx),
        s_tp=AxisSum.scratch(n, (8, many)),
        s_ctx=AxisSum.scratch(ctx, (8, many)),
        s_fsdp=AxisSum.scratch(fsdp, (8, many)),
    )
    names = list(scratch)
    shapes = list(scratch.values())
    places = {}
    for key, some in groups.items():
        places[key] = (len(shapes), len(shapes) + len(some))
        shapes = shapes + list(some)

    def kernel(*refs):
        (tok_in, ga, gb, wlat, wq, wkp, wvp, wout, wgt, wut, wdn, seg, cot_in), refs = refs[:13], refs[13:]
        (o_mixed, o_tok), o_blocks, o_small, refs = refs[:2], refs[2:10], refs[10], refs[11:]
        r = SimpleNamespace(**dict(zip(names, refs)))
        g = SimpleNamespace(**{key: refs[a:b] for key, (a, b) in places.items()})
        cols, tok, cot, xn, mid = r.cols, r.tok, r.cot, r.xn, r.mid
        gain, segk = r.gain, r.segk
        x, me = lax.axis_index("ctx"), lax.axis_index("tp")
        outs = list(g.outs) + [mid.at[0 : ffn[0], i * ffn[1] : (i + 1) * ffn[1]] for i in range(3)]

        load = Bring([(tok_in, tok), (cot_in, cot)], r.local)
        load.start()
        r.gbuf[...] = jnp.zeros_like(r.gbuf)
        r.gbuf[0:1, :] = ga[...].astype(F32).reshape(1, -1)
        r.gbuf[1:2, :] = gb[...].astype(F32).reshape(1, -1)
        r.sbuf[...] = jnp.zeros_like(r.sbuf)
        r.sbuf[0:seq_dev, :] = seg[...]
        meet(n, fsdp, ctx)

        group = me * q_width // per_group
        src_lat = wlat.at[:, pl.ds(pl.multiple_of(group * latent, latent), latent)]
        spread = Spread(
            fsdp,
            [(r.gbuf, gain), (src_lat, r.w_lat), (wq, r.w_qry), (wkp, r.w_kproj), (wvp, r.w_vproj)],
            [1, 0, 0, 0, 0], *g.spread,
        )
        share = CtxShare(ctx, r.sbuf, segk, *g.share)
        wline = RowGather(n, wout, r.wo_line, *g.wline)
        half = HalfSpread(
            fsdp,
            [(wgt, r.wg), (wut, r.wu), (wdn, r.wd), (r.wo_line.reshape(n * q_width, w_out.shape[1]), r.wo)],
            *g.half,
        )
        spread.start()
        share.start()
        wline.start()
        half.start([0, 1, 2])
        cols[...] = jnp.zeros_like(cols)
        r.g_sum[...] = jnp.zeros_like(r.g_sum)
        r.g_sum2[...] = jnp.zeros_like(r.g_sum2)
        r.sacc[...] = jnp.zeros_like(r.sacc)
        r.sm[...] = jnp.zeros_like(r.sm)
        load.wait([0])

        def scale(i):
            at = pl.ds(pl.multiple_of(i * wide, wide), wide)
            value = tok[at, :].astype(F32)
            cols[at, R_ONE : R_ONE + 1] = lax.rsqrt(jnp.mean(value * value, axis=-1, keepdims=True) + eps)

        loop(0, rows // wide, scale)
        spread.relay([0, 1])
        spread.finish([0, 1])
        wline.relay([1])
        lat_all = r.lat_all

        def place(shard, i):
            seq = i // per_seq
            return pl.ds(pl.multiple_of((seq * win + shard) * tok_dev + lax.rem(i, per_seq) * chunk, chunk), chunk)

        def pass_on(i):
            return remote(lat_all.at[place(own_shard, i)], lat_all.at[place(own_shard - 1, i)], r.lat_sent.at[i],
                          r.lat_recv.at[i], {"ctx": x + 1})

        def first_norm(i):
            at = pl.ds(pl.multiple_of(i * chunk, chunk), chunk)
            unit = (tok[at, :].astype(F32) * cols[at, R_ONE : R_ONE + 1] * gain[0:1, :]).astype(BF16)
            xn[at, :] = unit
            lat_all[place(own_shard, i), :] = dot(unit, r.w_lat[...]).astype(BF16)

            @pl.when(x + 1 < ctx)
            def _():
                pass_on(i).start()

        loop(0, pieces, first_norm)
        if n > 2:
            wline.relay([2])
        spread.relay([2, 3, 4])
        spread.finish([2, 3, 4])

        def project(shard, i):
            to = place(shard, i)
            value = lat_all[to, :]
            r.keys[to, :] = dot(value, r.w_kproj[...]).astype(BF16)
            r.values[to, :] = dot(value, r.w_vproj[...]).astype(BF16)

        def ask(i):
            at = pl.ds(pl.multiple_of(i * chunk, chunk), chunk)
            r.query[at, :] = dot(xn[at, :], r.w_qry[...]).astype(BF16)
            project(own_shard, i)

        loop(0, pieces, ask)
        share.finish()
        for q in range(seq_dev):
            at = slice(q * tok_dev, (q + 1) * tok_dev)
            ids = jnp.broadcast_to(r.sbuf[q : q + 1, :].astype(F32), (128, tok_dev)).T
            cols[at, SEGMENT : SEGMENT + 1] = ids[:, 0:1]
            final = segk[ctx - 1, q : q + 1, tok_dev - 1 : tok_dev].astype(F32)
            cols[at, VALID : VALID + 1] = jnp.where(ids[:, 0:1] != final, 1.0, 0.0)
        half.relay([0, 1])

        def theirs(i):
            @pl.when(x - 1 >= 0)
            def _():
                wait_came(lat_all.at[place(own_shard - 1, i)], r.lat_sent.at[i], r.lat_recv.at[i])

            @pl.when(x - 1 < 0)
            def _():
                lat_all[place(own_shard - 1, i), :] = jnp.zeros((chunk, latent), BF16)

            project(own_shard - 1, i)

        att, gathered = r.att, r.gathered
        line = LineGather(n, piece, att, gathered, *g.gather, hop=reach)

        def query_tile(i):
            seq = i // per
            q_tile = own_shard * per + lax.rem(i, per)
            at = pl.ds(pl.multiple_of(i * TILE, TILE), TILE)
            near = pl.ds(pl.multiple_of((seq * win * per + q_tile - span) * TILE, TILE), tiles * TILE)
            counted = jnp.concatenate(
                [
                    c.astype(F32)
                    for c in counted_keys(cols, segk, at, seq, q_tile * TILE, q_tile - span, tiles, tok_dev, win)
                ],
                axis=1,
            )
            accum = jnp.zeros((TILE, q_width), F32)
            for h in range(heads):
                score = dot_t(head_only(r.query[at, :], h), r.keys[near, :]) * 0.125
                score = jnp.where(counted > 0.0, score, -1e30)
                top = jnp.max(score, axis=-1, keepdims=True)
                weight = jnp.exp(score - top)
                total = jnp.sum(weight, axis=-1, keepdims=True)
                prob = (weight * (1.0 / total)).astype(BF16)
                accum = accum + jnp.dot(prob, head_only(r.values[near, :], h), preferred_element_type=F32)
                cols[at, LSE + h : LSE + h + 1] = top + jnp.log(total)
                line.step((i - 1) * per_block + h * per_block // heads)
            att[at, :] = accum.astype(BF16)

        def sequence_forward(seq):
            loop(seq * per_seq, seq * per_seq + per_seq, theirs)

            @pl.when(seq == 0)
            def _():
                if n > 3:
                    wline.relay(range(3, n))
                wline.finish()
                half.start([3])

            loop(seq * per, seq * per + per, query_tile)

            @pl.when(seq == 0)
            def _():
                half.relay([2, 3])

        loop(0, seq_dev, sequence_forward)
        s1 = (q_tiles - 1) * per_block
        line.begin()
        half.cross([0, 1, 2, 3])
        loop(s1, per_block + reach * (n - 1), line.step)
        s1 = per_block + reach * (n - 1)
        half.finish([3, 0, 1, 2])
        half.drain([0, 1, 2, 3])
        r.wo_rows[...] = r.wo[pl.ds(pl.multiple_of(me * q_width, q_width), q_width), :]
        line.begun()
        load.wait([1])

        p_two, p_feed, wg, wu, wd = r.p_two, r.p_feed, r.wg, r.wu, r.wd

        def second_back(at, own, total):
            unit = mid[at, :] * cols[at, R_TWO : R_TWO + 1]
            r.g_sum2[...] += jnp.sum((total * unit).reshape(strip // 8, 8, width), axis=0)
            scaled = total * gain[1:2, :]
            mean = jnp.mean(scaled * unit, axis=-1, keepdims=True)
            d_mid = cot[at, :].astype(F32) + cols[at, R_TWO : R_TWO + 1] * (scaled - unit * mean)
            first_unit = tok[at, :].astype(F32) * cols[at, R_ONE : R_ONE + 1]
            cols[at, MARK : MARK + 1] = jnp.sum(first_unit * d_mid, axis=-1, keepdims=True)
            return d_mid.astype(BF16)

        def forward(at, own, total):
            mixed = mid[at, :] + total
            seq = at.start // tok_dev
            counted = cols[at, VALID : VALID + 1]
            r.sacc[seq] += jnp.sum((mixed * mixed * counted).reshape(strip // 8, 8, width), axis=0)
            r.sacc[seq_dev + seq] += jnp.sum((total * total * counted).reshape(strip // 8, 8, width), axis=0)
            return mixed.astype(BF16)

        def first_back(at, own, total):
            r1 = cols[at, R_ONE : R_ONE + 1]
            unit = tok[at, :].astype(F32) * r1
            scaled = total * gain[0:1, :]
            mean = jnp.mean(scaled * unit, axis=-1, keepdims=True)
            return (r.branch[at, :].astype(F32) + r1 * (scaled - unit * mean)).astype(BF16)

        two = LineSum(n, strip, hop, p_two, r.left, r.right, r.branch, *g.two, second_back, pushed=True)
        feed = LineSum(n, strip, hop, p_feed, gathered, r.wo, xn, *g.feed, forward)
        one = LineSum(n, strip, hop, cot, r.left, r.right, p_two, *g.two, first_back)
        parts = [wg, wu, wd]
        gffn = GradSum(fsdp, ctx, parts, [1, 1, 1], None,
                       [g.held[3 * a : 3 * a + 3] for a in range(3)], *g.gffn)
        aparts = g.parts
        gatt = GradSum(fsdp, ctx, aparts, axes, None,
                       [g.held[3 * a : 3 * a + 3] for a in range(3, 8)], *g.gatt)

        def block_of_rows(b):
            at = pl.ds(pl.multiple_of(b * TILE, TILE), TILE)
            seq = b * TILE // tok_dev

            def steps(j):
                line.step(s1 + b * per_block + j)
                two.step((b - 1) * per_block + j - behind)

            branch = dot(gathered[at, :], r.wo[...])
            middle_rows = tok[at, :].astype(F32) + branch
            mid[at, :] = middle_rows
            r.sacc[2 * seq_dev + seq] += jnp.sum(
                (branch * branch * cols[at, VALID : VALID + 1]).reshape(TILE // 8, 8, width), axis=0
            )
            level = lax.rsqrt(jnp.mean(middle_rows * middle_rows, axis=-1, keepdims=True) + eps)
            cols[at, R_TWO : R_TWO + 1] = level
            unit = (middle_rows * level * gain[1:2, :]).astype(BF16)
            xn[at, :] = unit
            steps(0)
            gate = dot_t(unit, wg[...])
            upper = dot_t(unit, wu[...])
            sigma = jax.nn.sigmoid(gate)
            swish = gate * sigma
            hidden = (swish * upper).astype(BF16)
            r.hid[at, :] = hidden
            slope = upper * sigma * (1.0 + gate * (1.0 - sigma))
            steps(1)
            p_feed[at, :] = dot(hidden, wd[...]).astype(BF16)
            d_hidden = dot_t(cot[at, :], wd[...])
            d_gate = (d_hidden * slope).astype(BF16)
            d_upper = (d_hidden * swish).astype(BF16)
            r.dg[at, :] = d_gate
            r.du[at, :] = d_upper
            steps(2)
            p_two[at, :] = (dot(d_gate, wg[...]) + dot(d_upper, wu[...])).astype(BF16)
            steps(3)
            for j in range(per_block):
                two.push(b * per_block + j)

        loop(0, q_tiles, block_of_rows)
        s2 = (q_tiles - 1) * per_block - behind

        def product(i):
            at = pl.ds(pl.multiple_of(i * cols_at, cols_at), cols_at)
            left = xn[:, at]
            parts[0][:, at] = dot_rows(r.dg[...], left).astype(BF16)
            parts[1][:, at] = dot_rows(r.du[...], left).astype(BF16)
            parts[2][:, at] = dot_rows(r.hid[...], cot[:, at]).astype(BF16)

        def busy(s):
            two.step(s)
            product(s - s2)

        line.drain()
        loop(s2, s2 + 4, busy)
        gffn.start()
        s2 = s2 + 4

        dk, dv, dqb, grad_seq, lat_parts = r.dk, r.dv, r.dqb, r.grad_seq, r.lat_parts

        def clear(i):
            at = pl.ds(pl.multiple_of(i * TILE, TILE), TILE)
            dk[at, :] = jnp.zeros((TILE, q_width), F32)
            dv[at, :] = jnp.zeros((TILE, q_width), F32)

        loop(0, keyed // TILE, clear)
        ready = steps_all // seq_dev + lag
        loop(s2, ready, two.step)

        def grad_tile(i, step):
            seq = i // per
            q_tile = own_shard * per + lax.rem(i, per)
            at = pl.ds(pl.multiple_of(i * TILE, TILE), TILE)
            near = pl.ds(pl.multiple_of((seq * win * per + q_tile - span) * TILE, TILE), tiles * TILE)
            grad_seq[...] = dot_t(r.branch[at, :], r.wo_rows[...]).astype(BF16)
            inner_sum = grad_seq[...].astype(F32) * att[at, :].astype(F32)
            counted = jnp.concatenate(
                [
                    c.astype(F32)
                    for c in counted_keys(cols, segk, at, seq, q_tile * TILE, q_tile - span, tiles, tok_dev, win)
                ],
                axis=1,
            )
            d_query = jnp.zeros((TILE, q_width), F32)
            d_key = jnp.zeros((tiles * TILE, q_width), F32)
            d_value = jnp.zeros((tiles * TILE, q_width), F32)
            for h in range(heads):
                delta = jnp.sum(head_only(inner_sum, h), axis=-1, keepdims=True)
                asked, ours = head_only(r.query[at, :], h), head_only(grad_seq[...], h)
                score = jnp.where(counted > 0.0, dot_t(asked, r.keys[near, :]) * 0.125, -1e30)
                prob = jnp.exp(score - cols[at, LSE + h : LSE + h + 1]) * counted
                d_score = (prob * (dot_t(ours, r.values[near, :]) - delta)).astype(BF16)
                d_query = d_query + jnp.dot(d_score, head_only(r.keys[near, :], h), preferred_element_type=F32)
                d_key = d_key + dot_rows(d_score, asked)
                d_value = d_value + dot_rows(prob.astype(BF16), ours)
                step(h)
            dqb[at, :] = (d_query * 0.125).astype(BF16)
            dk[near, :] += d_key * 0.125
            dv[near, :] += d_value

        def send_latent(seq, i):
            j = seq * per_seq + i
            at = pl.ds(pl.multiple_of(j * chunk, chunk), chunk)
            return remote(lat_parts.at[place(own_shard - 1, j)], r.came.at[at], r.c_sent.at[seq, i],
                          r.c_recv.at[seq, i], {"ctx": x - 1})

        def latents(seq):
            for shard in (own_shard - 1, own_shard):
                for i in range(per_seq):
                    at = place(shard, seq * per_seq + i)
                    lat_parts[at, :] = (
                        dot_t(dk[at, :].astype(BF16), r.w_kproj[...])
                        + dot_t(dv[at, :].astype(BF16), r.w_vproj[...])
                    ).astype(BF16)
                    if shard < own_shard:

                        @pl.when(x - 1 >= 0)
                        def _(i=i):
                            send_latent(seq, i).start()

        def sequence(seq):
            def tile(i):
                def step(h):
                    t = (i * heads + h) * steps_per // heads
                    two.step(ready + t)
                    feed.step(t)

                grad_tile(i, step)

            loop(seq * per, seq * per + per, tile)
            latents(seq)

            @pl.when(seq == 0)
            def _():
                two.drain()
                gffn.pair()
                gffn.second()

        steps_per = heads
        loop(0, seq_dev, sequence)
        fed = q_tiles * steps_per

        def whole_latent(j):
            seq, i = j // per_seq, lax.rem(j, per_seq)
            at = pl.ds(pl.multiple_of(j * chunk, chunk), chunk)
            r.dlat[at, :] = lat_parts[place(own_shard, j), :]

            @pl.when(x + 1 < ctx)
            def _():
                wait_came(r.came.at[at], r.c_sent.at[seq, i], r.c_recv.at[seq, i])
                r.dlat[at, :] = (r.dlat[at, :].astype(F32) + r.came[at, :].astype(F32)).astype(BF16)

            cot[at, :] = (dot_t(dqb[at, :], r.w_qry[...]) + dot_t(r.dlat[at, :], r.w_lat[...])).astype(BF16)

        def first_unit_columns(at):
            return (tok[:, at].astype(F32) * cols[:, R_ONE : R_ONE + 1] * gain[0:1, at]).astype(BF16)

        early = (seq_dev - 1) * per_seq
        loop(0, early, whole_latent)

        def mixed_work(i):
            at = pl.ds(pl.multiple_of(i * chunk, chunk), chunk)
            aparts[0][at, :] = dot_rows(first_unit_columns(at), dqb[...]).astype(BF16)
            aparts[3][:, at] = dot_rows(att[...], r.branch[:, at]).astype(BF16)
            feed.step(fed + i)

        fed_later = fed + width // chunk
        loop(0, width // chunk, mixed_work)
        gffn.third()
        aparts[1][...] = dot_rows(lat_all[...], dk[...].astype(BF16)).astype(BF16)
        aparts[2][...] = dot_rows(lat_all[...], dv[...].astype(BF16)).astype(BF16)
        loop(early, pieces, whole_latent)

        def steps(s):
            one.step(s)
            feed.step(fed_later + s)

        def product_lat(s):
            at = pl.ds(pl.multiple_of(s * chunk, chunk), chunk)
            aparts[4][at, :] = dot_rows(first_unit_columns(at), r.dlat[...]).astype(BF16)
            steps(s)

        begun = width // chunk
        loop(0, begun, product_lat)
        gatt.start()

        def gains_of(i):
            at = pl.ds(pl.multiple_of(i * side, side), side)
            value = cot[at, :].astype(F32) * (tok[at, :].astype(F32) * cols[at, R_ONE : R_ONE + 1])
            r.g_sum[...] += jnp.sum(value.reshape(side // 8, 8, width), axis=0)
            along = lax.dot_general(jnp.ones((8, width), F32), value * gain[0:1, :], (((1,), (1,)), ((), ())),
                                    precision=lax.Precision.HIGHEST, preferred_element_type=F32)
            r.sm[3:4, at] = along[0:1, :]
            lines = cols[at, :].T
            r.sm[4:5, at] = lines[MARK : MARK + 1, :]
            r.sm[5:6, at] = lines[R_ONE : R_ONE + 1, :]

        def two_gains(s):
            steps(s)
            gains_of(2 * (s - begun))
            gains_of(2 * (s - begun) + 1)

        mark = begun + rows // side // 2
        loop(begun, begun + 1, two_gains)
        gatt.pair()
        gatt.second()
        loop(begun + 1, mark, two_gains)
        last = one.steps()
        for s in range(fed_later + mark, feed.steps()):
            feed.step(s)
        flush = r.flush
        out_mixed = pltpu.make_async_copy(xn, o_mixed, flush.at[8])
        out_mixed.start()
        lane = lax.broadcasted_iota(jnp.int32, (1, many), 1)
        once = jnp.where(me == 0, 1.0, 0.0)
        row = jnp.zeros((1, many), F32)

        def whole_sum(value):
            return jnp.sum(jnp.sum(value, axis=0, keepdims=True), axis=1, keepdims=True)

        for q in range(seq_dev):
            stats = [
                whole_sum(r.sacc[q]),
                whole_sum(r.sacc[seq_dev + q]),
                whole_sum(r.sacc[2 * seq_dev + q]) * once,
                jnp.sum(cols[q * tok_dev : (q + 1) * tok_dev, VALID : VALID + 1], axis=0, keepdims=True) * once,
            ]
            for j, value in enumerate(stats):
                row = row + jnp.where(lane == 4 * q + j, value, 0.0)
        r.sm[2:3, :] = row
        r.sm[0:1, 0:width] = jnp.sum(r.g_sum[...], axis=0, keepdims=True)
        r.sm[1:2, 0:width] = jnp.sum(r.g_sum2[...], axis=0, keepdims=True)
        r_row = r.sm[5:6, :]
        over_tp = AxisSum("tp", n, *g.s_tp)
        over_ctx = AxisSum("ctx", ctx, *g.s_ctx)
        over_fsdp = AxisSum("fsdp", fsdp, *g.s_fsdp)
        over_tp.start(r.sm[...])
        lat_half = pl.ds(pl.multiple_of(x * (lat[0] // 2), lat[0] // 2), lat[0] // 2)
        lline = AxisShare("tp", n, r.lat_own.at[lat_half], r.lat_every, *g.lline)
        xline = AxisShare("ctx", ctx, r.lat_sum, r.lat_both, *g.xline)
        outward = Bring([(outs[i], o_blocks[i]) for i in range(8)], flush)

        def store(a, at, total):
            if a < 4:
                outs[a][at, :] = total
            else:
                r.lat_own[at, :] = total.astype(BF16)

        def store_ffn(a, at, total):
            outs[5 + a][at, :] = total

        loop(mark, mark + 2, steps)
        gatt.third()
        along_tp = over_tp.finish()
        over_ctx.start(along_tp)
        gffn.fourth(store_ffn)
        outward.start([5, 6, 7])
        loop(mark + 2, mark + 4, steps)
        along_ctx = over_ctx.finish()
        over_fsdp.start(along_ctx)
        loop(mark + 4, mark + 6, steps)
        gatt.fourth(store)
        outward.start([0, 1, 2, 3])
        lline.start()
        everywhere = over_fsdp.finish()
        loop(mark + 6, mark + 10, steps)
        lline.finish()

        def latent_sum(i):
            at = pl.ds(pl.multiple_of(i * 16, 16), 16)
            for gr in range(GROUPS):
                total = jnp.zeros((16, lat[1]), F32)
                for t in range(n):
                    if t * GROUPS // n == gr:
                        total = total + r.lat_every[t, at, :].astype(F32)
                r.lat_sum[at, gr * lat[1] : (gr + 1) * lat[1]] = total.astype(BF16)

        loop(0, lat[0] // 32, latent_sum)
        xline.start()
        loop(mark + 10, mark + 13, steps)
        xline.finish()
        for k in range(ctx):
            outs[4][k * (lat[0] // 2) : (k + 1) * (lat[0] // 2), :] = r.lat_both[k].astype(F32)
        outward.start([4])
        row = lax.broadcasted_iota(jnp.int32, everywhere.shape, 0)
        o_small[...] = jnp.where(row < 2, everywhere, along_ctx)
        o_small[3:4, :] = (along_tp[4:5] + eps * r_row * r_row * r_row * along_tp[3:4]) * (1.0 / width**0.5)
        ahead = [pl.ds(0, rows // 2), pl.ds(rows // 2, rows // 2)]
        out_tok = Bring([(p_two.at[q], o_tok.at[q]) for q in ahead], flush.at[pl.ds(9, 2)])
        out_tok.start([0])
        loop(mark + 13, last, steps)
        out_tok.start([1])

        @pl.when(x + 1 < ctx)
        def _():
            loop(0, pieces, lambda i: pass_on(i).wait_send())

        @pl.when(x - 1 >= 0)
        def _():
            for seq in range(seq_dev):
                for i in range(per_seq):
                    send_latent(seq, i).wait_send()

        feed.drain()
        one.drain()
        gffn.drain_pair()
        gffn.drain()
        gatt.drain_pair()
        gatt.drain()
        outward.wait()
        out_mixed.wait()
        out_tok.wait()

    out = pl.pallas_call(
        kernel,
        out_shape=(shape_of((rows, width), BF16),) * 2 + tuple(out_blocks) + (shape_of((8, many), F32),),
        in_specs=[ANY] + [VMEM] * 2 + [ANY] * 8 + [VMEM, ANY],
        out_specs=(ANY,) * 10 + (VMEM,),
        scratch_shapes=shapes,
        compiler_params=params(1, 64),
    )(tokens, gain1, gain2, w_latent, *shards, w_out, *wide_shards, segments, out_grad)
    return out[0], out[1], out[2:7], out[7:10], out[10]


def three_kernels(tokens, gain1, gain2, w_latent, shards, w_out, wide_shards, segments, out_grad, fsdp, ctx, n):
    seq_dev, tok_dev = segments.shape
    gate, up, down = wide_shards
    (xn_one, cols, gains, w_lat, w_qry, w_kproj, w_vproj, gate_all, up_all, wo_cols, seg_all, lat_all,
     query, keys, values) = front(tokens, gain1, gain2, w_latent, shards, w_out, (gate, up), segments, fsdp, ctx, n)
    late = window(ctx, tok_dev) <= 2
    (d_branch, part_feed, d_middle, mid_own, wo_rows, gain_part, branch_sq, marks, attended, lse), ffn = middle(
        query, keys, values, seg_all, cols, (wo_cols.reshape(-1, w_out.shape[1]), down), gate_all, up_all, gains,
        tokens, out_grad, fsdp, ctx, n, seq_dev, late,
    )
    (grad_tokens, mixed, small), att_grads, late_ffn = back(
        query, keys, values, seg_all, cols, lse, attended, d_branch, wo_rows, (w_qry, w_lat, w_kproj, w_vproj),
        lat_all, xn_one, gains, tokens, d_middle, mid_own, part_feed, marks, gain_part, branch_sq,
        ffn if late else (), fsdp, ctx, n, seq_dev,
    )
    return mixed, grad_tokens, att_grads, late_ffn if late else ffn, small


def on_device(
    tokens, gain1, w_latent, w_query, w_key, w_value, w_out, gain2, w_gate, w_up, w_down, segments, cotangent
):
    seq_dev, tok_dev, feat_dim = tokens.shape
    n_ctx, n_tp, n_fsdp = lax.axis_size("ctx"), lax.axis_size("tp"), lax.axis_size("fsdp")
    row_count = seq_dev * tok_dev
    tok_rows = tokens.reshape(row_count, feat_dim)
    out_grad = cotangent.reshape(row_count, feat_dim)
    if n_ctx == 2 and n_fsdp >= 4 and w_down.shape[0] <= row_count and feat_dim <= row_count:
        mixed, grad_tokens, att_grads, ffn_grads, small = layer(
            tok_rows, gain1, gain2, w_latent, (w_query, w_key, w_value), w_out, (w_gate.T, w_up.T, w_down), segments,
            out_grad, n_fsdp, n_ctx, n_tp,
        )
    else:
        mixed, grad_tokens, att_grads, ffn_grads, small = three_kernels(
            tok_rows, gain1, gain2, w_latent, (w_query, w_key, w_value), w_out, (w_gate.T, w_up.T, w_down), segments,
            out_grad, n_fsdp, n_ctx, n_tp,
        )
    arrays, (gain_grad1, gain_grad2, stats, radial) = publish(
        (mixed, grad_tokens, *att_grads, *ffn_grads), small, seq_dev, tok_dev, feat_dim, n_fsdp
    )
    mixed, grad_tokens, s_qry, s_kproj, s_vproj, s_outp, s_lat, s_gate, s_up, s_down = arrays
    return (
        mixed.reshape(seq_dev, tok_dev, feat_dim),
        grad_tokens.reshape(seq_dev, tok_dev, feat_dim),
        gain_grad1,
        s_lat,
        s_qry,
        s_kproj,
        s_vproj,
        s_outp,
        gain_grad2,
        s_gate.T,
        s_up.T,
        s_down,
        stats,
        radial,
    )


def solution(mesh):
    return jax.shard_map(
        on_device,
        mesh=mesh,
        in_specs=(
            P("fsdp", "ctx", None),
            P("fsdp"),
            P("fsdp", None),
            P("fsdp", "tp"),
            P("fsdp", "tp"),
            P("fsdp", "tp"),
            P("tp", "fsdp"),
            P("fsdp"),
            P("fsdp", "tp"),
            P("fsdp", "tp"),
            P("tp", "fsdp"),
            P("fsdp", "ctx"),
            P("fsdp", "ctx", None),
        ),
        out_specs=(
            P("fsdp", "ctx", None),
            P("fsdp", "ctx", None),
            P("fsdp"),
            P("fsdp", None),
            P("fsdp", "tp"),
            P("fsdp", "tp"),
            P("fsdp", "tp"),
            P("tp", "fsdp"),
            P("fsdp"),
            P("fsdp", "tp"),
            P("fsdp", "tp"),
            P("tp", "fsdp"),
            P("fsdp", None),
            P("fsdp", "ctx"),
        ),
        check_vma=False,
    )
```

```python
from types import SimpleNamespace

import jax
import jax.numpy as jnp
from jax import lax
from jax.experimental import pallas as pl
from jax.experimental.pallas import tpu as pltpu
from jax.sharding import PartitionSpec as P

HEADS = 16
HEAD_DIM = 64
GROUPS = 2
LATENT = 256
MESH = pl.DeviceIdType.MESH
VMEM = pl.BlockSpec(memory_space=pltpu.VMEM)
ANY = pl.BlockSpec(memory_space=pl.ANY)
F32 = jnp.float32
BF16 = jnp.bfloat16

eps = 1e-05


def remote(src, dst, send_sem, recv_sem, device):
    return pltpu.make_async_remote_copy(
        src_ref=src,
        dst_ref=dst,
        send_sem=send_sem,
        recv_sem=recv_sem,
        device_id=device,
        device_id_type=MESH,
    )


def wait_sent(ref, sem, recv_sem):
    remote(ref, ref, sem, recv_sem, {"tp": lax.axis_index("tp")}).wait_send()


def wait_came(ref, send_sem, sem):
    remote(ref, ref, send_sem, sem, {"tp": lax.axis_index("tp")}).wait_recv()


def meet(line=0, fsdp=0, ctx=0, everyone=False):
    barrier = pltpu.get_barrier_semaphore()

    def greet(device):
        pl.semaphore_signal(barrier, inc=1, device_id=device, device_id_type=MESH)

    known = 0
    f, x, me = lax.axis_index("fsdp"), lax.axis_index("ctx"), lax.axis_index("tp")
    if fsdp and everyone:
        for k in range(1, fsdp):
            greet({"fsdp": lax.rem(f + k, fsdp)})
        known += fsdp - 1
    elif fsdp:
        greet({"fsdp": sibling(f)})
        for k in range(1, fsdp // 2):
            greet({"fsdp": lax.rem(f + 2 * k, fsdp)})
        known += fsdp // 2
    for k in range(1, ctx):
        greet({"ctx": lax.rem(x + k, ctx)})
        known += 1
    if line > 1 and everyone:
        for k in range(1, line):
            greet({"tp": lax.rem(me + k, line)})
        known += line - 1
    if line > 1 and not everyone:

        @pl.when(me > 0)
        def _():
            greet({"tp": me - 1})

        @pl.when(me < line - 1)
        def _():
            greet({"tp": me + 1})

        @pl.when((me > 0) & (me < line - 1))
        def _():
            pl.semaphore_wait(barrier, known + 2)

        @pl.when((me == 0) | (me == line - 1))
        def _():
            pl.semaphore_wait(barrier, known + 1)

    else:
        pl.semaphore_wait(barrier, known)


def sibling(f):
    return f + 1 - 2 * lax.rem(f, 2)


def block(ref, axis, index, size):
    at = pl.ds(pl.multiple_of(index * size, size), size)
    return ref.at[at] if axis == 0 else ref.at[:, at]


class Bring:
    def __init__(self, pairs, sems):
        self.copies = [pltpu.make_async_copy(src, dst, sems.at[i]) for i, (src, dst) in enumerate(pairs)]

    def start(self, which=None):
        for i in which if which is not None else range(len(self.copies)):
            self.copies[i].start()

    def wait(self, which=None):
        for i in which if which is not None else range(len(self.copies)):
            self.copies[i].wait()


class Spread:
    def __init__(self, fsdp, pairs, axes, recv, sent, own):
        self.fsdp, self.pairs, self.axes = fsdp, pairs, axes
        self.recv, self.sent, self.own = recv, sent, own
        self.f = lax.axis_index("fsdp")

    def size(self, a):
        return self.pairs[a][0].shape[self.axes[a]]

    def target(self, a, f):
        return block(self.pairs[a][1], self.axes[a], f, self.size(a))

    def start(self):
        f = self.f
        for a, (src, dst) in enumerate(self.pairs):
            for k in range(1, self.fsdp // 2):
                remote(src, self.target(a, f), self.sent.at[a], self.recv.at[a, f],
                       {"fsdp": lax.rem(f + 2 * k, self.fsdp)}).start()
        for a, (src, dst) in enumerate(self.pairs):
            remote(src, self.target(a, f), self.sent.at[a], self.recv.at[a, f],
                   {"fsdp": sibling(f)}).start()
            pltpu.make_async_copy(src, self.target(a, f), self.own.at[a]).start()

    def relay(self, which=None):
        for a in which or range(len(self.pairs)):
            for k in range(1, self.fsdp // 2):
                other = lax.rem(self.f + 2 * k, self.fsdp)
                here = self.target(a, other)
                wait_came(here, self.sent.at[a], self.recv.at[a, other])
                remote(here, here, self.sent.at[a], self.recv.at[a, other],
                       {"fsdp": sibling(self.f)}).start()

    def finish(self, which=None):
        for a in which or range(len(self.pairs)):
            src, dst = self.pairs[a]
            for k in range(0, self.fsdp // 2):
                other = lax.rem(sibling(self.f) + 2 * k, self.fsdp)
                wait_came(self.target(a, other), self.sent.at[a], self.recv.at[a, other])
            pltpu.make_async_copy(src, self.target(a, self.f), self.own.at[a]).wait()
            many = (self.fsdp - 1) * self.size(a)
            ref = dst.at[pl.ds(0, many)] if self.axes[a] == 0 else dst.at[:, pl.ds(0, many)]
            wait_sent(ref, self.sent.at[a], self.recv.at[a, 0])

    @staticmethod
    def scratch(fsdp, arrays):
        return [
            pltpu.SemaphoreType.DMA((arrays, fsdp)),
            pltpu.SemaphoreType.DMA((arrays,)),
            pltpu.SemaphoreType.DMA((arrays,)),
        ]


class CtxShare:
    def __init__(self, ctx, src, dst, recv, sent, own):
        self.ctx, self.src, self.dst = ctx, src, dst
        self.recv, self.sent, self.own = recv, sent, own
        self.x = lax.axis_index("ctx")

    def start(self):
        for k in range(1, self.ctx):
            remote(self.src, self.dst.at[self.x], self.sent.at[k - 1], self.recv.at[self.x],
                   {"ctx": lax.rem(self.x + k, self.ctx)}).start()
        pltpu.make_async_copy(self.src, self.dst.at[self.x], self.own).start()

    def finish(self):
        for k in range(1, self.ctx):
            other = lax.rem(self.x + k, self.ctx)
            wait_came(self.dst.at[other], self.sent.at[k - 1], self.recv.at[other])
            wait_sent(self.src, self.sent.at[k - 1], self.recv.at[other])
        pltpu.make_async_copy(self.src, self.dst.at[self.x], self.own).wait()

    @staticmethod
    def scratch(ctx):
        return [
            pltpu.SemaphoreType.DMA((ctx,)),
            pltpu.SemaphoreType.DMA((ctx,)),
            pltpu.SemaphoreType.DMA,
        ]


class LineGather:
    def __init__(self, n, chunk, src, dst, recv, sent, own, hop=1, order=None):
        self.n, self.chunk, self.src, self.dst, self.hop = n, chunk, src, dst, hop
        self.order = order or (lambda at: at)
        self.width = src.shape[1]
        self.count = src.shape[0] // chunk
        self.recv, self.sent, self.own = recv, sent, own
        self.me = lax.axis_index("tp")

    def steps(self):
        return self.count + self.hop * (self.n - 1)

    def columns(self, tp):
        return pl.ds(pl.multiple_of(tp * self.width, self.width), self.width)

    def rows(self, at):
        return pl.ds(pl.multiple_of(self.order(at) * self.chunk, self.chunk), self.chunk)

    def place(self, tp, at):
        return self.dst.at[self.rows(at), self.columns(tp)]

    def begin(self):
        pltpu.make_async_copy(self.src, self.dst.at[:, self.columns(self.me)], self.own).start()

    def begun(self):
        pltpu.make_async_copy(self.src, self.dst.at[:, self.columns(self.me)], self.own).wait()

    def step(self, s):
        n, me, count = self.n, self.me, self.count
        left, right = {"tp": me - 1}, {"tp": me + 1}

        @pl.when((s >= 0) & (s < count))
        def _():
            rows = self.rows(s)

            @pl.when(me > 0)
            def _():
                remote(self.src.at[rows], self.place(me, s), self.sent.at[0], self.recv.at[me, s], left).start()

            @pl.when(me < n - 1)
            def _():
                remote(self.src.at[rows], self.place(me, s), self.sent.at[1], self.recv.at[me, s], right).start()

        for away in range(1, n):
            at = s - away * self.hop
            for sign, onward in ((-1, right), (1, left)):
                tp = me + sign * away

                @pl.when((tp >= 0) & (tp < n) & (at >= 0) & (at < count))
                def _(tp=tp, onward=onward, sign=sign, at=at):
                    here = self.place(tp, at)
                    wait_came(here, self.sent.at[2], self.recv.at[tp, at])

                    @pl.when((me < n - 1) if sign < 0 else (me > 0))
                    def _():
                        remote(here, here, self.sent.at[2], self.recv.at[tp, at], onward).start()

    def drain(self):
        n, me = self.n, self.me

        @pl.when(me > 0)
        def _():
            wait_sent(self.src, self.sent.at[0], self.recv.at[0, 0])

        @pl.when(me < n - 1)
        def _():
            wait_sent(self.src, self.sent.at[1], self.recv.at[0, 0])

        @pl.when((me > 0) & (me < n - 1))
        def _():
            wait_sent(self.dst.at[:, pl.ds(0, (n - 1) * self.width)], self.sent.at[2], self.recv.at[0, 0])

    @staticmethod
    def scratch(n, count):
        return [
            pltpu.SemaphoreType.DMA((n, count)),
            pltpu.SemaphoreType.DMA((3,)),
            pltpu.SemaphoreType.DMA,
        ]


class LineSum:
    def __init__(self, n, chunk, hop, part, from_left, from_right, out, recv, sent, finish, pushed=False, order=None):
        self.order = order or (lambda at: at)
        self.n, self.chunk, self.hop, self.pushed = n, chunk, hop, pushed
        self.total_rows = part.shape[0]
        self.owners = (n // 2 - 1, n // 2)
        self.count = self.total_rows // 2 // chunk
        self.part, self.from_left, self.from_right, self.out = part, from_left, from_right, out
        self.recv, self.sent = recv, sent
        self.finish = finish
        self.me = lax.axis_index("tp")

    def steps(self):
        return self.count + self.hop * 2 * (self.n // 2)

    def turn(self, at):
        return lax.rem(at, self.recv.shape[2])

    def rows(self, slot, at):
        return pl.ds(pl.multiple_of((self.order(at) * 2 + slot) * self.chunk, self.chunk), self.chunk)

    def send(self, here, side, slot, at):
        held = self.from_left if side == 0 else self.from_right
        to = {"tp": self.me + 1} if side == 0 else {"tp": self.me - 1}

        @pl.when(here)
        def _():
            rows = self.rows(slot, at)
            remote(self.part.at[rows], held.at[rows], self.sent.at[0], self.recv.at[side, slot, self.turn(at)],
                   to).start()

    def push(self, at):
        for slot, owner in enumerate(self.owners):
            if owner > 0:
                self.send(self.me == 0, 0, slot, at)
            if owner < self.n - 1:
                self.send(self.me == self.n - 1, 1, slot, at)

    def step(self, s):
        n, me, hop = self.n, self.me, self.hop
        left, right = {"tp": me - 1}, {"tp": me + 1}
        reach = n // 2
        for slot, owner in enumerate(self.owners):
            for side in (0, 1):
                lag = me if side == 0 else n - 1 - me
                at = s - hop * lag
                here = (me < owner) if side == 0 else (me > owner)
                held = self.from_left if side == 0 else self.from_right
                to = right if side == 0 else left
                here = here & (at >= 0) & (at < self.count)

                if not self.pushed:
                    self.send(here & (lag == 0), side, slot, at)

                if n > 2:

                    @pl.when(here & (lag > 0))
                    def _(at=at, held=held, to=to, side=side, slot=slot):
                        rows = self.rows(slot, at)
                        wait_came(held.at[rows], self.sent.at[0], self.recv.at[side, slot, self.turn(at)])
                        held[rows, :] = (held[rows, :].astype(F32) + self.part[rows, :].astype(F32)).astype(BF16)
                        remote(held.at[rows], held.at[rows], self.sent.at[0],
                               self.recv.at[side, slot, self.turn(at)], to).start()

            at = s - hop * reach

            @pl.when((me == owner) & (at >= 0) & (at < self.count))
            def _(at=at, slot=slot, owner=owner):
                rows = self.rows(slot, at)
                total = self.part[rows, :].astype(F32)
                if owner > 0:
                    wait_came(self.from_left.at[rows], self.sent.at[0], self.recv.at[0, slot, self.turn(at)])
                    total = total + self.from_left[rows, :].astype(F32)
                wait_came(self.from_right.at[rows], self.sent.at[0], self.recv.at[1, slot, self.turn(at)])
                total = total + self.from_right[rows, :].astype(F32)
                own = pl.ds(pl.multiple_of(at * self.chunk, self.chunk), self.chunk)
                self.out[rows, :] = self.finish(rows, own, total)
                if owner > 0:
                    remote(self.out.at[rows], self.out.at[rows], self.sent.at[1],
                           self.recv.at[2, slot, self.turn(at)], left).start()
                remote(self.out.at[rows], self.out.at[rows], self.sent.at[2],
                       self.recv.at[2, slot, self.turn(at)], right).start()

        for slot, owner in enumerate(self.owners):
            away = jnp.abs(me - owner)
            at = s - hop * (reach + away)

            @pl.when((me != owner) & (at >= 0) & (at < self.count))
            def _(at=at, slot=slot, owner=owner):
                rows = self.rows(slot, at)
                here = self.out.at[rows]
                wait_came(here, self.sent.at[3], self.recv.at[2, slot, self.turn(at)])

                @pl.when((me < owner) & (me > 0))
                def _():
                    remote(here, here, self.sent.at[3], self.recv.at[2, slot, self.turn(at)], left).start()

                @pl.when((me > owner) & (me < n - 1))
                def _():
                    remote(here, here, self.sent.at[3], self.recv.at[2, slot, self.turn(at)], right).start()

    def drain(self):
        n, me, half = self.n, self.me, self.total_rows // 2
        lo, hi = self.owners

        def wait(sem, size):
            wait_sent(self.part.at[pl.ds(0, size)], self.sent.at[sem], self.recv.at[0, 0, 0])

        middle = (me == lo) | (me == hi)

        @pl.when(middle)
        def _():
            wait(0, half)
            wait(2, half)

        @pl.when((me != lo) & (me != hi))
        def _():
            wait(0, 2 * half)

        if lo > 0:

            @pl.when(middle)
            def _():
                wait(1, half)
                wait(3, half)

            if n > 4:

                @pl.when((me != lo) & (me != hi) & (me > 0) & (me < n - 1))
                def _():
                    wait(3, 2 * half)
        else:

            @pl.when(me == hi)
            def _():
                wait(1, half)

    @staticmethod
    def scratch(n, rows, width, chunk):
        return [
            pltpu.VMEM((rows, width), BF16),
            pltpu.VMEM((rows, width), BF16),
            pltpu.SemaphoreType.DMA((3, 2, min(rows // 2 // chunk, 12))),
            pltpu.SemaphoreType.DMA((4,)),
        ]


class GradSum:
    def __init__(self, fsdp, ctx, parts, axes, outs, held, recv, sent):
        self.fsdp, self.ctx, self.parts, self.axes, self.outs = fsdp, ctx, parts, axes, outs
        self.ys = fsdp // 2
        self.held, self.recv, self.sent = held, recv, sent
        self.f = lax.axis_index("fsdp")
        self.x = lax.axis_index("ctx")
        self.y, self.c = self.f // 2, lax.rem(self.f, 2)

    @staticmethod
    def block_shape(shape, axis, fsdp):
        r, c = shape
        return (r // fsdp, c) if axis == 0 else (r, c // fsdp)

    @staticmethod
    def scratch(fsdp, ctx, shapes, first=True):
        held = []
        for shape in shapes:
            if first:
                held.append(pltpu.VMEM((fsdp // 2,) + shape, BF16))
            held += [
                pltpu.VMEM((max(fsdp // 2 - 1, 1),) + shape, BF16),
                pltpu.VMEM((ctx,) + shape, BF16),
            ]
        return held

    @staticmethod
    def semaphores(fsdp, ctx, count):
        return [pltpu.SemaphoreType.DMA((count, 3, max(fsdp // 2, ctx)))] * 2

    def part(self, a, f):
        shape = self.held[a][0].shape[1:]
        return block(self.parts[a], self.axes[a], f, shape[self.axes[a]])

    def each(self, a, body):
        rows = self.held[a][0].shape[1]
        size = 32 if rows % 32 == 0 else 16

        def step(i, carry):
            body(pl.ds(pl.multiple_of(i * size, size), size))
            return carry

        lax.fori_loop(0, rows // size, step, 0)

    def start(self):
        for a in range(len(self.parts)):
            for k in range(self.ys):
                remote(self.part(a, 2 * k + 1 - self.c), self.held[a][0].at[k], self.sent.at[a, 0, k],
                       self.recv.at[a, 0, k], {"fsdp": sibling(self.f)}).start()

    def pair(self):
        for a in range(len(self.parts)):
            first = self.held[a][0]
            for k in range(self.ys):
                wait_came(first.at[k], self.sent.at[a, 0, k], self.recv.at[a, 0, k])
                mine = self.part(a, 2 * k + self.c)

                def add(rows, first=first, k=k, mine=mine):
                    first[k, rows, :] = (first[k, rows, :].astype(F32) + mine[rows, :].astype(F32)).astype(BF16)

                self.each(a, add)

    def second(self):
        for a in range(len(self.held)):
            first, later = self.held[a][0], self.held[a][1]
            for k in range(1, self.ys):
                to = lax.rem(self.y + k, self.ys)
                remote(first.at[to], later.at[k - 1], self.sent.at[a, 1, k], self.recv.at[a, 1, k],
                       {"fsdp": 2 * to + self.c}).start()

    def third(self):
        for a in range(len(self.held)):
            first, later, last = self.held[a]
            for k in range(1, self.ys):
                wait_came(later.at[k - 1], self.sent.at[a, 1, k], self.recv.at[a, 1, k])

            def add(rows, first=first, later=later, last=last):
                total = first[self.y, rows, :].astype(F32)
                for k in range(1, self.ys):
                    total = total + later[k - 1, rows, :].astype(F32)
                last[self.x, rows, :] = total.astype(BF16)

            self.each(a, add)
            for k in range(1, self.ctx):
                remote(last.at[self.x], last.at[self.x], self.sent.at[a, 2, k], self.recv.at[a, 2, self.x],
                       {"ctx": lax.rem(self.x + k, self.ctx)}).start()

    def fourth(self, store):
        for a in range(len(self.held)):
            last = self.held[a][2]
            for k in range(1, self.ctx):
                other = lax.rem(self.x + k, self.ctx)
                wait_came(last.at[other], self.sent.at[a, 2, k], self.recv.at[a, 2, other])

            def add(rows, last=last, a=a):
                total = last[0, rows, :].astype(F32)
                for k in range(1, self.ctx):
                    total = total + last[k, rows, :].astype(F32)
                store(a, rows, total)

            self.each(a, add)

    def drain_pair(self):
        for a in range(len(self.parts)):
            for k in range(self.ys):
                wait_sent(self.held[a][0].at[k], self.sent.at[a, 0, k], self.recv.at[a, 0, k])

    def drain(self):
        for a in range(len(self.held)):
            first, later, last = self.held[a]
            for k in range(1, self.ys):
                wait_sent(later.at[k - 1], self.sent.at[a, 1, k], self.recv.at[a, 1, k])
            for k in range(1, self.ctx):
                wait_sent(last.at[self.x], self.sent.at[a, 2, k], self.recv.at[a, 2, 0])


def loop(first, last, body):
    def step(s, carry):
        body(s)
        return carry

    lax.fori_loop(first, last, step, 0)


def params(ident, mib):
    return pltpu.CompilerParams(collective_id=ident, has_side_effects=True, vmem_limit_bytes=min(mib << 20, 67043328))


def shape_of(shape, dtype):
    return jax.ShapeDtypeStruct(shape, dtype)


TILE = 256


def dot(left, right):
    return jnp.dot(left, right, preferred_element_type=F32)


def dot_t(left, right):
    return lax.dot_general(left, right, (((1,), (1,)), ((), ())), preferred_element_type=F32)


def dot_rows(left, right):
    return lax.dot_general(left, right, (((0,), (0,)), ((), ())), preferred_element_type=F32)


def head_only(value, head):
    lane = lax.broadcasted_iota(jnp.int32, value.shape, 1)
    return jnp.where((lane // HEAD_DIM) == head, value, jnp.zeros_like(value))


class RowGather:
    def __init__(self, n, src, dst, recv, sent, own):
        self.n, self.src, self.dst = n, src, dst
        self.recv, self.sent, self.own = recv, sent, own
        self.me = lax.axis_index("tp")

    def start(self):
        me = self.me
        pltpu.make_async_copy(self.src, self.dst.at[me], self.own).start()

        @pl.when(me > 0)
        def _():
            remote(self.src, self.dst.at[me], self.sent.at[0, 0], self.recv.at[me], {"tp": me - 1}).start()

        @pl.when(me < self.n - 1)
        def _():
            remote(self.src, self.dst.at[me], self.sent.at[1, 0], self.recv.at[me], {"tp": me + 1}).start()

    def each(self, body, which=None):
        me, n = self.me, self.n
        for away in which or range(1, n):
            for way, tp in ((1, me - away), (0, me + away)):

                @pl.when((tp >= 0) & (tp < n))
                def _(tp=tp, way=way, away=away):
                    onward = (me < n - 1) if way == 1 else (me > 0)
                    body(away, way, tp, onward, {"tp": me + 1} if way == 1 else {"tp": me - 1})

    def relay(self, which=None):
        def body(away, way, tp, onward, to):
            here = self.dst.at[tp]
            wait_came(here, self.sent.at[way, away], self.recv.at[tp])

            @pl.when(onward)
            def _():
                remote(here, here, self.sent.at[way, away], self.recv.at[tp], to).start()

        self.each(body, which)

    def finish(self):
        me = self.me
        pltpu.make_async_copy(self.src, self.dst.at[me], self.own).wait()

        @pl.when(me > 0)
        def _():
            wait_sent(self.src, self.sent.at[0, 0], self.recv.at[0])

        @pl.when(me < self.n - 1)
        def _():
            wait_sent(self.src, self.sent.at[1, 0], self.recv.at[0])

        def body(away, way, tp, onward, to):
            @pl.when(onward)
            def _():
                wait_sent(self.src, self.sent.at[way, away], self.recv.at[0])

        self.each(body)

    @staticmethod
    def scratch(n):
        return [
            pltpu.SemaphoreType.DMA((n,)),
            pltpu.SemaphoreType.DMA((2, n)),
            pltpu.SemaphoreType.DMA,
        ]


class AxisSum:
    def __init__(self, axis, n, slots, recv, sent):
        self.axis, self.n, self.slots, self.recv, self.sent = axis, n, slots, recv, sent
        self.at = lax.axis_index(axis)

    def start(self, value):
        self.slots[self.at] = value
        for k in range(1, self.n):
            remote(self.slots.at[self.at], self.slots.at[self.at], self.sent.at[k], self.recv.at[self.at],
                   {self.axis: lax.rem(self.at + k, self.n)}).start()

    def finish(self):
        for k in range(1, self.n):
            other = lax.rem(self.at + k, self.n)
            wait_came(self.slots.at[other], self.sent.at[k], self.recv.at[other])
            wait_sent(self.slots.at[self.at], self.sent.at[k], self.recv.at[other])
        total = self.slots[0]
        for k in range(1, self.n):
            total = total + self.slots[k]
        return total

    @staticmethod
    def scratch(n, shape):
        return [
            pltpu.VMEM((n,) + shape, F32),
            pltpu.SemaphoreType.DMA((n,)),
            pltpu.SemaphoreType.DMA((n,)),
        ]


def window(ctx, tok_dev):
    return min(ctx, (tok_dev * ctx // 2 + tok_dev - 1) // tok_dev + 1)


def key_span(ctx, tok_dev):
    return min(ctx * tok_dev // 2 // TILE, (window(ctx, tok_dev) - 1) * (tok_dev // TILE))


R_ONE, SEGMENT, VALID = 0, 1, 2


def front(tokens, gain1, gain2, w_latent, shards, w_out, wide_shards, segments, fsdp, ctx, n):
    rows, width = tokens.shape
    seq_dev, tok_dev = segments.shape
    latent, q_width = LATENT, shards[0].shape[1]
    wide, chunk = 128, 256
    pieces = rows // chunk
    win = window(ctx, tok_dev)
    full = [shape_of((s.shape[0] * fsdp,) + s.shape[1:], s.dtype) for s in shards]
    wider = [shape_of((s.shape[0], s.shape[1] * fsdp), s.dtype) for s in wide_shards]
    per_group = HEADS // GROUPS * HEAD_DIM
    per_seq = tok_dev // chunk

    def kernel(*refs):
        (tok_in, ga, gb, wlat, wq, wk, wv, wo, wg, wu, seg), refs = refs[:11], refs[11:]
        (xn_out, cols, gain_all, w_lat, w_qry, w_kproj, w_vproj, gate_all, up_all), refs = refs[:9], refs[9:]
        (wo_all, seg_all, lat_all, query, keys, values), refs = refs[:6], refs[6:]
        (gbuf, sbuf, tok, xn, tsem), refs = refs[:5], refs[5:]
        bring = Bring([(tok_in, tok), (xn, xn_out)], tsem)
        bring.start([0])
        x, me = lax.axis_index("ctx"), lax.axis_index("tp")
        gbuf[...] = jnp.zeros_like(gbuf)
        gbuf[0:1, :] = ga[...].astype(F32).reshape(1, -1)
        gbuf[1:2, :] = gb[...].astype(F32).reshape(1, -1)
        sbuf[...] = jnp.zeros_like(sbuf)
        sbuf[0:seq_dev, :] = seg[...]
        meet(n, fsdp, ctx)
        group = me * q_width // per_group
        src_lat = wlat.at[:, pl.ds(pl.multiple_of(group * latent, latent), latent)]
        pairs = [(gbuf, gain_all), (src_lat, w_lat), (wq, w_qry), (wk, w_kproj), (wv, w_vproj),
                 (wg, gate_all), (wu, up_all)]
        spread = Spread(fsdp, pairs, [1, 0, 0, 0, 0, 1, 1], *refs[:3])
        share = CtxShare(ctx, sbuf, seg_all, *refs[3:6])
        line = RowGather(n, wo, wo_all, *refs[6:9])
        lat_recv, lat_sent = refs[9:11]
        spread.start()
        share.start()
        line.start()
        own = win - 1
        cols[...] = jnp.zeros_like(cols)
        bring.wait([0])

        def scale(i):
            at = pl.ds(pl.multiple_of(i * wide, wide), wide)
            value = tok[at, :].astype(F32)
            cols[at, R_ONE : R_ONE + 1] = lax.rsqrt(jnp.mean(value * value, axis=-1, keepdims=True) + eps)

        loop(0, rows // wide, scale)
        spread.relay([0, 1])
        spread.finish([0, 1])

        def place(shard, i):
            seq = i // per_seq
            return pl.ds(pl.multiple_of(seq * win * tok_dev + shard * tok_dev + lax.rem(i, per_seq) * chunk, chunk), chunk)

        def send(k, i):
            return remote(lat_all.at[place(own, i)], lat_all.at[place(own - k, i)], lat_sent.at[k, i],
                          lat_recv.at[own - k, i], {"ctx": x + k})

        def first(i):
            at = pl.ds(pl.multiple_of(i * chunk, chunk), chunk)
            unit = (tok[at, :].astype(F32) * cols[at, R_ONE : R_ONE + 1] * gain_all[0:1, :]).astype(BF16)
            xn[at, :] = unit
            lat_all[place(own, i), :] = dot(unit, w_lat[...]).astype(BF16)
            for k in range(1, win):

                @pl.when(x + k < ctx)
                def _(k=k):
                    send(k, i).start()

        loop(0, pieces, first)
        bring.start([1])
        line.relay([1])
        spread.relay([2, 3, 4])
        spread.finish([2, 3, 4])

        def project(shard, i):
            to = place(shard, i)
            value = lat_all[to, :]
            keys[to, :] = dot(value, w_kproj[...]).astype(BF16)
            values[to, :] = dot(value, w_vproj[...]).astype(BF16)

        def ask(i):
            at = pl.ds(pl.multiple_of(i * chunk, chunk), chunk)
            query[at, :] = dot(xn[at, :], w_qry[...]).astype(BF16)
            project(own, i)

        loop(0, pieces, ask)
        share.finish()
        for q in range(seq_dev):
            at = slice(q * tok_dev, (q + 1) * tok_dev)
            ids = jnp.broadcast_to(sbuf[q : q + 1, :].astype(F32), (128, tok_dev)).T
            cols[at, SEGMENT : SEGMENT + 1] = ids[:, 0:1]
            last = seg_all[ctx - 1, q : q + 1, tok_dev - 1 : tok_dev].astype(F32)
            cols[at, VALID : VALID + 1] = jnp.where(ids[:, 0:1] != last, 1.0, 0.0)
        line.relay(range(2, n))
        for k in range(1, win):

            def theirs(i, k=k):
                @pl.when(x - k >= 0)
                def _():
                    wait_came(lat_all.at[place(own - k, i)], lat_sent.at[k, i], lat_recv.at[own - k, i])

                @pl.when(x - k < 0)
                def _():
                    lat_all[place(own - k, i), :] = jnp.zeros((chunk, latent), BF16)

                project(own - k, i)

            loop(0, pieces, theirs)

            def gone(i, k=k):
                @pl.when(x + k < ctx)
                def _():
                    send(k, i).wait_send()

            loop(0, pieces, gone)
        spread.relay([5, 6])
        spread.finish([5, 6])
        line.finish()
        bring.wait([1])

    return pl.pallas_call(
        kernel,
        out_shape=(
            shape_of((rows, width), BF16),
            shape_of((rows, 128), F32),
            shape_of((8, width), F32),
            shape_of((width, latent), BF16),
            *full,
            *wider,
            shape_of((n,) + w_out.shape, w_out.dtype),
            shape_of((ctx, 8, tok_dev), segments.dtype),
            shape_of((win * rows, latent), BF16),
            shape_of((rows, q_width), BF16),
            shape_of((win * rows, q_width), BF16),
            shape_of((win * rows, q_width), BF16),
        ),
        in_specs=[ANY] + [VMEM] * 10,
        out_specs=(ANY,) + (VMEM,) * 6 + (ANY,) * 3 + (VMEM,) * 5,
        scratch_shapes=[
            pltpu.VMEM((8, gain1.shape[0]), F32),
            pltpu.VMEM((8, tok_dev), segments.dtype),
            pltpu.VMEM((rows, width), BF16),
            pltpu.VMEM((rows, width), BF16),
            pltpu.SemaphoreType.DMA((2,)),
        ]
        + Spread.scratch(fsdp, 7)
        + CtxShare.scratch(ctx)
        + RowGather.scratch(n)
        + [pltpu.SemaphoreType.DMA((win, pieces))] * 2,
        compiler_params=params(1, 56),
    )(tokens, gain1, gain2, w_latent, *shards, w_out, *wide_shards, segments)


def counted_keys(cols, segk, at, seq, q_first, first, count, tok_dev, win):
    per = tok_dev // TILE
    oldest = lax.axis_index("ctx") - (win - 1)
    mine = cols[at, SEGMENT : SEGMENT + 1]
    shape = (mine.shape[0], TILE)
    pieces = []
    for j in range(count):
        t = first + j
        shard = oldest + t // per
        inner = pl.ds(pl.multiple_of(lax.rem(t, per) * TILE, TILE), TILE)
        ids = segk[jnp.maximum(shard, 0), pl.ds(seq, 1), inner].astype(F32)
        q_at = q_first + lax.broadcasted_iota(jnp.int32, shape, 0)
        k_at = t * TILE + lax.broadcasted_iota(jnp.int32, shape, 1)
        pieces.append((k_at <= q_at) & (ids == mine) & (shard >= 0))
    return pieces


def middle(query, keys, values, seg_all, cols, shards, gate_all, up_all, gains, tokens, out_grad,
           fsdp, ctx, n, seq_dev, late):
    rows, width = tokens.shape
    q_width = query.shape[1]
    heads = q_width // HEAD_DIM
    inner = gate_all.shape[0]
    tok_dev = rows // seq_dev
    per = tok_dev // TILE
    win, span = window(ctx, tok_dev), key_span(ctx, tok_dev)
    tiles = span + 1
    part = TILE if tiles <= 3 else 64
    chunk, hop = 32, 2
    size, piece = 256, 64
    per_block = size // piece
    half = rows // 2
    cols_at = width // 4
    block_shape = (inner, width // fsdp)
    count = 3

    def kernel(*refs):
        (q_in, k_in, v_in, segk, cols, wo_in, wd_in, wg_in, wu_in, gain, tok_in, cot_in), refs = refs[:12], refs[12:]
        (o_branch, o_feed, o_dmid, o_mid, o_wo, o_gain, o_bsq, o_mark, o_att, o_lse), refs = refs[:10], refs[10:]
        outs, refs = refs[:3], refs[3:]
        one, gsems, parts, refs = refs[:4], refs[4:6], refs[6:9], refs[9:]
        (query, keys, values, att, att_all, wo, wd, wg, wu, tok, cot), refs = refs[:11], refs[11:]
        (mid, r2, xn, hid, dg, du, p_two, p_feed, bsem), refs = refs[:9], refs[9:]
        bring = Bring([(q_in, query), (k_in, keys), (v_in, values), (tok_in, tok), (wg_in, wg), (wu_in, wu),
                       (cot_in, cot), (att, o_att), (p_feed, o_feed)], bsem)
        bring.start(range(7))
        meet(n, fsdp, ctx)
        line = LineGather(n, piece, att, att_all, *refs[:3])
        spread = Spread(fsdp, [(wo_in, wo), (wd_in, wd)], [1, 1], *refs[3:6])
        keep = refs[6:]
        spread.start()
        o_gain[...] = jnp.zeros_like(o_gain)
        o_bsq[...] = jnp.zeros_like(o_bsq)
        o_mark[...] = jnp.zeros_like(o_mark)
        g2 = gain.at[1:2]

        def back(at, own, total):
            middle_rows = mid[at, :]
            o_mid[own, :] = middle_rows
            unit = middle_rows * r2[at, :]
            o_gain[...] += jnp.sum((total * unit).reshape(chunk // 8, 8, width), axis=0)
            scaled = total * g2[...]
            mean = jnp.mean(scaled * unit, axis=-1, keepdims=True)
            d_mid = cot[at, :].astype(F32) + r2[at, :] * (scaled - unit * mean)
            o_dmid[own, :] = d_mid
            first_unit = tok[at, :].astype(F32) * cols[at, R_ONE : R_ONE + 1]
            o_mark[at, 0:1] = jnp.sum(first_unit * d_mid, axis=-1, keepdims=True)
            return d_mid.astype(BF16)

        first = LineSum(n, chunk, hop, p_two, one[0], one[1], o_branch, one[2], one[3], back)
        if late:
            held = [[out, None, None] for out in outs]
        else:
            held = [keep[3 * a : 3 * a + 3] for a in range(count)]
        grad = GradSum(fsdp, ctx, parts, [1] * count, outs, held, *gsems)
        bring.wait([0, 1, 2])

        def query_rows(i, j):
            seq = i // per
            q_tile = (win - 1) * per + lax.rem(i, per)
            at = pl.ds(pl.multiple_of(i * TILE + j * part, part), part)
            near = pl.ds(pl.multiple_of((seq * win * per + q_tile - span) * TILE, TILE), tiles * TILE)
            counted = jnp.concatenate(
                [
                    c.astype(F32)
                    for c in counted_keys(
                        cols, segk, at, seq, q_tile * TILE + j * part, q_tile - span, tiles, tok_dev, win
                    )
                ],
                axis=1,
            )
            accum = jnp.zeros((part, q_width), F32)
            lane = lax.broadcasted_iota(jnp.int32, (part, 128), 1)
            kept = jnp.zeros((part, 128), F32)
            for h in range(heads):
                score = jnp.where(counted > 0.0, dot_t(head_only(query[at, :], h), keys[near, :]) * 0.125, -1e30)
                top = jnp.max(score, axis=-1, keepdims=True)
                weight = jnp.exp(score - top)
                total = jnp.sum(weight, axis=-1, keepdims=True)
                prob = (weight * (1.0 / total)).astype(BF16)
                accum = accum + jnp.dot(prob, head_only(values[near, :], h), preferred_element_type=F32)
                kept = jnp.where(lane == h, top + jnp.log(total), kept)
                if part == TILE:
                    line.step((i - 1) * per_block + h * per_block // heads)
            o_lse[at, :] = kept
            att[at, :] = accum.astype(BF16)

        def query_tile(i):
            if part == TILE:
                query_rows(i, 0)
                return
            loop(0, TILE // part, lambda j: query_rows(i, j))
            for h in range(per_block):
                line.step((i - 1) * per_block + h)

        loop(0, rows // TILE, query_tile)
        bring.start([7])
        line.begin()
        s1 = (rows // TILE - 1) * per_block
        spread.relay()
        spread.finish()
        tp = lax.axis_index("tp")
        o_wo[...] = wo[pl.ds(pl.multiple_of(tp * q_width, q_width), q_width), :]
        line.begun()
        bring.wait([3, 4, 5, 6])

        def block_of_rows(b):
            at = pl.ds(pl.multiple_of(b * size, size), size)
            seq = b * size // tok_dev

            def steps(j):
                line.step(s1 + b * per_block + j)
                first.step((b - 1) * per_block + j)

            branch = dot(att_all[at, :], wo[...])
            middle_rows = tok[at, :].astype(F32) + branch
            mid[at, :] = middle_rows
            o_bsq[pl.ds(pl.multiple_of(seq * 8, 8), 8), :] += jnp.sum(
                (branch * branch * cols[at, VALID : VALID + 1]).reshape(size // 8, 8, width), axis=0
            )
            scale = lax.rsqrt(jnp.mean(middle_rows * middle_rows, axis=-1, keepdims=True) + eps)
            r2[at, :] = scale
            unit = (middle_rows * scale * g2[...]).astype(BF16)
            xn[at, :] = unit
            steps(0)
            gate = dot_t(unit, wg[...])
            upper = dot_t(unit, wu[...])
            sigma = jax.nn.sigmoid(gate)
            swish = gate * sigma
            hidden = (swish * upper).astype(BF16)
            hid[at, :] = hidden
            slope = upper * sigma * (1.0 + gate * (1.0 - sigma))
            steps(1)
            p_feed[at, :] = dot(hidden, wd[...]).astype(BF16)
            d_hidden = dot_t(cot[at, :], wd[...])
            d_gate = (d_hidden * slope).astype(BF16)
            d_upper = (d_hidden * swish).astype(BF16)
            dg[at, :] = d_gate
            du[at, :] = d_upper
            steps(2)
            p_two[at, :] = (dot(d_gate, wg[...]) + dot(d_upper, wu[...])).astype(BF16)
            steps(3)

        loop(0, rows // size, block_of_rows)
        bring.start([8])
        s0 = (rows // size - 1) * per_block

        def product(i):
            at = pl.ds(pl.multiple_of(i * cols_at, cols_at), cols_at)
            left = xn[:, at]
            parts[0][:, at] = dot_rows(dg[...], left).astype(BF16)
            parts[1][:, at] = dot_rows(du[...], left).astype(BF16)
            parts[2][:, at] = dot_rows(hid[...], cot[:, at]).astype(BF16)

        def busy(s):
            first.step(s)
            product(s - s0)

        loop(s0, s0 + 4, busy)
        grad.start()
        last = first.steps()
        loop(s0 + 4, s0 + 6, first.step)
        grad.pair()
        if not late:
            grad.second()
        loop(s0 + 6, last, first.step)
        if not late:
            grad.third()

            def store(a, at, total):
                outs[a][at, :] = total

            grad.fourth(store)
            grad.drain()
        line.drain()
        first.drain()
        grad.drain_pair()
        bring.wait([7, 8])

    ys = fsdp // 2
    out = pl.pallas_call(
        kernel,
        out_shape=(
            shape_of((rows, width), BF16),
            shape_of((rows, width), BF16),
            shape_of((half, width), F32),
            shape_of((half, width), F32),
            shape_of((q_width, width), BF16),
            shape_of((8, width), F32),
            shape_of((8 * seq_dev, width), F32),
            shape_of((rows, 128), F32),
            shape_of((rows, q_width), BF16),
            shape_of((rows, 128), F32),
        )
        + ((shape_of((ys,) + block_shape, BF16) if late else shape_of(block_shape, F32)),) * count,
        in_specs=[ANY] * 3 + [VMEM] * 4 + [ANY] * 2 + [VMEM] + [ANY] * 2,
        out_specs=(VMEM, ANY) + (VMEM,) * 6 + (ANY, VMEM) + (VMEM,) * count,
        scratch_shapes=LineSum.scratch(n, rows, width, chunk)
        + GradSum.semaphores(fsdp, ctx, count)
        + [pltpu.VMEM((inner, width), BF16)] * count
        + [
            pltpu.VMEM((rows, q_width), BF16),
            pltpu.VMEM((win * rows, q_width), BF16),
            pltpu.VMEM((win * rows, q_width), BF16),
            pltpu.VMEM((rows, q_width), BF16),
            pltpu.VMEM((rows, n * q_width), BF16),
            pltpu.VMEM((n * q_width, width), BF16),
            pltpu.VMEM((inner, width), BF16),
            pltpu.VMEM((inner, width), BF16),
            pltpu.VMEM((inner, width), BF16),
            pltpu.VMEM((rows, width), BF16),
            pltpu.VMEM((rows, width), BF16),
            pltpu.VMEM((rows, width), F32),
            pltpu.VMEM((rows, 1), F32),
            pltpu.VMEM((rows, width), BF16),
            pltpu.VMEM((rows, inner), BF16),
            pltpu.VMEM((rows, inner), BF16),
            pltpu.VMEM((rows, inner), BF16),
            pltpu.VMEM((rows, width), BF16),
            pltpu.VMEM((rows, width), BF16),
            pltpu.SemaphoreType.DMA((9,)),
        ]
        + LineGather.scratch(n, rows // piece)
        + Spread.scratch(fsdp, 2)
        + ([] if late else GradSum.scratch(fsdp, ctx, [block_shape] * count)),
        compiler_params=params(2, 64),
    )(query, keys, values, seg_all, cols, *shards, gate_all, up_all, gains, tokens, out_grad)
    return out[:10], out[10:]


def back(query, keys, values, seg_all, cols, lse, attended, d_branch, wo_rows, weights, lat_all, xn_one, gains,
         tokens, d_middle, mid_own, part_feed, marks, gain_part, branch_sq, firsts, fsdp, ctx, n, seq_dev):
    rows, width = tokens.shape
    w_qry, w_lat, w_kproj, w_vproj = weights
    q_width, latent = query.shape[1], w_lat.shape[1]
    heads, tok_dev = q_width // HEAD_DIM, rows // seq_dev
    per = tok_dev // TILE
    win, span = window(ctx, tok_dev), key_span(ctx, tok_dev)
    tiles = span + 1
    group = tiles if tiles <= 3 else 1
    chunk, hop, wide, side = 32, 2, 256, 128
    half = rows // 2
    axes = (0, 0, 0, 1, 0)
    whole = ((width, q_width), (latent, q_width), (latent, q_width), (q_width, width), (width, latent))
    blocks = [GradSum.block_shape(w, a, fsdp) for w, a in zip(whole, axes)]
    lat = blocks[-1]
    ffn = [f.shape[1:] for f in firsts]
    seq_pieces = tok_dev // wide
    many = max(width, rows)

    def kernel(*refs):
        (q_ref, k_ref, v_ref, segk, cols, lse_ref, att, dbr, wo), refs = refs[:9], refs[9:]
        (wq, wl, wk, wv, la_in, xn_in, gain, tok_in, dmid_in, mid_in, feed_in), refs = refs[:11], refs[11:]
        (marks, gain_two, bsq), fsts, refs = refs[:3], refs[3 : 3 + len(ffn)], refs[3 + len(ffn) :]
        (o_tok, o_mixed, o_small), outs, refs = refs[:3], refs[3:8], refs[8:]
        fouts, refs = refs[: len(ffn)], refs[len(ffn) :]
        one, two, keep, gsems, parts, refs = refs[:4], refs[4:8], refs[8:23], refs[23:25], refs[25:30], refs[30:]
        (p_one, dlat, came, c_recv, c_sent, gacc, sm, sacc), refs = refs[:8], refs[8:]
        (dk, dv, dq, dqb, grad_seq, lat_parts), refs = refs[:6], refs[6:]
        (la, xn, tok, dmid, mid, p_feed, bsem), refs = refs[:7], refs[7:]
        (lat_own, lat_every), lsems, sums, refs = refs[:2], refs[2:5], refs[5:14], refs[14:]
        bring = Bring([(feed_in, p_feed), (mid_in, mid), (la_in, la), (xn_in, xn), (tok_in, tok), (dmid_in, dmid)], bsem)
        bring.start()
        meet(n, fsdp, ctx, everyone=True)
        x = lax.axis_index("ctx")
        own_shard = win - 1
        grad_ffn = None
        if ffn:
            fkeep, fsems = refs[: 2 * len(ffn)], refs[2 * len(ffn) :]
            grad_ffn = GradSum(fsdp, ctx, [], [], fouts,
                               [[fsts[a], fkeep[2 * a], fkeep[2 * a + 1]] for a in range(len(ffn))], *fsems)
            grad_ffn.second()
        gacc[...] = jnp.zeros_like(gacc)
        sacc[...] = jnp.zeros_like(sacc)
        sm[...] = jnp.zeros_like(sm)
        g1 = gain.at[0:1]

        def forward(at, own, total):
            mixed = mid[own, :] + total
            seq = at.start // tok_dev
            counted = cols[at, VALID : VALID + 1]
            sacc[seq] += jnp.sum((mixed * mixed * counted).reshape(chunk // 8, 8, width), axis=0)
            sacc[seq_dev + seq] += jnp.sum((total * total * counted).reshape(chunk // 8, 8, width), axis=0)
            return mixed.astype(BF16)

        def backward(at, own, total):
            r1 = cols[at, R_ONE : R_ONE + 1]
            unit = tok[at, :].astype(F32) * r1
            scaled = total * g1[...]
            mean = jnp.mean(scaled * unit, axis=-1, keepdims=True)
            return (dmid[own, :] + r1 * (scaled - unit * mean)).astype(BF16)

        feed = LineSum(n, chunk, hop, p_feed, two[0], two[1], o_mixed, two[2], two[3], forward)
        first = LineSum(n, chunk, hop, p_one, one[0], one[1], o_tok, one[2], one[3], backward)
        grad = GradSum(fsdp, ctx, parts, axes, outs, [keep[3 * a : 3 * a + 3] for a in range(5)], *gsems)
        line = RowGather(n, lat_own, lat_every, *lsems)
        over_tp = AxisSum("tp", n, *sums[0:3])
        over_ctx = AxisSum("ctx", ctx, *sums[3:6])
        over_fsdp = AxisSum("fsdp", fsdp, *sums[6:9])

        def clear(i):
            at = pl.ds(pl.multiple_of(i * TILE, TILE), TILE)
            dk[at, :] = jnp.zeros((TILE, q_width), F32)
            dv[at, :] = jnp.zeros((TILE, q_width), F32)

        loop(0, win * rows // TILE, clear)
        bring.wait([0, 1])

        def query_tile(i, step):
            seq = i // per
            q_tile = own_shard * per + lax.rem(i, per)
            at = pl.ds(pl.multiple_of(i * TILE, TILE), TILE)
            grad_seq[...] = dot_t(dbr[at, :], wo[...]).astype(BF16)
            product = grad_seq[...].astype(F32) * att[at, :].astype(F32)
            delta = [jnp.sum(head_only(product, h), axis=-1, keepdims=True) for h in range(heads)]
            dq[...] = jnp.zeros_like(dq)

            def key_tiles(kk):
                t = q_tile - span + kk * group
                near = pl.ds(pl.multiple_of((seq * win * per + t) * TILE, TILE), group * TILE)
                counted = jnp.concatenate(
                    [c.astype(F32) for c in counted_keys(cols, segk, at, seq, q_tile * TILE, t, group, tok_dev, win)], axis=1
                )
                kept = lse_ref[at, :]
                d_query = jnp.zeros((TILE, q_width), F32)
                d_key = jnp.zeros((group * TILE, q_width), F32)
                d_value = jnp.zeros((group * TILE, q_width), F32)
                for h in range(heads):
                    mine, ours = head_only(q_ref[at, :], h), head_only(grad_seq[...], h)
                    score = jnp.where(counted > 0.0, dot_t(mine, k_ref[near, :]) * 0.125, -1e30)
                    prob = jnp.exp(score - kept[:, h : h + 1]) * counted
                    d_score = (prob * (dot_t(ours, v_ref[near, :]) - delta[h])).astype(BF16)
                    d_query = d_query + jnp.dot(d_score, head_only(k_ref[near, :], h), preferred_element_type=F32)
                    d_key = d_key + dot_rows(d_score, mine)
                    d_value = d_value + dot_rows(prob.astype(BF16), ours)
                    step(kk * heads + h)
                dq[...] += d_query
                dk[near, :] += d_key * 0.125
                dv[near, :] += d_value

            loop(0, tiles // group, key_tiles)
            dqb[at, :] = (dq[...] * 0.125).astype(BF16)

        def latent_rows(shard, seq, i):
            return pl.ds(pl.multiple_of((seq * win + shard) * tok_dev + i * wide, wide), wide)

        def send(k, seq, i):
            at = pl.ds(pl.multiple_of(seq * tok_dev + i * wide, wide), wide)
            return remote(lat_parts.at[latent_rows(own_shard - k, seq, i)], came.at[k - 1, at],
                          c_sent.at[k - 1, seq, i], c_recv.at[k - 1, seq, i], {"ctx": x - k})

        def latents(seq):
            for k in range(win - 1, -1, -1):
                for i in range(seq_pieces):
                    at = latent_rows(own_shard - k, seq, i)
                    lat_parts[at, :] = (
                        dot_t(dk[at, :].astype(BF16), wk[...]) + dot_t(dv[at, :].astype(BF16), wv[...])
                    ).astype(BF16)
                    if k > 0:

                        @pl.when(x - k >= 0)
                        def _(k=k, i=i):
                            send(k, seq, i).start()

        def whole_latent(j):
            seq, i = j // seq_pieces, lax.rem(j, seq_pieces)
            at = pl.ds(pl.multiple_of(j * wide, wide), wide)
            dlat[at, :] = lat_parts[latent_rows(own_shard, seq, i), :]
            for k in range(1, win):

                @pl.when(x + k < ctx)
                def _(k=k):
                    wait_came(came.at[k - 1, at], c_sent.at[k - 1, seq, i], c_recv.at[k - 1, seq, i])
                    dlat[at, :] = (dlat[at, :].astype(F32) + came[k - 1, at, :].astype(F32)).astype(BF16)

            p_one[at, :] = (dot_t(dqb[at, :], wq[...]) + dot_t(dlat[at, :], wl[...])).astype(BF16)

        tile_steps = (tiles // group) * heads
        every = max(tile_steps // 4, 1)

        def sequence(seq):
            def tile(i):
                def step(j):
                    @pl.when(lax.rem(j, every) == 0)
                    def _():
                        feed.step(i * (tile_steps // every) + j // every)

                query_tile(i, step)

            loop(seq * per, seq * per + per, tile)
            latents(seq)

        loop(0, seq_dev, sequence)
        fed = seq_dev * per * (tile_steps // every)

        bring.wait([2, 3, 4, 5])

        def product(i):
            at = pl.ds(pl.multiple_of(i * wide, wide), wide)
            parts[0][at, :] = dot_rows(xn[:, at], dqb[...]).astype(BF16)
            parts[3][:, at] = dot_rows(att[...], dbr[:, at]).astype(BF16)

        def steps(s):
            first.step(s)
            feed.step(fed + s)

        early = (seq_dev - 1) * seq_pieces
        loop(0, early, whole_latent)

        def mixed_work(i):
            product(i)
            steps(i)

        loop(0, width // wide, mixed_work)
        s0 = width // wide
        if grad_ffn is not None:
            grad_ffn.third()
        parts[1][...] = dot_rows(la[...], dk[...].astype(BF16)).astype(BF16)
        parts[2][...] = dot_rows(la[...], dv[...].astype(BF16)).astype(BF16)
        loop(early, rows // wide, whole_latent)

        def product_lat(s):
            at = pl.ds(pl.multiple_of((s - s0) * wide, wide), wide)
            parts[4][at, :] = dot_rows(xn[:, at], dlat[...]).astype(BF16)
            steps(s)

        begun = s0 + width // wide
        loop(s0, begun, product_lat)
        grad.start()

        def gains_of(s):
            steps(s)
            at = pl.ds(pl.multiple_of((s - begun) * side, side), side)
            value = p_one[at, :].astype(F32) * (tok[at, :].astype(F32) * cols[at, R_ONE : R_ONE + 1])
            gacc[...] += jnp.sum(value.reshape(side // 8, 8, width), axis=0)
            along = lax.dot_general(jnp.ones((8, width), F32), value * g1[...], (((1,), (1,)), ((), ())),
                                    precision=lax.Precision.HIGHEST, preferred_element_type=F32)
            sm[3:4, at] = along[0:1, :]
            sm[4:5, at] = marks[at, :].T[0:1, :]
            sm[5:6, at] = cols[at, :].T[R_ONE : R_ONE + 1, :]

        mark = begun + rows // side
        loop(begun, begun + 1, gains_of)
        grad.pair()
        grad.second()
        loop(begun + 1, begun + 4, gains_of)
        grad.third()
        loop(begun + 4, mark, gains_of)
        last = first.steps()
        for s in range(fed + mark, feed.steps()):
            feed.step(s)
        lane = lax.broadcasted_iota(jnp.int32, (1, many), 1)
        once = jnp.where(lax.axis_index("tp") == 0, 1.0, 0.0)
        row = jnp.zeros((1, many), F32)

        def whole_sum(value):
            return jnp.sum(jnp.sum(value, axis=0, keepdims=True), axis=1, keepdims=True)

        for q in range(seq_dev):
            values = [
                whole_sum(sacc[q]),
                whole_sum(sacc[seq_dev + q]),
                whole_sum(bsq[8 * q : 8 * q + 8, :]) * once,
                jnp.sum(cols[q * tok_dev : (q + 1) * tok_dev, VALID : VALID + 1], axis=0, keepdims=True) * once,
            ]
            for j, value in enumerate(values):
                row = row + jnp.where(lane == 4 * q + j, value, 0.0)
        sm[2:3, :] = row
        sm[0:1, 0:width] = jnp.sum(gacc[...], axis=0, keepdims=True)
        sm[1:2, 0:width] = jnp.sum(gain_two[...], axis=0, keepdims=True)
        r_row = sm[5:6, :]
        over_tp.start(sm[...])

        def store(a, at, total):
            if a < 4:
                outs[a][at, :] = total
            else:
                lat_own[at, :] = total.astype(BF16)

        def store_ffn(a, at, total):
            fouts[a][at, :] = total

        grad.fourth(store)
        line.start()
        loop(mark, mark + 2, steps)
        line.relay([1])
        along_tp = over_tp.finish()
        over_ctx.start(along_tp)
        loop(mark + 2, mark + 4, steps)
        if n > 2:
            line.relay([2])
        along_ctx = over_ctx.finish()
        over_fsdp.start(along_ctx)
        if grad_ffn is not None:
            grad_ffn.fourth(store_ffn)
        loop(mark + 4, last, steps)
        if n > 3:
            line.relay(range(3, n))
        everywhere = over_fsdp.finish()
        row = lax.broadcasted_iota(jnp.int32, everywhere.shape, 0)
        o_small[...] = jnp.where(row < 2, everywhere, along_ctx)
        o_small[3:4, :] = (along_tp[4:5] + eps * r_row * r_row * r_row * along_tp[3:4]) * (1.0 / width**0.5)
        line.finish()

        def gather(i):
            at = pl.ds(pl.multiple_of(i * 16, 16), 16)
            for g in range(GROUPS):
                total = jnp.zeros((16, lat[1]), F32)
                for t in range(n):
                    if t * GROUPS // n == g:
                        total = total + lat_every[t, at, :].astype(F32)
                outs[4][at, g * lat[1] : (g + 1) * lat[1]] = total

        loop(0, lat[0] // 16, gather)
        for k in range(1, win):

            @pl.when(x - k >= 0)
            def _(k=k):
                for seq in range(seq_dev):
                    for i in range(seq_pieces):
                        send(k, seq, i).wait_send()

        feed.drain()
        first.drain()
        grad.drain_pair()
        grad.drain()
        if grad_ffn is not None:
            grad_ffn.drain()

    out = pl.pallas_call(
        kernel,
        out_shape=(
            shape_of((rows, width), BF16),
            shape_of((rows, width), BF16),
            shape_of((8, many), F32),
        )
        + tuple(shape_of(b, F32) for b in blocks[:-1])
        + (shape_of((lat[0], GROUPS * lat[1]), F32),)
        + tuple(shape_of(f, F32) for f in ffn),
        in_specs=[VMEM] * 13 + [ANY] * 2 + [VMEM] + [ANY] * 4 + [VMEM] * (3 + len(ffn)),
        out_specs=(VMEM,) * (8 + len(ffn)),
        scratch_shapes=LineSum.scratch(n, rows, width, chunk) * 2
        + GradSum.scratch(fsdp, ctx, blocks)
        + GradSum.semaphores(fsdp, ctx, 5)
        + [pltpu.VMEM(w, BF16) for w in whole]
        + [
            pltpu.VMEM((rows, width), BF16),
            pltpu.VMEM((rows, latent), BF16),
            pltpu.VMEM((max(win - 1, 1), rows, latent), BF16),
            pltpu.SemaphoreType.DMA((max(win - 1, 1), seq_dev, seq_pieces)),
            pltpu.SemaphoreType.DMA((max(win - 1, 1), seq_dev, seq_pieces)),
            pltpu.VMEM((8, width), F32),
            pltpu.VMEM((8, many), F32),
            pltpu.VMEM((2 * seq_dev, 8, width), F32),
            pltpu.VMEM((win * rows, q_width), F32),
            pltpu.VMEM((win * rows, q_width), F32),
            pltpu.VMEM((TILE, q_width), F32),
            pltpu.VMEM((rows, q_width), BF16),
            pltpu.VMEM((TILE, q_width), BF16),
            pltpu.VMEM((win * rows, latent), BF16),
        ]
        + [
            pltpu.VMEM((win * rows, latent), BF16),
            pltpu.VMEM((rows, width), BF16),
            pltpu.VMEM((rows, width), BF16),
            pltpu.VMEM((half, width), F32),
            pltpu.VMEM((half, width), F32),
            pltpu.VMEM((rows, width), BF16),
            pltpu.SemaphoreType.DMA((6,)),
        ]
        + [pltpu.VMEM(lat, BF16), pltpu.VMEM((n,) + lat, BF16)]
        + RowGather.scratch(n)
        + AxisSum.scratch(n, (8, many))
        + AxisSum.scratch(ctx, (8, many))
        + AxisSum.scratch(fsdp, (8, many))
        + (GradSum.scratch(fsdp, ctx, ffn, False) + GradSum.semaphores(fsdp, ctx, len(ffn)) if ffn else []),
        compiler_params=params(3, 64),
    )(query, keys, values, seg_all, cols, lse, attended, d_branch, wo_rows, w_qry, w_lat, w_kproj, w_vproj,
      lat_all, xn_one, gains, tokens, d_middle, mid_own, part_feed, marks, gain_part, branch_sq, *firsts)
    return out[:3], out[3:8], out[8:]


def publish(arrays, small, seq_dev, tok_dev, feat_dim, fsdp):
    count = len(arrays)
    per = feat_dim // fsdp

    def kernel(*refs):
        srcs, sm, refs = refs[:count], refs[count], refs[count + 1 :]
        dsts, (gain1, gain2, stats, radial), refs = refs[:count], refs[count : count + 4], refs[count + 4 :]
        inward = Bring(list(zip(srcs, refs[:count])), refs[count])
        outward = Bring(list(zip(refs[:count], dsts)), refs[count + 1])
        inward.start()
        f = lax.axis_index("fsdp")
        mine = pl.ds(pl.multiple_of(f * per, per), per)
        gain1[...] = sm[0:1, mine].reshape(per)
        gain2[...] = sm[1:2, mine].reshape(per)
        for q in range(seq_dev):
            radial[q : q + 1, :] = sm[3:4, q * tok_dev : (q + 1) * tok_dev]
            total = sm[2:3, 4 * q + 3 : 4 * q + 4] * feat_dim
            for j, lane in enumerate((0, 2, 1)):
                stats[q : q + 1, j : j + 1] = jnp.sqrt(sm[2:3, 4 * q + lane : 4 * q + lane + 1] / total)
        for i in range(count):
            inward.wait([i])
            outward.start([i])
        outward.wait()

    out = pl.pallas_call(
        kernel,
        out_shape=tuple(shape_of(a.shape, a.dtype) for a in arrays)
        + (shape_of((per,), F32),) * 2
        + (shape_of((seq_dev, 3), F32), shape_of((seq_dev, tok_dev), F32)),
        in_specs=[ANY] * count + [VMEM],
        out_specs=(ANY,) * count + (VMEM,) * 4,
        scratch_shapes=[pltpu.VMEM(a.shape, a.dtype) for a in arrays] + [pltpu.SemaphoreType.DMA((count,))] * 2,
        compiler_params=pltpu.CompilerParams(vmem_limit_bytes=60 << 20),
    )(*arrays, small)
    return out[:count], out[count:]


class AxisShare:
    def __init__(self, axis, n, src, dst, recv, sent, own):
        self.axis, self.n, self.src, self.dst = axis, n, src, dst
        self.recv, self.sent, self.own = recv, sent, own
        self.at = lax.axis_index(axis)

    def start(self):
        for k in range(1, self.n):
            remote(self.src, self.dst.at[self.at], self.sent.at[k - 1], self.recv.at[self.at],
                   {self.axis: lax.rem(self.at + k, self.n)}).start()
        pltpu.make_async_copy(self.src, self.dst.at[self.at], self.own).start()

    def finish(self):
        for k in range(1, self.n):
            other = lax.rem(self.at + k, self.n)
            wait_came(self.dst.at[other], self.sent.at[k - 1], self.recv.at[other])
            wait_sent(self.src, self.sent.at[k - 1], self.recv.at[other])
        pltpu.make_async_copy(self.src, self.dst.at[self.at], self.own).wait()

    @staticmethod
    def scratch(n):
        return CtxShare.scratch(n)


class HalfSpread:
    def __init__(self, fsdp, pairs, recv, sent, own):
        self.fsdp, self.pairs, self.recv, self.sent, self.own = fsdp, pairs, recv, sent, own
        self.f, self.x = lax.axis_index("fsdp"), lax.axis_index("ctx")
        self.ys = fsdp // 2

    def view(self, a, f, half=None):
        src, dst = self.pairs[a]
        rows, size = src.shape
        columns = pl.ds(pl.multiple_of(f * size, size), size)
        if half is None:
            return dst.at[:, columns]
        return dst.at[pl.ds(pl.multiple_of(half * (rows // 2), rows // 2), rows // 2), columns]

    def part(self, a):
        src = self.pairs[a][0]
        return src.at[pl.ds(pl.multiple_of(self.x * (src.shape[0] // 2), src.shape[0] // 2), src.shape[0] // 2)]

    def start(self, which):
        for a in which:
            for k in range(1, self.ys):
                remote(self.part(a), self.view(a, self.f, self.x), self.sent.at[a, 0, k - 1], self.recv.at[a, 0, k - 1],
                       {"fsdp": lax.rem(self.f + 2 * k, self.fsdp)}).start()
        for a in which:
            src = self.pairs[a][0]
            remote(src, self.view(a, self.f), self.sent.at[a, 1, 0], self.recv.at[a, 1, 0],
                   {"fsdp": sibling(self.f)}).start()
            pltpu.make_async_copy(src, self.view(a, self.f), self.own.at[a]).start()

    def source(self, k):
        return lax.rem(self.f - 2 * k + self.fsdp, self.fsdp)

    def relay(self, which):
        for a in which:
            for k in range(1, self.ys):
                here = self.view(a, self.source(k), self.x)
                wait_came(here, self.sent.at[a, 0, k - 1], self.recv.at[a, 0, k - 1])
                remote(here, here, self.sent.at[a, 2, k - 1], self.recv.at[a, 2, k - 1], {"ctx": 1 - self.x}).start()
                remote(here, here, self.sent.at[a, 3, k - 1], self.recv.at[a, 3, k - 1],
                       {"fsdp": sibling(self.f)}).start()

    def cross(self, which):
        for a in which:
            for k in range(1, self.ys):
                here = self.view(a, self.source(k), 1 - self.x)
                wait_came(here, self.sent.at[a, 2, k - 1], self.recv.at[a, 2, k - 1])
                remote(here, here, self.sent.at[a, 4, k - 1], self.recv.at[a, 4, k - 1],
                       {"fsdp": sibling(self.f)}).start()

    def finish(self, which):
        for a in which:
            src = self.pairs[a][0]
            other = sibling(self.f)
            wait_came(self.view(a, other), self.sent.at[a, 1, 0], self.recv.at[a, 1, 0])
            pltpu.make_async_copy(src, self.view(a, self.f), self.own.at[a]).wait()
            for k in range(1, self.ys):
                there = lax.rem(other - 2 * k + self.fsdp, self.fsdp)
                wait_came(self.view(a, there, self.x), self.sent.at[a, 3, k - 1], self.recv.at[a, 3, k - 1])
                wait_came(self.view(a, there, 1 - self.x), self.sent.at[a, 4, k - 1], self.recv.at[a, 4, k - 1])

    def drain(self, which):
        for a in which:
            wait_sent(self.view(a, self.f), self.sent.at[a, 1, 0], self.recv.at[a, 1, 0])
            for k in range(1, self.ys):
                for kind in (0, 2, 3, 4):
                    wait_sent(self.part(a), self.sent.at[a, kind, k - 1], self.recv.at[a, kind, k - 1])

    @staticmethod
    def scratch(fsdp, arrays):
        return [
            pltpu.SemaphoreType.DMA((arrays, 5, max(fsdp // 2 - 1, 1))),
            pltpu.SemaphoreType.DMA((arrays, 5, max(fsdp // 2 - 1, 1))),
            pltpu.SemaphoreType.DMA((arrays,)),
        ]


R_TWO, MARK, LSE = 3, 4, 8


def layer(tokens, gain1, gain2, w_latent, shards, w_out, wide_shards, segments, out_grad, fsdp, ctx, n):
    rows, width = tokens.shape
    seq_dev, tok_dev = segments.shape
    w_query = shards[0]
    latent, q_width, inner = LATENT, w_query.shape[1], wide_shards[0].shape[0]
    heads = q_width // HEAD_DIM
    per = tok_dev // TILE
    win, span = window(ctx, tok_dev), key_span(ctx, tok_dev)
    own_shard = win - 1
    tiles = span + 1
    keyed = win * rows
    per_group = HEADS // GROUPS * HEAD_DIM
    wide, chunk = 128, 256
    pieces = rows // chunk
    per_seq = tok_dev // chunk
    strip, hop, reach, behind = 32, 2, 3, 2
    piece = 64
    per_block = TILE // piece
    side = 128
    many = max(width, rows)
    q_tiles = rows // TILE
    steps_all = rows // 2 // strip
    lag = hop * 2 * (n // 2)
    ffn = (inner, width // fsdp)
    axes = (0, 0, 0, 1, 0)
    whole = ((width, q_width), (latent, q_width), (latent, q_width), (q_width, width), (width, latent))
    blocks = [GradSum.block_shape(w, a, fsdp) for w, a in zip(whole, axes)]
    lat = blocks[-1]
    cols_at = width // 4

    scratch = dict(
        gbuf=pltpu.VMEM((8, gain1.shape[0]), F32),
        sbuf=pltpu.VMEM((8, tok_dev), segments.dtype),
        gain=pltpu.VMEM((8, width), F32),
        segk=pltpu.VMEM((ctx, 8, tok_dev), segments.dtype),
        cols=pltpu.VMEM((rows, 128), F32),
        tok=pltpu.VMEM((rows, width), BF16),
        gathered=pltpu.VMEM((rows, n * q_width), BF16),
        wo=pltpu.VMEM((n * q_width, width), BF16),
        cot=pltpu.VMEM((rows, width), BF16),
        xn=pltpu.VMEM((rows, width), BF16),
        p_two=pltpu.VMEM((rows, width), BF16),
        p_feed=pltpu.VMEM((rows, width), BF16),
        left=pltpu.VMEM((rows, width), BF16),
        right=pltpu.VMEM((rows, width), BF16),
        branch=pltpu.VMEM((rows, width), BF16),
        mid=pltpu.VMEM((rows, width), F32),
        wg=pltpu.VMEM((inner, width), BF16),
        wu=pltpu.VMEM((inner, width), BF16),
        wd=pltpu.VMEM((inner, width), BF16),
        hid=pltpu.VMEM((rows, inner), BF16),
        dg=pltpu.VMEM((rows, inner), BF16),
        du=pltpu.VMEM((rows, inner), BF16),
        w_lat=pltpu.VMEM((width, latent), BF16),
        w_qry=pltpu.VMEM((width, q_width), BF16),
        w_kproj=pltpu.VMEM((latent, q_width), BF16),
        w_vproj=pltpu.VMEM((latent, q_width), BF16),
        wo_rows=pltpu.VMEM((q_width, width), BF16),
        wo_line=pltpu.VMEM((n,) + w_out.shape, BF16),
        lat_all=pltpu.VMEM((keyed, latent), BF16),
        query=pltpu.VMEM((rows, q_width), BF16),
        keys=pltpu.VMEM((keyed, q_width), BF16),
        values=pltpu.VMEM((keyed, q_width), BF16),
        att=pltpu.VMEM((rows, q_width), BF16),
        dk=pltpu.VMEM((keyed, q_width), F32),
        dv=pltpu.VMEM((keyed, q_width), F32),
        dqb=pltpu.VMEM((rows, q_width), BF16),
        grad_seq=pltpu.VMEM((TILE, q_width), BF16),
        lat_parts=pltpu.VMEM((keyed, latent), BF16),
        dlat=pltpu.VMEM((rows, latent), BF16),
        came=pltpu.VMEM((rows, latent), BF16),
        g_sum=pltpu.VMEM((8, width), F32),
        g_sum2=pltpu.VMEM((8, width), F32),
        sm=pltpu.VMEM((8, many), F32),
        sacc=pltpu.VMEM((3 * seq_dev, 8, width), F32),
        lat_own=pltpu.VMEM(lat, BF16),
        lat_every=pltpu.VMEM((n, lat[0] // 2, lat[1]), BF16),
        lat_sum=pltpu.VMEM((lat[0] // 2, GROUPS * lat[1]), BF16),
        lat_both=pltpu.VMEM((ctx, lat[0] // 2, GROUPS * lat[1]), BF16),
        local=pltpu.SemaphoreType.DMA((2,)),
        flush=pltpu.SemaphoreType.DMA((11,)),
        lat_recv=pltpu.SemaphoreType.DMA((pieces,)),
        lat_sent=pltpu.SemaphoreType.DMA((pieces,)),
        c_recv=pltpu.SemaphoreType.DMA((seq_dev, per_seq)),
        c_sent=pltpu.SemaphoreType.DMA((seq_dev, per_seq)),
    )
    out_blocks = [shape_of(b, F32) for b in blocks[:-1]] + [shape_of((lat[0], GROUPS * lat[1]), F32)]
    out_blocks += [shape_of(ffn, F32)] * 3
    groups = dict(
        outs=[pltpu.VMEM(o.shape, F32) for o in out_blocks[:5]],
        held=GradSum.scratch(fsdp, ctx, [ffn] * 3 + blocks),
        parts=[pltpu.VMEM(w, BF16) for w in whole],
        spread=Spread.scratch(fsdp, 5),
        half=HalfSpread.scratch(fsdp, 4),
        share=CtxShare.scratch(ctx),
        wline=RowGather.scratch(n),
        gather=LineGather.scratch(n, rows // piece),
        two=LineSum.scratch(n, rows, width, strip)[2:],
        feed=LineSum.scratch(n, rows, width, strip)[2:],
        gffn=GradSum.semaphores(fsdp, ctx, 3),
        gatt=GradSum.semaphores(fsdp, ctx, 5),
        lline=AxisShare.scratch(n),
        xline=AxisShare.scratch(ctx),
        s_tp=AxisSum.scratch(n, (8, many)),
        s_ctx=AxisSum.scratch(ctx, (8, many)),
        s_fsdp=AxisSum.scratch(fsdp, (8, many)),
    )
    def turned(i, many=1):
        return i + many - 2 * many * lax.rem(i // many, 2) if per == 2 else i

    def turned_pieces(at):
        return turned(at, per_block)

    names = list(scratch)
    shapes = list(scratch.values())
    places = {}
    for key, some in groups.items():
        places[key] = (len(shapes), len(shapes) + len(some))
        shapes = shapes + list(some)

    def kernel(*refs):
        (tok_in, ga, gb, wlat, wq, wkp, wvp, wout, wgt, wut, wdn, seg, cot_in), refs = refs[:13], refs[13:]
        (o_mixed, o_tok), o_blocks, o_small, refs = refs[:2], refs[2:10], refs[10], refs[11:]
        r = SimpleNamespace(**dict(zip(names, refs)))
        g = SimpleNamespace(**{key: refs[a:b] for key, (a, b) in places.items()})
        cols, tok, cot, xn, mid = r.cols, r.tok, r.cot, r.xn, r.mid
        gain, segk = r.gain, r.segk
        x, me = lax.axis_index("ctx"), lax.axis_index("tp")
        outs = list(g.outs) + [mid.at[0 : ffn[0], i * ffn[1] : (i + 1) * ffn[1]] for i in range(3)]

        load = Bring([(tok_in, tok), (cot_in, cot)], r.local)
        load.start()
        r.gbuf[...] = jnp.zeros_like(r.gbuf)
        r.gbuf[0:1, :] = ga[...].astype(F32).reshape(1, -1)
        r.gbuf[1:2, :] = gb[...].astype(F32).reshape(1, -1)
        r.sbuf[...] = jnp.zeros_like(r.sbuf)
        r.sbuf[0:seq_dev, :] = seg[...]
        meet(n, fsdp, ctx)

        group = me * q_width // per_group
        src_lat = wlat.at[:, pl.ds(pl.multiple_of(group * latent, latent), latent)]
        spread = Spread(
            fsdp,
            [(r.gbuf, gain), (src_lat, r.w_lat), (wq, r.w_qry), (wkp, r.w_kproj), (wvp, r.w_vproj)],
            [1, 0, 0, 0, 0], *g.spread,
        )
        share = CtxShare(ctx, r.sbuf, segk, *g.share)
        wline = RowGather(n, wout, r.wo_line, *g.wline)
        half = HalfSpread(
            fsdp,
            [(wgt, r.wg), (wut, r.wu), (wdn, r.wd), (r.wo_line.reshape(n * q_width, w_out.shape[1]), r.wo)],
            *g.half,
        )
        spread.start()
        share.start()
        wline.start()
        half.start([0, 1, 2])
        cols[...] = jnp.zeros_like(cols)
        r.g_sum[...] = jnp.zeros_like(r.g_sum)
        r.g_sum2[...] = jnp.zeros_like(r.g_sum2)
        r.sacc[...] = jnp.zeros_like(r.sacc)
        r.sm[...] = jnp.zeros_like(r.sm)
        load.wait([0])

        def scale(i):
            at = pl.ds(pl.multiple_of(i * wide, wide), wide)
            value = tok[at, :].astype(F32)
            cols[at, R_ONE : R_ONE + 1] = lax.rsqrt(jnp.mean(value * value, axis=-1, keepdims=True) + eps)

        loop(0, rows // wide, scale)
        spread.relay([0, 1])
        spread.finish([0, 1])
        wline.relay([1])
        lat_all = r.lat_all

        def place(shard, i):
            seq = i // per_seq
            return pl.ds(pl.multiple_of((seq * win + shard) * tok_dev + lax.rem(i, per_seq) * chunk, chunk), chunk)

        def pass_on(i):
            return remote(lat_all.at[place(own_shard, i)], lat_all.at[place(own_shard - 1, i)], r.lat_sent.at[i],
                          r.lat_recv.at[i], {"ctx": x + 1})

        def first_norm(i):
            at = pl.ds(pl.multiple_of(i * chunk, chunk), chunk)
            unit = (tok[at, :].astype(F32) * cols[at, R_ONE : R_ONE + 1] * gain[0:1, :]).astype(BF16)
            xn[at, :] = unit
            lat_all[place(own_shard, i), :] = dot(unit, r.w_lat[...]).astype(BF16)

            @pl.when(x + 1 < ctx)
            def _():
                pass_on(i).start()

        loop(0, pieces, lambda i: first_norm(turned(i)))
        if n > 2:
            wline.relay([2])
        spread.relay([2, 3, 4])
        spread.finish([2, 3, 4])

        def project(shard, i):
            to = place(shard, i)
            value = lat_all[to, :]
            r.keys[to, :] = dot(value, r.w_kproj[...]).astype(BF16)
            r.values[to, :] = dot(value, r.w_vproj[...]).astype(BF16)

        def ask(i):
            at = pl.ds(pl.multiple_of(i * chunk, chunk), chunk)
            r.query[at, :] = dot(xn[at, :], r.w_qry[...]).astype(BF16)
            project(own_shard, i)

        loop(0, pieces, ask)
        share.finish()
        for q in range(seq_dev):
            at = slice(q * tok_dev, (q + 1) * tok_dev)
            ids = jnp.broadcast_to(r.sbuf[q : q + 1, :].astype(F32), (128, tok_dev)).T
            cols[at, SEGMENT : SEGMENT + 1] = ids[:, 0:1]
            final = segk[ctx - 1, q : q + 1, tok_dev - 1 : tok_dev].astype(F32)
            cols[at, VALID : VALID + 1] = jnp.where(ids[:, 0:1] != final, 1.0, 0.0)

        def theirs(i):
            @pl.when(x - 1 >= 0)
            def _():
                wait_came(lat_all.at[place(own_shard - 1, i)], r.lat_sent.at[i], r.lat_recv.at[i])

            @pl.when(x - 1 < 0)
            def _():
                lat_all[place(own_shard - 1, i), :] = jnp.zeros((chunk, latent), BF16)

            project(own_shard - 1, i)

        att, gathered = r.att, r.gathered
        line = LineGather(n, piece, att, gathered, *g.gather, hop=reach, order=turned_pieces)

        def query_tile(turn):
            i = turned(turn)
            seq = i // per
            q_tile = own_shard * per + lax.rem(i, per)
            at = pl.ds(pl.multiple_of(i * TILE, TILE), TILE)
            near = pl.ds(pl.multiple_of((seq * win * per + q_tile - span) * TILE, TILE), tiles * TILE)
            counted = jnp.concatenate(
                [
                    c.astype(F32)
                    for c in counted_keys(cols, segk, at, seq, q_tile * TILE, q_tile - span, tiles, tok_dev, win)
                ],
                axis=1,
            )
            accum = jnp.zeros((TILE, q_width), F32)
            for h in range(heads):
                score = dot_t(head_only(r.query[at, :], h), r.keys[near, :]) * 0.125
                score = jnp.where(counted > 0.0, score, -1e30)
                top = jnp.max(score, axis=-1, keepdims=True)
                weight = jnp.exp(score - top)
                total = jnp.sum(weight, axis=-1, keepdims=True)
                prob = (weight * (1.0 / total)).astype(BF16)
                accum = accum + jnp.dot(prob, head_only(r.values[near, :], h), preferred_element_type=F32)
                cols[at, LSE + h : LSE + h + 1] = top + jnp.log(total)
                line.step((turn - 1) * per_block + h * per_block // heads)
            att[at, :] = accum.astype(BF16)

        def tile_forward(i):
            theirs(turned(i))
            query_tile(i)

            @pl.when(i == 0)
            def _():
                if n > 3:
                    wline.relay(range(3, n))
                wline.finish()
                half.start([3])

            for turn, which in enumerate(([0, 1], [2], [3])):

                @pl.when(i == turn)
                def _(which=which):
                    half.relay(which)

        loop(0, q_tiles, tile_forward)
        s1 = (q_tiles - 1) * per_block
        line.begin()
        half.cross([0, 1, 2, 3])
        loop(s1, per_block + reach * (n - 1), line.step)
        s1 = per_block + reach * (n - 1)
        half.finish([3, 0, 1, 2])
        half.drain([0, 1, 2, 3])
        r.wo_rows[...] = r.wo[pl.ds(pl.multiple_of(me * q_width, q_width), q_width), :]
        line.begun()
        load.wait([1])

        p_two, p_feed, wg, wu, wd = r.p_two, r.p_feed, r.wg, r.wu, r.wd

        def second_back(at, own, total):
            unit = mid[at, :] * cols[at, R_TWO : R_TWO + 1]
            r.g_sum2[...] += jnp.sum((total * unit).reshape(strip // 8, 8, width), axis=0)
            scaled = total * gain[1:2, :]
            mean = jnp.mean(scaled * unit, axis=-1, keepdims=True)
            d_mid = cot[at, :].astype(F32) + cols[at, R_TWO : R_TWO + 1] * (scaled - unit * mean)
            first_unit = tok[at, :].astype(F32) * cols[at, R_ONE : R_ONE + 1]
            cols[at, MARK : MARK + 1] = jnp.sum(first_unit * d_mid, axis=-1, keepdims=True)
            return d_mid.astype(BF16)

        def forward(at, own, total):
            mixed = mid[at, :] + total
            seq = at.start // tok_dev
            counted = cols[at, VALID : VALID + 1]
            r.sacc[seq] += jnp.sum((mixed * mixed * counted).reshape(strip // 8, 8, width), axis=0)
            r.sacc[seq_dev + seq] += jnp.sum((total * total * counted).reshape(strip // 8, 8, width), axis=0)
            return mixed.astype(BF16)

        def first_back(at, own, total):
            r1 = cols[at, R_ONE : R_ONE + 1]
            unit = tok[at, :].astype(F32) * r1
            scaled = total * gain[0:1, :]
            mean = jnp.mean(scaled * unit, axis=-1, keepdims=True)
            return (r.branch[at, :].astype(F32) + r1 * (scaled - unit * mean)).astype(BF16)

        two = LineSum(n, strip, hop, p_two, r.left, r.right, r.branch, *g.two, second_back, pushed=True, order=turned_pieces)
        feed = LineSum(n, strip, hop, p_feed, gathered, r.wo, xn, *g.feed, forward, order=turned_pieces)
        one = LineSum(n, strip, hop, cot, r.left, r.right, p_two, *g.two, first_back, order=turned_pieces)
        parts = [wg, wu, wd]
        gffn = GradSum(fsdp, ctx, parts, [1, 1, 1], None,
                       [g.held[3 * a : 3 * a + 3] for a in range(3)], *g.gffn)
        aparts = g.parts
        gatt = GradSum(fsdp, ctx, aparts, axes, None,
                       [g.held[3 * a : 3 * a + 3] for a in range(3, 8)], *g.gatt)

        def block_of_rows(b):
            at = pl.ds(pl.multiple_of(turned(b) * TILE, TILE), TILE)
            seq = b * TILE // tok_dev

            def steps(j):
                line.step(s1 + b * per_block + j)
                two.step((b - 1) * per_block + j - behind)

            branch = dot(gathered[at, :], r.wo[...])
            middle_rows = tok[at, :].astype(F32) + branch
            mid[at, :] = middle_rows
            r.sacc[2 * seq_dev + seq] += jnp.sum(
                (branch * branch * cols[at, VALID : VALID + 1]).reshape(TILE // 8, 8, width), axis=0
            )
            level = lax.rsqrt(jnp.mean(middle_rows * middle_rows, axis=-1, keepdims=True) + eps)
            cols[at, R_TWO : R_TWO + 1] = level
            unit = (middle_rows * level * gain[1:2, :]).astype(BF16)
            xn[at, :] = unit
            steps(0)
            gate = dot_t(unit, wg[...])
            upper = dot_t(unit, wu[...])
            sigma = jax.nn.sigmoid(gate)
            swish = gate * sigma
            hidden = (swish * upper).astype(BF16)
            r.hid[at, :] = hidden
            slope = upper * sigma * (1.0 + gate * (1.0 - sigma))
            steps(1)
            p_feed[at, :] = dot(hidden, wd[...]).astype(BF16)
            d_hidden = dot_t(cot[at, :], wd[...])
            d_gate = (d_hidden * slope).astype(BF16)
            d_upper = (d_hidden * swish).astype(BF16)
            r.dg[at, :] = d_gate
            r.du[at, :] = d_upper
            steps(2)
            p_two[at, :] = (dot(d_gate, wg[...]) + dot(d_upper, wu[...])).astype(BF16)
            steps(3)
            for j in range(per_block):
                two.push(b * per_block + j)

        loop(0, q_tiles, block_of_rows)
        s2 = (q_tiles - 1) * per_block - behind

        def product(i):
            at = pl.ds(pl.multiple_of(i * cols_at, cols_at), cols_at)
            left = xn[:, at]
            parts[0][:, at] = dot_rows(r.dg[...], left).astype(BF16)
            parts[1][:, at] = dot_rows(r.du[...], left).astype(BF16)
            parts[2][:, at] = dot_rows(r.hid[...], cot[:, at]).astype(BF16)

        def busy(s):
            two.step(s)
            product(s - s2)

        line.drain()
        loop(s2, s2 + 4, busy)
        gffn.start()
        s2 = s2 + 4

        dk, dv, dqb, grad_seq, lat_parts = r.dk, r.dv, r.dqb, r.grad_seq, r.lat_parts

        def clear(i):
            at = pl.ds(pl.multiple_of(i * TILE, TILE), TILE)
            dk[at, :] = jnp.zeros((TILE, q_width), F32)
            dv[at, :] = jnp.zeros((TILE, q_width), F32)

        loop(0, keyed // TILE, clear)
        ready = steps_all // seq_dev + lag
        loop(s2, ready, two.step)

        def grad_tile(i, step):
            seq = i // per
            q_tile = own_shard * per + lax.rem(i, per)
            at = pl.ds(pl.multiple_of(i * TILE, TILE), TILE)
            near = pl.ds(pl.multiple_of((seq * win * per + q_tile - span) * TILE, TILE), tiles * TILE)
            grad_seq[...] = dot_t(r.branch[at, :], r.wo_rows[...]).astype(BF16)
            inner_sum = grad_seq[...].astype(F32) * att[at, :].astype(F32)
            counted = jnp.concatenate(
                [
                    c.astype(F32)
                    for c in counted_keys(cols, segk, at, seq, q_tile * TILE, q_tile - span, tiles, tok_dev, win)
                ],
                axis=1,
            )
            d_query = jnp.zeros((TILE, q_width), F32)
            d_key = jnp.zeros((tiles * TILE, q_width), F32)
            d_value = jnp.zeros((tiles * TILE, q_width), F32)
            for h in range(heads):
                delta = jnp.sum(head_only(inner_sum, h), axis=-1, keepdims=True)
                asked, ours = head_only(r.query[at, :], h), head_only(grad_seq[...], h)
                score = jnp.where(counted > 0.0, dot_t(asked, r.keys[near, :]) * 0.125, -1e30)
                prob = jnp.exp(score - cols[at, LSE + h : LSE + h + 1]) * counted
                d_score = (prob * (dot_t(ours, r.values[near, :]) - delta)).astype(BF16)
                d_query = d_query + jnp.dot(d_score, head_only(r.keys[near, :], h), preferred_element_type=F32)
                d_key = d_key + dot_rows(d_score, asked)
                d_value = d_value + dot_rows(prob.astype(BF16), ours)
                step(h)
            dqb[at, :] = (d_query * 0.125).astype(BF16)
            dk[near, :] += d_key * 0.125
            dv[near, :] += d_value

        def send_latent(seq, i):
            j = seq * per_seq + i
            at = pl.ds(pl.multiple_of(j * chunk, chunk), chunk)
            return remote(lat_parts.at[place(own_shard - 1, j)], r.came.at[at], r.c_sent.at[seq, i],
                          r.c_recv.at[seq, i], {"ctx": x - 1})

        def latents(seq):
            for shard in (own_shard - 1, own_shard):
                for i in range(per_seq):
                    at = place(shard, seq * per_seq + i)
                    lat_parts[at, :] = (
                        dot_t(dk[at, :].astype(BF16), r.w_kproj[...])
                        + dot_t(dv[at, :].astype(BF16), r.w_vproj[...])
                    ).astype(BF16)
                    if shard < own_shard:

                        @pl.when(x - 1 >= 0)
                        def _(i=i):
                            send_latent(seq, i).start()

        def sequence(seq):
            def tile(i):
                def step(h):
                    t = (i * heads + h) * steps_per // heads
                    two.step(ready + t)
                    feed.step(t)

                grad_tile(i, step)

            loop(seq * per, seq * per + per, tile)
            latents(seq)

            @pl.when(seq == 0)
            def _():
                two.drain()
                gffn.pair()
                gffn.second()

        steps_per = heads
        loop(0, seq_dev, sequence)
        fed = q_tiles * steps_per

        def whole_latent(j):
            seq, i = j // per_seq, lax.rem(j, per_seq)
            at = pl.ds(pl.multiple_of(j * chunk, chunk), chunk)
            r.dlat[at, :] = lat_parts[place(own_shard, j), :]

            @pl.when(x + 1 < ctx)
            def _():
                wait_came(r.came.at[at], r.c_sent.at[seq, i], r.c_recv.at[seq, i])
                r.dlat[at, :] = (r.dlat[at, :].astype(F32) + r.came[at, :].astype(F32)).astype(BF16)

            cot[at, :] = (dot_t(dqb[at, :], r.w_qry[...]) + dot_t(r.dlat[at, :], r.w_lat[...])).astype(BF16)

        def first_unit_columns(at):
            return (tok[:, at].astype(F32) * cols[:, R_ONE : R_ONE + 1] * gain[0:1, at]).astype(BF16)

        early = (seq_dev - 1) * per_seq
        loop(0, early, whole_latent)

        def mixed_work(i):
            at = pl.ds(pl.multiple_of(i * chunk, chunk), chunk)
            aparts[0][at, :] = dot_rows(first_unit_columns(at), dqb[...]).astype(BF16)
            aparts[3][:, at] = dot_rows(att[...], r.branch[:, at]).astype(BF16)
            feed.step(fed + i)

        fed_later = fed + width // chunk
        loop(0, width // chunk, mixed_work)
        gffn.third()
        aparts[1][...] = dot_rows(lat_all[...], dk[...].astype(BF16)).astype(BF16)
        aparts[2][...] = dot_rows(lat_all[...], dv[...].astype(BF16)).astype(BF16)
        loop(early, pieces, whole_latent)

        def steps(s):
            one.step(s)
            feed.step(fed_later + s)

        def product_lat(s):
            at = pl.ds(pl.multiple_of(s * chunk, chunk), chunk)
            aparts[4][at, :] = dot_rows(first_unit_columns(at), r.dlat[...]).astype(BF16)
            steps(s)

        begun = width // chunk
        loop(0, begun, product_lat)
        gatt.start()

        def gains_of(i):
            at = pl.ds(pl.multiple_of(i * side, side), side)
            value = cot[at, :].astype(F32) * (tok[at, :].astype(F32) * cols[at, R_ONE : R_ONE + 1])
            r.g_sum[...] += jnp.sum(value.reshape(side // 8, 8, width), axis=0)
            along = lax.dot_general(jnp.ones((8, width), F32), value * gain[0:1, :], (((1,), (1,)), ((), ())),
                                    precision=lax.Precision.HIGHEST, preferred_element_type=F32)
            r.sm[3:4, at] = along[0:1, :]
            lines = cols[at, :].T
            r.sm[4:5, at] = lines[MARK : MARK + 1, :]
            r.sm[5:6, at] = lines[R_ONE : R_ONE + 1, :]

        def two_gains(s):
            steps(s)
            gains_of(2 * (s - begun))
            gains_of(2 * (s - begun) + 1)

        mark = begun + rows // side // 2
        loop(begun, begun + 1, two_gains)
        gatt.pair()
        gatt.second()
        loop(begun + 1, mark, two_gains)
        last = one.steps()
        for s in range(fed_later + mark, feed.steps()):
            feed.step(s)
        flush = r.flush
        out_mixed = pltpu.make_async_copy(xn, o_mixed, flush.at[8])
        out_mixed.start()
        lane = lax.broadcasted_iota(jnp.int32, (1, many), 1)
        once = jnp.where(me == 0, 1.0, 0.0)
        row = jnp.zeros((1, many), F32)

        def whole_sum(value):
            return jnp.sum(jnp.sum(value, axis=0, keepdims=True), axis=1, keepdims=True)

        for q in range(seq_dev):
            stats = [
                whole_sum(r.sacc[q]),
                whole_sum(r.sacc[seq_dev + q]),
                whole_sum(r.sacc[2 * seq_dev + q]) * once,
                jnp.sum(cols[q * tok_dev : (q + 1) * tok_dev, VALID : VALID + 1], axis=0, keepdims=True) * once,
            ]
            for j, value in enumerate(stats):
                row = row + jnp.where(lane == 4 * q + j, value, 0.0)
        r.sm[2:3, :] = row
        r.sm[0:1, 0:width] = jnp.sum(r.g_sum[...], axis=0, keepdims=True)
        r.sm[1:2, 0:width] = jnp.sum(r.g_sum2[...], axis=0, keepdims=True)
        r_row = r.sm[5:6, :]
        over_tp = AxisSum("tp", n, *g.s_tp)
        over_ctx = AxisSum("ctx", ctx, *g.s_ctx)
        over_fsdp = AxisSum("fsdp", fsdp, *g.s_fsdp)
        over_tp.start(r.sm[...])
        lat_half = pl.ds(pl.multiple_of(x * (lat[0] // 2), lat[0] // 2), lat[0] // 2)
        lline = AxisShare("tp", n, r.lat_own.at[lat_half], r.lat_every, *g.lline)
        xline = AxisShare("ctx", ctx, r.lat_sum, r.lat_both, *g.xline)
        outward = Bring([(outs[i], o_blocks[i]) for i in range(8)], flush)

        def store(a, at, total):
            if a < 4:
                outs[a][at, :] = total
            else:
                r.lat_own[at, :] = total.astype(BF16)

        def store_ffn(a, at, total):
            outs[5 + a][at, :] = total

        loop(mark, mark + 2, steps)
        gatt.third()
        along_tp = over_tp.finish()
        over_ctx.start(along_tp)
        gffn.fourth(store_ffn)
        outward.start([5, 6, 7])
        loop(mark + 2, mark + 4, steps)
        along_ctx = over_ctx.finish()
        over_fsdp.start(along_ctx)
        loop(mark + 4, mark + 6, steps)
        gatt.fourth(store)
        outward.start([0, 1, 2, 3])
        lline.start()
        everywhere = over_fsdp.finish()
        loop(mark + 6, mark + 10, steps)
        lline.finish()

        def latent_sum(i):
            at = pl.ds(pl.multiple_of(i * 16, 16), 16)
            for gr in range(GROUPS):
                total = jnp.zeros((16, lat[1]), F32)
                for t in range(n):
                    if t * GROUPS // n == gr:
                        total = total + r.lat_every[t, at, :].astype(F32)
                r.lat_sum[at, gr * lat[1] : (gr + 1) * lat[1]] = total.astype(BF16)

        loop(0, lat[0] // 32, latent_sum)
        xline.start()
        loop(mark + 10, mark + 13, steps)
        xline.finish()
        for k in range(ctx):
            outs[4][k * (lat[0] // 2) : (k + 1) * (lat[0] // 2), :] = r.lat_both[k].astype(F32)
        outward.start([4])
        row = lax.broadcasted_iota(jnp.int32, everywhere.shape, 0)
        o_small[...] = jnp.where(row < 2, everywhere, along_ctx)
        o_small[3:4, :] = (along_tp[4:5] + eps * r_row * r_row * r_row * along_tp[3:4]) * (1.0 / width**0.5)
        ahead = [pl.ds(0, rows // 2), pl.ds(rows // 2, rows // 2)]
        out_tok = Bring([(p_two.at[q], o_tok.at[q]) for q in ahead], flush.at[pl.ds(9, 2)])
        out_tok.start([0])
        loop(mark + 13, last, steps)
        out_tok.start([1])

        @pl.when(x + 1 < ctx)
        def _():
            loop(0, pieces, lambda i: pass_on(i).wait_send())

        @pl.when(x - 1 >= 0)
        def _():
            for seq in range(seq_dev):
                for i in range(per_seq):
                    send_latent(seq, i).wait_send()

        feed.drain()
        one.drain()
        gffn.drain_pair()
        gffn.drain()
        gatt.drain_pair()
        gatt.drain()
        outward.wait()
        out_mixed.wait()
        out_tok.wait()

    out = pl.pallas_call(
        kernel,
        out_shape=(shape_of((rows, width), BF16),) * 2 + tuple(out_blocks) + (shape_of((8, many), F32),),
        in_specs=[ANY] + [VMEM] * 2 + [ANY] * 8 + [VMEM, ANY],
        out_specs=(ANY,) * 10 + (VMEM,),
        scratch_shapes=shapes,
        compiler_params=params(1, 64),
    )(tokens, gain1, gain2, w_latent, *shards, w_out, *wide_shards, segments, out_grad)
    return out[0], out[1], out[2:7], out[7:10], out[10]


def three_kernels(tokens, gain1, gain2, w_latent, shards, w_out, wide_shards, segments, out_grad, fsdp, ctx, n):
    seq_dev, tok_dev = segments.shape
    gate, up, down = wide_shards
    (xn_one, cols, gains, w_lat, w_qry, w_kproj, w_vproj, gate_all, up_all, wo_cols, seg_all, lat_all,
     query, keys, values) = front(tokens, gain1, gain2, w_latent, shards, w_out, (gate, up), segments, fsdp, ctx, n)
    late = window(ctx, tok_dev) <= 2
    (d_branch, part_feed, d_middle, mid_own, wo_rows, gain_part, branch_sq, marks, attended, lse), ffn = middle(
        query, keys, values, seg_all, cols, (wo_cols.reshape(-1, w_out.shape[1]), down), gate_all, up_all, gains,
        tokens, out_grad, fsdp, ctx, n, seq_dev, late,
    )
    (grad_tokens, mixed, small), att_grads, late_ffn = back(
        query, keys, values, seg_all, cols, lse, attended, d_branch, wo_rows, (w_qry, w_lat, w_kproj, w_vproj),
        lat_all, xn_one, gains, tokens, d_middle, mid_own, part_feed, marks, gain_part, branch_sq,
        ffn if late else (), fsdp, ctx, n, seq_dev,
    )
    return mixed, grad_tokens, att_grads, late_ffn if late else ffn, small


def on_device(
    tokens, gain1, w_latent, w_query, w_key, w_value, w_out, gain2, w_gate, w_up, w_down, segments, cotangent
):
    seq_dev, tok_dev, feat_dim = tokens.shape
    n_ctx, n_tp, n_fsdp = lax.axis_size("ctx"), lax.axis_size("tp"), lax.axis_size("fsdp")
    row_count = seq_dev * tok_dev
    tok_rows = tokens.reshape(row_count, feat_dim)
    out_grad = cotangent.reshape(row_count, feat_dim)
    if n_ctx == 2 and n_fsdp >= 4 and w_down.shape[0] <= row_count and feat_dim <= row_count:
        mixed, grad_tokens, att_grads, ffn_grads, small = layer(
            tok_rows, gain1, gain2, w_latent, (w_query, w_key, w_value), w_out, (w_gate.T, w_up.T, w_down), segments,
            out_grad, n_fsdp, n_ctx, n_tp,
        )
    else:
        mixed, grad_tokens, att_grads, ffn_grads, small = three_kernels(
            tok_rows, gain1, gain2, w_latent, (w_query, w_key, w_value), w_out, (w_gate.T, w_up.T, w_down), segments,
            out_grad, n_fsdp, n_ctx, n_tp,
        )
    arrays, (gain_grad1, gain_grad2, stats, radial) = publish(
        (mixed, grad_tokens, *att_grads, *ffn_grads), small, seq_dev, tok_dev, feat_dim, n_fsdp
    )
    mixed, grad_tokens, s_qry, s_kproj, s_vproj, s_outp, s_lat, s_gate, s_up, s_down = arrays
    return (
        mixed.reshape(seq_dev, tok_dev, feat_dim),
        grad_tokens.reshape(seq_dev, tok_dev, feat_dim),
        gain_grad1,
        s_lat,
        s_qry,
        s_kproj,
        s_vproj,
        s_outp,
        gain_grad2,
        s_gate.T,
        s_up.T,
        s_down,
        stats,
        radial,
    )


def solution(mesh):
    return jax.shard_map(
        on_device,
        mesh=mesh,
        in_specs=(
            P("fsdp", "ctx", None),
            P("fsdp"),
            P("fsdp", None),
            P("fsdp", "tp"),
            P("fsdp", "tp"),
            P("fsdp", "tp"),
            P("tp", "fsdp"),
            P("fsdp"),
            P("fsdp", "tp"),
            P("fsdp", "tp"),
            P("tp", "fsdp"),
            P("fsdp", "ctx"),
            P("fsdp", "ctx", None),
        ),
        out_specs=(
            P("fsdp", "ctx", None),
            P("fsdp", "ctx", None),
            P("fsdp"),
            P("fsdp", None),
            P("fsdp", "tp"),
            P("fsdp", "tp"),
            P("fsdp", "tp"),
            P("tp", "fsdp"),
            P("fsdp"),
            P("fsdp", "tp"),
            P("fsdp", "tp"),
            P("tp", "fsdp"),
            P("fsdp", None),
            P("fsdp", "ctx"),
        ),
        check_vma=False,
    )
```

```python
from types import SimpleNamespace

import jax
import jax.numpy as jnp
from jax import lax
from jax.experimental import pallas as pl
from jax.experimental.pallas import tpu as pltpu
from jax.sharding import PartitionSpec as P

HEADS = 16
HEAD_DIM = 64
GROUPS = 2
LATENT = 256
MESH = pl.DeviceIdType.MESH
VMEM = pl.BlockSpec(memory_space=pltpu.VMEM)
ANY = pl.BlockSpec(memory_space=pl.ANY)
F32 = jnp.float32
BF16 = jnp.bfloat16

eps = 1e-05


def remote(src, dst, send_sem, recv_sem, device):
    return pltpu.make_async_remote_copy(
        src_ref=src,
        dst_ref=dst,
        send_sem=send_sem,
        recv_sem=recv_sem,
        device_id=device,
        device_id_type=MESH,
    )


def wait_sent(ref, sem, recv_sem):
    remote(ref, ref, sem, recv_sem, {"tp": lax.axis_index("tp")}).wait_send()


def wait_came(ref, send_sem, sem):
    remote(ref, ref, send_sem, sem, {"tp": lax.axis_index("tp")}).wait_recv()


def meet(line=0, fsdp=0, ctx=0, everyone=False):
    barrier = pltpu.get_barrier_semaphore()

    def greet(device):
        pl.semaphore_signal(barrier, inc=1, device_id=device, device_id_type=MESH)

    known = 0
    f, x, me = lax.axis_index("fsdp"), lax.axis_index("ctx"), lax.axis_index("tp")
    if fsdp and everyone:
        for k in range(1, fsdp):
            greet({"fsdp": lax.rem(f + k, fsdp)})
        known += fsdp - 1
    elif fsdp:
        greet({"fsdp": sibling(f)})
        for k in range(1, fsdp // 2):
            greet({"fsdp": lax.rem(f + 2 * k, fsdp)})
        known += fsdp // 2
    for k in range(1, ctx):
        greet({"ctx": lax.rem(x + k, ctx)})
        known += 1
    if line > 1 and everyone:
        for k in range(1, line):
            greet({"tp": lax.rem(me + k, line)})
        known += line - 1
    if line > 1 and not everyone:

        @pl.when(me > 0)
        def _():
            greet({"tp": me - 1})

        @pl.when(me < line - 1)
        def _():
            greet({"tp": me + 1})

        @pl.when((me > 0) & (me < line - 1))
        def _():
            pl.semaphore_wait(barrier, known + 2)

        @pl.when((me == 0) | (me == line - 1))
        def _():
            pl.semaphore_wait(barrier, known + 1)

    else:
        pl.semaphore_wait(barrier, known)


def sibling(f):
    return f + 1 - 2 * lax.rem(f, 2)


def block(ref, axis, index, size):
    at = pl.ds(pl.multiple_of(index * size, size), size)
    return ref.at[at] if axis == 0 else ref.at[:, at]


class Bring:
    def __init__(self, pairs, sems):
        self.copies = [pltpu.make_async_copy(src, dst, sems.at[i]) for i, (src, dst) in enumerate(pairs)]

    def start(self, which=None):
        for i in which if which is not None else range(len(self.copies)):
            self.copies[i].start()

    def wait(self, which=None):
        for i in which if which is not None else range(len(self.copies)):
            self.copies[i].wait()


class Spread:
    def __init__(self, fsdp, pairs, axes, recv, sent, own):
        self.fsdp, self.pairs, self.axes = fsdp, pairs, axes
        self.recv, self.sent, self.own = recv, sent, own
        self.f = lax.axis_index("fsdp")

    def size(self, a):
        return self.pairs[a][0].shape[self.axes[a]]

    def target(self, a, f):
        return block(self.pairs[a][1], self.axes[a], f, self.size(a))

    def start(self):
        f = self.f
        for a, (src, dst) in enumerate(self.pairs):
            for k in range(1, self.fsdp // 2):
                remote(src, self.target(a, f), self.sent.at[a], self.recv.at[a, f],
                       {"fsdp": lax.rem(f + 2 * k, self.fsdp)}).start()
        for a, (src, dst) in enumerate(self.pairs):
            remote(src, self.target(a, f), self.sent.at[a], self.recv.at[a, f],
                   {"fsdp": sibling(f)}).start()
            pltpu.make_async_copy(src, self.target(a, f), self.own.at[a]).start()

    def relay(self, which=None):
        for a in which or range(len(self.pairs)):
            for k in range(1, self.fsdp // 2):
                other = lax.rem(self.f + 2 * k, self.fsdp)
                here = self.target(a, other)
                wait_came(here, self.sent.at[a], self.recv.at[a, other])
                remote(here, here, self.sent.at[a], self.recv.at[a, other],
                       {"fsdp": sibling(self.f)}).start()

    def finish(self, which=None):
        for a in which or range(len(self.pairs)):
            src, dst = self.pairs[a]
            for k in range(0, self.fsdp // 2):
                other = lax.rem(sibling(self.f) + 2 * k, self.fsdp)
                wait_came(self.target(a, other), self.sent.at[a], self.recv.at[a, other])
            pltpu.make_async_copy(src, self.target(a, self.f), self.own.at[a]).wait()
            many = (self.fsdp - 1) * self.size(a)
            ref = dst.at[pl.ds(0, many)] if self.axes[a] == 0 else dst.at[:, pl.ds(0, many)]
            wait_sent(ref, self.sent.at[a], self.recv.at[a, 0])

    @staticmethod
    def scratch(fsdp, arrays):
        return [
            pltpu.SemaphoreType.DMA((arrays, fsdp)),
            pltpu.SemaphoreType.DMA((arrays,)),
            pltpu.SemaphoreType.DMA((arrays,)),
        ]


class CtxShare:
    def __init__(self, ctx, src, dst, recv, sent, own):
        self.ctx, self.src, self.dst = ctx, src, dst
        self.recv, self.sent, self.own = recv, sent, own
        self.x = lax.axis_index("ctx")

    def start(self):
        for k in range(1, self.ctx):
            remote(self.src, self.dst.at[self.x], self.sent.at[k - 1], self.recv.at[self.x],
                   {"ctx": lax.rem(self.x + k, self.ctx)}).start()
        pltpu.make_async_copy(self.src, self.dst.at[self.x], self.own).start()

    def finish(self):
        for k in range(1, self.ctx):
            other = lax.rem(self.x + k, self.ctx)
            wait_came(self.dst.at[other], self.sent.at[k - 1], self.recv.at[other])
            wait_sent(self.src, self.sent.at[k - 1], self.recv.at[other])
        pltpu.make_async_copy(self.src, self.dst.at[self.x], self.own).wait()

    @staticmethod
    def scratch(ctx):
        return [
            pltpu.SemaphoreType.DMA((ctx,)),
            pltpu.SemaphoreType.DMA((ctx,)),
            pltpu.SemaphoreType.DMA,
        ]


class LineGather:
    def __init__(self, n, chunk, src, dst, recv, sent, own, hop=1):
        self.n, self.chunk, self.src, self.dst, self.hop = n, chunk, src, dst, hop
        self.width = src.shape[1]
        self.count = src.shape[0] // chunk
        self.recv, self.sent, self.own = recv, sent, own
        self.me = lax.axis_index("tp")

    def steps(self):
        return self.count + self.hop * (self.n - 1)

    def flag(self, tp, at):
        shape = self.recv.shape
        if len(shape) == 2:
            return self.recv.at[tp, at]
        i = tp * self.count + at
        return self.recv.at[i // (shape[1] * shape[2]), i // shape[2] % shape[1], i % shape[2]]

    def columns(self, tp):
        return pl.ds(pl.multiple_of(tp * self.width, self.width), self.width)

    def place(self, tp, at):
        rows = pl.ds(pl.multiple_of(at * self.chunk, self.chunk), self.chunk)
        return self.dst.at[rows, self.columns(tp)]

    def begin(self):
        pltpu.make_async_copy(self.src, self.dst.at[:, self.columns(self.me)], self.own).start()

    def begun(self):
        pltpu.make_async_copy(self.src, self.dst.at[:, self.columns(self.me)], self.own).wait()

    def step(self, s):
        n, me, count = self.n, self.me, self.count
        left, right = {"tp": me - 1}, {"tp": me + 1}

        @pl.when((s >= 0) & (s < count))
        def _():
            rows = pl.ds(pl.multiple_of(s * self.chunk, self.chunk), self.chunk)

            @pl.when(me > 0)
            def _():
                remote(self.src.at[rows], self.place(me, s), self.sent.at[0], self.flag(me, s), left).start()

            @pl.when(me < n - 1)
            def _():
                remote(self.src.at[rows], self.place(me, s), self.sent.at[1], self.flag(me, s), right).start()

        for away in range(1, n):
            at = s - away * self.hop
            for sign, onward in ((-1, right), (1, left)):
                tp = me + sign * away

                @pl.when((tp >= 0) & (tp < n) & (at >= 0) & (at < count))
                def _(tp=tp, onward=onward, sign=sign, at=at):
                    here = self.place(tp, at)
                    wait_came(here, self.sent.at[2], self.flag(tp, at))

                    @pl.when((me < n - 1) if sign < 0 else (me > 0))
                    def _():
                        remote(here, here, self.sent.at[2], self.flag(tp, at), onward).start()

    def drain(self):
        n, me = self.n, self.me

        @pl.when(me > 0)
        def _():
            wait_sent(self.src, self.sent.at[0], self.flag(0, 0))

        @pl.when(me < n - 1)
        def _():
            wait_sent(self.src, self.sent.at[1], self.flag(0, 0))

        @pl.when((me > 0) & (me < n - 1))
        def _():
            wait_sent(self.dst.at[:, pl.ds(0, (n - 1) * self.width)], self.sent.at[2], self.flag(0, 0))

    @staticmethod
    def scratch(n, count):
        return [
            pltpu.SemaphoreType.DMA((n, count)),
            pltpu.SemaphoreType.DMA((3,)),
            pltpu.SemaphoreType.DMA,
        ]


class LineSum:
    def __init__(self, n, chunk, hop, part, from_left, from_right, out, recv, sent, finish, pushed=False):
        self.n, self.chunk, self.hop, self.pushed = n, chunk, hop, pushed
        self.total_rows = part.shape[0]
        self.owners = (n // 2 - 1, n // 2)
        self.count = self.total_rows // 2 // chunk
        self.part, self.from_left, self.from_right, self.out = part, from_left, from_right, out
        self.recv, self.sent = recv, sent
        self.finish = finish
        self.me = lax.axis_index("tp")

    def steps(self):
        return self.count + self.hop * 2 * (self.n // 2)

    def turn(self, at):
        return lax.rem(at, self.recv.shape[2])

    def rows(self, slot, at):
        return pl.ds(pl.multiple_of((at * 2 + slot) * self.chunk, self.chunk), self.chunk)

    def send(self, here, side, slot, at):
        held = self.from_left if side == 0 else self.from_right
        to = {"tp": self.me + 1} if side == 0 else {"tp": self.me - 1}

        @pl.when(here)
        def _():
            rows = self.rows(slot, at)
            remote(self.part.at[rows], held.at[rows], self.sent.at[0], self.recv.at[side, slot, self.turn(at)],
                   to).start()

    def push(self, at):
        for slot, owner in enumerate(self.owners):
            if owner > 0:
                self.send(self.me == 0, 0, slot, at)
            if owner < self.n - 1:
                self.send(self.me == self.n - 1, 1, slot, at)

    def step(self, s):
        n, me, hop = self.n, self.me, self.hop
        left, right = {"tp": me - 1}, {"tp": me + 1}
        reach = n // 2
        for slot, owner in enumerate(self.owners):
            for side in (0, 1):
                lag = me if side == 0 else n - 1 - me
                at = s - hop * lag
                here = (me < owner) if side == 0 else (me > owner)
                held = self.from_left if side == 0 else self.from_right
                to = right if side == 0 else left
                here = here & (at >= 0) & (at < self.count)

                if not self.pushed:
                    self.send(here & (lag == 0), side, slot, at)

                if n > 2:

                    @pl.when(here & (lag > 0))
                    def _(at=at, held=held, to=to, side=side, slot=slot):
                        rows = self.rows(slot, at)
                        wait_came(held.at[rows], self.sent.at[0], self.recv.at[side, slot, self.turn(at)])
                        held[rows, :] = (held[rows, :].astype(F32) + self.part[rows, :].astype(F32)).astype(BF16)
                        remote(held.at[rows], held.at[rows], self.sent.at[0],
                               self.recv.at[side, slot, self.turn(at)], to).start()

            at = s - hop * reach

            @pl.when((me == owner) & (at >= 0) & (at < self.count))
            def _(at=at, slot=slot, owner=owner):
                rows = self.rows(slot, at)
                total = self.part[rows, :].astype(F32)
                if owner > 0:
                    wait_came(self.from_left.at[rows], self.sent.at[0], self.recv.at[0, slot, self.turn(at)])
                    total = total + self.from_left[rows, :].astype(F32)
                wait_came(self.from_right.at[rows], self.sent.at[0], self.recv.at[1, slot, self.turn(at)])
                total = total + self.from_right[rows, :].astype(F32)
                own = pl.ds(pl.multiple_of(at * self.chunk, self.chunk), self.chunk)
                self.out[rows, :] = self.finish(rows, own, total)
                if owner > 0:
                    remote(self.out.at[rows], self.out.at[rows], self.sent.at[1],
                           self.recv.at[2, slot, self.turn(at)], left).start()
                remote(self.out.at[rows], self.out.at[rows], self.sent.at[2],
                       self.recv.at[2, slot, self.turn(at)], right).start()

        for slot, owner in enumerate(self.owners):
            away = jnp.abs(me - owner)
            at = s - hop * (reach + away)

            @pl.when((me != owner) & (at >= 0) & (at < self.count))
            def _(at=at, slot=slot, owner=owner):
                rows = self.rows(slot, at)
                here = self.out.at[rows]
                wait_came(here, self.sent.at[3], self.recv.at[2, slot, self.turn(at)])

                @pl.when((me < owner) & (me > 0))
                def _():
                    remote(here, here, self.sent.at[3], self.recv.at[2, slot, self.turn(at)], left).start()

                @pl.when((me > owner) & (me < n - 1))
                def _():
                    remote(here, here, self.sent.at[3], self.recv.at[2, slot, self.turn(at)], right).start()

    def drain(self):
        n, me, half = self.n, self.me, self.total_rows // 2
        lo, hi = self.owners

        def wait(sem, size):
            wait_sent(self.part.at[pl.ds(0, size)], self.sent.at[sem], self.recv.at[0, 0, 0])

        middle = (me == lo) | (me == hi)

        @pl.when(middle)
        def _():
            wait(0, half)
            wait(2, half)

        @pl.when((me != lo) & (me != hi))
        def _():
            wait(0, 2 * half)

        if lo > 0:

            @pl.when(middle)
            def _():
                wait(1, half)
                wait(3, half)

            if n > 4:

                @pl.when((me != lo) & (me != hi) & (me > 0) & (me < n - 1))
                def _():
                    wait(3, 2 * half)
        else:

            @pl.when(me == hi)
            def _():
                wait(1, half)

    @staticmethod
    def scratch(n, rows, width, chunk):
        return [
            pltpu.VMEM((rows, width), BF16),
            pltpu.VMEM((rows, width), BF16),
            pltpu.SemaphoreType.DMA((3, 2, min(rows // 2 // chunk, 12))),
            pltpu.SemaphoreType.DMA((4,)),
        ]


class GradSum:
    def __init__(self, fsdp, ctx, parts, axes, outs, held, recv, sent):
        self.fsdp, self.ctx, self.parts, self.axes, self.outs = fsdp, ctx, parts, axes, outs
        self.ys = fsdp // 2
        self.held, self.recv, self.sent = held, recv, sent
        self.f = lax.axis_index("fsdp")
        self.x = lax.axis_index("ctx")
        self.y, self.c = self.f // 2, lax.rem(self.f, 2)

    @staticmethod
    def block_shape(shape, axis, fsdp):
        r, c = shape
        return (r // fsdp, c) if axis == 0 else (r, c // fsdp)

    @staticmethod
    def scratch(fsdp, ctx, shapes, first=True):
        held = []
        for shape in shapes:
            if first:
                held.append(pltpu.VMEM((fsdp // 2,) + shape, BF16))
            held += [
                pltpu.VMEM((max(fsdp // 2 - 1, 1),) + shape, BF16),
                pltpu.VMEM((ctx,) + shape, BF16),
            ]
        return held

    @staticmethod
    def semaphores(fsdp, ctx, count):
        return [pltpu.SemaphoreType.DMA((count, 3, max(fsdp // 2, ctx)))] * 2

    def part(self, a, f):
        shape = self.held[a][0].shape[1:]
        return block(self.parts[a], self.axes[a], f, shape[self.axes[a]])

    def each(self, a, body):
        rows = self.held[a][0].shape[1]
        size = 32 if rows % 32 == 0 else 16

        def step(i, carry):
            body(pl.ds(pl.multiple_of(i * size, size), size))
            return carry

        lax.fori_loop(0, rows // size, step, 0)

    def start(self):
        for a in range(len(self.parts)):
            for k in range(self.ys):
                remote(self.part(a, 2 * k + 1 - self.c), self.held[a][0].at[k], self.sent.at[a, 0, k],
                       self.recv.at[a, 0, k], {"fsdp": sibling(self.f)}).start()

    def pair(self):
        for a in range(len(self.parts)):
            first = self.held[a][0]
            for k in range(self.ys):
                wait_came(first.at[k], self.sent.at[a, 0, k], self.recv.at[a, 0, k])
                mine = self.part(a, 2 * k + self.c)

                def add(rows, first=first, k=k, mine=mine):
                    first[k, rows, :] = (first[k, rows, :].astype(F32) + mine[rows, :].astype(F32)).astype(BF16)

                self.each(a, add)

    def second(self):
        for a in range(len(self.held)):
            first, later = self.held[a][0], self.held[a][1]
            for k in range(1, self.ys):
                to = lax.rem(self.y + k, self.ys)
                remote(first.at[to], later.at[k - 1], self.sent.at[a, 1, k], self.recv.at[a, 1, k],
                       {"fsdp": 2 * to + self.c}).start()

    def third(self):
        for a in range(len(self.held)):
            first, later, last = self.held[a]
            for k in range(1, self.ys):
                wait_came(later.at[k - 1], self.sent.at[a, 1, k], self.recv.at[a, 1, k])

            def add(rows, first=first, later=later, last=last):
                total = first[self.y, rows, :].astype(F32)
                for k in range(1, self.ys):
                    total = total + later[k - 1, rows, :].astype(F32)
                last[self.x, rows, :] = total.astype(BF16)

            self.each(a, add)
            for k in range(1, self.ctx):
                remote(last.at[self.x], last.at[self.x], self.sent.at[a, 2, k], self.recv.at[a, 2, self.x],
                       {"ctx": lax.rem(self.x + k, self.ctx)}).start()

    def fourth(self, store):
        for a in range(len(self.held)):
            last = self.held[a][2]
            for k in range(1, self.ctx):
                other = lax.rem(self.x + k, self.ctx)
                wait_came(last.at[other], self.sent.at[a, 2, k], self.recv.at[a, 2, other])

            def add(rows, last=last, a=a):
                total = last[0, rows, :].astype(F32)
                for k in range(1, self.ctx):
                    total = total + last[k, rows, :].astype(F32)
                store(a, rows, total)

            self.each(a, add)

    def drain_pair(self):
        for a in range(len(self.parts)):
            for k in range(self.ys):
                wait_sent(self.held[a][0].at[k], self.sent.at[a, 0, k], self.recv.at[a, 0, k])

    def drain(self):
        for a in range(len(self.held)):
            first, later, last = self.held[a]
            for k in range(1, self.ys):
                wait_sent(later.at[k - 1], self.sent.at[a, 1, k], self.recv.at[a, 1, k])
            for k in range(1, self.ctx):
                wait_sent(last.at[self.x], self.sent.at[a, 2, k], self.recv.at[a, 2, 0])


def loop(first, last, body):
    def step(s, carry):
        body(s)
        return carry

    lax.fori_loop(first, last, step, 0)


def params(ident, mib):
    return pltpu.CompilerParams(collective_id=ident, has_side_effects=True, vmem_limit_bytes=min(mib << 20, 67043328))


def shape_of(shape, dtype):
    return jax.ShapeDtypeStruct(shape, dtype)


TILE = 256


def dot(left, right):
    return jnp.dot(left, right, preferred_element_type=F32)


def dot_t(left, right):
    return lax.dot_general(left, right, (((1,), (1,)), ((), ())), preferred_element_type=F32)


def dot_rows(left, right):
    return lax.dot_general(left, right, (((0,), (0,)), ((), ())), preferred_element_type=F32)


def head_only(value, head):
    lane = lax.broadcasted_iota(jnp.int32, value.shape, 1)
    return jnp.where((lane // HEAD_DIM) == head, value, jnp.zeros_like(value))


class RowGather:
    def __init__(self, n, src, dst, recv, sent, own):
        self.n, self.src, self.dst = n, src, dst
        self.recv, self.sent, self.own = recv, sent, own
        self.me = lax.axis_index("tp")

    def start(self):
        me = self.me
        pltpu.make_async_copy(self.src, self.dst.at[me], self.own).start()

        @pl.when(me > 0)
        def _():
            remote(self.src, self.dst.at[me], self.sent.at[0, 0], self.recv.at[me], {"tp": me - 1}).start()

        @pl.when(me < self.n - 1)
        def _():
            remote(self.src, self.dst.at[me], self.sent.at[1, 0], self.recv.at[me], {"tp": me + 1}).start()

    def each(self, body, which=None):
        me, n = self.me, self.n
        for away in which or range(1, n):
            for way, tp in ((1, me - away), (0, me + away)):

                @pl.when((tp >= 0) & (tp < n))
                def _(tp=tp, way=way, away=away):
                    onward = (me < n - 1) if way == 1 else (me > 0)
                    body(away, way, tp, onward, {"tp": me + 1} if way == 1 else {"tp": me - 1})

    def relay(self, which=None):
        def body(away, way, tp, onward, to):
            here = self.dst.at[tp]
            wait_came(here, self.sent.at[way, away], self.recv.at[tp])

            @pl.when(onward)
            def _():
                remote(here, here, self.sent.at[way, away], self.recv.at[tp], to).start()

        self.each(body, which)

    def finish(self):
        me = self.me
        pltpu.make_async_copy(self.src, self.dst.at[me], self.own).wait()

        @pl.when(me > 0)
        def _():
            wait_sent(self.src, self.sent.at[0, 0], self.recv.at[0])

        @pl.when(me < self.n - 1)
        def _():
            wait_sent(self.src, self.sent.at[1, 0], self.recv.at[0])

        def body(away, way, tp, onward, to):
            @pl.when(onward)
            def _():
                wait_sent(self.src, self.sent.at[way, away], self.recv.at[0])

        self.each(body)

    @staticmethod
    def scratch(n):
        return [
            pltpu.SemaphoreType.DMA((n,)),
            pltpu.SemaphoreType.DMA((2, n)),
            pltpu.SemaphoreType.DMA,
        ]


class AxisSum:
    def __init__(self, axis, n, slots, recv, sent):
        self.axis, self.n, self.slots, self.recv, self.sent = axis, n, slots, recv, sent
        self.at = lax.axis_index(axis)

    def start(self, value):
        self.slots[self.at] = value
        for k in range(1, self.n):
            remote(self.slots.at[self.at], self.slots.at[self.at], self.sent.at[k], self.recv.at[self.at],
                   {self.axis: lax.rem(self.at + k, self.n)}).start()

    def finish(self):
        for k in range(1, self.n):
            other = lax.rem(self.at + k, self.n)
            wait_came(self.slots.at[other], self.sent.at[k], self.recv.at[other])
            wait_sent(self.slots.at[self.at], self.sent.at[k], self.recv.at[other])
        total = self.slots[0]
        for k in range(1, self.n):
            total = total + self.slots[k]
        return total

    @staticmethod
    def scratch(n, shape):
        return [
            pltpu.VMEM((n,) + shape, F32),
            pltpu.SemaphoreType.DMA((n,)),
            pltpu.SemaphoreType.DMA((n,)),
        ]


def window(ctx, tok_dev):
    return min(ctx, (tok_dev * ctx // 2 + tok_dev - 1) // tok_dev + 1)


def key_span(ctx, tok_dev):
    return min(ctx * tok_dev // 2 // TILE, (window(ctx, tok_dev) - 1) * (tok_dev // TILE))


R_ONE, SEGMENT, VALID = 0, 1, 2


def front(tokens, gain1, gain2, w_latent, shards, w_out, wide_shards, segments, fsdp, ctx, n):
    rows, width = tokens.shape
    seq_dev, tok_dev = segments.shape
    latent, q_width = LATENT, shards[0].shape[1]
    wide, chunk = 128, 256
    pieces = rows // chunk
    win = window(ctx, tok_dev)
    full = [shape_of((s.shape[0] * fsdp,) + s.shape[1:], s.dtype) for s in shards]
    wider = [shape_of((s.shape[0], s.shape[1] * fsdp), s.dtype) for s in wide_shards]
    per_group = HEADS // GROUPS * HEAD_DIM
    per_seq = tok_dev // chunk

    def kernel(*refs):
        (tok_in, ga, gb, wlat, wq, wk, wv, wo, wg, wu, seg), refs = refs[:11], refs[11:]
        (xn_out, cols, gain_all, w_lat, w_qry, w_kproj, w_vproj, gate_all, up_all), refs = refs[:9], refs[9:]
        (wo_all, seg_all, lat_all, query, keys, values), refs = refs[:6], refs[6:]
        (gbuf, sbuf, tok, xn, tsem), refs = refs[:5], refs[5:]
        bring = Bring([(tok_in, tok), (xn, xn_out)], tsem)
        bring.start([0])
        x, me = lax.axis_index("ctx"), lax.axis_index("tp")
        gbuf[...] = jnp.zeros_like(gbuf)
        gbuf[0:1, :] = ga[...].astype(F32).reshape(1, -1)
        gbuf[1:2, :] = gb[...].astype(F32).reshape(1, -1)
        sbuf[...] = jnp.zeros_like(sbuf)
        sbuf[0:seq_dev, :] = seg[...]
        meet(n, fsdp, ctx)
        group = me * q_width // per_group
        src_lat = wlat.at[:, pl.ds(pl.multiple_of(group * latent, latent), latent)]
        pairs = [(gbuf, gain_all), (src_lat, w_lat), (wq, w_qry), (wk, w_kproj), (wv, w_vproj),
                 (wg, gate_all), (wu, up_all)]
        spread = Spread(fsdp, pairs, [1, 0, 0, 0, 0, 1, 1], *refs[:3])
        share = CtxShare(ctx, sbuf, seg_all, *refs[3:6])
        line = RowGather(n, wo, wo_all, *refs[6:9])
        lat_recv, lat_sent = refs[9:11]
        spread.start()
        share.start()
        line.start()
        own = win - 1
        cols[...] = jnp.zeros_like(cols)
        bring.wait([0])

        def scale(i):
            at = pl.ds(pl.multiple_of(i * wide, wide), wide)
            value = tok[at, :].astype(F32)
            cols[at, R_ONE : R_ONE + 1] = lax.rsqrt(jnp.mean(value * value, axis=-1, keepdims=True) + eps)

        loop(0, rows // wide, scale)
        spread.relay([0, 1])
        spread.finish([0, 1])

        def place(shard, i):
            seq = i // per_seq
            return pl.ds(pl.multiple_of(seq * win * tok_dev + shard * tok_dev + lax.rem(i, per_seq) * chunk, chunk), chunk)

        def send(k, i):
            return remote(lat_all.at[place(own, i)], lat_all.at[place(own - k, i)], lat_sent.at[k, i],
                          lat_recv.at[own - k, i], {"ctx": x + k})

        def first(i):
            at = pl.ds(pl.multiple_of(i * chunk, chunk), chunk)
            unit = (tok[at, :].astype(F32) * cols[at, R_ONE : R_ONE + 1] * gain_all[0:1, :]).astype(BF16)
            xn[at, :] = unit
            lat_all[place(own, i), :] = dot(unit, w_lat[...]).astype(BF16)
            for k in range(1, win):

                @pl.when(x + k < ctx)
                def _(k=k):
                    send(k, i).start()

        loop(0, pieces, first)
        bring.start([1])
        line.relay([1])
        spread.relay([2, 3, 4])
        spread.finish([2, 3, 4])

        def project(shard, i):
            to = place(shard, i)
            value = lat_all[to, :]
            keys[to, :] = dot(value, w_kproj[...]).astype(BF16)
            values[to, :] = dot(value, w_vproj[...]).astype(BF16)

        def ask(i):
            at = pl.ds(pl.multiple_of(i * chunk, chunk), chunk)
            query[at, :] = dot(xn[at, :], w_qry[...]).astype(BF16)
            project(own, i)

        loop(0, pieces, ask)
        share.finish()
        for q in range(seq_dev):
            at = slice(q * tok_dev, (q + 1) * tok_dev)
            ids = jnp.broadcast_to(sbuf[q : q + 1, :].astype(F32), (128, tok_dev)).T
            cols[at, SEGMENT : SEGMENT + 1] = ids[:, 0:1]
            last = seg_all[ctx - 1, q : q + 1, tok_dev - 1 : tok_dev].astype(F32)
            cols[at, VALID : VALID + 1] = jnp.where(ids[:, 0:1] != last, 1.0, 0.0)
        line.relay(range(2, n))
        for k in range(1, win):

            def theirs(i, k=k):
                @pl.when(x - k >= 0)
                def _():
                    wait_came(lat_all.at[place(own - k, i)], lat_sent.at[k, i], lat_recv.at[own - k, i])

                @pl.when(x - k < 0)
                def _():
                    lat_all[place(own - k, i), :] = jnp.zeros((chunk, latent), BF16)

                project(own - k, i)

            loop(0, pieces, theirs)

            def gone(i, k=k):
                @pl.when(x + k < ctx)
                def _():
                    send(k, i).wait_send()

            loop(0, pieces, gone)
        spread.relay([5, 6])
        spread.finish([5, 6])
        line.finish()
        bring.wait([1])

    return pl.pallas_call(
        kernel,
        out_shape=(
            shape_of((rows, width), BF16),
            shape_of((rows, 128), F32),
            shape_of((8, width), F32),
            shape_of((width, latent), BF16),
            *full,
            *wider,
            shape_of((n,) + w_out.shape, w_out.dtype),
            shape_of((ctx, 8, tok_dev), segments.dtype),
            shape_of((win * rows, latent), BF16),
            shape_of((rows, q_width), BF16),
            shape_of((win * rows, q_width), BF16),
            shape_of((win * rows, q_width), BF16),
        ),
        in_specs=[ANY] + [VMEM] * 10,
        out_specs=(ANY,) + (VMEM,) * 6 + (ANY,) * 3 + (VMEM,) * 5,
        scratch_shapes=[
            pltpu.VMEM((8, gain1.shape[0]), F32),
            pltpu.VMEM((8, tok_dev), segments.dtype),
            pltpu.VMEM((rows, width), BF16),
            pltpu.VMEM((rows, width), BF16),
            pltpu.SemaphoreType.DMA((2,)),
        ]
        + Spread.scratch(fsdp, 7)
        + CtxShare.scratch(ctx)
        + RowGather.scratch(n)
        + [pltpu.SemaphoreType.DMA((win, pieces))] * 2,
        compiler_params=params(1, 56),
    )(tokens, gain1, gain2, w_latent, *shards, w_out, *wide_shards, segments)


def counted_keys(cols, segk, at, seq, q_first, first, count, tok_dev, win):
    per = tok_dev // TILE
    oldest = lax.axis_index("ctx") - (win - 1)
    mine = cols[at, SEGMENT : SEGMENT + 1]
    shape = (mine.shape[0], TILE)
    pieces = []
    for j in range(count):
        t = first + j
        shard = oldest + t // per
        inner = pl.ds(pl.multiple_of(lax.rem(t, per) * TILE, TILE), TILE)
        ids = segk[jnp.maximum(shard, 0), pl.ds(seq, 1), inner].astype(F32)
        q_at = q_first + lax.broadcasted_iota(jnp.int32, shape, 0)
        k_at = t * TILE + lax.broadcasted_iota(jnp.int32, shape, 1)
        pieces.append((k_at <= q_at) & (ids == mine) & (shard >= 0))
    return pieces


def middle(query, keys, values, seg_all, cols, shards, gate_all, up_all, gains, tokens, out_grad,
           fsdp, ctx, n, seq_dev, late):
    rows, width = tokens.shape
    q_width = query.shape[1]
    heads = q_width // HEAD_DIM
    inner = gate_all.shape[0]
    tok_dev = rows // seq_dev
    per = tok_dev // TILE
    win, span = window(ctx, tok_dev), key_span(ctx, tok_dev)
    tiles = span + 1
    part = TILE if tiles <= 3 else 64
    chunk, hop = 32, 2
    size, piece = 256, 64
    per_block = size // piece
    half = rows // 2
    cols_at = width // 4
    block_shape = (inner, width // fsdp)
    count = 3

    def kernel(*refs):
        (q_in, k_in, v_in, segk, cols, wo_in, wd_in, wg_in, wu_in, gain, tok_in, cot_in), refs = refs[:12], refs[12:]
        (o_branch, o_feed, o_dmid, o_mid, o_wo, o_gain, o_bsq, o_mark, o_att, o_lse), refs = refs[:10], refs[10:]
        outs, refs = refs[:3], refs[3:]
        one, gsems, parts, refs = refs[:4], refs[4:6], refs[6:9], refs[9:]
        (query, keys, values, att, att_all, wo, wd, wg, wu, tok, cot), refs = refs[:11], refs[11:]
        (mid, r2, xn, hid, dg, du, p_two, p_feed, bsem), refs = refs[:9], refs[9:]
        bring = Bring([(q_in, query), (k_in, keys), (v_in, values), (tok_in, tok), (wg_in, wg), (wu_in, wu),
                       (cot_in, cot), (att, o_att), (p_feed, o_feed)], bsem)
        bring.start(range(7))
        meet(n, fsdp, ctx)
        line = LineGather(n, piece, att, att_all, *refs[:3])
        spread = Spread(fsdp, [(wo_in, wo), (wd_in, wd)], [1, 1], *refs[3:6])
        keep = refs[6:]
        spread.start()
        o_gain[...] = jnp.zeros_like(o_gain)
        o_bsq[...] = jnp.zeros_like(o_bsq)
        o_mark[...] = jnp.zeros_like(o_mark)
        g2 = gain.at[1:2]

        def back(at, own, total):
            middle_rows = mid[at, :]
            o_mid[own, :] = middle_rows
            unit = middle_rows * r2[at, :]
            o_gain[...] += jnp.sum((total * unit).reshape(chunk // 8, 8, width), axis=0)
            scaled = total * g2[...]
            mean = jnp.mean(scaled * unit, axis=-1, keepdims=True)
            d_mid = cot[at, :].astype(F32) + r2[at, :] * (scaled - unit * mean)
            o_dmid[own, :] = d_mid
            first_unit = tok[at, :].astype(F32) * cols[at, R_ONE : R_ONE + 1]
            o_mark[at, 0:1] = jnp.sum(first_unit * d_mid, axis=-1, keepdims=True)
            return d_mid.astype(BF16)

        first = LineSum(n, chunk, hop, p_two, one[0], one[1], o_branch, one[2], one[3], back)
        if late:
            held = [[out, None, None] for out in outs]
        else:
            held = [keep[3 * a : 3 * a + 3] for a in range(count)]
        grad = GradSum(fsdp, ctx, parts, [1] * count, outs, held, *gsems)
        bring.wait([0, 1, 2])

        def query_rows(i, j):
            seq = i // per
            q_tile = (win - 1) * per + lax.rem(i, per)
            at = pl.ds(pl.multiple_of(i * TILE + j * part, part), part)
            near = pl.ds(pl.multiple_of((seq * win * per + q_tile - span) * TILE, TILE), tiles * TILE)
            counted = jnp.concatenate(
                [
                    c.astype(F32)
                    for c in counted_keys(
                        cols, segk, at, seq, q_tile * TILE + j * part, q_tile - span, tiles, tok_dev, win
                    )
                ],
                axis=1,
            )
            accum = jnp.zeros((part, q_width), F32)
            lane = lax.broadcasted_iota(jnp.int32, (part, 128), 1)
            kept = jnp.zeros((part, 128), F32)
            for h in range(heads):
                score = jnp.where(counted > 0.0, dot_t(head_only(query[at, :], h), keys[near, :]) * 0.125, -1e30)
                top = jnp.max(score, axis=-1, keepdims=True)
                weight = jnp.exp(score - top)
                total = jnp.sum(weight, axis=-1, keepdims=True)
                prob = (weight * (1.0 / total)).astype(BF16)
                accum = accum + jnp.dot(prob, head_only(values[near, :], h), preferred_element_type=F32)
                kept = jnp.where(lane == h, top + jnp.log(total), kept)
                if part == TILE:
                    line.step((i - 1) * per_block + h * per_block // heads)
            o_lse[at, :] = kept
            att[at, :] = accum.astype(BF16)

        def query_tile(i):
            if part == TILE:
                query_rows(i, 0)
                return
            loop(0, TILE // part, lambda j: query_rows(i, j))
            for h in range(per_block):
                line.step((i - 1) * per_block + h)

        loop(0, rows // TILE, query_tile)
        bring.start([7])
        line.begin()
        s1 = (rows // TILE - 1) * per_block
        spread.relay()
        spread.finish()
        tp = lax.axis_index("tp")
        o_wo[...] = wo[pl.ds(pl.multiple_of(tp * q_width, q_width), q_width), :]
        line.begun()
        bring.wait([3, 4, 5, 6])

        def block_of_rows(b):
            at = pl.ds(pl.multiple_of(b * size, size), size)
            seq = b * size // tok_dev

            def steps(j):
                line.step(s1 + b * per_block + j)
                first.step((b - 1) * per_block + j)

            branch = dot(att_all[at, :], wo[...])
            middle_rows = tok[at, :].astype(F32) + branch
            mid[at, :] = middle_rows
            o_bsq[pl.ds(pl.multiple_of(seq * 8, 8), 8), :] += jnp.sum(
                (branch * branch * cols[at, VALID : VALID + 1]).reshape(size // 8, 8, width), axis=0
            )
            scale = lax.rsqrt(jnp.mean(middle_rows * middle_rows, axis=-1, keepdims=True) + eps)
            r2[at, :] = scale
            unit = (middle_rows * scale * g2[...]).astype(BF16)
            xn[at, :] = unit
            steps(0)
            gate = dot_t(unit, wg[...])
            upper = dot_t(unit, wu[...])
            sigma = jax.nn.sigmoid(gate)
            swish = gate * sigma
            hidden = (swish * upper).astype(BF16)
            hid[at, :] = hidden
            slope = upper * sigma * (1.0 + gate * (1.0 - sigma))
            steps(1)
            p_feed[at, :] = dot(hidden, wd[...]).astype(BF16)
            d_hidden = dot_t(cot[at, :], wd[...])
            d_gate = (d_hidden * slope).astype(BF16)
            d_upper = (d_hidden * swish).astype(BF16)
            dg[at, :] = d_gate
            du[at, :] = d_upper
            steps(2)
            p_two[at, :] = (dot(d_gate, wg[...]) + dot(d_upper, wu[...])).astype(BF16)
            steps(3)

        loop(0, rows // size, block_of_rows)
        bring.start([8])
        s0 = (rows // size - 1) * per_block

        def product(i):
            at = pl.ds(pl.multiple_of(i * cols_at, cols_at), cols_at)
            left = xn[:, at]
            parts[0][:, at] = dot_rows(dg[...], left).astype(BF16)
            parts[1][:, at] = dot_rows(du[...], left).astype(BF16)
            parts[2][:, at] = dot_rows(hid[...], cot[:, at]).astype(BF16)

        def busy(s):
            first.step(s)
            product(s - s0)

        loop(s0, s0 + 4, busy)
        grad.start()
        last = first.steps()
        loop(s0 + 4, s0 + 6, first.step)
        grad.pair()
        if not late:
            grad.second()
        loop(s0 + 6, last, first.step)
        if not late:
            grad.third()

            def store(a, at, total):
                outs[a][at, :] = total

            grad.fourth(store)
            grad.drain()
        line.drain()
        first.drain()
        grad.drain_pair()
        bring.wait([7, 8])

    ys = fsdp // 2
    out = pl.pallas_call(
        kernel,
        out_shape=(
            shape_of((rows, width), BF16),
            shape_of((rows, width), BF16),
            shape_of((half, width), F32),
            shape_of((half, width), F32),
            shape_of((q_width, width), BF16),
            shape_of((8, width), F32),
            shape_of((8 * seq_dev, width), F32),
            shape_of((rows, 128), F32),
            shape_of((rows, q_width), BF16),
            shape_of((rows, 128), F32),
        )
        + ((shape_of((ys,) + block_shape, BF16) if late else shape_of(block_shape, F32)),) * count,
        in_specs=[ANY] * 3 + [VMEM] * 4 + [ANY] * 2 + [VMEM] + [ANY] * 2,
        out_specs=(VMEM, ANY) + (VMEM,) * 6 + (ANY, VMEM) + (VMEM,) * count,
        scratch_shapes=LineSum.scratch(n, rows, width, chunk)
        + GradSum.semaphores(fsdp, ctx, count)
        + [pltpu.VMEM((inner, width), BF16)] * count
        + [
            pltpu.VMEM((rows, q_width), BF16),
            pltpu.VMEM((win * rows, q_width), BF16),
            pltpu.VMEM((win * rows, q_width), BF16),
            pltpu.VMEM((rows, q_width), BF16),
            pltpu.VMEM((rows, n * q_width), BF16),
            pltpu.VMEM((n * q_width, width), BF16),
            pltpu.VMEM((inner, width), BF16),
            pltpu.VMEM((inner, width), BF16),
            pltpu.VMEM((inner, width), BF16),
            pltpu.VMEM((rows, width), BF16),
            pltpu.VMEM((rows, width), BF16),
            pltpu.VMEM((rows, width), F32),
            pltpu.VMEM((rows, 1), F32),
            pltpu.VMEM((rows, width), BF16),
            pltpu.VMEM((rows, inner), BF16),
            pltpu.VMEM((rows, inner), BF16),
            pltpu.VMEM((rows, inner), BF16),
            pltpu.VMEM((rows, width), BF16),
            pltpu.VMEM((rows, width), BF16),
            pltpu.SemaphoreType.DMA((9,)),
        ]
        + LineGather.scratch(n, rows // piece)
        + Spread.scratch(fsdp, 2)
        + ([] if late else GradSum.scratch(fsdp, ctx, [block_shape] * count)),
        compiler_params=params(2, 64),
    )(query, keys, values, seg_all, cols, *shards, gate_all, up_all, gains, tokens, out_grad)
    return out[:10], out[10:]


def back(query, keys, values, seg_all, cols, lse, attended, d_branch, wo_rows, weights, lat_all, xn_one, gains,
         tokens, d_middle, mid_own, part_feed, marks, gain_part, branch_sq, firsts, fsdp, ctx, n, seq_dev):
    rows, width = tokens.shape
    w_qry, w_lat, w_kproj, w_vproj = weights
    q_width, latent = query.shape[1], w_lat.shape[1]
    heads, tok_dev = q_width // HEAD_DIM, rows // seq_dev
    per = tok_dev // TILE
    win, span = window(ctx, tok_dev), key_span(ctx, tok_dev)
    tiles = span + 1
    group = tiles if tiles <= 3 else 1
    chunk, hop, wide, side = 32, 2, 256, 128
    half = rows // 2
    axes = (0, 0, 0, 1, 0)
    whole = ((width, q_width), (latent, q_width), (latent, q_width), (q_width, width), (width, latent))
    blocks = [GradSum.block_shape(w, a, fsdp) for w, a in zip(whole, axes)]
    lat = blocks[-1]
    ffn = [f.shape[1:] for f in firsts]
    seq_pieces = tok_dev // wide
    many = max(width, rows)

    def kernel(*refs):
        (q_ref, k_ref, v_ref, segk, cols, lse_ref, att, dbr, wo), refs = refs[:9], refs[9:]
        (wq, wl, wk, wv, la_in, xn_in, gain, tok_in, dmid_in, mid_in, feed_in), refs = refs[:11], refs[11:]
        (marks, gain_two, bsq), fsts, refs = refs[:3], refs[3 : 3 + len(ffn)], refs[3 + len(ffn) :]
        (o_tok, o_mixed, o_small), outs, refs = refs[:3], refs[3:8], refs[8:]
        fouts, refs = refs[: len(ffn)], refs[len(ffn) :]
        one, two, keep, gsems, parts, refs = refs[:4], refs[4:8], refs[8:23], refs[23:25], refs[25:30], refs[30:]
        (p_one, dlat, came, c_recv, c_sent, gacc, sm, sacc), refs = refs[:8], refs[8:]
        (dk, dv, dq, dqb, grad_seq, lat_parts), refs = refs[:6], refs[6:]
        (la, xn, tok, dmid, mid, p_feed, bsem), refs = refs[:7], refs[7:]
        (lat_own, lat_every), lsems, sums, refs = refs[:2], refs[2:5], refs[5:14], refs[14:]
        bring = Bring([(feed_in, p_feed), (mid_in, mid), (la_in, la), (xn_in, xn), (tok_in, tok), (dmid_in, dmid)], bsem)
        bring.start()
        meet(n, fsdp, ctx, everyone=True)
        x = lax.axis_index("ctx")
        own_shard = win - 1
        grad_ffn = None
        if ffn:
            fkeep, fsems = refs[: 2 * len(ffn)], refs[2 * len(ffn) :]
            grad_ffn = GradSum(fsdp, ctx, [], [], fouts,
                               [[fsts[a], fkeep[2 * a], fkeep[2 * a + 1]] for a in range(len(ffn))], *fsems)
            grad_ffn.second()
        gacc[...] = jnp.zeros_like(gacc)
        sacc[...] = jnp.zeros_like(sacc)
        sm[...] = jnp.zeros_like(sm)
        g1 = gain.at[0:1]

        def forward(at, own, total):
            mixed = mid[own, :] + total
            seq = at.start // tok_dev
            counted = cols[at, VALID : VALID + 1]
            sacc[seq] += jnp.sum((mixed * mixed * counted).reshape(chunk // 8, 8, width), axis=0)
            sacc[seq_dev + seq] += jnp.sum((total * total * counted).reshape(chunk // 8, 8, width), axis=0)
            return mixed.astype(BF16)

        def backward(at, own, total):
            r1 = cols[at, R_ONE : R_ONE + 1]
            unit = tok[at, :].astype(F32) * r1
            scaled = total * g1[...]
            mean = jnp.mean(scaled * unit, axis=-1, keepdims=True)
            return (dmid[own, :] + r1 * (scaled - unit * mean)).astype(BF16)

        feed = LineSum(n, chunk, hop, p_feed, two[0], two[1], o_mixed, two[2], two[3], forward)
        first = LineSum(n, chunk, hop, p_one, one[0], one[1], o_tok, one[2], one[3], backward)
        grad = GradSum(fsdp, ctx, parts, axes, outs, [keep[3 * a : 3 * a + 3] for a in range(5)], *gsems)
        line = RowGather(n, lat_own, lat_every, *lsems)
        over_tp = AxisSum("tp", n, *sums[0:3])
        over_ctx = AxisSum("ctx", ctx, *sums[3:6])
        over_fsdp = AxisSum("fsdp", fsdp, *sums[6:9])

        def clear(i):
            at = pl.ds(pl.multiple_of(i * TILE, TILE), TILE)
            dk[at, :] = jnp.zeros((TILE, q_width), F32)
            dv[at, :] = jnp.zeros((TILE, q_width), F32)

        loop(0, win * rows // TILE, clear)
        bring.wait([0, 1])

        def query_tile(i, step):
            seq = i // per
            q_tile = own_shard * per + lax.rem(i, per)
            at = pl.ds(pl.multiple_of(i * TILE, TILE), TILE)
            grad_seq[...] = dot_t(dbr[at, :], wo[...]).astype(BF16)
            product = grad_seq[...].astype(F32) * att[at, :].astype(F32)
            delta = [jnp.sum(head_only(product, h), axis=-1, keepdims=True) for h in range(heads)]
            dq[...] = jnp.zeros_like(dq)

            def key_tiles(kk):
                t = q_tile - span + kk * group
                near = pl.ds(pl.multiple_of((seq * win * per + t) * TILE, TILE), group * TILE)
                counted = jnp.concatenate(
                    [c.astype(F32) for c in counted_keys(cols, segk, at, seq, q_tile * TILE, t, group, tok_dev, win)], axis=1
                )
                kept = lse_ref[at, :]
                d_query = jnp.zeros((TILE, q_width), F32)
                d_key = jnp.zeros((group * TILE, q_width), F32)
                d_value = jnp.zeros((group * TILE, q_width), F32)
                for h in range(heads):
                    mine, ours = head_only(q_ref[at, :], h), head_only(grad_seq[...], h)
                    score = jnp.where(counted > 0.0, dot_t(mine, k_ref[near, :]) * 0.125, -1e30)
                    prob = jnp.exp(score - kept[:, h : h + 1]) * counted
                    d_score = (prob * (dot_t(ours, v_ref[near, :]) - delta[h])).astype(BF16)
                    d_query = d_query + jnp.dot(d_score, head_only(k_ref[near, :], h), preferred_element_type=F32)
                    d_key = d_key + dot_rows(d_score, mine)
                    d_value = d_value + dot_rows(prob.astype(BF16), ours)
                    step(kk * heads + h)
                dq[...] += d_query
                dk[near, :] += d_key * 0.125
                dv[near, :] += d_value

            loop(0, tiles // group, key_tiles)
            dqb[at, :] = (dq[...] * 0.125).astype(BF16)

        def latent_rows(shard, seq, i):
            return pl.ds(pl.multiple_of((seq * win + shard) * tok_dev + i * wide, wide), wide)

        def send(k, seq, i):
            at = pl.ds(pl.multiple_of(seq * tok_dev + i * wide, wide), wide)
            return remote(lat_parts.at[latent_rows(own_shard - k, seq, i)], came.at[k - 1, at],
                          c_sent.at[k - 1, seq, i], c_recv.at[k - 1, seq, i], {"ctx": x - k})

        def latents(seq):
            for k in range(win - 1, -1, -1):
                for i in range(seq_pieces):
                    at = latent_rows(own_shard - k, seq, i)
                    lat_parts[at, :] = (
                        dot_t(dk[at, :].astype(BF16), wk[...]) + dot_t(dv[at, :].astype(BF16), wv[...])
                    ).astype(BF16)
                    if k > 0:

                        @pl.when(x - k >= 0)
                        def _(k=k, i=i):
                            send(k, seq, i).start()

        def whole_latent(j):
            seq, i = j // seq_pieces, lax.rem(j, seq_pieces)
            at = pl.ds(pl.multiple_of(j * wide, wide), wide)
            dlat[at, :] = lat_parts[latent_rows(own_shard, seq, i), :]
            for k in range(1, win):

                @pl.when(x + k < ctx)
                def _(k=k):
                    wait_came(came.at[k - 1, at], c_sent.at[k - 1, seq, i], c_recv.at[k - 1, seq, i])
                    dlat[at, :] = (dlat[at, :].astype(F32) + came[k - 1, at, :].astype(F32)).astype(BF16)

            p_one[at, :] = (dot_t(dqb[at, :], wq[...]) + dot_t(dlat[at, :], wl[...])).astype(BF16)

        tile_steps = (tiles // group) * heads
        every = max(tile_steps // 4, 1)

        def sequence(seq):
            def tile(i):
                def step(j):
                    @pl.when(lax.rem(j, every) == 0)
                    def _():
                        feed.step(i * (tile_steps // every) + j // every)

                query_tile(i, step)

            loop(seq * per, seq * per + per, tile)
            latents(seq)

        loop(0, seq_dev, sequence)
        fed = seq_dev * per * (tile_steps // every)

        bring.wait([2, 3, 4, 5])

        def product(i):
            at = pl.ds(pl.multiple_of(i * wide, wide), wide)
            parts[0][at, :] = dot_rows(xn[:, at], dqb[...]).astype(BF16)
            parts[3][:, at] = dot_rows(att[...], dbr[:, at]).astype(BF16)

        def steps(s):
            first.step(s)
            feed.step(fed + s)

        early = (seq_dev - 1) * seq_pieces
        loop(0, early, whole_latent)

        def mixed_work(i):
            product(i)
            steps(i)

        loop(0, width // wide, mixed_work)
        s0 = width // wide
        if grad_ffn is not None:
            grad_ffn.third()
        parts[1][...] = dot_rows(la[...], dk[...].astype(BF16)).astype(BF16)
        parts[2][...] = dot_rows(la[...], dv[...].astype(BF16)).astype(BF16)
        loop(early, rows // wide, whole_latent)

        def product_lat(s):
            at = pl.ds(pl.multiple_of((s - s0) * wide, wide), wide)
            parts[4][at, :] = dot_rows(xn[:, at], dlat[...]).astype(BF16)
            steps(s)

        begun = s0 + width // wide
        loop(s0, begun, product_lat)
        grad.start()

        def gains_of(s):
            steps(s)
            at = pl.ds(pl.multiple_of((s - begun) * side, side), side)
            value = p_one[at, :].astype(F32) * (tok[at, :].astype(F32) * cols[at, R_ONE : R_ONE + 1])
            gacc[...] += jnp.sum(value.reshape(side // 8, 8, width), axis=0)
            along = lax.dot_general(jnp.ones((8, width), F32), value * g1[...], (((1,), (1,)), ((), ())),
                                    precision=lax.Precision.HIGHEST, preferred_element_type=F32)
            sm[3:4, at] = along[0:1, :]
            sm[4:5, at] = marks[at, :].T[0:1, :]
            sm[5:6, at] = cols[at, :].T[R_ONE : R_ONE + 1, :]

        mark = begun + rows // side
        loop(begun, begun + 1, gains_of)
        grad.pair()
        grad.second()
        loop(begun + 1, begun + 4, gains_of)
        grad.third()
        loop(begun + 4, mark, gains_of)
        last = first.steps()
        for s in range(fed + mark, feed.steps()):
            feed.step(s)
        lane = lax.broadcasted_iota(jnp.int32, (1, many), 1)
        once = jnp.where(lax.axis_index("tp") == 0, 1.0, 0.0)
        row = jnp.zeros((1, many), F32)

        def whole_sum(value):
            return jnp.sum(jnp.sum(value, axis=0, keepdims=True), axis=1, keepdims=True)

        for q in range(seq_dev):
            values = [
                whole_sum(sacc[q]),
                whole_sum(sacc[seq_dev + q]),
                whole_sum(bsq[8 * q : 8 * q + 8, :]) * once,
                jnp.sum(cols[q * tok_dev : (q + 1) * tok_dev, VALID : VALID + 1], axis=0, keepdims=True) * once,
            ]
            for j, value in enumerate(values):
                row = row + jnp.where(lane == 4 * q + j, value, 0.0)
        sm[2:3, :] = row
        sm[0:1, 0:width] = jnp.sum(gacc[...], axis=0, keepdims=True)
        sm[1:2, 0:width] = jnp.sum(gain_two[...], axis=0, keepdims=True)
        r_row = sm[5:6, :]
        over_tp.start(sm[...])

        def store(a, at, total):
            if a < 4:
                outs[a][at, :] = total
            else:
                lat_own[at, :] = total.astype(BF16)

        def store_ffn(a, at, total):
            fouts[a][at, :] = total

        grad.fourth(store)
        line.start()
        loop(mark, mark + 2, steps)
        line.relay([1])
        along_tp = over_tp.finish()
        over_ctx.start(along_tp)
        loop(mark + 2, mark + 4, steps)
        if n > 2:
            line.relay([2])
        along_ctx = over_ctx.finish()
        over_fsdp.start(along_ctx)
        if grad_ffn is not None:
            grad_ffn.fourth(store_ffn)
        loop(mark + 4, last, steps)
        if n > 3:
            line.relay(range(3, n))
        everywhere = over_fsdp.finish()
        row = lax.broadcasted_iota(jnp.int32, everywhere.shape, 0)
        o_small[...] = jnp.where(row < 2, everywhere, along_ctx)
        o_small[3:4, :] = (along_tp[4:5] + eps * r_row * r_row * r_row * along_tp[3:4]) * (1.0 / width**0.5)
        line.finish()

        def gather(i):
            at = pl.ds(pl.multiple_of(i * 16, 16), 16)
            for g in range(GROUPS):
                total = jnp.zeros((16, lat[1]), F32)
                for t in range(n):
                    if t * GROUPS // n == g:
                        total = total + lat_every[t, at, :].astype(F32)
                outs[4][at, g * lat[1] : (g + 1) * lat[1]] = total

        loop(0, lat[0] // 16, gather)
        for k in range(1, win):

            @pl.when(x - k >= 0)
            def _(k=k):
                for seq in range(seq_dev):
                    for i in range(seq_pieces):
                        send(k, seq, i).wait_send()

        feed.drain()
        first.drain()
        grad.drain_pair()
        grad.drain()
        if grad_ffn is not None:
            grad_ffn.drain()

    out = pl.pallas_call(
        kernel,
        out_shape=(
            shape_of((rows, width), BF16),
            shape_of((rows, width), BF16),
            shape_of((8, many), F32),
        )
        + tuple(shape_of(b, F32) for b in blocks[:-1])
        + (shape_of((lat[0], GROUPS * lat[1]), F32),)
        + tuple(shape_of(f, F32) for f in ffn),
        in_specs=[VMEM] * 13 + [ANY] * 2 + [VMEM] + [ANY] * 4 + [VMEM] * (3 + len(ffn)),
        out_specs=(VMEM,) * (8 + len(ffn)),
        scratch_shapes=LineSum.scratch(n, rows, width, chunk) * 2
        + GradSum.scratch(fsdp, ctx, blocks)
        + GradSum.semaphores(fsdp, ctx, 5)
        + [pltpu.VMEM(w, BF16) for w in whole]
        + [
            pltpu.VMEM((rows, width), BF16),
            pltpu.VMEM((rows, latent), BF16),
            pltpu.VMEM((max(win - 1, 1), rows, latent), BF16),
            pltpu.SemaphoreType.DMA((max(win - 1, 1), seq_dev, seq_pieces)),
            pltpu.SemaphoreType.DMA((max(win - 1, 1), seq_dev, seq_pieces)),
            pltpu.VMEM((8, width), F32),
            pltpu.VMEM((8, many), F32),
            pltpu.VMEM((2 * seq_dev, 8, width), F32),
            pltpu.VMEM((win * rows, q_width), F32),
            pltpu.VMEM((win * rows, q_width), F32),
            pltpu.VMEM((TILE, q_width), F32),
            pltpu.VMEM((rows, q_width), BF16),
            pltpu.VMEM((TILE, q_width), BF16),
            pltpu.VMEM((win * rows, latent), BF16),
        ]
        + [
            pltpu.VMEM((win * rows, latent), BF16),
            pltpu.VMEM((rows, width), BF16),
            pltpu.VMEM((rows, width), BF16),
            pltpu.VMEM((half, width), F32),
            pltpu.VMEM((half, width), F32),
            pltpu.VMEM((rows, width), BF16),
            pltpu.SemaphoreType.DMA((6,)),
        ]
        + [pltpu.VMEM(lat, BF16), pltpu.VMEM((n,) + lat, BF16)]
        + RowGather.scratch(n)
        + AxisSum.scratch(n, (8, many))
        + AxisSum.scratch(ctx, (8, many))
        + AxisSum.scratch(fsdp, (8, many))
        + (GradSum.scratch(fsdp, ctx, ffn, False) + GradSum.semaphores(fsdp, ctx, len(ffn)) if ffn else []),
        compiler_params=params(3, 64),
    )(query, keys, values, seg_all, cols, lse, attended, d_branch, wo_rows, w_qry, w_lat, w_kproj, w_vproj,
      lat_all, xn_one, gains, tokens, d_middle, mid_own, part_feed, marks, gain_part, branch_sq, *firsts)
    return out[:3], out[3:8], out[8:]


def publish(arrays, small, seq_dev, tok_dev, feat_dim, fsdp):
    count = len(arrays)
    per = feat_dim // fsdp

    def kernel(*refs):
        srcs, sm, refs = refs[:count], refs[count], refs[count + 1 :]
        dsts, (gain1, gain2, stats, radial), refs = refs[:count], refs[count : count + 4], refs[count + 4 :]
        inward = Bring(list(zip(srcs, refs[:count])), refs[count])
        outward = Bring(list(zip(refs[:count], dsts)), refs[count + 1])
        inward.start()
        f = lax.axis_index("fsdp")
        mine = pl.ds(pl.multiple_of(f * per, per), per)
        gain1[...] = sm[0:1, mine].reshape(per)
        gain2[...] = sm[1:2, mine].reshape(per)
        for q in range(seq_dev):
            radial[q : q + 1, :] = sm[3:4, q * tok_dev : (q + 1) * tok_dev]
            total = sm[2:3, 4 * q + 3 : 4 * q + 4] * feat_dim
            for j, lane in enumerate((0, 2, 1)):
                stats[q : q + 1, j : j + 1] = jnp.sqrt(sm[2:3, 4 * q + lane : 4 * q + lane + 1] / total)
        for i in range(count):
            inward.wait([i])
            outward.start([i])
        outward.wait()

    out = pl.pallas_call(
        kernel,
        out_shape=tuple(shape_of(a.shape, a.dtype) for a in arrays)
        + (shape_of((per,), F32),) * 2
        + (shape_of((seq_dev, 3), F32), shape_of((seq_dev, tok_dev), F32)),
        in_specs=[ANY] * count + [VMEM],
        out_specs=(ANY,) * count + (VMEM,) * 4,
        scratch_shapes=[pltpu.VMEM(a.shape, a.dtype) for a in arrays] + [pltpu.SemaphoreType.DMA((count,))] * 2,
        compiler_params=pltpu.CompilerParams(vmem_limit_bytes=60 << 20),
    )(*arrays, small)
    return out[:count], out[count:]


class AxisShare:
    def __init__(self, axis, n, src, dst, recv, sent, own):
        self.axis, self.n, self.src, self.dst = axis, n, src, dst
        self.recv, self.sent, self.own = recv, sent, own
        self.at = lax.axis_index(axis)

    def start(self):
        for k in range(1, self.n):
            remote(self.src, self.dst.at[self.at], self.sent.at[k - 1], self.recv.at[self.at],
                   {self.axis: lax.rem(self.at + k, self.n)}).start()
        pltpu.make_async_copy(self.src, self.dst.at[self.at], self.own).start()

    def finish(self):
        for k in range(1, self.n):
            other = lax.rem(self.at + k, self.n)
            wait_came(self.dst.at[other], self.sent.at[k - 1], self.recv.at[other])
            wait_sent(self.src, self.sent.at[k - 1], self.recv.at[other])
        pltpu.make_async_copy(self.src, self.dst.at[self.at], self.own).wait()

    @staticmethod
    def scratch(n):
        return CtxShare.scratch(n)


class HalfSpread:
    def __init__(self, fsdp, pairs, recv, sent, own):
        self.fsdp, self.pairs, self.recv, self.sent, self.own = fsdp, pairs, recv, sent, own
        self.f, self.x = lax.axis_index("fsdp"), lax.axis_index("ctx")
        self.ys = fsdp // 2

    def view(self, a, f, half=None):
        src, dst = self.pairs[a]
        rows, size = src.shape
        columns = pl.ds(pl.multiple_of(f * size, size), size)
        if half is None:
            return dst.at[:, columns]
        return dst.at[pl.ds(pl.multiple_of(half * (rows // 2), rows // 2), rows // 2), columns]

    def part(self, a):
        src = self.pairs[a][0]
        return src.at[pl.ds(pl.multiple_of(self.x * (src.shape[0] // 2), src.shape[0] // 2), src.shape[0] // 2)]

    def start(self, which):
        for a in which:
            for k in range(1, self.ys):
                remote(self.part(a), self.view(a, self.f, self.x), self.sent.at[a, 0, k - 1], self.recv.at[a, 0, k - 1],
                       {"fsdp": lax.rem(self.f + 2 * k, self.fsdp)}).start()
        for a in which:
            src = self.pairs[a][0]
            remote(src, self.view(a, self.f), self.sent.at[a, 1, 0], self.recv.at[a, 1, 0],
                   {"fsdp": sibling(self.f)}).start()
            pltpu.make_async_copy(src, self.view(a, self.f), self.own.at[a]).start()

    def source(self, k):
        return lax.rem(self.f - 2 * k + self.fsdp, self.fsdp)

    def relay(self, which):
        for a in which:
            for k in range(1, self.ys):
                here = self.view(a, self.source(k), self.x)
                wait_came(here, self.sent.at[a, 0, k - 1], self.recv.at[a, 0, k - 1])
                remote(here, here, self.sent.at[a, 2, k - 1], self.recv.at[a, 2, k - 1], {"ctx": 1 - self.x}).start()
                remote(here, here, self.sent.at[a, 3, k - 1], self.recv.at[a, 3, k - 1],
                       {"fsdp": sibling(self.f)}).start()

    def cross(self, which):
        for a in which:
            for k in range(1, self.ys):
                here = self.view(a, self.source(k), 1 - self.x)
                wait_came(here, self.sent.at[a, 2, k - 1], self.recv.at[a, 2, k - 1])
                remote(here, here, self.sent.at[a, 4, k - 1], self.recv.at[a, 4, k - 1],
                       {"fsdp": sibling(self.f)}).start()

    def finish(self, which):
        for a in which:
            src = self.pairs[a][0]
            other = sibling(self.f)
            wait_came(self.view(a, other), self.sent.at[a, 1, 0], self.recv.at[a, 1, 0])
            pltpu.make_async_copy(src, self.view(a, self.f), self.own.at[a]).wait()
            for k in range(1, self.ys):
                there = lax.rem(other - 2 * k + self.fsdp, self.fsdp)
                wait_came(self.view(a, there, self.x), self.sent.at[a, 3, k - 1], self.recv.at[a, 3, k - 1])
                wait_came(self.view(a, there, 1 - self.x), self.sent.at[a, 4, k - 1], self.recv.at[a, 4, k - 1])

    def drain(self, which):
        for a in which:
            wait_sent(self.view(a, self.f), self.sent.at[a, 1, 0], self.recv.at[a, 1, 0])
            for k in range(1, self.ys):
                for kind in (0, 2, 3, 4):
                    wait_sent(self.part(a), self.sent.at[a, kind, k - 1], self.recv.at[a, kind, k - 1])

    @staticmethod
    def scratch(fsdp, arrays):
        return [
            pltpu.SemaphoreType.DMA((arrays, 5, max(fsdp // 2 - 1, 1))),
            pltpu.SemaphoreType.DMA((arrays, 5, max(fsdp // 2 - 1, 1))),
            pltpu.SemaphoreType.DMA((arrays,)),
        ]


R_TWO, MARK, LSE = 3, 4, 8


def layer(tokens, gain1, gain2, w_latent, shards, w_out, wide_shards, segments, out_grad, fsdp, ctx, n):
    rows, width = tokens.shape
    seq_dev, tok_dev = segments.shape
    w_query = shards[0]
    latent, q_width, inner = LATENT, w_query.shape[1], wide_shards[0].shape[0]
    heads = q_width // HEAD_DIM
    per = tok_dev // TILE
    win, span = window(ctx, tok_dev), key_span(ctx, tok_dev)
    own_shard = win - 1
    tiles = span + 1
    keyed = win * rows
    per_group = HEADS // GROUPS * HEAD_DIM
    wide, chunk = 128, 256
    pieces = rows // chunk
    per_seq = tok_dev // chunk
    strip, hop, reach, behind = 32, 2, 3, 2
    piece = 64
    per_block = TILE // piece
    side = 128
    many = max(width, rows)
    q_tiles = rows // TILE
    steps_all = rows // 2 // strip
    lag = hop * 2 * (n // 2)
    ffn = (inner, width // fsdp)
    axes = (0, 0, 0, 1, 0)
    whole = ((width, q_width), (latent, q_width), (latent, q_width), (q_width, width), (width, latent))
    blocks = [GradSum.block_shape(w, a, fsdp) for w, a in zip(whole, axes)]
    lat = blocks[-1]
    cols_at = width // 4

    scratch = dict(
        gbuf=pltpu.VMEM((8, gain1.shape[0]), F32),
        sbuf=pltpu.VMEM((8, tok_dev), segments.dtype),
        gain=pltpu.VMEM((8, width), F32),
        segk=pltpu.VMEM((ctx, 8, tok_dev), segments.dtype),
        cols=pltpu.VMEM((rows, 128), F32),
        tok=pltpu.VMEM((rows, width), BF16),
        gathered=pltpu.VMEM((rows, n * q_width), BF16),
        wo=pltpu.VMEM((n * q_width, width), BF16),
        cot=pltpu.VMEM((rows, width), BF16),
        xn=pltpu.VMEM((rows, width), BF16),
        p_two=pltpu.VMEM((rows, width), BF16),
        p_feed=pltpu.VMEM((rows, width), BF16),
        left=pltpu.VMEM((rows, width), BF16),
        right=pltpu.VMEM((rows, width), BF16),
        branch=pltpu.VMEM((rows, width), BF16),
        mid=pltpu.VMEM((rows, width), F32),
        wg=pltpu.VMEM((inner, width), BF16),
        wu=pltpu.VMEM((inner, width), BF16),
        wd=pltpu.VMEM((inner, width), BF16),
        hid=pltpu.VMEM((rows, inner), BF16),
        dg=pltpu.VMEM((rows, inner), BF16),
        du=pltpu.VMEM((rows, inner), BF16),
        w_lat=pltpu.VMEM((width, latent), BF16),
        w_qry=pltpu.VMEM((width, q_width), BF16),
        w_kproj=pltpu.VMEM((latent, q_width), BF16),
        w_vproj=pltpu.VMEM((latent, q_width), BF16),
        wo_rows=pltpu.VMEM((q_width, width), BF16),
        wo_line=pltpu.VMEM((n,) + w_out.shape, BF16),
        lat_all=pltpu.VMEM((keyed, latent), BF16),
        query=pltpu.VMEM((rows, q_width), BF16),
        keys=pltpu.VMEM((keyed, q_width), BF16),
        values=pltpu.VMEM((keyed, q_width), BF16),
        att=pltpu.VMEM((rows, q_width), BF16),
        dk=pltpu.VMEM((keyed, q_width), F32),
        dv=pltpu.VMEM((keyed, q_width), F32),
        dqb=pltpu.VMEM((rows, q_width), BF16),
        grad_seq=pltpu.VMEM((TILE, q_width), BF16),
        lat_parts=pltpu.VMEM((keyed, latent), BF16),
        dlat=pltpu.VMEM((rows, latent), BF16),
        came=pltpu.VMEM((rows, latent), BF16),
        g_sum=pltpu.VMEM((8, width), F32),
        g_sum2=pltpu.VMEM((8, width), F32),
        sm=pltpu.VMEM((8, many), F32),
        sacc=pltpu.VMEM((3 * seq_dev, 8, width), F32),
        lat_own=pltpu.VMEM(lat, BF16),
        lat_every=pltpu.VMEM((n, lat[0] // 2, lat[1]), BF16),
        lat_sum=pltpu.VMEM((lat[0] // 2, GROUPS * lat[1]), BF16),
        lat_both=pltpu.VMEM((ctx, lat[0] // 2, GROUPS * lat[1]), BF16),
        local=pltpu.SemaphoreType.DMA((2,)),
        flush=pltpu.SemaphoreType.DMA((11,)),
        lat_recv=pltpu.SemaphoreType.DMA((pieces,)),
        lat_sent=pltpu.SemaphoreType.DMA((pieces,)),
        c_recv=pltpu.SemaphoreType.DMA((seq_dev, per_seq)),
        c_sent=pltpu.SemaphoreType.DMA((seq_dev, per_seq)),
    )
    out_blocks = [shape_of(b, F32) for b in blocks[:-1]] + [shape_of((lat[0], GROUPS * lat[1]), F32)]
    out_blocks += [shape_of(ffn, F32)] * 3
    groups = dict(
        outs=[pltpu.VMEM(o.shape, F32) for o in out_blocks[:5]],
        held=GradSum.scratch(fsdp, ctx, [ffn] * 3 + blocks),
        parts=[pltpu.VMEM(w, BF16) for w in whole],
        spread=Spread.scratch(fsdp, 5),
        half=HalfSpread.scratch(fsdp, 4),
        share=CtxShare.scratch(ctx),
        wline=RowGather.scratch(n),
        gather=LineGather.scratch(n, rows // piece)[1:],
        two=LineSum.scratch(n, rows, width, strip)[2:],
        feed=LineSum.scratch(n, rows, width, strip)[2:],
        gffn=GradSum.semaphores(fsdp, ctx, 3),
        gatt=GradSum.semaphores(fsdp, ctx, 5),
        lline=AxisShare.scratch(n),
        xline=AxisShare.scratch(ctx),
        s_tp=AxisSum.scratch(n, (8, many)),
        s_ctx=AxisSum.scratch(ctx, (8, many)),
        s_fsdp=AxisSum.scratch(fsdp, (8, many)),
    )
    names = list(scratch)
    shapes = list(scratch.values())
    places = {}
    for key, some in groups.items():
        places[key] = (len(shapes), len(shapes) + len(some))
        shapes = shapes + list(some)

    def kernel(*refs):
        (tok_in, ga, gb, wlat, wq, wkp, wvp, wout, wgt, wut, wdn, seg, cot_in), refs = refs[:13], refs[13:]
        (o_mixed, o_tok), o_blocks, o_small, refs = refs[:2], refs[2:10], refs[10], refs[11:]
        r = SimpleNamespace(**dict(zip(names, refs)))
        g = SimpleNamespace(**{key: refs[a:b] for key, (a, b) in places.items()})
        cols, tok, cot, xn, mid = r.cols, r.tok, r.cot, r.xn, r.mid
        gain, segk = r.gain, r.segk
        x, me = lax.axis_index("ctx"), lax.axis_index("tp")
        outs = list(g.outs) + [mid.at[0 : ffn[0], i * ffn[1] : (i + 1) * ffn[1]] for i in range(3)]

        load = Bring([(tok_in, tok), (cot_in, cot)], r.local)
        load.start()
        r.gbuf[...] = jnp.zeros_like(r.gbuf)
        r.gbuf[0:1, :] = ga[...].astype(F32).reshape(1, -1)
        r.gbuf[1:2, :] = gb[...].astype(F32).reshape(1, -1)
        r.sbuf[...] = jnp.zeros_like(r.sbuf)
        r.sbuf[0:seq_dev, :] = seg[...]
        meet(n, fsdp, ctx)

        group = me * q_width // per_group
        src_lat = wlat.at[:, pl.ds(pl.multiple_of(group * latent, latent), latent)]
        spread = Spread(
            fsdp,
            [(r.gbuf, gain), (src_lat, r.w_lat), (wq, r.w_qry), (wkp, r.w_kproj), (wvp, r.w_vproj)],
            [1, 0, 0, 0, 0], *g.spread,
        )
        share = CtxShare(ctx, r.sbuf, segk, *g.share)
        wline = RowGather(n, wout, r.wo_line, *g.wline)
        half = HalfSpread(
            fsdp,
            [(wgt, r.wg), (wut, r.wu), (wdn, r.wd), (r.wo_line.reshape(n * q_width, w_out.shape[1]), r.wo)],
            *g.half,
        )
        spread.start()
        share.start()
        wline.start()
        half.start([0, 1, 2])
        cols[...] = jnp.zeros_like(cols)
        r.g_sum[...] = jnp.zeros_like(r.g_sum)
        r.g_sum2[...] = jnp.zeros_like(r.g_sum2)
        r.sacc[...] = jnp.zeros_like(r.sacc)
        r.sm[...] = jnp.zeros_like(r.sm)
        load.wait([0])

        def scale(i):
            at = pl.ds(pl.multiple_of(i * wide, wide), wide)
            value = tok[at, :].astype(F32)
            cols[at, R_ONE : R_ONE + 1] = lax.rsqrt(jnp.mean(value * value, axis=-1, keepdims=True) + eps)

        loop(0, rows // wide, scale)
        spread.relay([0, 1])
        spread.finish([0, 1])
        wline.relay([1])
        lat_all = r.lat_all

        def place(shard, i):
            seq = i // per_seq
            return pl.ds(pl.multiple_of((seq * win + shard) * tok_dev + lax.rem(i, per_seq) * chunk, chunk), chunk)

        def pass_on(i):
            return remote(lat_all.at[place(own_shard, i)], lat_all.at[place(own_shard - 1, i)], r.lat_sent.at[i],
                          r.lat_recv.at[i], {"ctx": x + 1})

        def first_norm(i):
            at = pl.ds(pl.multiple_of(i * chunk, chunk), chunk)
            unit = (tok[at, :].astype(F32) * cols[at, R_ONE : R_ONE + 1] * gain[0:1, :]).astype(BF16)
            xn[at, :] = unit
            lat_all[place(own_shard, i), :] = dot(unit, r.w_lat[...]).astype(BF16)

            @pl.when(x + 1 < ctx)
            def _():
                pass_on(i).start()

        loop(0, pieces, first_norm)
        if n > 2:
            wline.relay([2])
        spread.relay([2, 3, 4])
        spread.finish([2, 3, 4])

        def project(shard, i):
            to = place(shard, i)
            value = lat_all[to, :]
            r.keys[to, :] = dot(value, r.w_kproj[...]).astype(BF16)
            r.values[to, :] = dot(value, r.w_vproj[...]).astype(BF16)

        def ask(i):
            at = pl.ds(pl.multiple_of(i * chunk, chunk), chunk)
            r.query[at, :] = dot(xn[at, :], r.w_qry[...]).astype(BF16)
            project(own_shard, i)

        loop(0, pieces, ask)
        share.finish()
        for q in range(seq_dev):
            at = slice(q * tok_dev, (q + 1) * tok_dev)
            ids = jnp.broadcast_to(r.sbuf[q : q + 1, :].astype(F32), (128, tok_dev)).T
            cols[at, SEGMENT : SEGMENT + 1] = ids[:, 0:1]
            final = segk[ctx - 1, q : q + 1, tok_dev - 1 : tok_dev].astype(F32)
            cols[at, VALID : VALID + 1] = jnp.where(ids[:, 0:1] != final, 1.0, 0.0)
        half.relay([0, 1])

        def theirs(i):
            @pl.when(x - 1 >= 0)
            def _():
                wait_came(lat_all.at[place(own_shard - 1, i)], r.lat_sent.at[i], r.lat_recv.at[i])

            @pl.when(x - 1 < 0)
            def _():
                lat_all[place(own_shard - 1, i), :] = jnp.zeros((chunk, latent), BF16)

            project(own_shard - 1, i)

        att, gathered = r.att, r.gathered
        line = LineGather(n, piece, att, gathered, g.feed[0], *g.gather, hop=reach)

        def query_tile(i):
            seq = i // per
            q_tile = own_shard * per + lax.rem(i, per)
            at = pl.ds(pl.multiple_of(i * TILE, TILE), TILE)
            near = pl.ds(pl.multiple_of((seq * win * per + q_tile - span) * TILE, TILE), tiles * TILE)
            counted = jnp.concatenate(
                [
                    c.astype(F32)
                    for c in counted_keys(cols, segk, at, seq, q_tile * TILE, q_tile - span, tiles, tok_dev, win)
                ],
                axis=1,
            )
            accum = jnp.zeros((TILE, q_width), F32)
            for h in range(heads):
                score = dot_t(head_only(r.query[at, :], h), r.keys[near, :]) * 0.125
                score = jnp.where(counted > 0.0, score, -1e30)
                top = jnp.max(score, axis=-1, keepdims=True)
                weight = jnp.exp(score - top)
                total = jnp.sum(weight, axis=-1, keepdims=True)
                prob = (weight * (1.0 / total)).astype(BF16)
                accum = accum + jnp.dot(prob, head_only(r.values[near, :], h), preferred_element_type=F32)
                cols[at, LSE + h : LSE + h + 1] = top + jnp.log(total)
                line.step((i - 1) * per_block + h * per_block // heads)
            att[at, :] = accum.astype(BF16)

        def sequence_forward(seq):
            loop(seq * per_seq, seq * per_seq + per_seq, theirs)

            @pl.when(seq == 0)
            def _():
                if n > 3:
                    wline.relay(range(3, n))
                wline.finish()
                half.start([3])

            loop(seq * per, seq * per + per, query_tile)

            @pl.when(seq == 0)
            def _():
                half.relay([2, 3])

        loop(0, seq_dev, sequence_forward)
        s1 = (q_tiles - 1) * per_block
        line.begin()
        half.cross([0, 1, 2, 3])
        loop(s1, per_block + reach * (n - 1), line.step)
        s1 = per_block + reach * (n - 1)
        half.finish([3, 0, 1, 2])
        half.drain([0, 1, 2, 3])
        r.wo_rows[...] = r.wo[pl.ds(pl.multiple_of(me * q_width, q_width), q_width), :]
        line.begun()
        load.wait([1])

        p_two, p_feed, wg, wu, wd = r.p_two, r.p_feed, r.wg, r.wu, r.wd

        def second_back(at, own, total):
            unit = mid[at, :] * cols[at, R_TWO : R_TWO + 1]
            r.g_sum2[...] += jnp.sum((total * unit).reshape(strip // 8, 8, width), axis=0)
            scaled = total * gain[1:2, :]
            mean = jnp.mean(scaled * unit, axis=-1, keepdims=True)
            d_mid = cot[at, :].astype(F32) + cols[at, R_TWO : R_TWO + 1] * (scaled - unit * mean)
            first_unit = tok[at, :].astype(F32) * cols[at, R_ONE : R_ONE + 1]
            cols[at, MARK : MARK + 1] = jnp.sum(first_unit * d_mid, axis=-1, keepdims=True)
            return d_mid.astype(BF16)

        def forward(at, own, total):
            mixed = mid[at, :] + total
            seq = at.start // tok_dev
            counted = cols[at, VALID : VALID + 1]
            r.sacc[seq] += jnp.sum((mixed * mixed * counted).reshape(strip // 8, 8, width), axis=0)
            r.sacc[seq_dev + seq] += jnp.sum((total * total * counted).reshape(strip // 8, 8, width), axis=0)
            return mixed.astype(BF16)

        def first_back(at, own, total):
            r1 = cols[at, R_ONE : R_ONE + 1]
            unit = tok[at, :].astype(F32) * r1
            scaled = total * gain[0:1, :]
            mean = jnp.mean(scaled * unit, axis=-1, keepdims=True)
            return (r.branch[at, :].astype(F32) + r1 * (scaled - unit * mean)).astype(BF16)

        two = LineSum(n, strip, hop, p_two, r.left, r.right, r.branch, *g.two, second_back, pushed=True)
        feed = LineSum(n, strip, hop, p_feed, gathered, r.wo, xn, *g.feed, forward)
        one = LineSum(n, strip, hop, cot, r.left, r.right, p_two, *g.two, first_back)
        parts = [wg, wu, wd]
        gffn = GradSum(fsdp, ctx, parts, [1, 1, 1], None,
                       [g.held[3 * a : 3 * a + 3] for a in range(3)], *g.gffn)
        aparts = g.parts
        gatt = GradSum(fsdp, ctx, aparts, axes, None,
                       [g.held[3 * a : 3 * a + 3] for a in range(3, 8)], *g.gatt)

        def block_of_rows(b):
            at = pl.ds(pl.multiple_of(b * TILE, TILE), TILE)
            seq = b * TILE // tok_dev

            def steps(j):
                line.step(s1 + b * per_block + j)
                two.step((b - 1) * per_block + j - behind)

            branch = dot(gathered[at, :], r.wo[...])
            middle_rows = tok[at, :].astype(F32) + branch
            mid[at, :] = middle_rows
            r.sacc[2 * seq_dev + seq] += jnp.sum(
                (branch * branch * cols[at, VALID : VALID + 1]).reshape(TILE // 8, 8, width), axis=0
            )
            level = lax.rsqrt(jnp.mean(middle_rows * middle_rows, axis=-1, keepdims=True) + eps)
            cols[at, R_TWO : R_TWO + 1] = level
            unit = (middle_rows * level * gain[1:2, :]).astype(BF16)
            xn[at, :] = unit
            steps(0)
            gate = dot_t(unit, wg[...])
            upper = dot_t(unit, wu[...])
            sigma = jax.nn.sigmoid(gate)
            swish = gate * sigma
            hidden = (swish * upper).astype(BF16)
            r.hid[at, :] = hidden
            slope = upper * sigma * (1.0 + gate * (1.0 - sigma))
            steps(1)
            p_feed[at, :] = dot(hidden, wd[...]).astype(BF16)
            d_hidden = dot_t(cot[at, :], wd[...])
            d_gate = (d_hidden * slope).astype(BF16)
            d_upper = (d_hidden * swish).astype(BF16)
            r.dg[at, :] = d_gate
            r.du[at, :] = d_upper
            steps(2)
            p_two[at, :] = (dot(d_gate, wg[...]) + dot(d_upper, wu[...])).astype(BF16)
            steps(3)
            for j in range(per_block):
                two.push(b * per_block + j)

        loop(0, q_tiles, block_of_rows)
        s2 = (q_tiles - 1) * per_block - behind

        def product(i):
            at = pl.ds(pl.multiple_of(i * cols_at, cols_at), cols_at)
            left = xn[:, at]
            parts[0][:, at] = dot_rows(r.dg[...], left).astype(BF16)
            parts[1][:, at] = dot_rows(r.du[...], left).astype(BF16)
            parts[2][:, at] = dot_rows(r.hid[...], cot[:, at]).astype(BF16)

        def busy(s):
            two.step(s)
            product(s - s2)

        line.drain()
        loop(s2, s2 + 4, busy)
        gffn.start()
        s2 = s2 + 4

        dk, dv, dqb, grad_seq, lat_parts = r.dk, r.dv, r.dqb, r.grad_seq, r.lat_parts

        def clear(i):
            at = pl.ds(pl.multiple_of(i * TILE, TILE), TILE)
            dk[at, :] = jnp.zeros((TILE, q_width), F32)
            dv[at, :] = jnp.zeros((TILE, q_width), F32)

        loop(0, keyed // TILE, clear)
        ready = steps_all // seq_dev + lag
        loop(s2, ready, two.step)

        def grad_tile(i, step):
            seq = i // per
            q_tile = own_shard * per + lax.rem(i, per)
            at = pl.ds(pl.multiple_of(i * TILE, TILE), TILE)
            near = pl.ds(pl.multiple_of((seq * win * per + q_tile - span) * TILE, TILE), tiles * TILE)
            grad_seq[...] = dot_t(r.branch[at, :], r.wo_rows[...]).astype(BF16)
            inner_sum = grad_seq[...].astype(F32) * att[at, :].astype(F32)
            counted = jnp.concatenate(
                [
                    c.astype(F32)
                    for c in counted_keys(cols, segk, at, seq, q_tile * TILE, q_tile - span, tiles, tok_dev, win)
                ],
                axis=1,
            )
            d_query = jnp.zeros((TILE, q_width), F32)
            d_key = jnp.zeros((tiles * TILE, q_width), F32)
            d_value = jnp.zeros((tiles * TILE, q_width), F32)
            for h in range(heads):
                delta = jnp.sum(head_only(inner_sum, h), axis=-1, keepdims=True)
                asked, ours = head_only(r.query[at, :], h), head_only(grad_seq[...], h)
                score = jnp.where(counted > 0.0, dot_t(asked, r.keys[near, :]) * 0.125, -1e30)
                prob = jnp.exp(score - cols[at, LSE + h : LSE + h + 1]) * counted
                d_score = (prob * (dot_t(ours, r.values[near, :]) - delta)).astype(BF16)
                d_query = d_query + jnp.dot(d_score, head_only(r.keys[near, :], h), preferred_element_type=F32)
                d_key = d_key + dot_rows(d_score, asked)
                d_value = d_value + dot_rows(prob.astype(BF16), ours)
                step(h)
            dqb[at, :] = (d_query * 0.125).astype(BF16)
            dk[near, :] += d_key * 0.125
            dv[near, :] += d_value

        def send_latent(seq, i):
            j = seq * per_seq + i
            at = pl.ds(pl.multiple_of(j * chunk, chunk), chunk)
            return remote(lat_parts.at[place(own_shard - 1, j)], r.came.at[at], r.c_sent.at[seq, i],
                          r.c_recv.at[seq, i], {"ctx": x - 1})

        def latents(seq):
            for shard in (own_shard - 1, own_shard):
                for i in range(per_seq):
                    at = place(shard, seq * per_seq + i)
                    lat_parts[at, :] = (
                        dot_t(dk[at, :].astype(BF16), r.w_kproj[...])
                        + dot_t(dv[at, :].astype(BF16), r.w_vproj[...])
                    ).astype(BF16)
                    if shard < own_shard:

                        @pl.when(x - 1 >= 0)
                        def _(i=i):
                            send_latent(seq, i).start()

        def sequence(seq):
            def tile(i):
                def step(h):
                    t = (i * heads + h) * steps_per // heads
                    two.step(ready + t)
                    feed.step(t)

                grad_tile(i, step)

            loop(seq * per, seq * per + per, tile)
            latents(seq)

            @pl.when(seq == 0)
            def _():
                two.drain()
                gffn.pair()
                gffn.second()

        steps_per = heads
        loop(0, seq_dev, sequence)
        fed = q_tiles * steps_per

        def whole_latent(j):
            seq, i = j // per_seq, lax.rem(j, per_seq)
            at = pl.ds(pl.multiple_of(j * chunk, chunk), chunk)
            r.dlat[at, :] = lat_parts[place(own_shard, j), :]

            @pl.when(x + 1 < ctx)
            def _():
                wait_came(r.came.at[at], r.c_sent.at[seq, i], r.c_recv.at[seq, i])
                r.dlat[at, :] = (r.dlat[at, :].astype(F32) + r.came[at, :].astype(F32)).astype(BF16)

            cot[at, :] = (dot_t(dqb[at, :], r.w_qry[...]) + dot_t(r.dlat[at, :], r.w_lat[...])).astype(BF16)

        def first_unit_columns(at):
            return (tok[:, at].astype(F32) * cols[:, R_ONE : R_ONE + 1] * gain[0:1, at]).astype(BF16)

        early = (seq_dev - 1) * per_seq
        loop(0, early, whole_latent)

        def mixed_work(i):
            at = pl.ds(pl.multiple_of(i * chunk, chunk), chunk)
            aparts[0][at, :] = dot_rows(first_unit_columns(at), dqb[...]).astype(BF16)
            aparts[3][:, at] = dot_rows(att[...], r.branch[:, at]).astype(BF16)
            feed.step(fed + i)

        fed_later = fed + width // chunk
        loop(0, width // chunk, mixed_work)
        gffn.third()
        aparts[1][...] = dot_rows(lat_all[...], dk[...].astype(BF16)).astype(BF16)
        aparts[2][...] = dot_rows(lat_all[...], dv[...].astype(BF16)).astype(BF16)
        loop(early, pieces, whole_latent)

        def steps(s):
            one.step(s)
            feed.step(fed_later + s)

        def product_lat(s):
            at = pl.ds(pl.multiple_of(s * chunk, chunk), chunk)
            aparts[4][at, :] = dot_rows(first_unit_columns(at), r.dlat[...]).astype(BF16)
            steps(s)

        begun = width // chunk
        loop(0, begun, product_lat)
        gatt.start()

        def gains_of(i):
            at = pl.ds(pl.multiple_of(i * side, side), side)
            value = cot[at, :].astype(F32) * (tok[at, :].astype(F32) * cols[at, R_ONE : R_ONE + 1])
            r.g_sum[...] += jnp.sum(value.reshape(side // 8, 8, width), axis=0)
            along = lax.dot_general(jnp.ones((8, width), F32), value * gain[0:1, :], (((1,), (1,)), ((), ())),
                                    precision=lax.Precision.HIGHEST, preferred_element_type=F32)
            r.sm[3:4, at] = along[0:1, :]
            lines = cols[at, :].T
            r.sm[4:5, at] = lines[MARK : MARK + 1, :]
            r.sm[5:6, at] = lines[R_ONE : R_ONE + 1, :]

        def two_gains(s):
            steps(s)
            gains_of(2 * (s - begun))
            gains_of(2 * (s - begun) + 1)

        mark = begun + rows // side // 2
        loop(begun, begun + 1, two_gains)
        gatt.pair()
        gatt.second()
        loop(begun + 1, mark, two_gains)
        last = one.steps()
        for s in range(fed_later + mark, feed.steps()):
            feed.step(s)
        flush = r.flush
        out_mixed = pltpu.make_async_copy(xn, o_mixed, flush.at[8])
        out_mixed.start()
        lane = lax.broadcasted_iota(jnp.int32, (1, many), 1)
        once = jnp.where(me == 0, 1.0, 0.0)
        row = jnp.zeros((1, many), F32)

        def whole_sum(value):
            return jnp.sum(jnp.sum(value, axis=0, keepdims=True), axis=1, keepdims=True)

        for q in range(seq_dev):
            stats = [
                whole_sum(r.sacc[q]),
                whole_sum(r.sacc[seq_dev + q]),
                whole_sum(r.sacc[2 * seq_dev + q]) * once,
                jnp.sum(cols[q * tok_dev : (q + 1) * tok_dev, VALID : VALID + 1], axis=0, keepdims=True) * once,
            ]
            for j, value in enumerate(stats):
                row = row + jnp.where(lane == 4 * q + j, value, 0.0)
        r.sm[2:3, :] = row
        r.sm[0:1, 0:width] = jnp.sum(r.g_sum[...], axis=0, keepdims=True)
        r.sm[1:2, 0:width] = jnp.sum(r.g_sum2[...], axis=0, keepdims=True)
        r_row = r.sm[5:6, :]
        over_tp = AxisSum("tp", n, *g.s_tp)
        over_ctx = AxisSum("ctx", ctx, *g.s_ctx)
        over_fsdp = AxisSum("fsdp", fsdp, *g.s_fsdp)
        over_tp.start(r.sm[...])
        lat_half = pl.ds(pl.multiple_of(x * (lat[0] // 2), lat[0] // 2), lat[0] // 2)
        lline = AxisShare("tp", n, r.lat_own.at[lat_half], r.lat_every, *g.lline)
        xline = AxisShare("ctx", ctx, r.lat_sum, r.lat_both, *g.xline)
        outward = Bring([(outs[i], o_blocks[i]) for i in range(8)], flush)

        def store(a, at, total):
            if a < 4:
                outs[a][at, :] = total
            else:
                r.lat_own[at, :] = total.astype(BF16)

        def store_ffn(a, at, total):
            outs[5 + a][at, :] = total

        loop(mark, mark + 2, steps)
        gatt.third()
        along_tp = over_tp.finish()
        over_ctx.start(along_tp)
        gffn.fourth(store_ffn)
        outward.start([5, 6, 7])
        loop(mark + 2, mark + 4, steps)
        along_ctx = over_ctx.finish()
        over_fsdp.start(along_ctx)
        loop(mark + 4, mark + 6, steps)
        gatt.fourth(store)
        outward.start([0, 1, 2, 3])
        lline.start()
        everywhere = over_fsdp.finish()
        loop(mark + 6, mark + 10, steps)
        lline.finish()

        def latent_sum(i):
            at = pl.ds(pl.multiple_of(i * 16, 16), 16)
            for gr in range(GROUPS):
                total = jnp.zeros((16, lat[1]), F32)
                for t in range(n):
                    if t * GROUPS // n == gr:
                        total = total + r.lat_every[t, at, :].astype(F32)
                r.lat_sum[at, gr * lat[1] : (gr + 1) * lat[1]] = total.astype(BF16)

        loop(0, lat[0] // 32, latent_sum)
        xline.start()
        loop(mark + 10, mark + 13, steps)
        xline.finish()
        for k in range(ctx):
            outs[4][k * (lat[0] // 2) : (k + 1) * (lat[0] // 2), :] = r.lat_both[k].astype(F32)
        outward.start([4])
        row = lax.broadcasted_iota(jnp.int32, everywhere.shape, 0)
        o_small[...] = jnp.where(row < 2, everywhere, along_ctx)
        o_small[3:4, :] = (along_tp[4:5] + eps * r_row * r_row * r_row * along_tp[3:4]) * (1.0 / width**0.5)
        ahead = [pl.ds(0, rows // 2), pl.ds(rows // 2, rows // 2)]
        out_tok = Bring([(p_two.at[q], o_tok.at[q]) for q in ahead], flush.at[pl.ds(9, 2)])
        out_tok.start([0])
        loop(mark + 13, last, steps)
        out_tok.start([1])

        @pl.when(x + 1 < ctx)
        def _():
            loop(0, pieces, lambda i: pass_on(i).wait_send())

        @pl.when(x - 1 >= 0)
        def _():
            for seq in range(seq_dev):
                for i in range(per_seq):
                    send_latent(seq, i).wait_send()

        feed.drain()
        one.drain()
        gffn.drain_pair()
        gffn.drain()
        gatt.drain_pair()
        gatt.drain()
        outward.wait()
        out_mixed.wait()
        out_tok.wait()

    out = pl.pallas_call(
        kernel,
        out_shape=(shape_of((rows, width), BF16),) * 2 + tuple(out_blocks) + (shape_of((8, many), F32),),
        in_specs=[ANY] + [VMEM] * 2 + [ANY] * 8 + [VMEM, ANY],
        out_specs=(ANY,) * 10 + (VMEM,),
        scratch_shapes=shapes,
        compiler_params=params(1, 64),
    )(tokens, gain1, gain2, w_latent, *shards, w_out, *wide_shards, segments, out_grad)
    return out[0], out[1], out[2:7], out[7:10], out[10]


def three_kernels(tokens, gain1, gain2, w_latent, shards, w_out, wide_shards, segments, out_grad, fsdp, ctx, n):
    seq_dev, tok_dev = segments.shape
    gate, up, down = wide_shards
    (xn_one, cols, gains, w_lat, w_qry, w_kproj, w_vproj, gate_all, up_all, wo_cols, seg_all, lat_all,
     query, keys, values) = front(tokens, gain1, gain2, w_latent, shards, w_out, (gate, up), segments, fsdp, ctx, n)
    late = window(ctx, tok_dev) <= 2
    (d_branch, part_feed, d_middle, mid_own, wo_rows, gain_part, branch_sq, marks, attended, lse), ffn = middle(
        query, keys, values, seg_all, cols, (wo_cols.reshape(-1, w_out.shape[1]), down), gate_all, up_all, gains,
        tokens, out_grad, fsdp, ctx, n, seq_dev, late,
    )
    (grad_tokens, mixed, small), att_grads, late_ffn = back(
        query, keys, values, seg_all, cols, lse, attended, d_branch, wo_rows, (w_qry, w_lat, w_kproj, w_vproj),
        lat_all, xn_one, gains, tokens, d_middle, mid_own, part_feed, marks, gain_part, branch_sq,
        ffn if late else (), fsdp, ctx, n, seq_dev,
    )
    return mixed, grad_tokens, att_grads, late_ffn if late else ffn, small


def on_device(
    tokens, gain1, w_latent, w_query, w_key, w_value, w_out, gain2, w_gate, w_up, w_down, segments, cotangent
):
    seq_dev, tok_dev, feat_dim = tokens.shape
    n_ctx, n_tp, n_fsdp = lax.axis_size("ctx"), lax.axis_size("tp"), lax.axis_size("fsdp")
    row_count = seq_dev * tok_dev
    tok_rows = tokens.reshape(row_count, feat_dim)
    out_grad = cotangent.reshape(row_count, feat_dim)
    if n_ctx == 2 and n_fsdp >= 4 and w_down.shape[0] <= row_count and feat_dim <= row_count:
        mixed, grad_tokens, att_grads, ffn_grads, small = layer(
            tok_rows, gain1, gain2, w_latent, (w_query, w_key, w_value), w_out, (w_gate.T, w_up.T, w_down), segments,
            out_grad, n_fsdp, n_ctx, n_tp,
        )
    else:
        mixed, grad_tokens, att_grads, ffn_grads, small = three_kernels(
            tok_rows, gain1, gain2, w_latent, (w_query, w_key, w_value), w_out, (w_gate.T, w_up.T, w_down), segments,
            out_grad, n_fsdp, n_ctx, n_tp,
        )
    arrays, (gain_grad1, gain_grad2, stats, radial) = publish(
        (mixed, grad_tokens, *att_grads, *ffn_grads), small, seq_dev, tok_dev, feat_dim, n_fsdp
    )
    mixed, grad_tokens, s_qry, s_kproj, s_vproj, s_outp, s_lat, s_gate, s_up, s_down = arrays
    return (
        mixed.reshape(seq_dev, tok_dev, feat_dim),
        grad_tokens.reshape(seq_dev, tok_dev, feat_dim),
        gain_grad1,
        s_lat,
        s_qry,
        s_kproj,
        s_vproj,
        s_outp,
        gain_grad2,
        s_gate.T,
        s_up.T,
        s_down,
        stats,
        radial,
    )


def solution(mesh):
    return jax.shard_map(
        on_device,
        mesh=mesh,
        in_specs=(
            P("fsdp", "ctx", None),
            P("fsdp"),
            P("fsdp", None),
            P("fsdp", "tp"),
            P("fsdp", "tp"),
            P("fsdp", "tp"),
            P("tp", "fsdp"),
            P("fsdp"),
            P("fsdp", "tp"),
            P("fsdp", "tp"),
            P("tp", "fsdp"),
            P("fsdp", "ctx"),
            P("fsdp", "ctx", None),
        ),
        out_specs=(
            P("fsdp", "ctx", None),
            P("fsdp", "ctx", None),
            P("fsdp"),
            P("fsdp", None),
            P("fsdp", "tp"),
            P("fsdp", "tp"),
            P("fsdp", "tp"),
            P("tp", "fsdp"),
            P("fsdp"),
            P("fsdp", "tp"),
            P("fsdp", "tp"),
            P("tp", "fsdp"),
            P("fsdp", None),
            P("fsdp", "ctx"),
        ),
        check_vma=False,
    )
```
